32 devices in a mesh: dp: 16 (over z, x, core), tensor: 2 (over y).
Axes of the slice: x: 2, y: 2, z: 4, core: 2. Of those that a mesh axis runs over, the one named last changes fastest.
Arguments:
- hidden_in: bfloat16 [4096, 1536], P('dp', 'tensor'), may hold values from -6 to 6
- out_grad: bfloat16 [4096, 1536], P('dp', 'tensor'), may hold values from -6 to 6
- seq_lengths: int32 [16, 8], P('dp'), may hold values from 0 to 256, as said below
- deal_to: int32 [4096], P('dp'), may hold values from 0 to 4095, as said below
- pre_gain: bfloat16 [1536], replicated, may hold values from 0.5 to 1.5
- w_in: bfloat16 [1536, 2, 3072], P(None, None, 'tensor'), may hold values from -1 to 1
- w_state: bfloat16 [1536, 256], replicated, may hold values from -0.15625 to 0.15625
- w_step: bfloat16 [1536, 48], P(None, 'tensor'), may hold values from -0.15625 to 0.15625
- conv_x: bfloat16 [4, 3072], P(None, 'tensor'), may hold values from -3 to 3
- conv_x_bias: bfloat16 [3072], P('tensor'), may hold values from -2 to 2
- conv_bc: bfloat16 [4, 256], replicated, may hold values from -3 to 3
- conv_bc_bias: bfloat16 [256], replicated, may hold values from -2 to 2
- step_bias: float32 [48], P('tensor'), may hold values from -7 to -2.5
- a_log: float32 [48], P('tensor'), may hold values from 0 to 2.5
- skip: float32 [48], P('tensor'), may hold values from 0.5 to 1.5
- norm_gain: bfloat16 [3072], P('tensor'), may hold values from 0.25 to 1.75
- w_out: bfloat16 [3072, 1536], P('tensor'), may hold values from -0.109375 to 0.109375
Outputs:
- output: bfloat16 [4096, 1536], P('dp', 'tensor')
- hidden_grad: bfloat16 [4096, 1536], P('dp', 'tensor')
- pre_gain_grad: float32 [1536], P('tensor')
- w_in_grad: float32 [1536, 2, 3072], P('dp', None, 'tensor')
- w_state_grad: float32 [1536, 256], P('dp', 'tensor')
- w_step_grad: float32 [1536, 48], P('dp', 'tensor')
- conv_x_grad: float32 [4, 3072], P(None, 'tensor')
- conv_x_bias_grad: float32 [3072], P('tensor')
- conv_bc_grad: float32 [4, 256], replicated
- conv_bc_bias_grad: float32 [256], replicated
- step_bias_grad: float32 [48], P('tensor')
- a_log_grad: float32 [48], P('tensor')
- skip_grad: float32 [48], P('tensor')
- norm_gain_grad: float32 [3072], P('tensor')
- w_out_grad: float32 [3072, 1536], P('tensor', 'dp')
The draws below stay inside these ranges and needn't reach their ends.
Inputs may be any that keep to these rules, and one draw needn't show every extreme that they name: `seq_lengths`: each row sums to 256; a slot of length 0 holds no sequence; in every draw some index of dp holds a single sequence of 256 tokens. `deal_to`: a permutation of the 4096 rows; the 256 given rows of each index of dp go 256 // 16 to the dealt block of every index of dp.
All inputs are finite; a program needn't handle non-finite values.
Results may differ from the reference program's by a relative error of at most 0.011.
Values may be sent and summed in bfloat16 or wider, within the bound.
A program may use at most 192 MiB of HBM per device.

```python
import math
from functools import partial
import jax
import jax.numpy as jnp
from jax import lax

D = 1536
HEADS = 48
HEADDIM = 64
STATE = 128
CONV = 4
GROUP = 256
TOK_DEV = 256
SLOTS = 8
INNER = 3072
TOKENS = 4096
N_DP = 16


def draw_seq_lengths(key, part):
    cut_key, row_key = jax.random.split(jax.random.fold_in(key, 17))
    cuts = jnp.sort(jax.random.randint(cut_key, (N_DP, SLOTS - 1), 0, TOK_DEV + 1), axis=1)
    bounds = jnp.concatenate([jnp.zeros((N_DP, 1), jnp.int32), cuts.astype(jnp.int32), jnp.full((N_DP, 1), TOK_DEV, jnp.int32)], axis=1)
    lengths = bounds[:, 1:] - bounds[:, :-1]
    single = jnp.concatenate([jnp.full((1,), TOK_DEV, jnp.int32), jnp.zeros((SLOTS - 1,), jnp.int32)])
    chosen = jax.random.randint(row_key, (), 0, N_DP)
    rows = jnp.arange(N_DP)
    return jnp.where((rows == chosen)[:, None], single[None, :], lengths).astype(jnp.int32)


def draw_deal_to(key, part):
    first_key, second_key = jax.random.split(jax.random.fold_in(key, 29))
    shuffle = jax.vmap(lambda sub: jax.random.permutation(sub, TOK_DEV))(jax.random.split(first_key, N_DP))
    spread = jax.vmap(lambda sub: jax.random.permutation(sub, TOK_DEV))(jax.random.split(second_key, N_DP))
    quota = TOK_DEV // N_DP
    dest = jnp.arange(N_DP, dtype=jnp.int32)
    position = jnp.arange(TOK_DEV, dtype=jnp.int32)
    source = (position[None, :] // quota + dest[:, None]) % N_DP
    slot = dest[:, None] * quota + position[None, :] % quota
    local = spread[source, slot]
    given = source * TOK_DEV + local
    dealt = dest[:, None] * TOK_DEV + shuffle
    return jnp.zeros((TOKENS,), jnp.int32).at[given.reshape(-1)].set(dealt.reshape(-1).astype(jnp.int32))


def draw_w_in(key, part):
    column = jnp.arange(INNER, dtype=jnp.float32) / INNER
    base = jax.random.normal(key, (D, 2, INNER), jnp.float32)
    rising = 0.5 * jnp.power(3.0, column)
    scale = jnp.stack([rising, jnp.ones((INNER,), jnp.float32)])
    return (base * scale[None] / math.sqrt(D)).astype(jnp.bfloat16)


def shard_levels(rng, dims, cuts, smallest, high):
    level, own = 1.0, jax.random.fold_in(rng, 6)
    for axis_at, blocks in cuts:
        heights = jnp.exp(jax.random.uniform(jax.random.fold_in(own, axis_at), (blocks,), jnp.float32, smallest / len(cuts), high / len(cuts)))
        level = level * jnp.repeat(heights, dims[axis_at] // blocks).reshape([-1 if axis == axis_at else 1 for axis in range(len(dims))])
    return level


def gaussian(stream_key, extent, width, most, cuts=(), held_as=jnp.bfloat16):
    array = jax.random.normal(stream_key, extent, jnp.float32) * width
    if len(cuts) > 0:
        array = shard_levels(stream_key, extent, cuts, -0.22, 0.18) * array
    return jnp.clip(array, min=-most, max=most).astype(held_as)


def setup_inputs(seed: int = 0) -> dict:
    key_list = jax.random.split(jax.random.key(seed), 18)
    hidden_in = gaussian(key_list[0], (TOKENS, D), 1.0, 6.0, ((0, 16), (1, 2)))
    out_grad = gaussian(key_list[1], (TOKENS, D), 1.0, 6.0, ((0, 16), (1, 2)))
    seq_lengths = draw_seq_lengths(jax.random.fold_in(key_list[17], 71), 0)
    deal_to = draw_deal_to(jax.random.fold_in(key_list[17], 71), 0)
    pre_gain = jnp.clip(1.0 + 0.1 * jax.random.normal(key_list[4], (D,), jnp.float32), 0.5, 1.5).astype(jnp.bfloat16)
    w_in = draw_w_in(jax.random.fold_in(key_list[17], 71), 0)
    w_state = gaussian(key_list[6], (D, 2 * STATE), D ** -0.5, 0.15625)
    w_step = gaussian(key_list[7], (D, HEADS), D ** -0.5, 0.15625, ((1, 2),))
    conv_x = gaussian(key_list[8], (CONV, INNER), 0.5, 3.0, ((1, 2),))
    conv_x_bias = gaussian(key_list[9], (INNER,), 0.3, 2.0, ((0, 2),))
    conv_bc = gaussian(key_list[10], (CONV, 2 * STATE), 0.5, 3.0)
    conv_bc_bias = gaussian(key_list[11], (2 * STATE,), 0.3, 2.0)
    step_bias = jnp.clip(-7.0 + 4.5 * jax.random.uniform(key_list[12], (HEADS,), jnp.float32) ** shard_levels(key_list[12], (HEADS,), ((0, 2),), -0.2, 0.2), -7.0, -2.5)
    a_log = jnp.clip(2.5 * jax.random.uniform(key_list[13], (HEADS,), jnp.float32) ** shard_levels(key_list[13], (HEADS,), ((0, 2),), -0.2, 0.2), 0.0, 2.5)
    skip = jnp.clip(0.5 + 1.0 * jax.random.uniform(key_list[14], (HEADS,), jnp.float32) ** shard_levels(key_list[14], (HEADS,), ((0, 2),), -0.2, 0.2), 0.5, 1.5)
    norm_gain = jnp.clip(1.0 + 0.15 * jax.random.normal(key_list[15], (INNER,), jnp.float32), 0.25, 1.75).astype(jnp.bfloat16)
    w_out = gaussian(key_list[16], (INNER, D), INNER ** -0.5, 0.109375, ((0, 2),))
    return dict(hidden_in=hidden_in, out_grad=out_grad, seq_lengths=seq_lengths, deal_to=deal_to, pre_gain=pre_gain, w_in=w_in, w_state=w_state, w_step=w_step, conv_x=conv_x, conv_x_bias=conv_x_bias, conv_bc=conv_bc, conv_bc_bias=conv_bc_bias, step_bias=step_bias, a_log=a_log, skip=skip, norm_gain=norm_gain, w_out=w_out)


norm_eps = 1e-05

@jax.custom_vjp
def low(v):
    return lax.optimization_barrier(v.astype(jnp.bfloat16)).astype(jnp.float32)

@jax.custom_vjp
def low_back(v):
    return v

def low_keep(v):
    return (low(v), None)

def low_pass(kept, grad):
    return (grad,)

def back_keep(v):
    return (v, None)

def back_low(kept, grad):
    return (low(grad),)
low.defvjp(low_keep, low_pass)
low_back.defvjp(back_keep, back_low)

def precise_dot(left, right):
    return jnp.dot(left, right, precision=lax.Precision.HIGHEST)

def segment_ids(lengths):
    ends = jnp.cumsum(lengths).astype(jnp.int32)
    position = jnp.arange(TOK_DEV, dtype=jnp.int32)
    return lax.optimization_barrier(jnp.sum((position[:, None] >= ends[None, :]).astype(jnp.int32), axis=1, dtype=jnp.int32))

def causal_conv(signal, kernel, kernel_bias, segment):
    total = kernel_bias[None, :] + kernel[CONV - 1][None, :] * signal
    for offset in range(1, CONV):
        moved = jnp.concatenate([jnp.zeros((offset, signal.shape[1]), signal.dtype), signal[:-offset]], axis=0)
        earlier = jnp.concatenate([jnp.full((offset,), -1, jnp.int32), segment[:-offset]])
        inside = (earlier == segment).astype(signal.dtype)
        total = total + kernel[CONV - 1 - offset][None, :] * moved * inside[:, None]
    return total

def state_space(xval, b_rows, c_rows, step, decay, segment):
    highest = lax.Precision.HIGHEST
    blocks = xval.shape[0] // GROUP
    head_count = xval.shape[1]
    x_block = xval.reshape(blocks, GROUP, head_count, xval.shape[2])
    b_block = b_rows.reshape(blocks, GROUP, b_rows.shape[1])
    c_block = c_rows.reshape(blocks, GROUP, c_rows.shape[1])
    step_block = step.reshape(blocks, GROUP, head_count).transpose(0, 2, 1)
    rate_block = step_block * decay[None, :, None]
    seg_block = segment.reshape(blocks, GROUP)
    before = jnp.concatenate([jnp.full((1,), -1, jnp.int32), segment[:-1]]).reshape(blocks, GROUP)[:, 0]
    cumulative = jnp.cumsum(rate_block, axis=2)
    lower_mask = jnp.tril(jnp.ones((GROUP, GROUP), dtype=bool))
    linked = (seg_block[:, :, None] == seg_block[:, None, :]) & lower_mask[None]
    spread = cumulative[:, :, :, None] - cumulative[:, :, None, :]
    weight = jnp.exp(jnp.where(linked[:, None], spread, -10000.0))
    scores = jnp.einsum('cin,cjn->cij', c_block, b_block, precision=highest)
    mixing = weight * scores[:, None] * step_block[:, :, None, :]
    inside_out = jnp.einsum('chij,cjhp->cihp', mixing, x_block, precision=highest)
    final_cum = cumulative[:, :, -1]
    last_same = (seg_block == seg_block[:, -1:]).astype(step.dtype)
    tail_weight = jnp.exp(final_cum[:, :, None] - cumulative) * last_same[:, None, :] * step_block
    fresh_state = jnp.einsum('chj,cjhp,cjn->chpn', tail_weight, x_block, b_block, precision=highest)
    carried = jnp.zeros(fresh_state.shape[1:], step.dtype)
    entering = []
    for block_index in range(blocks):
        entering.append(carried)
        continues = (seg_block[block_index, -1] == before[block_index]).astype(step.dtype)
        carried = jnp.exp(final_cum[block_index])[:, None, None] * carried * continues + fresh_state[block_index]
    entering = jnp.stack(entering)
    first_same = (seg_block == before[:, None]).astype(step.dtype)
    head_decay = jnp.exp(cumulative) * first_same[:, None, :]
    carried_out = jnp.einsum('chi,cin,chpn->cihp', head_decay, c_block, entering, precision=highest)
    return (inside_out + carried_out).reshape(xval.shape)

def block_forward(stream, params, segment):
    pre_gain, w_in, w_state, w_step, conv_x, conv_x_bias, conv_bc, conv_bc_bias, step_bias, a_log, skip, norm_gain, w_out = params
    normed = low(stream * lax.rsqrt(lax.optimization_barrier(jnp.mean(stream * stream, axis=1, keepdims=True)) + norm_eps) * pre_gain)
    proj_pair = low_back(precise_dot(normed, w_in.reshape(D, 2 * INNER)))
    gate_pre = proj_pair[:, :INNER]
    value_pre = proj_pair[:, INNER:]
    state_pre = low_back(precise_dot(normed, w_state))
    step_pre = low_back(precise_dot(normed, w_step))
    value_conv = low(jax.nn.silu(causal_conv(value_pre, conv_x, conv_x_bias, segment)))
    state_conv = low(jax.nn.silu(causal_conv(state_pre, conv_bc, conv_bc_bias, segment)))
    step = jax.nn.softplus(step_pre + step_bias)
    decay = -jnp.exp(a_log)
    heads_in = value_conv.reshape(TOK_DEV, HEADS, HEADDIM)
    mixed = state_space(heads_in, state_conv[:, :STATE], state_conv[:, STATE:], step, decay, segment)
    mixed = (mixed + skip[None, :, None] * heads_in).reshape(TOK_DEV, INNER)
    gated = mixed * jax.nn.silu(gate_pre)
    scaled = low(gated * lax.rsqrt(lax.optimization_barrier(jnp.mean(gated * gated, axis=1, keepdims=True)) + norm_eps) * norm_gain)
    return stream + precise_dot(scaled, w_out)

def reference(hidden_in, out_grad, seq_lengths, deal_to, pre_gain, w_in, w_state, w_step, conv_x, conv_x_bias, conv_bc, conv_bc_bias, step_bias, a_log, skip, norm_gain, w_out):
    dealt_in = jnp.zeros((TOKENS, D), jnp.float32).at[deal_to].set(hidden_in.astype(jnp.float32))
    dealt_grad = jnp.zeros((TOKENS, D), jnp.float32).at[deal_to].set(out_grad.astype(jnp.float32))
    params = tuple((weight_arg.astype(jnp.float32) for weight_arg in (pre_gain, w_in, w_state, w_step, conv_x, conv_x_bias, conv_bc, conv_bc_bias, step_bias, a_log, skip, norm_gain, w_out)))

    def one_device(totals, pieces):
        stream, upstream, lengths = pieces
        segment = segment_ids(lengths)
        result, pull = jax.vjp(partial(block_forward, segment=segment), stream, params)
        grad_stream, grad_params = pull(upstream)
        summed = tuple((total_sum + new_term for total_sum, new_term in zip(totals, grad_params)))
        return (summed, (result, grad_stream))
    start = tuple((jnp.zeros_like(weight_arg) for weight_arg in params))
    totals, (results, grads) = lax.scan(one_device, start, (dealt_in.reshape(N_DP, TOK_DEV, D), dealt_grad.reshape(N_DP, TOK_DEV, D), seq_lengths))
    output = results.reshape(TOKENS, D)[deal_to].astype(jnp.bfloat16)
    hidden_grad = grads.reshape(TOKENS, D)[deal_to].astype(jnp.bfloat16)
    return (output, hidden_grad, totals[0], totals[1], totals[2], totals[3], totals[4], totals[5], totals[6], totals[7], totals[8], totals[9], totals[10], totals[11], totals[12])
```

```python
from functools import partial

import jax
import jax.numpy as jnp
from jax import lax
from jax.experimental import pallas as pl
from jax.experimental.pallas import tpu as pltpu
from jax.sharding import PartitionSpec as P

D = 1536
GROUP = 256
INNER = 3072


norm_eps = 1e-05


def segment_ids(lengths, row_count):
    index = jnp.arange(lengths.shape[0])
    ends = jnp.sum(jnp.where(index[None, :] <= index[:, None], lengths[None, :], 0), axis=1)
    position = jnp.arange(row_count, dtype=jnp.int32)
    return jnp.sum((position[:, None] >= ends[None, :]).astype(jnp.int32), axis=1, dtype=jnp.int32)


def causal_conv(signal, kernel, kernel_bias, segment):
    width = kernel.shape[0]
    total = kernel_bias[None, :] + kernel[width - 1][None, :] * signal
    for offset in range(1, width):
        moved = jnp.concatenate(
            [jnp.zeros((offset, signal.shape[1]), signal.dtype), signal[:-offset]], axis=0
        )
        earlier = jnp.concatenate([jnp.full((offset,), -1, jnp.int32), segment[:-offset]])
        inside = (earlier == segment).astype(signal.dtype)
        total = total + kernel[width - 1 - offset][None, :] * moved * inside[:, None]
    return total


def state_space(xval, b_rows, c_rows, step, decay, segment):
    highest = lax.Precision.HIGHEST
    blocks = xval.shape[0] // GROUP
    head_count = xval.shape[1]
    x_block = xval.reshape(blocks, GROUP, head_count, xval.shape[2])
    b_block = b_rows.reshape(blocks, GROUP, b_rows.shape[1])
    c_block = c_rows.reshape(blocks, GROUP, c_rows.shape[1])
    step_block = step.reshape(blocks, GROUP, head_count).transpose(0, 2, 1)
    rate_block = step_block * decay[None, :, None]
    seg_block = segment.reshape(blocks, GROUP)
    before = jnp.concatenate([jnp.full((1,), -1, jnp.int32), segment[:-1]]).reshape(blocks, GROUP)[
        :, 0
    ]
    lower_mask = jnp.tril(jnp.ones((GROUP, GROUP), dtype=bool))
    cumulative = jnp.einsum("chj,ij->chi", rate_block, lower_mask.astype(jnp.float32), precision=highest)
    linked = (seg_block[:, :, None] == seg_block[:, None, :]) & lower_mask[None]
    spread = cumulative[:, :, :, None] - cumulative[:, :, None, :]
    weight = jnp.exp(jnp.where(linked[:, None], spread, -10000.0))
    scores = jnp.einsum("cin,cjn->cij", c_block, b_block, precision=highest)
    mixing = weight * scores[:, None] * step_block[:, :, None, :]
    inside_out = jnp.einsum("chij,cjhp->cihp", mixing, x_block, precision=highest)
    final_cum = cumulative[:, :, -1]
    last_same = (seg_block == seg_block[:, -1:]).astype(jnp.float32)
    tail_weight = jnp.exp(final_cum[:, :, None] - cumulative) * last_same[:, None, :] * step_block
    fresh_state = jnp.einsum("chj,cjhp,cjn->chpn", tail_weight, x_block, b_block, precision=highest)
    carried = jnp.zeros(fresh_state.shape[1:], jnp.float32)
    entering = []
    entering.append(carried)
    entering = jnp.stack(entering)
    first_same = (seg_block == before[:, None]).astype(jnp.float32)
    head_decay = jnp.exp(cumulative) * first_same[:, None, :]
    carried_out = jnp.einsum("chi,cin,chpn->cihp", head_decay, c_block, entering, precision=highest)
    return (inside_out + carried_out).reshape(xval.shape)


def pre_norm(stream, gain):
    return stream * lax.rsqrt(jnp.mean(stream * stream, axis=1, keepdims=True) + norm_eps) * gain


def conv_piece(value_pre, state_pre, conv_x, conv_x_bias, conv_bc, conv_bc_bias, segment):
    value_conv = jax.nn.silu(causal_conv(value_pre, conv_x, conv_x_bias, segment))
    state_conv = jax.nn.silu(causal_conv(state_pre, conv_bc, conv_bc_bias, segment))
    return (value_conv, state_conv)


def mixer_piece(value_conv, state_conv, step_pre, step_bias, a_log, skip, segment):
    head_count = step_bias.shape[0]
    row_count = value_conv.shape[0]
    heads_in = value_conv.reshape(row_count, head_count, value_conv.shape[1] // head_count)
    step = jax.nn.softplus(step_pre + step_bias)
    decay = -jnp.exp(a_log)
    half_state = state_conv.shape[1] // 2
    mixed = state_space(
        heads_in, state_conv[:, :half_state], state_conv[:, half_state:], step, decay, segment
    )
    return (mixed + skip[None, :, None] * heads_in).reshape(row_count, value_conv.shape[1])


def rounded(values):
    return lax.optimization_barrier(values.astype(jnp.bfloat16)).astype(jnp.float32)


def shards(
    hidden_in,
    out_grad,
    seq_lengths,
    deal_to,
    pre_gain,
    w_in,
    w_state,
    w_step,
    conv_x,
    conv_x_bias,
    conv_bc,
    conv_bc_bias,
    step_bias,
    a_log,
    skip,
    norm_gain,
    w_out,
):
    dp_count = lax.axis_size("dp")
    row_count = hidden_in.shape[0]
    per_peer = row_count // dp_count
    feat_half = hidden_in.shape[1]
    tensor_index = lax.axis_index("tensor")
    send_order = jnp.argsort(deal_to)
    back_order = jnp.argsort(send_order)
    sent_in = hidden_in[send_order].reshape(dp_count, per_peer, feat_half)
    sent_grad = out_grad[send_order].reshape(dp_count, per_peer, feat_half)
    got_in, got_grad = (
        lax.all_to_all(sent_in, "dp", split_axis=0, concat_axis=0, tiled=True),
        lax.all_to_all(sent_grad, "dp", split_axis=0, concat_axis=0, tiled=True),
    )
    got_ids = lax.all_to_all(
        deal_to[send_order].reshape(dp_count, per_peer),
        "dp",
        split_axis=0,
        concat_axis=0,
        tiled=True,
    )
    dealt_slot = got_ids.reshape(row_count) % row_count
    settle_order = jnp.argsort(dealt_slot)
    dealt_half = got_in.reshape(row_count, feat_half)[settle_order]
    grad_half = got_grad.reshape(row_count, feat_half)[settle_order]
    full_in, grad_full = (
        lax.all_gather(dealt_half, "tensor", axis=1, tiled=True),
        lax.all_gather(grad_half, "tensor", axis=1, tiled=True),
    )
    segment = segment_ids(seq_lengths[0], row_count)
    stream = full_in.astype(jnp.float32)
    normed_f, norm_pull = jax.vjp(pre_norm, stream, pre_gain.astype(jnp.float32))
    normed = normed_f.astype(jnp.bfloat16)
    inner_half = w_in.shape[2]
    w_pair = w_in.reshape(w_in.shape[0], 2 * inner_half)
    proj_pair = jnp.dot(normed, w_pair, preferred_element_type=jnp.float32)
    gate_pre = proj_pair[:, :inner_half]
    value_pre = proj_pair[:, inner_half:]
    state_pre = jnp.dot(normed, w_state, preferred_element_type=jnp.float32)
    step_pre = jnp.dot(normed, w_step, preferred_element_type=jnp.float32)
    conv_args = (
        value_pre,
        state_pre,
        conv_x.astype(jnp.float32),
        conv_x_bias.astype(jnp.float32),
        conv_bc.astype(jnp.float32),
        conv_bc_bias.astype(jnp.float32),
    )
    (value_conv_f, state_conv_f), conv_pull = jax.vjp(
        partial(conv_piece, segment=segment), *conv_args
    )
    value_conv = rounded(value_conv_f)
    state_conv = rounded(state_conv_f)
    mixed, mixer_pull = jax.vjp(
        partial(mixer_piece, segment=segment),
        value_conv,
        state_conv,
        step_pre,
        step_bias,
        a_log,
        skip,
    )
    silu_gate = jax.nn.silu(gate_pre)
    gated = mixed * silu_gate
    total_squares = lax.psum(jnp.sum(gated * gated, axis=1), "tensor")
    inverse = lax.rsqrt(total_squares / INNER + norm_eps)
    gain_f = norm_gain.astype(jnp.float32)
    scaled = (gated * inverse[:, None] * gain_f).astype(jnp.bfloat16)
    partial_out = jnp.dot(scaled, w_out, preferred_element_type=jnp.float32)
    branch = lax.psum_scatter(partial_out, "tensor", scatter_dimension=1, tiled=True)
    result = (dealt_half.astype(jnp.float32) + branch).astype(jnp.bfloat16)
    back_out = lax.all_to_all(
        result[dealt_slot].reshape(dp_count, per_peer, feat_half),
        "dp",
        split_axis=0,
        concat_axis=0,
        tiled=True,
    )
    output = back_out.reshape(row_count, feat_half)[back_order]
    g_w_out = jnp.einsum("ti,td->id", scaled, grad_full, preferred_element_type=jnp.float32)
    d_scaled = jnp.einsum("td,id->ti", grad_full, w_out, preferred_element_type=jnp.float32)
    weighted = d_scaled * gain_f
    g_norm_gain = jnp.sum(d_scaled * gated * inverse[:, None], axis=0)
    cross_sum = lax.psum(jnp.sum(weighted * gated, axis=1), "tensor")
    d_gated = (
        inverse[:, None] * weighted
        - gated * (inverse * inverse * inverse / INNER * cross_sum)[:, None]
    )
    d_mixed = d_gated * silu_gate
    sigmoid_gate = jax.nn.sigmoid(gate_pre)
    d_gate = d_gated * mixed * (sigmoid_gate * (1.0 + gate_pre * (1.0 - sigmoid_gate)))
    d_value_conv, d_state_part, d_step_pre, g_step_bias, g_a_log, g_skip = mixer_pull(d_mixed)
    d_state_conv = lax.psum(d_state_part, "tensor")
    d_value_pre, d_state_pre, g_conv_x, g_conv_x_bias, g_conv_bc, g_conv_bc_bias = conv_pull(
        (d_value_conv, d_state_conv)
    )
    d_pair = jnp.concatenate([d_gate, d_value_pre], axis=1).astype(jnp.bfloat16)
    d_state_low = d_state_pre.astype(jnp.bfloat16)
    d_step_low = d_step_pre.astype(jnp.bfloat16)
    state_share = w_state.shape[1] // lax.axis_size("tensor")
    own_state = lax.dynamic_slice_in_dim(d_state_low, tensor_index * state_share, state_share, 1)
    own_weight = lax.dynamic_slice_in_dim(w_state, tensor_index * state_share, state_share, 1)
    g_w_in = jnp.einsum("td,tc->dc", normed, d_pair, preferred_element_type=jnp.float32).reshape(
        w_in.shape
    )
    g_w_state = jnp.einsum("td,tc->dc", normed, own_state, preferred_element_type=jnp.float32)
    g_w_step = jnp.einsum("td,th->dh", normed, d_step_low, preferred_element_type=jnp.float32)
    d_normed = jnp.einsum("tc,dc->td", d_pair, w_pair, preferred_element_type=jnp.float32)
    d_normed = d_normed + jnp.einsum(
        "th,dh->td", d_step_low, w_step, preferred_element_type=jnp.float32
    )
    d_normed = d_normed + jnp.einsum(
        "tc,dc->td", own_state, own_weight, preferred_element_type=jnp.float32
    )
    normed_share = lax.psum_scatter(d_normed, "tensor", scatter_dimension=1, tiled=True)
    row_scale = lax.rsqrt(jnp.mean(stream * stream, axis=1) + norm_eps)
    stream_share = dealt_half.astype(jnp.float32)
    gain_share = lax.dynamic_slice_in_dim(
        pre_gain.astype(jnp.float32), tensor_index * feat_half, feat_half, 0
    )
    row_cross = lax.psum(jnp.sum(gain_share * normed_share * stream_share, axis=1), "tensor")
    d_share = (
        row_scale[:, None] * gain_share * normed_share
        - stream_share * (row_scale * row_scale * row_scale / D * row_cross)[:, None]
    )
    g_pre_gain = jnp.sum(normed_share * stream_share * row_scale[:, None], axis=0)
    d_input = (d_share + grad_half.astype(jnp.float32)).astype(jnp.bfloat16)
    back_grad = lax.all_to_all(
        d_input[dealt_slot].reshape(dp_count, per_peer, feat_half),
        "dp",
        split_axis=0,
        concat_axis=0,
        tiled=True,
    )
    hidden_grad = back_grad.reshape(row_count, feat_half)[back_order]
    small = lax.psum(
        (
            g_pre_gain,
            g_conv_x,
            g_conv_x_bias,
            g_conv_bc,
            g_conv_bc_bias,
            g_step_bias,
            g_a_log,
            g_skip,
            g_norm_gain,
        ),
        "dp",
    )
    g_in_part, g_state_part, g_step_part, g_w_out_part = (
        lax.psum_scatter(g_w_in, "dp", scatter_dimension=0, tiled=True),
        lax.psum_scatter(g_w_state, "dp", scatter_dimension=0, tiled=True),
        lax.psum_scatter(g_w_step, "dp", scatter_dimension=0, tiled=True),
        lax.psum_scatter(g_w_out, "dp", scatter_dimension=1, tiled=True),
    )
    return (
        output,
        hidden_grad,
        small[0],
        g_in_part,
        g_state_part,
        g_step_part,
        small[1],
        small[2],
        small[3],
        small[4],
        small[5],
        small[6],
        small[7],
        small[8],
        g_w_out_part,
    )


F32, BF16, I32 = jnp.float32, jnp.bfloat16, jnp.int32
MESH = pl.DeviceIdType.MESH
LOG2E = 1.4426950408889634
HIGHEST = lax.Precision.HIGHEST

ROWS = 256
FULL = 1536
HALF = 768
CH = 1536
HEADS = 24
PEERS = 16
PER = ROWS // PEERS
SHARE = FULL // PEERS

UNITS = (
    ("out", "x", 0, 768),
    ("out", "z", 768, 768),
    ("gate", "x", 0, 512),
    ("gate", "z", 512, 1024),
    ("value", "x", 0, 768),
    ("value", "z", 768, 768),
    ("misc", "z", 0, 256),
)


def dot_t(a, b):
    return lax.dot_general(a, b, (((1,), (1,)), ((), ())), preferred_element_type=F32)


def dot(a, b):
    return jnp.dot(a, b, preferred_element_type=F32)


def sigmoid(v):
    return 1.0 / (1.0 + jnp.exp(-v))


def block_at(n, width):
    return pl.ds(pl.multiple_of(n * width, width), width)


class Sent:
    def __init__(self, copy):
        self.copy, self.left = copy, False

    def wait_recv(self):
        self.copy.wait_recv()

    def wait_send(self):
        if not self.left:
            self.copy.wait_send()
        self.left = True


def block_body(names, *refs):
    r = dict(zip(names, refs))
    hid, ogr, lens, deal_ref, vec = r["hid"], r["ogr"], r["lens"], r["deal"], r["vec"]
    wst, wsp = r["wst"], r["wsp"]
    ss, rs, ls = r["ss"], r["rs"], r["ls"]
    me, side = lax.axis_index("dp"), lax.axis_index("tensor")
    core = lax.rem(me, 2)
    xpos = lax.rem(me // 2, 2)
    zpos = me // 4
    sibling = (zpos * 4 + xpos * 2 + (1 - core), side)
    across = (zpos * 4 + (1 - xpos) * 2 + core, side)
    z_up, z_down, z_far = lax.rem(zpos + 1, 4), lax.rem(zpos + 3, 4), lax.rem(zpos + 2, 4)
    up = (z_up * 4 + xpos * 2 + core, side)
    down = (z_down * 4 + xpos * 2 + core, side)
    far = (z_far * 4 + xpos * 2 + core, side)
    z_pair = zpos + 1 - 2 * lax.rem(zpos, 2)
    near = (z_pair * 4 + xpos * 2 + core, side)
    other = (me, 1 - side)
    own_cols = pl.ds(pl.multiple_of(side * HALF, HALF), HALF)
    other_cols = pl.ds(pl.multiple_of((1 - side) * HALF, HALF), HALF)

    started = []

    def send(src, dst, device):
        n = len(started)
        copy = pltpu.make_async_remote_copy(
            src_ref=src,
            dst_ref=dst,
            send_sem=ss.at[n],
            recv_sem=rs.at[n],
            device_id=device,
            device_id_type=MESH,
        )
        copy.start()
        started.append(Sent(copy))
        return started[-1]

    loads = {}
    n_load = 0
    for name in ("wg", "wv"):
        for n in range(6):
            cols = pl.ds(n * 256, 256)
            loads[name, n] = pltpu.make_async_copy(
                r[name + "_hbm"].at[:, cols], r[name].at[:, cols], ls.at[n_load]
            )
            n_load += 1
    loads["wo"] = pltpu.make_async_copy(r["wo_hbm"], r["wo"], ls.at[n_load])
    for n in range(6):
        loads["wg", n].start()
        loads["wv", n].start()
    loads["wo"].start()

    barrier = pltpu.get_barrier_semaphore()
    for k in range(1, PEERS):
        pl.semaphore_signal(
            barrier, inc=1, device_id=(lax.rem(me + k, PEERS), side), device_id_type=MESH
        )
    pl.semaphore_signal(barrier, inc=1, device_id=other, device_id_type=MESH)

    i0 = lax.broadcasted_iota(I32, (ROWS, ROWS), 0)
    i1 = lax.broadcasted_iota(I32, (ROWS, ROWS), 1)
    deal = deal_ref[...]
    dest = lax.shift_right_logical(deal, 8)
    slot = jnp.bitwise_and(deal, ROWS - 1)
    member = (dest == lax.broadcasted_iota(I32, (PEERS, ROWS), 0)).astype(F32)
    before = dot(member.astype(BF16), (i0 < i1).astype(F32).astype(BF16))
    rank = jnp.sum(member * before, axis=0, keepdims=True)
    place = dest.astype(F32) * PER + rank
    hit = i0.astype(F32) == place
    to_send = hit.astype(F32)
    r["send_hot_t"][...] = to_send.T.astype(BF16)
    send_hot = to_send.astype(BF16)
    ident = jnp.sum(to_send * slot.astype(F32), axis=1, keepdims=True)
    sb_h, sb_g, rb_h, rb_g, yb_h, yb_g = (r[k] for k in ("sb_h", "sb_g", "rb_h", "rb_g", "yb_h", "yb_g"))
    sb_h[:, 0:HALF] = dot(send_hot, hid[...]).astype(BF16)
    sb_h[:, HALF : HALF + 128] = jnp.broadcast_to(ident, (ROWS, 128)).astype(BF16)

    pl.semaphore_wait(barrier, PEERS)

    def rows_of(device):
        return pl.ds(pl.multiple_of(device * PER, PER), PER)

    def deal_out(src, dst):
        copies = []
        for k in range(1, PEERS):
            to = lax.rem(me + k, PEERS)
            copies.append(send(src.at[rows_of(to)], dst.at[rows_of(me)], (to, side)))
        dst[rows_of(me), :] = src[rows_of(me), :]
        return copies

    def pass_on(copies, buf, dst):
        passed = []
        for k in range(PEERS):
            if k > 0:
                copies[k - 1].wait_recv()
            origin = rows_of(lax.rem(me + PEERS - k, PEERS))
            passed.append(send(buf.at[origin, pl.ds(0, HALF)], dst.at[origin], other))
        return passed

    dealt_h = deal_out(sb_h, rb_h)
    sb_g[...] = dot(send_hot, ogr[...]).astype(BF16)
    dealt_g = deal_out(sb_g, rb_g)

    ends, total = [], 0
    for k in range(8):
        total = total + lens[0, k]
        ends.append(total)

    def seg_at(pos):
        out = jnp.zeros(pos.shape, I32)
        for e in ends:
            out = out + (pos >= e).astype(I32)
        return out

    row_col = lax.broadcasted_iota(I32, (ROWS, 128), 0)
    seg_here = seg_at(row_col)
    for o in range(1, 4):
        same = (seg_at(row_col - o) == seg_here) & (row_col >= o)
        r["masks"][o - 1] = same.astype(F32)
    same = seg_at(i0) == seg_at(i1)
    r["linked"][...] = (same & (i0 >= i1)).astype(F32)
    r["linked_t"][...] = (same & (i0 <= i1)).astype(F32)
    r["small"][...] = jnp.zeros_like(r["small"])
    r["dst_acc"][...] = jnp.zeros((ROWS, ROWS), F32)
    r["drow"][...] = jnp.zeros((128, ROWS), F32)
    r["dcol"][...] = jnp.zeros((ROWS, 128), F32)
    r["dsd"][...] = jnp.zeros((ROWS, 128), F32)

    passed_h = pass_on(dealt_h, rb_h, yb_h)
    ids = rb_h[:, HALF : HALF + 128].astype(F32)
    r["hot_t"][...] = (ids[:, 0:1] == i1.astype(F32)).astype(F32).astype(BF16)
    r["hot"][...] = (ids.T[0:1, :] == i0.astype(F32)).astype(F32).astype(BF16)
    stream, upstream, normed = r["stream"], r["upstream"], r["normed"]
    stream[:, own_cols] = dot(r["hot"][...], rb_h[:, 0:HALF]).astype(BF16)
    for copy in passed_h:
        copy.wait_recv()
    stream[:, other_cols] = dot(r["hot"][...], yb_h[...]).astype(BF16)

    @pl.loop(0, 8)
    def _(n):
        rows = block_at(n, 32)
        s = stream[rows, :].astype(F32)
        scale = lax.rsqrt(jnp.sum(s * s, axis=1, keepdims=True) * (1.0 / FULL) + norm_eps)
        r["nscale"][rows, :] = jnp.broadcast_to(scale, (32, 128))
        normed[rows, :] = (s * scale * vec[6:7, :]).astype(BF16)

    masks = r["masks"]

    def conv_at(signal, taps, bias):
        out = bias + taps[3] * signal
        for o in range(1, 4):
            out = out + taps[3 - o] * (pltpu.roll(signal, o, 0) * masks[o - 1])
        return out

    def conv_back(signal, taps, bias, grad):
        pre = conv_at(signal, taps, bias)
        s = sigmoid(pre)
        d_pre = grad * (s * (1.0 + pre * (1.0 - s)))
        sums = [None] * 4
        sums[3] = jnp.sum(d_pre * signal, axis=0, keepdims=True)
        d_signal = taps[3] * d_pre
        for o in range(1, 4):
            masked = d_pre * masks[o - 1]
            sums[3 - o] = jnp.sum(masked * pltpu.roll(signal, o, 0), axis=0, keepdims=True)
            d_signal = d_signal + taps[3 - o] * pltpu.roll(masked, ROWS - o, 0)
        return d_signal, sums, jnp.sum(d_pre, axis=0, keepdims=True)

    def taps_at(first, cols):
        return [vec[pl.ds(first + k, 1), cols] for k in range(4)]

    gate_pre, value_pre, vconv = r["gate_pre"], r["value_pre"], r["vconv"]
    for n in range(6):
        loads["wg", n].wait()
        loads["wv", n].wait()

    @pl.loop(0, 6)
    def _(n):
        cols = block_at(n, 256)
        gate_pre[:, cols] = dot(normed[...], r["wg"][:, cols])
        value_pre[:, cols] = dot(normed[...], r["wv"][:, cols])

    @pl.loop(0, 12)
    def _(n):
        cols = block_at(n, 128)
        pre = conv_at(value_pre[:, cols], taps_at(0, cols), vec[4:5, cols])
        vconv[:, cols] = (pre * sigmoid(pre)).astype(BF16)

    state_pre, sconv = r["state_pre"], r["sconv"]
    state_pre[...] = dot(normed[...], wst[...])
    for n in range(2):
        cols = pl.ds(n * 128, 128)
        pre = conv_at(state_pre[:, cols], taps_at(8, cols), vec[12:13, cols])
        sconv[:, cols] = (pre * sigmoid(pre)).astype(BF16)

    step_in = dot(normed[...], wsp[...]) + vec[13:14, 0:128]
    small_e = jnp.exp(-jnp.abs(step_in))
    series = small_e * (1.0 - small_e * (0.5 - small_e * (1.0 / 3.0 - 0.25 * small_e)))
    step = jnp.maximum(step_in, 0.0) + jnp.where(small_e < 0.01, series, jnp.log(1.0 + small_e))
    decay = -jnp.exp(vec[14:15, 0:128])
    r["step_in"][...] = step_in
    r["step"][...] = step
    lower = (i0 >= i1).astype(F32)
    cum2 = jnp.dot(lower, step * decay, precision=HIGHEST, preferred_element_type=F32) * LOG2E
    r["cum2"][...] = cum2
    r["cum2_t"][...] = cum2.T
    r["cum2_ls"][...] = (cum2 - jnp.log(step) * LOG2E).T
    b_rows, c_rows = sconv[:, 0:128], sconv[:, 128:256]
    r["scores"][...] = dot_t(c_rows, b_rows) * r["linked"][...]
    r["scores_t"][...] = dot_t(b_rows, c_rows) * r["linked_t"][...]

    passed_g = pass_on(dealt_g, rb_g, yb_g)

    lane = lax.broadcasted_iota(I32, (ROWS, 128), 1)
    lane_half = lax.broadcasted_iota(I32, (128, 128), 1) < 64

    def column(ref, h):
        return jnp.sum(jnp.where(lane == h, ref[...], 0.0), axis=1, keepdims=True)

    mixed = r["mixed"]

    @pl.loop(0, HEADS // 2)
    def _(p):
        cols = block_at(p, 128)
        x = vconv[:, cols]
        tops, lows = [], []
        for a in range(2):
            h = 2 * p + a
            cc = column(r["cum2"], h)
            cr = r["cum2_ls"][pl.ds(h, 1), :]
            w = jnp.exp2(jnp.minimum(cc[0:128] - cr[:, 0:128], 100.0)) * r["scores"][0:128, 0:128]
            tops.append(dot(w.astype(BF16), x[0:128]))
            w = jnp.exp2(jnp.minimum(cc[128:256] - cr, 100.0)) * r["scores"][128:256, :]
            lows.append(dot(w.astype(BF16), x))
        skip = vec[7:8, cols]
        xf = x.astype(F32)
        mixed[0:128, cols] = jnp.where(lane_half, tops[0], tops[1]) + skip * xf[0:128]
        mixed[128:256, cols] = jnp.where(lane_half, lows[0], lows[1]) + skip * xf[128:256]

    upstream[:, own_cols] = dot(r["hot"][...], rb_g[...]).astype(BF16)
    for copy in passed_g:
        copy.wait_recv()
    upstream[:, other_cols] = dot(r["hot"][...], yb_g[...]).astype(BF16)
    loads["wo"].wait()
    d_scaled = r["d_scaled"]
    r["acc1"][...] = jnp.zeros((ROWS, 128), F32)
    r["acc2"][...] = jnp.zeros((ROWS, 128), F32)

    @pl.loop(0, 6)
    def _(n):
        cols = block_at(n, 256)
        ds = dot_t(upstream[...], r["wo"][cols, :])
        d_scaled[:, cols] = ds
        g = gate_pre[:, cols]
        gated = mixed[:, cols] * g * sigmoid(g)
        sq = gated * gated
        cr = vec[5:6, cols] * ds * gated
        r["acc1"][...] += sq[:, 0:128] + sq[:, 128:256]
        r["acc2"][...] += cr[:, 0:128] + cr[:, 128:256]

    def exchange_rows(col_a, col_b, out_buf, in_buf):
        both = jnp.where(lane == 0, col_a, jnp.where(lane == 1, col_b, 0.0))
        out_buf[...] = both.T[0:8, :]
        send(out_buf, in_buf, other).wait_recv()
        wide = jnp.concatenate([out_buf[...] + in_buf[...], jnp.zeros((120, ROWS), F32)], axis=0).T
        return wide[:, 0:1], wide[:, 1:2]

    sum_sq, sum_cross = exchange_rows(
        jnp.sum(r["acc1"][...], axis=1, keepdims=True),
        jnp.sum(r["acc2"][...], axis=1, keepdims=True),
        r["ex_a"],
        r["ex_b"],
    )
    inner = 2.0 * CH
    inverse = lax.rsqrt(sum_sq * (1.0 / inner) + norm_eps)
    cross = inverse * inverse * inverse * (1.0 / inner) * sum_cross
    r["acc1"][...] = jnp.broadcast_to(inverse, (ROWS, 128))
    r["acc2"][...] = jnp.broadcast_to(cross, (ROWS, 128))
    scaled2, gate2, value2, misc2 = r["scaled2"], r["gate2"], r["value2"], r["misc2"]
    here = pl.ds(0, ROWS)

    @pl.loop(0, 12)
    def _(n):
        cols = block_at(n, 128)
        inv, crs = r["acc1"][...], r["acc2"][...]
        g, m, ds, gain = gate_pre[:, cols], mixed[:, cols], d_scaled[:, cols], vec[5:6, cols]
        s = sigmoid(g)
        silu = g * s
        gated = m * silu
        gi = gated * inv
        scaled2[here, cols] = (gi * gain).astype(BF16)
        r["small"][5:6, cols] = jnp.sum(ds * gi, axis=0, keepdims=True)
        d_gated = inv * ds * gain - gated * crs
        mixed[:, cols] = d_gated * silu
        gate2[here, cols] = (d_gated * m * (s * (1.0 + g * (1.0 - s)))).astype(BF16)

    norm_t, up_t = r["norm_t"], r["up_t"]
    for source, keep, give in ((upstream, up_t, r["up_ts"]), (normed, norm_t, r["norm_ts"])):
        for n in range(4):
            flipped = source[:, n * 384 : (n + 1) * 384].astype(F32).T.astype(BF16)
            for i in range(4):
                k = 4 * n + i
                piece = flipped[i * SHARE : (i + 1) * SHARE]

                @pl.when(core == k % 2)
                def _(keep=keep, k=k, piece=piece):
                    keep[k // 2, :, 0:ROWS] = piece

                @pl.when(core != k % 2)
                def _(give=give, k=k, piece=piece):
                    give[k // 2] = piece

    there = pl.ds(ROWS, ROWS)
    swap_out = [
        send(r["up_ts"], up_t.at[:, :, there], sibling),
        send(scaled2.at[here], scaled2.at[there], sibling),
    ]
    swap_gate = [
        send(r["norm_ts"], norm_t.at[:, :, there], sibling),
        send(gate2.at[here], gate2.at[there], sibling),
    ]

    half_f, half_o, half_in = d_scaled.at[:, pl.ds(0, HALF)], r["half_o"], r["half_in"]

    @pl.loop(0, 3)
    def _(n):
        cols = pl.ds(pl.multiple_of((1 - side) * HALF + n * 256, 256), 256)
        half_o[:, block_at(n, 256)] = dot(scaled2[here, :], r["wo"][:, cols]).astype(BF16)

    share_out = send(half_o, half_in, other)

    @pl.loop(0, 3)
    def _(n):
        cols = pl.ds(pl.multiple_of(side * HALF + n * 256, 256), 256)
        half_f[:, block_at(n, 256)] = dot(scaled2[here, :], r["wo"][:, cols]) + stream[:, cols].astype(F32)

    left = {"out": up_t, "gate": norm_t, "value": norm_t, "misc": norm_t}
    right = {"out": scaled2, "gate": gate2, "value": value2, "misc": misc2}
    kept = {"out": r["o_wo"], "gate": r["o_gate"], "value": r["o_value"], "misc": r["o_misc"]}
    lo, hi = pl.ds(0, SHARE // 2), pl.ds(SHARE // 2, SHARE // 2)

    class Unit:
        def __init__(self, n):
            self.name, self.kind, self.first, self.width = UNITS[n]
            self.part = r[f"part{n}"]
            self.xbuf, self.abuf, self.bbuf, self.ubuf, self.dbuf = (r[f"{k}buf{n}"] for k in "xabud")

        def compute(self):
            lhs_ref, rhs_ref = left[self.name], right[self.name]
            first, part = self.first, self.part

            @pl.loop(0, self.width // 256)
            def _(n):
                lhs = lhs_ref[...].reshape(8 * SHARE, 2 * ROWS)
                rhs = rhs_ref[:, pl.ds(pl.multiple_of(first + n * 256, 256), 256)]
                part[:, :, :, block_at(n, 256)] = dot(lhs, rhs).astype(BF16).reshape(4, 2, SHARE, 256)

        def go(self, stage):
            getattr(self, f"{self.kind}{stage}")()

        def x0(self):
            self.compute()
            self.cx = send(self.part.at[:, 1 - xpos], self.xbuf, across)

        def x1(self):
            part = self.part
            self.cx.wait_recv()
            for k in range(4):
                part[k, xpos] = part[k, xpos] + self.xbuf[k]
            self.ca = send(part.at[z_far, xpos, lo], self.abuf, up)
            self.cb = send(part.at[z_far, xpos, hi], self.bbuf, down)

        def x2(self):
            part = self.part
            self.ca.wait_recv()
            part[z_up, xpos, lo] = part[z_up, xpos, lo] + self.abuf[...]
            self.cu = send(part.at[z_up, xpos], self.ubuf, up)
            self.cb.wait_recv()
            part[z_down, xpos, hi] = part[z_down, xpos, hi] + self.bbuf[...]
            self.cd = send(part.at[z_down, xpos], self.dbuf, down)

        def x3(self):
            self.cu.wait_recv()
            self.cd.wait_recv()
            self.keep(self.part[zpos, xpos].astype(F32) + self.ubuf[...].astype(F32) + self.dbuf[...].astype(F32))

        def z0(self):
            self.compute()
            self.ca = send(self.part.at[z_far, 0], self.abuf, up)
            self.cb = send(self.part.at[z_far, 1], self.bbuf, down)

        def z1(self):
            part = self.part
            self.ca.wait_recv()
            part[z_up, 0] = part[z_up, 0] + self.abuf[...]
            self.cu = send(part.at[z_up], self.ubuf, up)
            self.cb.wait_recv()
            part[z_down, 1] = part[z_down, 1] + self.bbuf[...]
            self.cd = send(part.at[z_down], self.dbuf, down)

        def z2(self):
            part = self.part
            self.cu.wait_recv()
            self.cd.wait_recv()
            give = part[zpos, 1 - xpos].astype(F32)
            part[zpos, 1 - xpos] = (
                give + self.ubuf[1 - xpos].astype(F32) + self.dbuf[1 - xpos].astype(F32)
            ).astype(BF16)
            self.cx = send(part.at[zpos, 1 - xpos], self.xbuf, across)

        def z3(self):
            self.cx.wait_recv()
            self.keep(
                self.part[zpos, xpos].astype(F32)
                + self.ubuf[xpos].astype(F32)
                + self.dbuf[xpos].astype(F32)
                + self.xbuf[...].astype(F32)
            )

        def keep(self, value):
            kept[self.name][:, self.first : self.first + self.width] = value

    units = [Unit(n) for n in range(len(UNITS))]
    for copy in swap_out:
        copy.wait_recv()
    units[0].go(0)
    units[1].go(0)
    for copy in swap_gate:
        copy.wait_recv()
    units[2].go(0)
    units[3].go(0)

    head_row = lax.broadcasted_iota(I32, (32, ROWS), 0)

    def mixer_back(p):
        cols = block_at(p, 128)
        x = vconv[:, cols]
        xf = x.astype(F32)
        dy = mixed[:, cols]
        dyb = dy.astype(BF16)
        r["small"][6:7, cols] = jnp.sum(dy * xf, axis=0, keepdims=True)
        d_tops, d_lows = [], []
        for a in range(2):
            h = 2 * p + a
            half = (lane < 64) if a == 0 else (lane >= 64)
            xa = jnp.where(half, xf, 0.0)
            xab = xa.astype(BF16)
            cc = column(r["cum2"], h)
            st = column(r["step"], h)
            cr = r["cum2_t"][pl.ds(h, 1), :]
            w = jnp.exp2(jnp.minimum(cr - cc[0:128], 0.0))
            sc = r["scores_t"][0:128, :]
            v_top = dot((w * sc).astype(BF16), dyb)
            q = dot_t(xab[0:128], dyb) * w * st[0:128]
            r["dst_acc"][0:128, :] += q
            g_top = q * sc
            w = jnp.exp2(jnp.minimum(cr[:, 128:256] - cc[128:256], 0.0))
            sc = r["scores_t"][128:256, 128:256]
            v_low = dot((w * sc).astype(BF16), dyb[128:256])
            q = dot_t(xab[128:256], dyb[128:256]) * w * st[128:256]
            r["dst_acc"][128:256, 128:256] += q
            g_low = q * sc
            top_sums = jnp.sum(g_top, axis=0, keepdims=True)
            low_sums = jnp.sum(g_low, axis=0, keepdims=True)
            col_sums = jnp.concatenate([top_sums[:, 0:128], top_sums[:, 128:256] + low_sums], axis=1)
            r["drow"][0:32, :] += jnp.where(head_row == h, col_sums, 0.0)
            row_sums = jnp.concatenate(
                [
                    jnp.sum(g_top[:, 0:128] + g_top[:, 128:256], axis=1, keepdims=True),
                    jnp.sum(g_low, axis=1, keepdims=True),
                ],
                axis=0,
            )
            direct = jnp.concatenate(
                [
                    jnp.sum(xa[0:128] * v_top, axis=1, keepdims=True),
                    jnp.sum(xa[128:256] * v_low, axis=1, keepdims=True),
                ],
                axis=0,
            )
            r["dcol"][...] += jnp.where(lane == h, row_sums, 0.0)
            r["dsd"][...] += jnp.where(lane == h, direct, 0.0)
            d_tops.append(st[0:128] * v_top)
            d_lows.append(st[128:256] * v_low)
        d_conv = jnp.concatenate(
            [jnp.where(lane_half, d_tops[0], d_tops[1]), jnp.where(lane_half, d_lows[0], d_lows[1])],
            axis=0,
        )
        d_conv = d_conv + vec[7:8, cols] * dy
        d_value, sums, bias_sum = conv_back(value_pre[:, cols], taps_at(0, cols), vec[4:5, cols], d_conv)
        value2[here, cols] = d_value.astype(BF16)
        for k in range(4):
            r["small"][k : k + 1, cols] = sums[k]
        r["small"][4:5, cols] = bias_sum

    pl.loop(0, 4)(mixer_back)
    units[0].go(1)
    units[1].go(1)
    pl.loop(4, 8)(mixer_back)

    share_out.wait_recv()
    back_o, back_g = r["back_o"], r["back_g"]
    result = (half_f[...] + half_in[...].astype(F32)).astype(BF16)
    yb_h[...] = dot(r["hot_t"][...], result).astype(BF16)

    def send_back(src, dst):
        copies = []
        for k in range(1, PEERS):
            to = lax.rem(me + k, PEERS)
            copies.append(send(src.at[rows_of(to)], dst.at[rows_of(me)], (to, side)))
        dst[rows_of(me), :] = src[rows_of(me), :]
        return copies

    returned_o = send_back(yb_h, back_o)
    units[2].go(1)
    units[0].go(2)
    units[1].go(2)
    pl.loop(8, 12)(mixer_back)
    swap_value = [send(value2.at[here], value2.at[there], sibling)]

    d_scores_t = r["dst_acc"][...] * r["linked_t"][...]
    d_conv_s = r["d_conv_s"]
    d_conv_s[:, 0:128] = dot(d_scores_t.astype(BF16), c_rows)
    d_conv_s[:, 128:256] = dot(d_scores_t.T.astype(BF16), b_rows)
    d_state = r["d_state"]
    for n in range(2):
        cols = pl.ds(n * 128, 128)
        d_pre, sums, bias_sum = conv_back(state_pre[:, cols], taps_at(8, cols), vec[12:13, cols], d_conv_s[:, cols])
        d_state[:, cols] = d_pre
        for k in range(4):
            r["small"][8 + k : 9 + k, cols] = sums[k]
        r["small"][12:13, cols] = bias_sum
    state_own = pl.ds(pl.multiple_of(side * 128, 128), 128)
    state_other = pl.ds(pl.multiple_of((1 - side) * 128, 128), 128)
    r["st_out"][...] = d_state[:, state_other].astype(BF16)
    share_state = send(r["st_out"], r["st_in"], other)
    d_cum = r["drow"][...].T - r["dcol"][...]
    upper = (i0 <= i1).astype(F32)
    d_rate = jnp.dot(upper, d_cum, precision=HIGHEST, preferred_element_type=F32)
    decay = -jnp.exp(vec[14:15, 0:128])
    d_step = (r["dsd"][...] + d_rate * decay) * sigmoid(r["step_in"][...])
    r["small"][13:14, 0:128] = jnp.sum(d_step, axis=0, keepdims=True)
    r["small"][14:15, 0:128] = jnp.sum(d_rate * r["step"][...], axis=0, keepdims=True) * decay
    misc2[here, 128:256] = d_step.astype(BF16)

    for copy in swap_value:
        copy.wait_recv()
    units[4].go(0)
    units[5].go(0)
    share_state.wait_recv()
    misc2[here, 0:128] = (d_state[:, state_own] + r["st_in"][...].astype(F32)).astype(BF16)
    swap_misc = send(misc2.at[here], misc2.at[there], sibling)

    dhalf_f, dhalf_o, dhalf_in = d_scaled.at[:, pl.ds(HALF, HALF)], r["dhalf_o"], r["dhalf_in"]
    r["acc1"][...] = jnp.zeros((ROWS, 128), F32)
    r["st_low"][...] = d_state[...].astype(BF16)

    def d_normed_at(first):
        rows = pl.ds(pl.multiple_of(first, 256), 256)
        out = dot_t(gate2[here, :], r["wg"][rows, :]) + dot_t(value2[here, :], r["wv"][rows, :])
        out = out + dot_t(r["st_low"][...], wst[rows, :])
        out = out + dot_t(misc2[here, 128:256], wsp[rows, :])
        part = out * vec[6:7, rows] * stream[:, rows].astype(F32)
        r["acc1"][...] += part[:, 0:128] + part[:, 128:256]
        return out

    @pl.loop(0, 3)
    def _(n):
        dhalf_o[:, block_at(n, 256)] = d_normed_at((1 - side) * HALF + n * 256).astype(BF16)

    share_norm = send(dhalf_o, dhalf_in, other)

    @pl.loop(0, 3)
    def _(n):
        dhalf_f[:, block_at(n, 256)] = d_normed_at(side * HALF + n * 256)

    swap_misc.wait_recv()
    units[6].go(0)
    units[3].go(1)
    units[2].go(2)
    units[0].go(3)
    row_cross, _ = exchange_rows(
        jnp.sum(r["acc1"][...], axis=1, keepdims=True), jnp.zeros((ROWS, 1), F32), r["ex_c"], r["ex_d"]
    )
    share_norm.wait_recv()
    share_out.wait_send()
    scale = r["nscale"][:, 0:1]
    factor = scale * scale * scale * (1.0 / FULL) * row_cross
    for n in range(6):
        cols = pl.ds(n * 128, 128)
        mine = pl.ds(pl.multiple_of(side * HALF + n * 128, 128), 128)
        dn = dhalf_f[:, cols] + dhalf_in[:, cols].astype(F32)
        s = stream[:, mine].astype(F32)
        r["small"][7:8, n * 128 : (n + 1) * 128] = jnp.sum(dn * s * scale, axis=0, keepdims=True)
        grad = upstream[:, mine].astype(F32) + scale * vec[6:7, mine] * dn - s * factor
        half_o[:, cols] = grad.astype(BF16)
    yb_g[...] = dot(r["hot_t"][...], half_o[...]).astype(BF16)
    returned_g = send_back(yb_g, back_g)

    small = r["small"]
    swap_small = send(small.at[pl.ds(8, 8), pl.ds(0, 256)], r["sm_y"], other)
    units[1].go(3)
    units[4].go(1)
    units[5].go(1)
    swap_small.wait_send()
    swap_small.wait_recv()
    keep_rows = lax.broadcasted_iota(I32, (8, 256), 0) < 5
    small[8:16, 0:256] = small[8:16, 0:256] + jnp.where(keep_rows, r["sm_y"][...], 0.0)

    def doubled(n, device):
        copies = [
            send(small.at[pl.ds(0, 8)], r[f"sm_a{n}"], device),
            send(small.at[pl.ds(8, 8), pl.ds(0, 256)], r[f"sm_b{n}"], device),
        ]

        def finish():
            for copy in copies:
                copy.wait_send()
                copy.wait_recv()
            small[0:8, :] = small[0:8, :] + r[f"sm_a{n}"][...]
            small[8:16, 0:256] = small[8:16, 0:256] + r[f"sm_b{n}"][...]

        return finish

    finish = doubled(0, sibling)
    units[6].go(1)
    finish()
    finish = doubled(1, across)
    units[3].go(2)
    finish()
    finish = doubled(2, near)
    units[2].go(3)
    units[4].go(2)
    finish()
    finish = doubled(3, far)
    for copy in returned_o:
        copy.wait_recv()
    r["o_out"][...] = dot(r["send_hot_t"][...], back_o[...]).astype(BF16)
    units[5].go(2)
    units[6].go(2)
    finish()
    r["o_small"][...] = small[...]
    for copy in returned_g:
        copy.wait_recv()
    r["o_hid"][...] = dot(r["send_hot_t"][...], back_g[...]).astype(BF16)
    units[3].go(3)
    units[4].go(3)
    units[5].go(3)
    units[6].go(3)

    for copy in started:
        copy.wait_send()


def scratch():
    vmem, dma = pltpu.VMEM, pltpu.SemaphoreType.DMA
    out = {
        "wg": vmem((FULL, CH), BF16),
        "wv": vmem((FULL, CH), BF16),
        "wo": vmem((CH, FULL), BF16),
        "send_hot_t": vmem((ROWS, ROWS), BF16),
        "hot": vmem((ROWS, ROWS), BF16),
        "hot_t": vmem((ROWS, ROWS), BF16),
        "sb_h": vmem((ROWS, HALF + 128), BF16),
        "rb_h": vmem((ROWS, HALF + 128), BF16),
        "masks": vmem((3, ROWS, 128), F32),
        "linked": vmem((ROWS, ROWS), F32),
        "linked_t": vmem((ROWS, ROWS), F32),
        "scores": vmem((ROWS, ROWS), F32),
        "scores_t": vmem((ROWS, ROWS), F32),
        "dst_acc": vmem((ROWS, ROWS), F32),
        "small": vmem((16, CH), F32),
        "drow": vmem((128, ROWS), F32),
        "cum2_t": vmem((128, ROWS), F32),
        "cum2_ls": vmem((128, ROWS), F32),
        "stream": vmem((ROWS, FULL), BF16),
        "upstream": vmem((ROWS, FULL), BF16),
        "normed": vmem((ROWS, FULL), BF16),
        "vconv": vmem((ROWS, CH), BF16),
        "gate_pre": vmem((ROWS, CH), F32),
        "value_pre": vmem((ROWS, CH), F32),
        "mixed": vmem((ROWS, CH), F32),
        "d_scaled": vmem((ROWS, CH), F32),
        "state_pre": vmem((ROWS, 256), F32),
        "d_state": vmem((ROWS, 256), F32),
        "d_conv_s": vmem((ROWS, 256), F32),
        "sconv": vmem((ROWS, 256), BF16),
        "st_low": vmem((ROWS, 256), BF16),
        "st_out": vmem((ROWS, 128), BF16),
        "st_in": vmem((ROWS, 128), BF16),
        "scaled2": vmem((2 * ROWS, CH), BF16),
        "gate2": vmem((2 * ROWS, CH), BF16),
        "value2": vmem((2 * ROWS, CH), BF16),
        "misc2": vmem((2 * ROWS, 256), BF16),
        "norm_t": vmem((8, SHARE, 2 * ROWS), BF16),
        "up_t": vmem((8, SHARE, 2 * ROWS), BF16),
        "norm_ts": vmem((8, SHARE, ROWS), BF16),
        "up_ts": vmem((8, SHARE, ROWS), BF16),
        "sm_y": vmem((8, 256), F32),
    }
    for name in ("nscale", "acc1", "acc2", "dcol", "dsd", "step_in", "step", "cum2"):
        out[name] = vmem((ROWS, 128), F32)
    for name in ("ex_a", "ex_b", "ex_c", "ex_d"):
        out[name] = vmem((8, ROWS), F32)
    for name in (
        "sb_g",
        "rb_g",
        "yb_h",
        "yb_g",
        "half_o",
        "half_in",
        "dhalf_o",
        "dhalf_in",
        "back_o",
        "back_g",
    ):
        out[name] = vmem((ROWS, HALF), BF16)
    for n, (_, kind, _, width) in enumerate(UNITS):
        out[f"part{n}"] = vmem((4, 2, SHARE, width), BF16)
        if kind == "x":
            shapes = [(4, SHARE), (SHARE // 2,), (SHARE // 2,), (SHARE,), (SHARE,)]
        else:
            shapes = [(SHARE,), (SHARE,), (SHARE,), (2, SHARE), (2, SHARE)]
        for key, shape in zip("xabud", shapes):
            out[f"{key}buf{n}"] = vmem((*shape, width), BF16)
    for n in range(4):
        out[f"sm_a{n}"] = vmem((8, CH), F32)
        out[f"sm_b{n}"] = vmem((8, 256), F32)
    out["ss"] = dma((SENDS,))
    out["rs"] = dma((SENDS,))
    out["ls"] = dma((13,))
    return out


SENDS = 2 * (PEERS - 1) + 2 * PEERS + 2 * (PEERS - 1) + 5 * len(UNITS) + 20


def one_kernel(
    hidden_in,
    out_grad,
    seq_lengths,
    deal_to,
    pre_gain,
    w_in,
    w_state,
    w_step,
    conv_x,
    conv_x_bias,
    conv_bc,
    conv_bc_bias,
    step_bias,
    a_log,
    skip,
    norm_gain,
    w_out,
):
    def row(v):
        v = v.astype(F32)
        v = v.reshape(-1, v.shape[-1])
        return jnp.pad(v, ((0, 0), (0, CH - v.shape[1])))

    heads = skip.shape[0]
    vec = jnp.concatenate(
        [
            row(conv_x),
            row(conv_x_bias),
            row(norm_gain),
            row(pre_gain),
            row(jnp.repeat(skip, CH // heads)),
            row(conv_bc),
            row(conv_bc_bias),
            row(step_bias),
            row(a_log),
            jnp.zeros((1, CH), F32),
        ],
        axis=0,
    )
    inputs = {
        "hid": hidden_in,
        "ogr": out_grad,
        "lens": seq_lengths,
        "deal": deal_to.reshape(1, ROWS),
        "vec": vec,
        "wg_hbm": w_in[:, 0, :],
        "wv_hbm": w_in[:, 1, :],
        "wo_hbm": w_out,
        "wst": w_state,
        "wsp": jnp.pad(w_step, ((0, 0), (0, 128 - heads))),
    }
    in_vmem = pl.BlockSpec(memory_space=pltpu.VMEM)
    places = {"lens": pltpu.SMEM, "wg_hbm": pl.ANY, "wv_hbm": pl.ANY, "wo_hbm": pl.ANY}
    outputs = {
        "o_out": ((ROWS, HALF), BF16),
        "o_hid": ((ROWS, HALF), BF16),
        "o_wo": ((SHARE, CH), F32),
        "o_gate": ((SHARE, CH), F32),
        "o_value": ((SHARE, CH), F32),
        "o_misc": ((SHARE, 256), F32),
        "o_small": ((16, CH), F32),
    }
    room = scratch()
    names = (*inputs, *outputs, *room)
    out = pl.pallas_call(
        partial(block_body, names),
        out_shape=[jax.ShapeDtypeStruct(s, t) for s, t in outputs.values()],
        in_specs=[pl.BlockSpec(memory_space=places.get(n, pltpu.VMEM)) for n in inputs],
        out_specs=[in_vmem] * len(outputs),
        scratch_shapes=list(room.values()),
        compiler_params=pltpu.CompilerParams(
            collective_id=0, has_side_effects=True, vmem_limit_bytes=63_000_000
        ),
        name="block",
    )(*inputs.values())
    output, hidden_grad, wo, gate, value, misc, small = out
    own_head = heads
    return (
        output,
        hidden_grad,
        small[7, :HALF],
        jnp.stack([gate, value], axis=1),
        misc[:, :128],
        misc[:, 128 : 128 + own_head],
        small[0:4],
        small[4],
        small[8:12, :256],
        small[12, :256],
        small[13, :own_head],
        small[14, :own_head],
        jnp.sum(small[6].reshape(own_head, CH // own_head), axis=1),
        small[5],
        wo.T,
    )


def fits(mesh, args):
    return mesh.shape["dp"] == PEERS and mesh.shape["tensor"] == 2 and args[0].shape == (PEERS * ROWS, FULL)


def solution(mesh):
    in_specs = (
        P("dp", "tensor"),
        P("dp", "tensor"),
        P("dp", None),
        P("dp"),
        P(),
        P(None, None, "tensor"),
        P(),
        P(None, "tensor"),
        P(None, "tensor"),
        P("tensor"),
        P(),
        P(),
        P("tensor"),
        P("tensor"),
        P("tensor"),
        P("tensor"),
        P("tensor", None),
    )
    out_specs = (
        P("dp", "tensor"),
        P("dp", "tensor"),
        P("tensor"),
        P("dp", None, "tensor"),
        P("dp", "tensor"),
        P("dp", "tensor"),
        P(None, "tensor"),
        P("tensor"),
        P(),
        P(),
        P("tensor"),
        P("tensor"),
        P("tensor"),
        P("tensor"),
        P("tensor", "dp"),
    )

    def whole(*args):
        local = one_kernel if fits(mesh, args) else shards
        mapped = jax.shard_map(
            local, mesh=mesh, in_specs=in_specs, out_specs=out_specs, check_vma=False
        )
        return mapped(*args)

    return whole
```

```python
from functools import partial
from types import SimpleNamespace

import jax
import jax.numpy as jnp
from jax import lax
from jax.experimental import pallas as pl
from jax.experimental.pallas import tpu as pltpu
from jax.sharding import PartitionSpec as P

D = 1536
GROUP = 256
INNER = 3072


norm_eps = 1e-05


def segment_ids(lengths, row_count):
    index = jnp.arange(lengths.shape[0])
    ends = jnp.sum(jnp.where(index[None, :] <= index[:, None], lengths[None, :], 0), axis=1)
    position = jnp.arange(row_count, dtype=jnp.int32)
    return jnp.sum((position[:, None] >= ends[None, :]).astype(jnp.int32), axis=1, dtype=jnp.int32)


def causal_conv(signal, kernel, kernel_bias, segment):
    width = kernel.shape[0]
    total = kernel_bias[None, :] + kernel[width - 1][None, :] * signal
    for offset in range(1, width):
        moved = jnp.concatenate(
            [jnp.zeros((offset, signal.shape[1]), signal.dtype), signal[:-offset]], axis=0
        )
        earlier = jnp.concatenate([jnp.full((offset,), -1, jnp.int32), segment[:-offset]])
        inside = (earlier == segment).astype(signal.dtype)
        total = total + kernel[width - 1 - offset][None, :] * moved * inside[:, None]
    return total


def state_space(xval, b_rows, c_rows, step, decay, segment):
    highest = lax.Precision.HIGHEST
    blocks = xval.shape[0] // GROUP
    head_count = xval.shape[1]
    x_block = xval.reshape(blocks, GROUP, head_count, xval.shape[2])
    b_block = b_rows.reshape(blocks, GROUP, b_rows.shape[1])
    c_block = c_rows.reshape(blocks, GROUP, c_rows.shape[1])
    step_block = step.reshape(blocks, GROUP, head_count).transpose(0, 2, 1)
    rate_block = step_block * decay[None, :, None]
    seg_block = segment.reshape(blocks, GROUP)
    before = jnp.concatenate([jnp.full((1,), -1, jnp.int32), segment[:-1]]).reshape(blocks, GROUP)[
        :, 0
    ]
    lower_mask = jnp.tril(jnp.ones((GROUP, GROUP), dtype=bool))
    cumulative = jnp.einsum("chj,ij->chi", rate_block, lower_mask.astype(jnp.float32), precision=highest)
    linked = (seg_block[:, :, None] == seg_block[:, None, :]) & lower_mask[None]
    spread = cumulative[:, :, :, None] - cumulative[:, :, None, :]
    weight = jnp.exp(jnp.where(linked[:, None], spread, -10000.0))
    scores = jnp.einsum("cin,cjn->cij", c_block, b_block, precision=highest)
    mixing = weight * scores[:, None] * step_block[:, :, None, :]
    inside_out = jnp.einsum("chij,cjhp->cihp", mixing, x_block, precision=highest)
    final_cum = cumulative[:, :, -1]
    last_same = (seg_block == seg_block[:, -1:]).astype(jnp.float32)
    tail_weight = jnp.exp(final_cum[:, :, None] - cumulative) * last_same[:, None, :] * step_block
    fresh_state = jnp.einsum("chj,cjhp,cjn->chpn", tail_weight, x_block, b_block, precision=highest)
    carried = jnp.zeros(fresh_state.shape[1:], jnp.float32)
    entering = []
    entering.append(carried)
    entering = jnp.stack(entering)
    first_same = (seg_block == before[:, None]).astype(jnp.float32)
    head_decay = jnp.exp(cumulative) * first_same[:, None, :]
    carried_out = jnp.einsum("chi,cin,chpn->cihp", head_decay, c_block, entering, precision=highest)
    return (inside_out + carried_out).reshape(xval.shape)


def pre_norm(stream, gain):
    return stream * lax.rsqrt(jnp.mean(stream * stream, axis=1, keepdims=True) + norm_eps) * gain


def conv_piece(value_pre, state_pre, conv_x, conv_x_bias, conv_bc, conv_bc_bias, segment):
    value_conv = jax.nn.silu(causal_conv(value_pre, conv_x, conv_x_bias, segment))
    state_conv = jax.nn.silu(causal_conv(state_pre, conv_bc, conv_bc_bias, segment))
    return (value_conv, state_conv)


def mixer_piece(value_conv, state_conv, step_pre, step_bias, a_log, skip, segment):
    head_count = step_bias.shape[0]
    row_count = value_conv.shape[0]
    heads_in = value_conv.reshape(row_count, head_count, value_conv.shape[1] // head_count)
    step = jax.nn.softplus(step_pre + step_bias)
    decay = -jnp.exp(a_log)
    half_state = state_conv.shape[1] // 2
    mixed = state_space(
        heads_in, state_conv[:, :half_state], state_conv[:, half_state:], step, decay, segment
    )
    return (mixed + skip[None, :, None] * heads_in).reshape(row_count, value_conv.shape[1])


def rounded(values):
    return lax.optimization_barrier(values.astype(jnp.bfloat16)).astype(jnp.float32)


def shards(
    hidden_in,
    out_grad,
    seq_lengths,
    deal_to,
    pre_gain,
    w_in,
    w_state,
    w_step,
    conv_x,
    conv_x_bias,
    conv_bc,
    conv_bc_bias,
    step_bias,
    a_log,
    skip,
    norm_gain,
    w_out,
):
    dp_count = lax.axis_size("dp")
    row_count = hidden_in.shape[0]
    per_peer = row_count // dp_count
    feat_half = hidden_in.shape[1]
    tensor_index = lax.axis_index("tensor")
    send_order = jnp.argsort(deal_to)
    back_order = jnp.argsort(send_order)
    sent_in = hidden_in[send_order].reshape(dp_count, per_peer, feat_half)
    sent_grad = out_grad[send_order].reshape(dp_count, per_peer, feat_half)
    got_in, got_grad = (
        lax.all_to_all(sent_in, "dp", split_axis=0, concat_axis=0, tiled=True),
        lax.all_to_all(sent_grad, "dp", split_axis=0, concat_axis=0, tiled=True),
    )
    got_ids = lax.all_to_all(
        deal_to[send_order].reshape(dp_count, per_peer),
        "dp",
        split_axis=0,
        concat_axis=0,
        tiled=True,
    )
    dealt_slot = got_ids.reshape(row_count) % row_count
    settle_order = jnp.argsort(dealt_slot)
    dealt_half = got_in.reshape(row_count, feat_half)[settle_order]
    grad_half = got_grad.reshape(row_count, feat_half)[settle_order]
    full_in, grad_full = (
        lax.all_gather(dealt_half, "tensor", axis=1, tiled=True),
        lax.all_gather(grad_half, "tensor", axis=1, tiled=True),
    )
    segment = segment_ids(seq_lengths[0], row_count)
    stream = full_in.astype(jnp.float32)
    normed_f, norm_pull = jax.vjp(pre_norm, stream, pre_gain.astype(jnp.float32))
    normed = normed_f.astype(jnp.bfloat16)
    inner_half = w_in.shape[2]
    w_pair = w_in.reshape(w_in.shape[0], 2 * inner_half)
    proj_pair = jnp.dot(normed, w_pair, preferred_element_type=jnp.float32)
    gate_pre = proj_pair[:, :inner_half]
    value_pre = proj_pair[:, inner_half:]
    state_pre = jnp.dot(normed, w_state, preferred_element_type=jnp.float32)
    step_pre = jnp.dot(normed, w_step, preferred_element_type=jnp.float32)
    conv_args = (
        value_pre,
        state_pre,
        conv_x.astype(jnp.float32),
        conv_x_bias.astype(jnp.float32),
        conv_bc.astype(jnp.float32),
        conv_bc_bias.astype(jnp.float32),
    )
    (value_conv_f, state_conv_f), conv_pull = jax.vjp(
        partial(conv_piece, segment=segment), *conv_args
    )
    value_conv = rounded(value_conv_f)
    state_conv = rounded(state_conv_f)
    mixed, mixer_pull = jax.vjp(
        partial(mixer_piece, segment=segment),
        value_conv,
        state_conv,
        step_pre,
        step_bias,
        a_log,
        skip,
    )
    silu_gate = jax.nn.silu(gate_pre)
    gated = mixed * silu_gate
    total_squares = lax.psum(jnp.sum(gated * gated, axis=1), "tensor")
    inverse = lax.rsqrt(total_squares / INNER + norm_eps)
    gain_f = norm_gain.astype(jnp.float32)
    scaled = (gated * inverse[:, None] * gain_f).astype(jnp.bfloat16)
    partial_out = jnp.dot(scaled, w_out, preferred_element_type=jnp.float32)
    branch = lax.psum_scatter(partial_out, "tensor", scatter_dimension=1, tiled=True)
    result = (dealt_half.astype(jnp.float32) + branch).astype(jnp.bfloat16)
    back_out = lax.all_to_all(
        result[dealt_slot].reshape(dp_count, per_peer, feat_half),
        "dp",
        split_axis=0,
        concat_axis=0,
        tiled=True,
    )
    output = back_out.reshape(row_count, feat_half)[back_order]
    g_w_out = jnp.einsum("ti,td->id", scaled, grad_full, preferred_element_type=jnp.float32)
    d_scaled = jnp.einsum("td,id->ti", grad_full, w_out, preferred_element_type=jnp.float32)
    weighted = d_scaled * gain_f
    g_norm_gain = jnp.sum(d_scaled * gated * inverse[:, None], axis=0)
    cross_sum = lax.psum(jnp.sum(weighted * gated, axis=1), "tensor")
    d_gated = (
        inverse[:, None] * weighted
        - gated * (inverse * inverse * inverse / INNER * cross_sum)[:, None]
    )
    d_mixed = d_gated * silu_gate
    sigmoid_gate = jax.nn.sigmoid(gate_pre)
    d_gate = d_gated * mixed * (sigmoid_gate * (1.0 + gate_pre * (1.0 - sigmoid_gate)))
    d_value_conv, d_state_part, d_step_pre, g_step_bias, g_a_log, g_skip = mixer_pull(d_mixed)
    d_state_conv = lax.psum(d_state_part, "tensor")
    d_value_pre, d_state_pre, g_conv_x, g_conv_x_bias, g_conv_bc, g_conv_bc_bias = conv_pull(
        (d_value_conv, d_state_conv)
    )
    d_pair = jnp.concatenate([d_gate, d_value_pre], axis=1).astype(jnp.bfloat16)
    d_state_low = d_state_pre.astype(jnp.bfloat16)
    d_step_low = d_step_pre.astype(jnp.bfloat16)
    state_share = w_state.shape[1] // lax.axis_size("tensor")
    own_state = lax.dynamic_slice_in_dim(d_state_low, tensor_index * state_share, state_share, 1)
    own_weight = lax.dynamic_slice_in_dim(w_state, tensor_index * state_share, state_share, 1)
    g_w_in = jnp.einsum("td,tc->dc", normed, d_pair, preferred_element_type=jnp.float32).reshape(
        w_in.shape
    )
    g_w_state = jnp.einsum("td,tc->dc", normed, own_state, preferred_element_type=jnp.float32)
    g_w_step = jnp.einsum("td,th->dh", normed, d_step_low, preferred_element_type=jnp.float32)
    d_normed = jnp.einsum("tc,dc->td", d_pair, w_pair, preferred_element_type=jnp.float32)
    d_normed = d_normed + jnp.einsum(
        "th,dh->td", d_step_low, w_step, preferred_element_type=jnp.float32
    )
    d_normed = d_normed + jnp.einsum(
        "tc,dc->td", own_state, own_weight, preferred_element_type=jnp.float32
    )
    normed_share = lax.psum_scatter(d_normed, "tensor", scatter_dimension=1, tiled=True)
    row_scale = lax.rsqrt(jnp.mean(stream * stream, axis=1) + norm_eps)
    stream_share = dealt_half.astype(jnp.float32)
    gain_share = lax.dynamic_slice_in_dim(
        pre_gain.astype(jnp.float32), tensor_index * feat_half, feat_half, 0
    )
    row_cross = lax.psum(jnp.sum(gain_share * normed_share * stream_share, axis=1), "tensor")
    d_share = (
        row_scale[:, None] * gain_share * normed_share
        - stream_share * (row_scale * row_scale * row_scale / D * row_cross)[:, None]
    )
    g_pre_gain = jnp.sum(normed_share * stream_share * row_scale[:, None], axis=0)
    d_input = (d_share + grad_half.astype(jnp.float32)).astype(jnp.bfloat16)
    back_grad = lax.all_to_all(
        d_input[dealt_slot].reshape(dp_count, per_peer, feat_half),
        "dp",
        split_axis=0,
        concat_axis=0,
        tiled=True,
    )
    hidden_grad = back_grad.reshape(row_count, feat_half)[back_order]
    small = lax.psum(
        (
            g_pre_gain,
            g_conv_x,
            g_conv_x_bias,
            g_conv_bc,
            g_conv_bc_bias,
            g_step_bias,
            g_a_log,
            g_skip,
            g_norm_gain,
        ),
        "dp",
    )
    g_in_part, g_state_part, g_step_part, g_w_out_part = (
        lax.psum_scatter(g_w_in, "dp", scatter_dimension=0, tiled=True),
        lax.psum_scatter(g_w_state, "dp", scatter_dimension=0, tiled=True),
        lax.psum_scatter(g_w_step, "dp", scatter_dimension=0, tiled=True),
        lax.psum_scatter(g_w_out, "dp", scatter_dimension=1, tiled=True),
    )
    return (
        output,
        hidden_grad,
        small[0],
        g_in_part,
        g_state_part,
        g_step_part,
        small[1],
        small[2],
        small[3],
        small[4],
        small[5],
        small[6],
        small[7],
        small[8],
        g_w_out_part,
    )


F32, BF16, I32 = jnp.float32, jnp.bfloat16, jnp.int32
MESH = pl.DeviceIdType.MESH
LOG2E = 1.4426950408889634
HIGHEST = lax.Precision.HIGHEST

ROWS = 256
FULL = 1536
HALF = 768
CH = 1536
HEADS = 24
PEERS = 16
PER = ROWS // PEERS
SHARE = FULL // PEERS

X_BIAS, NORM_GAIN, PRE_GAIN, BC_BIAS, STEP_BIAS, A_LOG = (slice(n, n + 1) for n in range(4, 10))

UNITS = (
    ("out", "x", 0, 256),
    ("out", "x", 256, 256),
    ("out", "x", 512, 256),
    ("out", "x", 768, 256),
    ("out", "x", 1024, 512),
    ("gate", "z", 0, 256),
    ("gate", "x", 256, 768),
    ("gate", "x", 1024, 512),
    ("value", "x", 0, 512),
    ("value", "x", 512, 512),
    ("value", "x", 1024, 256),
    ("value", "z", 1280, 256),
    ("misc", "x", 0, 256),
)


def dot_t(a, b):
    return lax.dot_general(a, b, (((1,), (1,)), ((), ())), preferred_element_type=F32)


def dot(a, b):
    return jnp.dot(a, b, preferred_element_type=F32)


def sigmoid(v):
    return 1.0 / (1.0 + jnp.exp(-v))


def block_at(n, width):
    return pl.ds(pl.multiple_of(n * width, width), width)


class Sent:
    def __init__(self, copy, by):
        self.copy, self.by, self.gone, self.here = copy, by, False, False

    def start(self):
        if self.by is None:
            self.copy.start()
        else:
            pl.when(self.by)(self.copy.start)

    def wait_recv(self):
        self.copy.wait_recv()
        self.here = True

    def wait_send(self):
        if not self.gone and self.by is None:
            self.copy.wait_send()
        elif not self.gone:
            pl.when(self.by)(self.copy.wait_send)
        self.gone = True


def block_body(room, *refs):
    left = list(refs)

    def take(shape):
        return [left.pop(0) for _ in shape] if isinstance(shape, list) else left.pop(0)

    r = SimpleNamespace(**{name: take(shape) for name, shape in room.items()})
    hid, lens, deal_ref, vec = r.hid, r.lens, r.deal, r.vec
    wst, wsp = r.wst, r.wsp
    ss, rs, ls = r.ss, r.rs, r.ls
    me, side = lax.axis_index("dp"), lax.axis_index("tensor")
    core = lax.rem(me, 2)
    xpos = lax.rem(me // 2, 2)
    zpos = me // 4
    sibling = (zpos * 4 + xpos * 2 + (1 - core), side)
    across = (zpos * 4 + (1 - xpos) * 2 + core, side)
    z_side = zpos // 2
    z_outer, z_inner = 3 * z_side, 1 + z_side
    far_outer, far_inner = 3 - z_outer, 3 - z_inner
    is_outer = zpos == z_outer
    is_inner = zpos == z_inner

    def at_z(z):
        return (z * 4 + xpos * 2 + core, side)

    near = at_z(z_outer + z_inner - zpos)
    facing = at_z(3 - zpos)
    other = (me, 1 - side)
    own_cols = pl.ds(pl.multiple_of(side * HALF, HALF), HALF)
    other_cols = pl.ds(pl.multiple_of((1 - side) * HALF, HALF), HALF)

    started = []

    def send(src, dst, device, by=None):
        n = len(started)
        copy = pltpu.make_async_remote_copy(
            src_ref=src,
            dst_ref=dst,
            send_sem=ss.at[n],
            recv_sem=rs.at[n],
            device_id=device,
            device_id_type=MESH,
        )
        started.append(Sent(copy, by))
        started[-1].start()
        return started[-1]

    wo_load = pltpu.make_async_copy(r.wo_hbm, r.wo, ls.at[2])
    ogr_load = pltpu.make_async_copy(r.ogr_hbm, r.ogr, ls.at[3])
    wst_load = pltpu.make_async_copy(r.wst_hbm, r.wst, ls.at[4])

    def pair_load(n, at):
        cols = pl.ds(pl.multiple_of(n * 128, 128), 128)
        return pltpu.make_async_copy(r.w_in.at[:, :, cols], r.pair.at[at], ls.at[at])

    pair_load(0, 0).start()
    pair_load(1, 1).start()
    ogr_load.start()
    wst_load.start()
    wo_load.start()

    barrier = pltpu.get_barrier_semaphore()
    for k in range(1, PEERS):
        pl.semaphore_signal(
            barrier, inc=1, device_id=(lax.rem(me + k, PEERS), side), device_id_type=MESH
        )
    pl.semaphore_signal(barrier, inc=1, device_id=other, device_id_type=MESH)

    i0 = lax.broadcasted_iota(I32, (ROWS, ROWS), 0)
    i1 = lax.broadcasted_iota(I32, (ROWS, ROWS), 1)
    deal = deal_ref[...]
    dest = lax.shift_right_logical(deal, 8)
    slot = jnp.bitwise_and(deal, ROWS - 1)
    member = (dest == lax.broadcasted_iota(I32, (PEERS, ROWS), 0)).astype(F32)
    before = dot(member.astype(BF16), (i0 < i1).astype(F32).astype(BF16))
    rank = jnp.sum(member * before, axis=0, keepdims=True)
    place = dest.astype(F32) * PER + rank
    hit = i0.astype(F32) == place
    to_send = hit.astype(F32)
    r.send_hot_t[...] = to_send.T.astype(BF16)
    send_hot = to_send.astype(BF16)
    ident = jnp.sum(to_send * slot.astype(F32), axis=1, keepdims=True)
    sb_h, sb_g, rb_h, rb_g, yb_h, yb_g = r.sb_h, r.sb_g, r.rb_h, r.rb_g, r.yb_h, r.yb_g
    sb_h[:, 0:HALF] = dot(send_hot, hid[...]).astype(BF16)
    sb_h[:, HALF : HALF + 128] = jnp.broadcast_to(ident, (ROWS, 128)).astype(BF16)

    pl.semaphore_wait(barrier, PEERS)

    def rows_of(device):
        return pl.ds(pl.multiple_of(device * PER, PER), PER)

    def away(dz, dx, dc):
        return lax.rem(zpos + dz + 4, 4) * 4 + lax.rem(xpos + dx, 2) * 2 + lax.rem(core + dc, 2)

    steps = [(dz, dx, dc) for dz in (2, 1, -1, 0) for dx in (0, 1) for dc in (0, 1)]

    def deal_out(src, dst):
        copies = {}
        for dz, dx, dc in steps:
            if (dz, dx, dc) != (0, 0, 0):
                to = away(dz, dx, dc)
                copies[dz, dx, dc] = send(src.at[rows_of(to)], dst.at[rows_of(me)], (to, side))
        dst[rows_of(me), :] = src[rows_of(me), :]
        return copies

    def pass_on(passed, group, copies, buf, dst):
        for dz, dx, dc in steps:
            if dz == group:
                if (dz, dx, dc) in copies:
                    copies[dz, dx, dc].wait_recv()
                origin = rows_of(away(-dz, dx, dc))
                passed.append(send(buf.at[origin, pl.ds(0, HALF)], dst.at[origin], other))

    dealt_h = deal_out(sb_h, rb_h)
    ogr_load.wait()
    sb_g[...] = dot(send_hot, r.ogr[...]).astype(BF16)

    ends, total = [], 0
    for k in range(8):
        total = total + lens[0, k]
        ends.append(total)

    def seg_at(pos):
        out = jnp.zeros(pos.shape, I32)
        for e in ends:
            out = out + (pos >= e).astype(I32)
        return out

    row_col = lax.broadcasted_iota(I32, (ROWS, 128), 0)
    seg_here = seg_at(row_col)
    for o in range(1, 4):
        same = (seg_at(row_col - o) == seg_here) & (row_col >= o)
        r.masks[o - 1] = same.astype(F32)
    same = seg_at(i0) == seg_at(i1)
    r.linked[...] = (same & (i0 >= i1)).astype(F32)
    r.linked_t[...] = (same & (i0 <= i1)).astype(F32)
    r.small[...] = jnp.zeros_like(r.small)
    vec[0:4, :] = r.conv_x[...].astype(F32)
    vec[4:12, :] = r.rows8[...]
    vec[12:16, 0:256] = r.conv_bc[...].astype(F32)
    wst_load.wait()
    wsp[...] = jnp.concatenate(
        [r.w_step[...].astype(F32), jnp.zeros((128 - HEADS, FULL), F32)], axis=0
    ).astype(BF16)
    r.dst_acc[...] = jnp.zeros((ROWS, ROWS), F32)
    r.drow[...] = jnp.zeros((128, ROWS), F32)
    r.dcol[...] = jnp.zeros((ROWS, 128), F32)
    r.dsd[...] = jnp.zeros((ROWS, 128), F32)

    picked = jnp.where(i0 < 128, 2 * i0, 2 * i0 - 255)
    apart = (picked == i1).astype(F32).astype(BF16)

    def take_apart(n):
        at = lax.rem(n, 2)
        pair_load(n, at).wait()
        cols = block_at(n, 128)
        flat = r.pair.at[at].reshape(2 * FULL, 128)
        for k in range(12):
            both = dot(apart, flat[k * 256 : (k + 1) * 256, :]).astype(BF16)
            r.wg[k * 128 : (k + 1) * 128, cols] = both[0:128]
            r.wv[k * 128 : (k + 1) * 128, cols] = both[128:256]

        @pl.when(n + 2 < 12)
        def _():
            pair_load(n + 2, at).start()

    passed_h, passed_g = [], []
    for first, last, group in ((0, 4, 0), (4, 7, 1), (7, 10, -1), (10, 12, 2)):
        pl.loop(first, last)(take_apart)
        pass_on(passed_h, group, dealt_h, rb_h, yb_h)
    dealt_g = deal_out(sb_g, rb_g)
    ids = rb_h[:, HALF : HALF + 128].astype(F32)
    r.hot_t[...] = (ids[:, 0:1] == i1.astype(F32)).astype(F32).astype(BF16)
    r.hot[...] = (ids.T[0:1, :] == i0.astype(F32)).astype(F32).astype(BF16)
    stream, upstream, normed = r.stream, r.upstream, r.normed
    stream[:, own_cols] = dot(r.hot[...], rb_h[:, 0:HALF]).astype(BF16)
    for copy in passed_h:
        copy.wait_recv()
    stream[:, other_cols] = dot(r.hot[...], yb_h[...]).astype(BF16)

    @pl.loop(0, 8)
    def _(n):
        rows = block_at(n, 32)
        s = stream[rows, :].astype(F32)
        scale = lax.rsqrt(jnp.sum(s * s, axis=1, keepdims=True) * (1.0 / FULL) + norm_eps)
        r.nscale[rows, :] = jnp.broadcast_to(scale, (32, 128))
        normed[rows, :] = (s * scale * vec[PRE_GAIN, :]).astype(BF16)

    there = pl.ds(ROWS, ROWS)
    norm_t, up_t = r.norm_t, r.up_t

    def swap_flipped(source, keep, give):
        for n in range(4):
            flipped = source[:, n * 384 : (n + 1) * 384].astype(F32).T.astype(BF16)
            for i in range(4):
                k = 4 * n + i
                piece = flipped[i * SHARE : (i + 1) * SHARE]

                @pl.when(core == k % 2)
                def _(k=k, piece=piece):
                    keep[k // 2, :, 0:ROWS] = piece

                @pl.when(core != k % 2)
                def _(k=k, piece=piece):
                    give[k // 2] = piece

        return send(give, keep.at[:, :, there], sibling)

    swap_norm = swap_flipped(normed, norm_t, r.norm_ts)

    masks = r.masks

    def conv_at(signal, taps, bias):
        out = bias + taps[3] * signal
        for o in range(1, 4):
            out = out + taps[3 - o] * (pltpu.roll(signal, o, 0) * masks[o - 1])
        return out

    def conv_back(signal, taps, bias, grad):
        pre = conv_at(signal, taps, bias)
        s = sigmoid(pre)
        d_pre = grad * (s * (1.0 + pre * (1.0 - s)))
        sums = [None] * 4
        sums[3] = jnp.sum(d_pre * signal, axis=0, keepdims=True)
        d_signal = taps[3] * d_pre
        for o in range(1, 4):
            masked = d_pre * masks[o - 1]
            sums[3 - o] = jnp.sum(masked * pltpu.roll(signal, o, 0), axis=0, keepdims=True)
            d_signal = d_signal + taps[3 - o] * pltpu.roll(masked, ROWS - o, 0)
        return d_signal, sums, jnp.sum(d_pre, axis=0, keepdims=True)

    def taps_at(first, cols):
        return [vec[pl.ds(first + k, 1), cols] for k in range(4)]

    gate_pre, value_pre, vconv = r.gate_pre, r.value_pre, r.vconv
    def project(n):
        cols = block_at(n, 256)
        gate_pre[:, cols] = dot(normed[...], r.wg[:, cols])
        value_pre[:, cols] = dot(normed[...], r.wv[:, cols])

    def convolve(n):
        cols = block_at(n, 128)
        pre = conv_at(value_pre[:, cols], taps_at(0, cols), vec[X_BIAS, cols])
        vconv[:, cols] = (pre * sigmoid(pre)).astype(BF16)

    for first, last, work, group in ((0, 4, project, 0), (4, 6, project, 1), (0, 6, convolve, -1), (6, 12, convolve, 2)):
        pl.loop(first, last)(work)
        pass_on(passed_g, group, dealt_g, rb_g, yb_g)

    state_pre, sconv = r.state_pre, r.sconv
    state_pre[...] = dot(normed[...], wst[...])
    for n in range(2):
        cols = pl.ds(n * 128, 128)
        pre = conv_at(state_pre[:, cols], taps_at(12, cols), vec[BC_BIAS, cols])
        sconv[:, cols] = (pre * sigmoid(pre)).astype(BF16)

    step_in = dot_t(normed[...], wsp[...]) + vec[STEP_BIAS, 0:128]
    small_e = jnp.exp(-jnp.abs(step_in))
    series = small_e * (1.0 - small_e * (0.5 - small_e * (1.0 / 3.0 - 0.25 * small_e)))
    step = jnp.maximum(step_in, 0.0) + jnp.where(small_e < 0.01, series, jnp.log(1.0 + small_e))
    decay = -jnp.exp(vec[A_LOG, 0:128])
    r.step_in[...] = step_in
    r.step[...] = step
    lower = (i0 >= i1).astype(F32)
    cum2 = jnp.dot(lower, step * decay, precision=HIGHEST, preferred_element_type=F32) * LOG2E
    r.cum2[...] = cum2
    r.cum2_t[...] = cum2.T
    r.cum2_ls[...] = (cum2 - jnp.log(step) * LOG2E).T
    b_rows, c_rows = sconv[:, 0:128], sconv[:, 128:256]
    r.scores[...] = dot_t(c_rows, b_rows) * r.linked[...]
    r.scores_t[...] = dot_t(b_rows, c_rows) * r.linked_t[...]

    lane = lax.broadcasted_iota(I32, (ROWS, 128), 1)
    lane_half = lax.broadcasted_iota(I32, (128, 128), 1) < 64

    def column(ref, h):
        return jnp.sum(jnp.where(lane == h, ref[...], 0.0), axis=1, keepdims=True)

    mixed = r.mixed

    @pl.loop(0, HEADS // 2)
    def _(p):
        cols = block_at(p, 128)
        x = vconv[:, cols]
        tops, lows = [], []
        for a in range(2):
            h = 2 * p + a
            cc = column(r.cum2, h)
            cr = r.cum2_ls[pl.ds(h, 1), :]
            w = jnp.exp2(jnp.minimum(cc[0:128] - cr[:, 0:128], 100.0)) * r.scores[0:128, 0:128]
            tops.append(dot(w.astype(BF16), x[0:128]))
            w = jnp.exp2(jnp.minimum(cc[128:256] - cr, 100.0)) * r.scores[128:256, :]
            lows.append(dot(w.astype(BF16), x))
        skip = jnp.where(lane_half[0:1], r.skip[2 * p], r.skip[2 * p + 1])
        xf = x.astype(F32)
        mixed[0:128, cols] = jnp.where(lane_half, tops[0], tops[1]) + skip * xf[0:128]
        mixed[128:256, cols] = jnp.where(lane_half, lows[0], lows[1]) + skip * xf[128:256]

    upstream[:, own_cols] = dot(r.hot[...], rb_g[...]).astype(BF16)
    for copy in passed_g:
        copy.wait_recv()
    upstream[:, other_cols] = dot(r.hot[...], yb_g[...]).astype(BF16)
    wo_load.wait()
    d_scaled = r.d_scaled
    r.acc1[...] = jnp.zeros((ROWS, 128), F32)
    r.acc2[...] = jnp.zeros((ROWS, 128), F32)

    @pl.loop(0, 6)
    def _(n):
        cols = block_at(n, 256)
        ds = dot_t(upstream[...], r.wo[cols, :])
        d_scaled[:, cols] = ds
        g = gate_pre[:, cols]
        gated = mixed[:, cols] * g * sigmoid(g)
        sq = gated * gated
        cr = vec[NORM_GAIN, cols] * ds * gated
        r.acc1[...] += sq[:, 0:128] + sq[:, 128:256]
        r.acc2[...] += cr[:, 0:128] + cr[:, 128:256]

    def exchange_rows(col_a, col_b, out_buf, in_buf):
        both = jnp.where(lane == 0, col_a, jnp.where(lane == 1, col_b, 0.0))
        out_buf[...] = both.T[0:8, :]
        copy = send(out_buf, in_buf, other)

        def finish():
            copy.wait_recv()
            both = jnp.concatenate([out_buf[...] + in_buf[...], jnp.zeros((120, ROWS), F32)], axis=0)
            return both.T[:, 0:1], both.T[:, 1:2]

        return finish

    row_sums = exchange_rows(
        jnp.sum(r.acc1[...], axis=1, keepdims=True),
        jnp.sum(r.acc2[...], axis=1, keepdims=True),
        r.ex_a,
        r.ex_b,
    )
    swap_up = swap_flipped(upstream, up_t, r.up_ts)
    sum_sq, sum_cross = row_sums()
    inner = 2.0 * CH
    inverse = lax.rsqrt(sum_sq * (1.0 / inner) + norm_eps)
    cross = inverse * inverse * inverse * (1.0 / inner) * sum_cross
    r.acc1[...] = jnp.broadcast_to(inverse, (ROWS, 128))
    r.acc2[...] = jnp.broadcast_to(cross, (ROWS, 128))
    scaled2, gate2, value2, misc2 = r.scaled2, r.gate2, r.value2, r.misc2
    here = pl.ds(0, ROWS)

    def gated_back(n):
        cols = block_at(n, 128)
        inv, crs = r.acc1[...], r.acc2[...]
        g, m, ds, gain = gate_pre[:, cols], mixed[:, cols], d_scaled[:, cols], vec[NORM_GAIN, cols]
        s = sigmoid(g)
        silu = g * s
        gated = m * silu
        gi = gated * inv
        scaled2[here, cols] = (gi * gain).astype(BF16)
        r.small[5:6, cols] = jnp.sum(ds * gi, axis=0, keepdims=True)
        d_gated = inv * ds * gain - gated * crs
        mixed[:, cols] = d_gated * silu
        gate2[here, cols] = (d_gated * m * (s * (1.0 + g * (1.0 - s)))).astype(BF16)

    def swap_columns(ref, first, width):
        cols = pl.ds(first, width)
        return send(ref.at[here, cols], ref.at[there, cols], sibling)

    swaps = {}
    for n in range(2):
        pl.loop(6 * n, 6 * n + 6)(gated_back)
        swaps["out", n] = swap_columns(scaled2, 768 * n, 768)
    for n in range(2):
        swaps["gate", n] = swap_columns(gate2, 768 * n, 768)

    half_f, half_o, half_in = d_scaled.at[:, pl.ds(0, HALF)], normed.at[:, pl.ds(0, HALF)], r.half_in
    flying = {}

    def project_other():
        @pl.loop(0, 3)
        def _(n):
            cols = pl.ds(pl.multiple_of((1 - side) * HALF + n * 256, 256), 256)
            half_o[:, block_at(n, 256)] = dot(scaled2[here, :], r.wo[:, cols]).astype(BF16)

        flying["out"] = send(half_o, half_in, other)

    def project_own():
        @pl.loop(0, 3)
        def _(n):
            cols = pl.ds(pl.multiple_of(side * HALF + n * 256, 256), 256)
            half_f[:, block_at(n, 256)] = dot(scaled2[here, :], r.wo[:, cols]) + stream[:, cols].astype(F32)

    lefts = {"out": up_t, "gate": norm_t, "value": norm_t, "misc": norm_t}
    rights = {"out": scaled2, "gate": gate2, "value": value2, "misc": misc2}
    kept = {"out": r.o_wo, "gate": r.o_gate, "value": r.o_value, "misc": r.o_misc}
    swap_width = {"out": 768, "gate": 768, "value": 384, "misc": 256}

    def ready(copy):
        if not copy.here:
            copy.wait_recv()

    class Unit:
        def __init__(self, n):
            self.name, self.kind, self.first, self.width = UNITS[n]
            self.part, self.xbuf, self.zbuf = r.part[n], r.xbuf[n], r.zbuf[n]
            line = [self.send_in, self.pass_outer, self.pass_inner, self.send_out]
            if self.kind == "x":
                self.stages = [self.compute, self.take_across, *line[1:], self.keep_line]
            else:
                self.stages = [self.compute, *line[1:], self.give_across, self.keep_across]

        def go(self, stage):
            self.stages[stage]()

        def at(self, z):
            return (z, xpos) if self.kind == "x" else (z,)

        def add(self, z, ref):
            if self.kind == "x":
                self.part[z, xpos] = self.part[z, xpos] + ref[0]
            else:
                for k in range(2):
                    self.part[z, k] = self.part[z, k] + ref[k]

        def hop(self, z, slot, device, by):
            if self.kind == "x":
                return send(self.part.at[z, xpos], self.zbuf.at[slot, 0], device, by)
            return send(self.part.at[z], self.zbuf.at[slot], device, by)

        def compute(self):
            lhs_ref, rhs_ref = lefts[self.name], rights[self.name]
            first, part = self.first, self.part
            ready(swap_up if self.name == "out" else swap_norm)
            for (name, n), copy in swaps.items():
                start = n * swap_width[name]
                if name == self.name and start < first + self.width and first < start + swap_width[name]:
                    ready(copy)

            @pl.loop(0, self.width // 256)
            def _(n):
                lhs = lhs_ref[...].reshape(8 * SHARE, 2 * ROWS)
                rhs = rhs_ref[:, pl.ds(pl.multiple_of(first + n * 256, 256), 256)]
                part[:, :, :, block_at(n, 256)] = dot(lhs, rhs).astype(BF16).reshape(4, 2, SHARE, 256)

            if self.kind == "x":
                self.cx = send(self.part.at[:, 1 - xpos], self.xbuf, across)
            else:
                self.send_in()

        def take_across(self):
            self.cx.wait_recv()
            for k in range(4):
                self.part[k, xpos] = self.part[k, xpos] + self.xbuf[k]
            self.send_in()

        def send_in(self):
            self.c3 = self.hop(far_outer, 0, near, is_outer)
            self.c2 = self.hop(far_inner, 1, near, is_outer)
            self.c1 = self.hop(z_inner, 2, near, is_outer)

        def pass_outer(self):
            @pl.when(is_inner)
            def _():
                self.c3.wait_recv()
                self.add(far_outer, self.zbuf.at[0])

            self.d2 = self.hop(far_outer, 3, facing, is_inner)

        def pass_inner(self):
            @pl.when(is_inner)
            def _():
                self.c2.wait_recv()
                self.add(far_inner, self.zbuf.at[1])

            self.d1 = self.hop(far_inner, 4, facing, is_inner)

        def send_out(self):
            @pl.when(is_inner)
            def _():
                self.d2.wait_recv()
                self.add(z_outer, self.zbuf.at[3])

            self.e1 = self.hop(z_outer, 0, near, is_inner)

        def line_end(self, use):
            @pl.when(is_outer)
            def _():
                self.e1.wait_recv()
                use(lambda k: self.zbuf[0, k].astype(F32))

            @pl.when(is_inner)
            def _():
                self.c1.wait_recv()
                self.d1.wait_recv()
                use(lambda k: self.zbuf[2, k].astype(F32) + self.zbuf[4, k].astype(F32))

        def keep_line(self):
            self.line_end(lambda came: self.keep(self.part[zpos, xpos].astype(F32) + came(0)))

        def give_across(self):
            def use(came):
                give = self.part[zpos, 1 - xpos].astype(F32) + came(1 - xpos)
                self.part[zpos, 1 - xpos] = give.astype(BF16)
                self.keep(self.part[zpos, xpos].astype(F32) + came(xpos))

            self.line_end(use)
            self.cx = send(self.part.at[zpos, 1 - xpos], self.xbuf, across)

        def keep_across(self):
            self.cx.wait_recv()
            cols = slice(self.first, self.first + self.width)
            kept[self.name][:, cols] = kept[self.name][:, cols] + self.xbuf[...].astype(F32)

        def keep(self, value):
            kept[self.name][:, self.first : self.first + self.width] = value

    units = [Unit(n) for n in range(len(UNITS))]
    head_row = lax.broadcasted_iota(I32, (32, ROWS), 0)

    def mixer_back(p):
        cols = block_at(p, 128)
        x = vconv[:, cols]
        xf = x.astype(F32)
        dy = mixed[:, cols]
        dyb = dy.astype(BF16)
        r.small[6:7, cols] = jnp.sum(dy * xf, axis=0, keepdims=True)
        d_tops, d_lows = [], []
        for a in range(2):
            h = 2 * p + a
            half = (lane < 64) if a == 0 else (lane >= 64)
            xa = jnp.where(half, xf, 0.0)
            xab = xa.astype(BF16)
            cc = column(r.cum2, h)
            st = column(r.step, h)
            cr = r.cum2_t[pl.ds(h, 1), :]
            w = jnp.exp2(jnp.minimum(cr - cc[0:128], 0.0))
            sc = r.scores_t[0:128, :]
            v_top = dot((w * sc).astype(BF16), dyb)
            q = dot_t(xab[0:128], dyb) * w * st[0:128]
            r.dst_acc[0:128, :] += q
            g_top = q * sc
            w = jnp.exp2(jnp.minimum(cr[:, 128:256] - cc[128:256], 0.0))
            sc = r.scores_t[128:256, 128:256]
            v_low = dot((w * sc).astype(BF16), dyb[128:256])
            q = dot_t(xab[128:256], dyb[128:256]) * w * st[128:256]
            r.dst_acc[128:256, 128:256] += q
            g_low = q * sc
            top_sums = jnp.sum(g_top, axis=0, keepdims=True)
            low_sums = jnp.sum(g_low, axis=0, keepdims=True)
            col_sums = jnp.concatenate([top_sums[:, 0:128], top_sums[:, 128:256] + low_sums], axis=1)
            r.drow[0:32, :] += jnp.where(head_row == h, col_sums, 0.0)
            row_sums = jnp.concatenate(
                [
                    jnp.sum(g_top[:, 0:128] + g_top[:, 128:256], axis=1, keepdims=True),
                    jnp.sum(g_low, axis=1, keepdims=True),
                ],
                axis=0,
            )
            direct = jnp.concatenate(
                [
                    jnp.sum(xa[0:128] * v_top, axis=1, keepdims=True),
                    jnp.sum(xa[128:256] * v_low, axis=1, keepdims=True),
                ],
                axis=0,
            )
            r.dcol[...] += jnp.where(lane == h, row_sums, 0.0)
            r.dsd[...] += jnp.where(lane == h, direct, 0.0)
            d_tops.append(st[0:128] * v_top)
            d_lows.append(st[128:256] * v_low)
        d_conv = jnp.concatenate(
            [jnp.where(lane_half, d_tops[0], d_tops[1]), jnp.where(lane_half, d_lows[0], d_lows[1])],
            axis=0,
        )
        d_conv = d_conv + jnp.where(lane_half[0:1], r.skip[2 * p], r.skip[2 * p + 1]) * dy
        d_value, sums, bias_sum = conv_back(value_pre[:, cols], taps_at(0, cols), vec[X_BIAS, cols], d_conv)
        value2[here, cols] = d_value.astype(BF16)
        for k in range(4):
            r.small[k : k + 1, cols] = sums[k]
        r.small[4:5, cols] = bias_sum

    def mixer_part(n):
        pl.loop(3 * n, 3 * n + 3)(mixer_back)
        swaps["value", n] = swap_columns(value2, 384 * n, 384)

    def send_back(src, dst):
        copies = []
        for step in steps:
            if step != (0, 0, 0):
                to = away(*step)
                copies.append(send(src.at[rows_of(to)], dst.at[rows_of(me)], (to, side)))
        dst[rows_of(me), :] = src[rows_of(me), :]
        return copies

    def return_out():
        ready(flying["out"])
        result = (half_f[...] + half_in[...].astype(F32)).astype(BF16)
        yb_h[...] = dot(r.hot_t[...], result).astype(BF16)
        flying["back_o"] = send_back(yb_h, r.back_o)

    def finish_out():
        for copy in flying["back_o"]:
            copy.wait_recv()
        r.o_out[...] = dot(r.send_hot_t[...], r.back_o[...]).astype(BF16)

    d_state = r.d_state
    state_own = pl.ds(pl.multiple_of(side * 128, 128), 128)
    state_other = pl.ds(pl.multiple_of((1 - side) * 128, 128), 128)

    def states_back():
        d_scores_t = r.dst_acc[...] * r.linked_t[...]
        d_conv_s = r.d_conv_s
        d_conv_s[:, 0:128] = dot(d_scores_t.astype(BF16), c_rows)
        d_conv_s[:, 128:256] = dot(d_scores_t.T.astype(BF16), b_rows)
        for n in range(2):
            cols = pl.ds(n * 128, 128)
            d_pre, sums, bias_sum = conv_back(
                state_pre[:, cols], taps_at(12, cols), vec[BC_BIAS, cols], d_conv_s[:, cols]
            )
            d_state[:, cols] = d_pre
            for k in range(4):
                r.small[8 + k : 9 + k, cols] = sums[k]
            r.small[12:13, cols] = bias_sum
        r.st_out[...] = d_state[:, state_other].astype(BF16)
        flying["state"] = send(r.st_out, r.st_in, other)
        d_cum = r.drow[...].T - r.dcol[...]
        upper = (i0 <= i1).astype(F32)
        d_rate = jnp.dot(upper, d_cum, precision=HIGHEST, preferred_element_type=F32)
        d_step = (r.dsd[...] + d_rate * decay) * sigmoid(r.step_in[...])
        r.small[13:14, 0:128] = jnp.sum(d_step, axis=0, keepdims=True)
        r.small[14:15, 0:128] = jnp.sum(d_rate * r.step[...], axis=0, keepdims=True) * decay
        misc2[here, 128:256] = d_step.astype(BF16)
        r.acc1[...] = jnp.zeros((ROWS, 128), F32)
        r.st_low[...] = d_state[...].astype(BF16)

    def swap_state():
        ready(flying["state"])
        misc2[here, 0:128] = (d_state[:, state_own] + r.st_in[...].astype(F32)).astype(BF16)
        swaps["misc", 0] = swap_columns(misc2, 0, 256)

    dhalf_f, dhalf_o, dhalf_in = d_scaled.at[:, pl.ds(HALF, HALF)], normed.at[:, pl.ds(HALF, HALF)], r.dhalf_in

    def d_normed_at(first):
        rows = pl.ds(pl.multiple_of(first, 256), 256)
        out = dot_t(gate2[here, :], r.wg[rows, :]) + dot_t(value2[here, :], r.wv[rows, :])
        out = out + dot_t(r.st_low[...], r.wst[rows, :])
        out = out + dot(misc2[here, 128:256], wsp[:, rows])
        part = out * vec[PRE_GAIN, rows] * stream[:, rows].astype(F32)
        r.acc1[...] += part[:, 0:128] + part[:, 128:256]
        return out

    def normed_other():
        @pl.loop(0, 3)
        def _(n):
            dhalf_o[:, block_at(n, 256)] = d_normed_at((1 - side) * HALF + n * 256).astype(BF16)

        flying["norm"] = send(dhalf_o, dhalf_in, other)

    def normed_own():
        @pl.loop(0, 3)
        def _(n):
            dhalf_f[:, block_at(n, 256)] = d_normed_at(side * HALF + n * 256)

        flying["rows"] = exchange_rows(
            jnp.sum(r.acc1[...], axis=1, keepdims=True), jnp.zeros((ROWS, 1), F32), r.ex_c, r.ex_d
        )

    small = r.small

    def return_grad():
        row_cross, _ = flying["rows"]()
        ready(flying["norm"])
        flying["out"].wait_send()
        scale = r.nscale[:, 0:1]
        factor = scale * scale * scale * (1.0 / FULL) * row_cross
        for n in range(6):
            cols = pl.ds(n * 128, 128)
            mine = pl.ds(pl.multiple_of(side * HALF + n * 128, 128), 128)
            dn = dhalf_f[:, cols] + dhalf_in[:, cols].astype(F32)
            s = stream[:, mine].astype(F32)
            small[7:8, n * 128 : (n + 1) * 128] = jnp.sum(dn * s * scale, axis=0, keepdims=True)
            grad = upstream[:, mine].astype(F32) + scale * vec[PRE_GAIN, mine] * dn - s * factor
            half_o[:, cols] = grad.astype(BF16)
        yb_g[...] = dot(r.hot_t[...], half_o[...]).astype(BF16)
        flying["back_g"] = send_back(yb_g, r.back_g)

    def finish_grad():
        for copy in flying["back_g"]:
            copy.wait_recv()
        r.o_hid[...] = dot(r.send_hot_t[...], r.back_g[...]).astype(BF16)

    def small_tensor():
        flying["small"] = send(small.at[pl.ds(8, 8), pl.ds(0, 256)], r.sm_y, other)

    def small_tensor_end():
        copy = flying["small"]
        copy.wait_send()
        copy.wait_recv()
        keep_rows = lax.broadcasted_iota(I32, (8, 256), 0) < 5
        small[8:16, 0:256] = small[8:16, 0:256] + jnp.where(keep_rows, r.sm_y[...], 0.0)

    partners = [sibling, across, near, facing]

    def small_start(n):
        flying[n] = [
            send(small.at[pl.ds(0, 8)], r.sm_a[n], partners[n]),
            send(small.at[pl.ds(8, 8), pl.ds(0, 256)], r.sm_b[n], partners[n]),
        ]

    def small_end(n):
        for copy in flying[n]:
            copy.wait_send()
            copy.wait_recv()
        small[0:8, :] = small[0:8, :] + r.sm_a[n][...]
        small[8:16, 0:256] = small[8:16, 0:256] + r.sm_b[n][...]

    project_other()
    mixer_part(0)
    units[0].go(0)
    units[1].go(0)
    units[2].go(0)
    units[3].go(0)
    units[4].go(0)
    units[5].go(0)
    units[6].go(0)
    units[7].go(0)
    mixer_part(1)
    units[5].go(1)
    units[0].go(1)
    mixer_part(2)
    units[5].go(2)
    units[1].go(1)
    units[8].go(0)
    units[0].go(2)
    units[5].go(3)
    mixer_part(3)
    units[1].go(2)
    units[0].go(3)
    units[2].go(1)
    units[0].go(4)
    units[1].go(3)
    units[9].go(0)
    states_back()
    units[1].go(4)
    units[2].go(2)
    units[5].go(4)
    units[2].go(3)
    units[10].go(0)
    units[3].go(1)
    units[11].go(0)
    normed_other()
    units[2].go(4)
    units[3].go(2)
    units[3].go(3)
    swap_state()
    units[0].go(5)
    units[1].go(5)
    project_own()
    units[11].go(1)
    return_out()
    units[3].go(4)
    units[12].go(0)
    units[11].go(2)
    normed_own()
    units[11].go(3)
    units[4].go(1)
    units[2].go(5)
    return_grad()
    small_tensor()
    small_tensor_end()
    small_start(0)
    units[3].go(5)
    units[4].go(2)
    small_end(0)
    small_start(1)
    units[4].go(3)
    units[11].go(4)
    units[6].go(1)
    units[7].go(1)
    units[4].go(4)
    units[6].go(2)
    units[6].go(3)
    units[6].go(4)
    units[7].go(2)
    units[7].go(3)
    units[7].go(4)
    units[4].go(5)
    units[8].go(1)
    units[8].go(2)
    units[8].go(3)
    units[8].go(4)
    units[6].go(5)
    units[9].go(1)
    units[5].go(5)
    units[9].go(2)
    units[9].go(3)
    units[9].go(4)
    units[7].go(5)
    units[10].go(1)
    units[10].go(2)
    units[10].go(3)
    units[10].go(4)
    finish_out()
    units[8].go(5)
    units[12].go(1)
    units[12].go(2)
    units[12].go(3)
    units[9].go(5)
    finish_grad()
    units[10].go(5)
    small_end(1)
    small_start(2)
    units[11].go(5)
    units[12].go(4)
    small_end(2)
    small_start(3)
    units[12].go(5)
    small_end(3)
    r.o_small[...] = small[...]
    for copy in started:
        copy.wait_send()


def scratch():
    vmem, dma = pltpu.VMEM, pltpu.SemaphoreType.DMA
    square, wide = (ROWS, ROWS), (ROWS, CH)
    def rows(dtype, width):
        return vmem((ROWS, width), dtype)

    return dict(
        wg=vmem((FULL, CH), BF16),
        wv=vmem((FULL, CH), BF16),
        wo=vmem((CH, FULL), BF16),
        pair=vmem((2, FULL, 2, 128), BF16),
        send_hot_t=vmem(square, BF16),
        hot=vmem(square, BF16),
        hot_t=vmem(square, BF16),
        sb_h=rows(BF16, HALF + 128),
        rb_h=rows(BF16, HALF + 128),
        sb_g=rows(BF16, HALF),
        rb_g=rows(BF16, HALF),
        yb_h=rows(BF16, HALF),
        yb_g=rows(BF16, HALF),
        half_in=rows(BF16, HALF),
        dhalf_in=rows(BF16, HALF),
        back_o=rows(BF16, HALF),
        back_g=rows(BF16, HALF),
        masks=vmem((3, ROWS, 128), F32),
        linked=vmem(square, F32),
        linked_t=vmem(square, F32),
        scores=vmem(square, F32),
        scores_t=vmem(square, F32),
        dst_acc=vmem(square, F32),
        small=vmem((16, CH), F32),
        vec=vmem((16, CH), F32),
        wsp=vmem((128, FULL), BF16),
        ogr=rows(BF16, HALF),
        wst=vmem((FULL, 256), BF16),
        drow=vmem((128, ROWS), F32),
        cum2_t=vmem((128, ROWS), F32),
        cum2_ls=vmem((128, ROWS), F32),
        stream=vmem(wide, BF16),
        upstream=vmem(wide, BF16),
        normed=vmem(wide, BF16),
        vconv=vmem(wide, BF16),
        gate_pre=vmem(wide, F32),
        value_pre=vmem(wide, F32),
        mixed=vmem(wide, F32),
        d_scaled=vmem(wide, F32),
        state_pre=rows(F32, 256),
        d_state=rows(F32, 256),
        d_conv_s=rows(F32, 256),
        sconv=rows(BF16, 256),
        st_low=rows(BF16, 256),
        st_out=rows(BF16, 128),
        st_in=rows(BF16, 128),
        scaled2=vmem((2 * ROWS, CH), BF16),
        gate2=vmem((2 * ROWS, CH), BF16),
        value2=vmem((2 * ROWS, CH), BF16),
        misc2=vmem((2 * ROWS, 256), BF16),
        norm_t=vmem((8, SHARE, 2 * ROWS), BF16),
        up_t=vmem((8, SHARE, 2 * ROWS), BF16),
        norm_ts=vmem((8, SHARE, ROWS), BF16),
        up_ts=vmem((8, SHARE, ROWS), BF16),
        nscale=rows(F32, 128),
        acc1=rows(F32, 128),
        acc2=rows(F32, 128),
        dcol=rows(F32, 128),
        dsd=rows(F32, 128),
        step_in=rows(F32, 128),
        step=rows(F32, 128),
        cum2=rows(F32, 128),
        ex_a=vmem((8, ROWS), F32),
        ex_b=vmem((8, ROWS), F32),
        ex_c=vmem((8, ROWS), F32),
        ex_d=vmem((8, ROWS), F32),
        sm_y=vmem((8, 256), F32),
        sm_a=[vmem((8, CH), F32) for _ in range(4)],
        sm_b=[vmem((8, 256), F32) for _ in range(4)],
        part=[vmem((4, 2, SHARE, width), BF16) for _, _, _, width in UNITS],
        xbuf=[vmem((*([4] if kind == "x" else []), SHARE, width), BF16) for _, kind, _, width in UNITS],
        zbuf=[vmem((5, 1 if kind == "x" else 2, SHARE, width), BF16) for _, kind, _, width in UNITS],
        ss=dma((SENDS,)),
        rs=dma((SENDS,)),
        ls=dma((5,)),
    )


SENDS = 6 * PEERS + 7 * len(UNITS) + 30


def finish_body(wo, gate, value, misc, small, out, hid, *outs):
    (
        o_out, o_hid, o_pre, o_in, o_state, o_step, o_cx, o_cxb, o_cb, o_cbb, o_bias, o_log, o_skip, o_gain, o_wo
    ) = outs
    o_out[...] = out[...]
    o_hid[...] = hid[...]
    o_pre[...] = small[7, 0:HALF]
    o_in[:, 0, :] = gate[...]
    o_in[:, 1, :] = value[...]
    o_state[...] = misc[:, 0:128]
    o_step[...] = misc[:, 128:256].T[0:HEADS]
    o_cx[...] = small[0:4, :]
    o_cxb[...] = small[4, :]
    o_cb[...] = small[8:12, 0:256]
    o_cbb[...] = small[12, 0:256]
    o_bias[...] = small[13, 0:HEADS]
    o_log[...] = small[14, 0:HEADS]
    head = lax.broadcasted_iota(I32, (CH, 128), 0) // (CH // HEADS)
    mine = (head == lax.broadcasted_iota(I32, (CH, 128), 1)).astype(F32)
    skips = jnp.dot(small[0:8, :], mine, precision=HIGHEST, preferred_element_type=F32)
    o_skip[...] = skips[6, 0:HEADS]
    o_gain[...] = small[5, :]
    o_wo[...] = wo[...]


def one_kernel(
    hidden_in,
    out_grad,
    seq_lengths,
    deal_to,
    pre_gain,
    w_in,
    w_state,
    w_step,
    conv_x,
    conv_x_bias,
    conv_bc,
    conv_bc_bias,
    step_bias,
    a_log,
    skip,
    norm_gain,
    w_out,
):
    at = lax.broadcasted_iota(I32, (8, CH), 0)
    rows8 = jnp.zeros((8, CH), F32)
    for n, v in enumerate((conv_x_bias, norm_gain, pre_gain, conv_bc_bias, step_bias, a_log)):
        v = jnp.pad(v.astype(F32), (0, CH - v.shape[0]))
        rows8 = jnp.where(at == n, v[None, :], rows8)
    inputs = dict(
        hid=hidden_in,
        ogr_hbm=out_grad,
        lens=seq_lengths,
        deal=deal_to.reshape(1, ROWS),
        rows8=rows8,
        conv_x=conv_x,
        conv_bc=conv_bc,
        skip=skip,
        w_in=w_in,
        wo_hbm=w_out,
        wst_hbm=w_state,
        w_step=w_step.T,
    )
    in_vmem = pl.BlockSpec(memory_space=pltpu.VMEM)
    places = dict(lens=pltpu.SMEM, skip=pltpu.SMEM)
    for name in ("ogr_hbm", "w_in", "wo_hbm", "wst_hbm"):
        places[name] = pl.ANY
    f32_out = partial(jax.ShapeDtypeStruct, dtype=F32)
    half = jax.ShapeDtypeStruct((ROWS, HALF), BF16)
    outputs = dict(
        o_wo=f32_out((SHARE, CH)),
        o_gate=f32_out((SHARE, CH)),
        o_value=f32_out((SHARE, CH)),
        o_misc=f32_out((SHARE, 256)),
        o_small=f32_out((16, CH)),
        o_out=half,
        o_hid=half,
    )
    room = scratch()
    flat = [ref for shape in room.values() for ref in (shape if isinstance(shape, list) else [shape])]
    made = pl.pallas_call(
        partial(block_body, {**inputs, **outputs, **room}),
        out_shape=list(outputs.values()),
        in_specs=[pl.BlockSpec(memory_space=places.get(n, pltpu.VMEM)) for n in inputs],
        out_specs=[in_vmem] * len(outputs),
        scratch_shapes=flat,
        compiler_params=pltpu.CompilerParams(
            collective_id=0, has_side_effects=True, vmem_limit_bytes=VMEM_BYTES
        ),
        name="block",
    )(*inputs.values())
    shapes = [(HALF,), (SHARE, 2, CH), (SHARE, 128), (HEADS, SHARE), (4, CH), (CH,), (4, 256), (256,)]
    shapes += [(HEADS,)] * 3 + [(CH,), (SHARE, CH)]
    results = pl.pallas_call(
        finish_body,
        out_shape=[half, half, *(f32_out(s) for s in shapes)],
        in_specs=[in_vmem] * len(made),
        out_specs=[in_vmem] * (len(shapes) + 2),
        compiler_params=pltpu.CompilerParams(vmem_limit_bytes=VMEM_BYTES),
        name="finish",
    )(*made)
    return (*results[:5], results[5].T, *results[6:14], results[14].T)


VMEM_BYTES = 65_000_000


def fits(mesh, args):
    return mesh.shape["dp"] == PEERS and mesh.shape["tensor"] == 2 and args[0].shape == (PEERS * ROWS, FULL)


def solution(mesh):
    in_specs = (
        P("dp", "tensor"),
        P("dp", "tensor"),
        P("dp", None),
        P("dp"),
        P(),
        P(None, None, "tensor"),
        P(),
        P(None, "tensor"),
        P(None, "tensor"),
        P("tensor"),
        P(),
        P(),
        P("tensor"),
        P("tensor"),
        P("tensor"),
        P("tensor"),
        P("tensor", None),
    )
    out_specs = (
        P("dp", "tensor"),
        P("dp", "tensor"),
        P("tensor"),
        P("dp", None, "tensor"),
        P("dp", "tensor"),
        P("dp", "tensor"),
        P(None, "tensor"),
        P("tensor"),
        P(),
        P(),
        P("tensor"),
        P("tensor"),
        P("tensor"),
        P("tensor"),
        P("tensor", "dp"),
    )

    def whole(*args):
        local = one_kernel if fits(mesh, args) else shards
        mapped = jax.shard_map(
            local, mesh=mesh, in_specs=in_specs, out_specs=out_specs, check_vma=False
        )
        return mapped(*args)

    return whole
```

```python
from functools import partial
from types import SimpleNamespace

import jax
import jax.numpy as jnp
from jax import lax
from jax.experimental import pallas as pl
from jax.experimental.pallas import tpu as pltpu
from jax.sharding import PartitionSpec as P

D = 1536
GROUP = 256
INNER = 3072


norm_eps = 1e-05


def segment_ids(lengths, row_count):
    index = jnp.arange(lengths.shape[0])
    ends = jnp.sum(jnp.where(index[None, :] <= index[:, None], lengths[None, :], 0), axis=1)
    position = jnp.arange(row_count, dtype=jnp.int32)
    return jnp.sum((position[:, None] >= ends[None, :]).astype(jnp.int32), axis=1, dtype=jnp.int32)


def causal_conv(signal, kernel, kernel_bias, segment):
    width = kernel.shape[0]
    total = kernel_bias[None, :] + kernel[width - 1][None, :] * signal
    for offset in range(1, width):
        moved = jnp.concatenate(
            [jnp.zeros((offset, signal.shape[1]), signal.dtype), signal[:-offset]], axis=0
        )
        earlier = jnp.concatenate([jnp.full((offset,), -1, jnp.int32), segment[:-offset]])
        inside = (earlier == segment).astype(signal.dtype)
        total = total + kernel[width - 1 - offset][None, :] * moved * inside[:, None]
    return total


def state_space(xval, b_rows, c_rows, step, decay, segment):
    highest = lax.Precision.HIGHEST
    blocks = xval.shape[0] // GROUP
    head_count = xval.shape[1]
    x_block = xval.reshape(blocks, GROUP, head_count, xval.shape[2])
    b_block = b_rows.reshape(blocks, GROUP, b_rows.shape[1])
    c_block = c_rows.reshape(blocks, GROUP, c_rows.shape[1])
    step_block = step.reshape(blocks, GROUP, head_count).transpose(0, 2, 1)
    rate_block = step_block * decay[None, :, None]
    seg_block = segment.reshape(blocks, GROUP)
    before = jnp.concatenate([jnp.full((1,), -1, jnp.int32), segment[:-1]]).reshape(blocks, GROUP)[
        :, 0
    ]
    lower_mask = jnp.tril(jnp.ones((GROUP, GROUP), dtype=bool))
    cumulative = jnp.einsum("chj,ij->chi", rate_block, lower_mask.astype(jnp.float32), precision=highest)
    linked = (seg_block[:, :, None] == seg_block[:, None, :]) & lower_mask[None]
    spread = cumulative[:, :, :, None] - cumulative[:, :, None, :]
    weight = jnp.exp(jnp.where(linked[:, None], spread, -10000.0))
    scores = jnp.einsum("cin,cjn->cij", c_block, b_block, precision=highest)
    mixing = weight * scores[:, None] * step_block[:, :, None, :]
    inside_out = jnp.einsum("chij,cjhp->cihp", mixing, x_block, precision=highest)
    final_cum = cumulative[:, :, -1]
    last_same = (seg_block == seg_block[:, -1:]).astype(jnp.float32)
    tail_weight = jnp.exp(final_cum[:, :, None] - cumulative) * last_same[:, None, :] * step_block
    fresh_state = jnp.einsum("chj,cjhp,cjn->chpn", tail_weight, x_block, b_block, precision=highest)
    carried = jnp.zeros(fresh_state.shape[1:], jnp.float32)
    entering = []
    entering.append(carried)
    entering = jnp.stack(entering)
    first_same = (seg_block == before[:, None]).astype(jnp.float32)
    head_decay = jnp.exp(cumulative) * first_same[:, None, :]
    carried_out = jnp.einsum("chi,cin,chpn->cihp", head_decay, c_block, entering, precision=highest)
    return (inside_out + carried_out).reshape(xval.shape)


def pre_norm(stream, gain):
    return stream * lax.rsqrt(jnp.mean(stream * stream, axis=1, keepdims=True) + norm_eps) * gain


def conv_piece(value_pre, state_pre, conv_x, conv_x_bias, conv_bc, conv_bc_bias, segment):
    value_conv = jax.nn.silu(causal_conv(value_pre, conv_x, conv_x_bias, segment))
    state_conv = jax.nn.silu(causal_conv(state_pre, conv_bc, conv_bc_bias, segment))
    return (value_conv, state_conv)


def mixer_piece(value_conv, state_conv, step_pre, step_bias, a_log, skip, segment):
    head_count = step_bias.shape[0]
    row_count = value_conv.shape[0]
    heads_in = value_conv.reshape(row_count, head_count, value_conv.shape[1] // head_count)
    step = jax.nn.softplus(step_pre + step_bias)
    decay = -jnp.exp(a_log)
    half_state = state_conv.shape[1] // 2
    mixed = state_space(
        heads_in, state_conv[:, :half_state], state_conv[:, half_state:], step, decay, segment
    )
    return (mixed + skip[None, :, None] * heads_in).reshape(row_count, value_conv.shape[1])


def rounded(values):
    return lax.optimization_barrier(values.astype(jnp.bfloat16)).astype(jnp.float32)


def shards(
    hidden_in,
    out_grad,
    seq_lengths,
    deal_to,
    pre_gain,
    w_in,
    w_state,
    w_step,
    conv_x,
    conv_x_bias,
    conv_bc,
    conv_bc_bias,
    step_bias,
    a_log,
    skip,
    norm_gain,
    w_out,
):
    dp_count = lax.axis_size("dp")
    row_count = hidden_in.shape[0]
    per_peer = row_count // dp_count
    feat_half = hidden_in.shape[1]
    tensor_index = lax.axis_index("tensor")
    send_order = jnp.argsort(deal_to)
    back_order = jnp.argsort(send_order)
    sent_in = hidden_in[send_order].reshape(dp_count, per_peer, feat_half)
    sent_grad = out_grad[send_order].reshape(dp_count, per_peer, feat_half)
    got_in, got_grad = (
        lax.all_to_all(sent_in, "dp", split_axis=0, concat_axis=0, tiled=True),
        lax.all_to_all(sent_grad, "dp", split_axis=0, concat_axis=0, tiled=True),
    )
    got_ids = lax.all_to_all(
        deal_to[send_order].reshape(dp_count, per_peer),
        "dp",
        split_axis=0,
        concat_axis=0,
        tiled=True,
    )
    dealt_slot = got_ids.reshape(row_count) % row_count
    settle_order = jnp.argsort(dealt_slot)
    dealt_half = got_in.reshape(row_count, feat_half)[settle_order]
    grad_half = got_grad.reshape(row_count, feat_half)[settle_order]
    full_in, grad_full = (
        lax.all_gather(dealt_half, "tensor", axis=1, tiled=True),
        lax.all_gather(grad_half, "tensor", axis=1, tiled=True),
    )
    segment = segment_ids(seq_lengths[0], row_count)
    stream = full_in.astype(jnp.float32)
    normed_f, norm_pull = jax.vjp(pre_norm, stream, pre_gain.astype(jnp.float32))
    normed = normed_f.astype(jnp.bfloat16)
    inner_half = w_in.shape[2]
    w_pair = w_in.reshape(w_in.shape[0], 2 * inner_half)
    proj_pair = jnp.dot(normed, w_pair, preferred_element_type=jnp.float32)
    gate_pre = proj_pair[:, :inner_half]
    value_pre = proj_pair[:, inner_half:]
    state_pre = jnp.dot(normed, w_state, preferred_element_type=jnp.float32)
    step_pre = jnp.dot(normed, w_step, preferred_element_type=jnp.float32)
    conv_args = (
        value_pre,
        state_pre,
        conv_x.astype(jnp.float32),
        conv_x_bias.astype(jnp.float32),
        conv_bc.astype(jnp.float32),
        conv_bc_bias.astype(jnp.float32),
    )
    (value_conv_f, state_conv_f), conv_pull = jax.vjp(
        partial(conv_piece, segment=segment), *conv_args
    )
    value_conv = rounded(value_conv_f)
    state_conv = rounded(state_conv_f)
    mixed, mixer_pull = jax.vjp(
        partial(mixer_piece, segment=segment),
        value_conv,
        state_conv,
        step_pre,
        step_bias,
        a_log,
        skip,
    )
    silu_gate = jax.nn.silu(gate_pre)
    gated = mixed * silu_gate
    total_squares = lax.psum(jnp.sum(gated * gated, axis=1), "tensor")
    inverse = lax.rsqrt(total_squares / INNER + norm_eps)
    gain_f = norm_gain.astype(jnp.float32)
    scaled = (gated * inverse[:, None] * gain_f).astype(jnp.bfloat16)
    partial_out = jnp.dot(scaled, w_out, preferred_element_type=jnp.float32)
    branch = lax.psum_scatter(partial_out, "tensor", scatter_dimension=1, tiled=True)
    result = (dealt_half.astype(jnp.float32) + branch).astype(jnp.bfloat16)
    back_out = lax.all_to_all(
        result[dealt_slot].reshape(dp_count, per_peer, feat_half),
        "dp",
        split_axis=0,
        concat_axis=0,
        tiled=True,
    )
    output = back_out.reshape(row_count, feat_half)[back_order]
    g_w_out = jnp.einsum("ti,td->id", scaled, grad_full, preferred_element_type=jnp.float32)
    d_scaled = jnp.einsum("td,id->ti", grad_full, w_out, preferred_element_type=jnp.float32)
    weighted = d_scaled * gain_f
    g_norm_gain = jnp.sum(d_scaled * gated * inverse[:, None], axis=0)
    cross_sum = lax.psum(jnp.sum(weighted * gated, axis=1), "tensor")
    d_gated = (
        inverse[:, None] * weighted
        - gated * (inverse * inverse * inverse / INNER * cross_sum)[:, None]
    )
    d_mixed = d_gated * silu_gate
    sigmoid_gate = jax.nn.sigmoid(gate_pre)
    d_gate = d_gated * mixed * (sigmoid_gate * (1.0 + gate_pre * (1.0 - sigmoid_gate)))
    d_value_conv, d_state_part, d_step_pre, g_step_bias, g_a_log, g_skip = mixer_pull(d_mixed)
    d_state_conv = lax.psum(d_state_part, "tensor")
    d_value_pre, d_state_pre, g_conv_x, g_conv_x_bias, g_conv_bc, g_conv_bc_bias = conv_pull(
        (d_value_conv, d_state_conv)
    )
    d_pair = jnp.concatenate([d_gate, d_value_pre], axis=1).astype(jnp.bfloat16)
    d_state_low = d_state_pre.astype(jnp.bfloat16)
    d_step_low = d_step_pre.astype(jnp.bfloat16)
    state_share = w_state.shape[1] // lax.axis_size("tensor")
    own_state = lax.dynamic_slice_in_dim(d_state_low, tensor_index * state_share, state_share, 1)
    own_weight = lax.dynamic_slice_in_dim(w_state, tensor_index * state_share, state_share, 1)
    g_w_in = jnp.einsum("td,tc->dc", normed, d_pair, preferred_element_type=jnp.float32).reshape(
        w_in.shape
    )
    g_w_state = jnp.einsum("td,tc->dc", normed, own_state, preferred_element_type=jnp.float32)
    g_w_step = jnp.einsum("td,th->dh", normed, d_step_low, preferred_element_type=jnp.float32)
    d_normed = jnp.einsum("tc,dc->td", d_pair, w_pair, preferred_element_type=jnp.float32)
    d_normed = d_normed + jnp.einsum(
        "th,dh->td", d_step_low, w_step, preferred_element_type=jnp.float32
    )
    d_normed = d_normed + jnp.einsum(
        "tc,dc->td", own_state, own_weight, preferred_element_type=jnp.float32
    )
    normed_share = lax.psum_scatter(d_normed, "tensor", scatter_dimension=1, tiled=True)
    row_scale = lax.rsqrt(jnp.mean(stream * stream, axis=1) + norm_eps)
    stream_share = dealt_half.astype(jnp.float32)
    gain_share = lax.dynamic_slice_in_dim(
        pre_gain.astype(jnp.float32), tensor_index * feat_half, feat_half, 0
    )
    row_cross = lax.psum(jnp.sum(gain_share * normed_share * stream_share, axis=1), "tensor")
    d_share = (
        row_scale[:, None] * gain_share * normed_share
        - stream_share * (row_scale * row_scale * row_scale / D * row_cross)[:, None]
    )
    g_pre_gain = jnp.sum(normed_share * stream_share * row_scale[:, None], axis=0)
    d_input = (d_share + grad_half.astype(jnp.float32)).astype(jnp.bfloat16)
    back_grad = lax.all_to_all(
        d_input[dealt_slot].reshape(dp_count, per_peer, feat_half),
        "dp",
        split_axis=0,
        concat_axis=0,
        tiled=True,
    )
    hidden_grad = back_grad.reshape(row_count, feat_half)[back_order]
    small = lax.psum(
        (
            g_pre_gain,
            g_conv_x,
            g_conv_x_bias,
            g_conv_bc,
            g_conv_bc_bias,
            g_step_bias,
            g_a_log,
            g_skip,
            g_norm_gain,
        ),
        "dp",
    )
    g_in_part, g_state_part, g_step_part, g_w_out_part = (
        lax.psum_scatter(g_w_in, "dp", scatter_dimension=0, tiled=True),
        lax.psum_scatter(g_w_state, "dp", scatter_dimension=0, tiled=True),
        lax.psum_scatter(g_w_step, "dp", scatter_dimension=0, tiled=True),
        lax.psum_scatter(g_w_out, "dp", scatter_dimension=1, tiled=True),
    )
    return (
        output,
        hidden_grad,
        small[0],
        g_in_part,
        g_state_part,
        g_step_part,
        small[1],
        small[2],
        small[3],
        small[4],
        small[5],
        small[6],
        small[7],
        small[8],
        g_w_out_part,
    )


F32, BF16, I32 = jnp.float32, jnp.bfloat16, jnp.int32
MESH = pl.DeviceIdType.MESH
LOG2E = 1.4426950408889634
HIGHEST = lax.Precision.HIGHEST

ROWS = 256
FULL = 1536
HALF = 768
CH = 1536
HEADS = 24
PEERS = 16
PER = ROWS // PEERS
SHARE = FULL // PEERS

X_BIAS, NORM_GAIN, PRE_GAIN, BC_BIAS, STEP_BIAS, A_LOG = (slice(n, n + 1) for n in range(4, 10))

UNITS = (
    ("gate", 0, 256),
    ("gate", 256, 256),
    ("gate", 512, 512),
    ("gate", 1024, 512),
    ("out", 0, 512),
    ("out", 512, 512),
    ("out", 1024, 512),
    ("value", 0, 512),
    ("value", 512, 512),
    ("value", 1024, 512),
    ("misc", 0, 256),
)


def dot_t(a, b):
    return lax.dot_general(a, b, (((1,), (1,)), ((), ())), preferred_element_type=F32)


def dot(a, b):
    return jnp.dot(a, b, preferred_element_type=F32)


def sigmoid(v):
    return 1.0 / (1.0 + jnp.exp(-v))


def block_at(n, width):
    return pl.ds(pl.multiple_of(n * width, width), width)


class Sent:
    def __init__(self, copy):
        self.copy, self.gone, self.here = copy, False, False

    def wait_recv(self):
        self.copy.wait_recv()
        self.here = True

    def wait_send(self):
        if not self.gone:
            self.copy.wait_send()
        self.gone = True


def await_bytes(sem, ref):
    pltpu.make_async_copy(ref, ref, sem).wait()


def block_body(room, *refs):
    left = list(refs)

    def take(shape):
        return [left.pop(0) for _ in shape] if isinstance(shape, list) else left.pop(0)

    r = SimpleNamespace(**{name: take(shape) for name, shape in room.items()})
    lens, deal_ref, vec = r.lens, r.deal, r.vec
    wst, wsp = r.wst, r.wsp
    ss, rs, ls = r.ss, r.rs, r.ls
    me, side = lax.axis_index("dp"), lax.axis_index("tensor")
    core = lax.rem(me, 2)
    xpos = lax.rem(me // 2, 2)
    zpos = me // 4
    sibling = (zpos * 4 + xpos * 2 + (1 - core), side)
    across = (zpos * 4 + (1 - xpos) * 2 + core, side)
    z_side = zpos // 2
    z_outer, z_inner = 3 * z_side, 1 + z_side
    far_outer, far_inner = 3 - z_outer, 3 - z_inner
    is_outer = zpos == z_outer
    is_inner = zpos == z_inner

    def at_z(z):
        return (z * 4 + xpos * 2 + core, side)

    near = at_z(z_outer + z_inner - zpos)
    facing = at_z(3 - zpos)
    other = (me, 1 - side)
    own_cols = pl.ds(pl.multiple_of(side * HALF, HALF), HALF)
    other_cols = pl.ds(pl.multiple_of((1 - side) * HALF, HALF), HALF)

    started, taken, leaving = [], ({}, {}), []

    def semaphore(sems, key):
        count = taken[sems is rs]
        return sems.at[count.setdefault(("own", len(count)) if key is None else key, len(count))]

    def group(key, ref):
        leaving.append((semaphore(ss, key), ref))
        return key

    def send(src, dst, device, by=None, gone=None, came=None):
        copy = pltpu.make_async_remote_copy(
            src_ref=src,
            dst_ref=dst,
            send_sem=semaphore(ss, gone),
            recv_sem=semaphore(rs, came),
            device_id=device,
            device_id_type=MESH,
        )
        if by is None:
            copy.start()
        else:
            pl.when(by)(copy.start)
        one = Sent(copy)
        if gone is None:
            started.append(one)
        return one

    def load(src, dst, n):
        copy = pltpu.make_async_copy(src, dst, ls.at[n])
        copy.start()
        return copy

    def pair_load(n, at):
        cols = pl.ds(pl.multiple_of(n * 128, 128), 128)
        return pltpu.make_async_copy(r.w_in.at[:, :, cols], r.pair.at[at], ls.at[at])

    hid_load = load(r.hid, r.half_in, 3)
    pair_load(0, 0).start()
    pair_load(1, 1).start()
    pair_load(2, 2).start()
    ogr_load = load(r.ogr, r.dhalf_in, 4)
    small_loads = [load(src, dst, 5 + n) for n, (src, dst) in enumerate(((r.conv_x, r.conv_x_v), (r.conv_bc, r.conv_bc_v), (r.w_step, r.w_step_v), (r.rows8, r.rows8_v)))]
    wst_load = load(r.wst_hbm, r.wst, 9)
    wo_load = load(r.wo_hbm, r.wo, 10)

    barrier = pltpu.get_barrier_semaphore()
    for k in range(1, PEERS):
        pl.semaphore_signal(
            barrier, inc=1, device_id=(lax.rem(me + k, PEERS), side), device_id_type=MESH
        )
    pl.semaphore_signal(barrier, inc=1, device_id=other, device_id_type=MESH)

    i0 = lax.broadcasted_iota(I32, (ROWS, ROWS), 0)
    i1 = lax.broadcasted_iota(I32, (ROWS, ROWS), 1)
    deal = deal_ref[...]
    dest = lax.shift_right_logical(deal, 8)
    slot = jnp.bitwise_and(deal, ROWS - 1)
    member = (dest == lax.broadcasted_iota(I32, (PEERS, ROWS), 0)).astype(F32)
    before = dot(member.astype(BF16), (i0 < i1).astype(F32).astype(BF16))
    rank = jnp.sum(member * before, axis=0, keepdims=True)
    place = dest.astype(F32) * PER + rank
    hit = i0.astype(F32) == place
    to_send = hit.astype(F32)
    send_hot = to_send.astype(BF16)
    ident = jnp.sum(to_send * slot.astype(F32), axis=1, keepdims=True)
    sb_h, sb_g, rb_h, rb_g, yb_h, yb_g = r.sb_h, r.sb_g, r.rb_h, r.rb_g, r.yb_h, r.yb_g
    hid_load.wait()
    sb_h[...] = dot(send_hot, r.half_in[...]).astype(BF16)
    row_w = lax.broadcasted_iota(I32, (ROWS, 128), 0)
    lane_w = lax.broadcasted_iota(I32, (ROWS, 128), 1)
    in_place = lax.rem(row_w, PER) == lane_w
    spread = jnp.where(in_place, ident, 0.0).astype(BF16)
    row_n = lax.broadcasted_iota(I32, (PEERS, ROWS), 0)
    lane_n = lax.broadcasted_iota(I32, (PEERS, ROWS), 1)
    gather_ids = (row_n == lane_n // PER).astype(F32).astype(BF16)
    r.sb_i[...] = dot(gather_ids, spread).reshape(PEERS, 1, 128)

    pl.semaphore_wait(barrier, PEERS)

    def rows_of(device):
        return pl.ds(pl.multiple_of(device * PER, PER), PER)

    line = (zpos, z_outer + z_inner - zpos, lax.rem(zpos + 2, 4), 3 - zpos)

    def away(dz, dx, dc):
        return line[dz] * 4 + lax.rem(xpos + dx, 2) * 2 + lax.rem(core + dc, 2)

    steps = [(dz, dx, dc) for dz in (2, 3, 1, 0) for dx in (0, 1) for dc in (0, 1)]

    def deal(dz, src, dst, gone, came, rows=rows_of):
        for step in steps:
            if step[0] == dz and step != (0, 0, 0):
                to = away(*step)
                send(src.at[rows(to)], dst.at[rows(me)], (to, side), gone=gone, came=came)

    def pass_group(name, dz, buf, dst):
        count = 4 * PER - (PER if dz == 0 else 0)
        await_bytes(semaphore(rs, (name, dz)), buf.at[pl.ds(0, count)])
        for step in steps:
            if step[0] == dz:
                origin = rows_of(away(*step))
                send(buf.at[origin], dst.at[origin], other, gone=(name, 9), came=(name, 9))

    def first_wave(name, src, dst):
        for dz in (3, 1, 0):
            deal(dz, src, dst, (name, 3) if dz == 3 else name, (name, dz))
        group(name, src.at[pl.ds(0, 11 * PER)])

    def second_wave(name, src, dst):
        await_bytes(semaphore(ss, (name, 3)), src.at[pl.ds(0, 4 * PER)])
        deal(2, src, dst, name, (name, 2))

    def same(device):
        return device

    for dz in (2, 3, 1, 0):
        deal(dz, r.sb_i, r.rb_i, "ids", "ids", same)
    group("ids", r.sb_i.at[pl.ds(0, PEERS - 1)])
    first_wave("hid", sb_h, rb_h)
    r.rb_i[me] = r.sb_i[me]
    rb_h[rows_of(me)] = sb_h[rows_of(me)]
    ogr_load.wait()
    sb_g[...] = dot(send_hot, r.dhalf_in[...]).astype(BF16)
    rb_g[rows_of(me)] = sb_g[rows_of(me)]
    r.send_hot_t[...] = to_send.T.astype(BF16)

    ends, total = [], 0
    for k in range(8):
        total = total + lens[0, k]
        ends.append(total)

    def seg_at(pos):
        out = jnp.zeros(pos.shape, I32)
        for e in ends:
            out = out + (pos >= e).astype(I32)
        return out

    row_col = lax.broadcasted_iota(I32, (ROWS, 128), 0)
    seg_here = seg_at(row_col)
    for o in range(1, 4):
        same = (seg_at(row_col - o) == seg_here) & (row_col >= o)
        r.masks[o - 1] = same.astype(F32)
    same = seg_at(i0) == seg_at(i1)
    r.linked[...] = (same & (i0 >= i1)).astype(F32)
    r.linked_t[...] = (same & (i0 <= i1)).astype(F32)
    r.small[...] = jnp.zeros((8, CH + 256), F32)
    for copy in small_loads:
        copy.wait()
    vec[0:4, :] = r.conv_x_v[...].astype(F32)
    vec[4:12, :] = r.rows8_v[...]
    vec[12:16, 0:256] = r.conv_bc_v[...].astype(F32)
    wst_load.wait()
    wsp[...] = jnp.concatenate(
        [r.w_step_v[...].astype(F32), jnp.zeros((128 - HEADS, FULL), F32)], axis=0
    ).astype(BF16)
    r.dst_acc[...] = jnp.zeros((ROWS, ROWS), F32)
    r.dcol[...] = jnp.zeros((ROWS, 128), F32)
    r.dsd[...] = jnp.zeros((ROWS, 128), F32)

    picked = jnp.where(i0 < 128, 2 * i0, 2 * i0 - 255)
    apart = (picked == i1).astype(F32).astype(BF16)

    def take_apart(n):
        at = lax.rem(n, 3)
        pair_load(n, at).wait()
        cols = block_at(n, 128)
        flat = r.pair.at[at].reshape(2 * FULL, 128)
        for k in range(12):
            both = dot(apart, flat[k * 256 : (k + 1) * 256, :]).astype(BF16)
            r.wg[k * 128 : (k + 1) * 128, cols] = both[0:128]
            r.wv[k * 128 : (k + 1) * 128, cols] = both[128:256]

        @pl.when(n + 3 < 12)
        def _():
            pair_load(n + 3, at).start()

    group(("hid", 9), rb_h)
    group(("grad", 9), rb_g)
    pl.loop(0, 4)(take_apart)
    pass_group("hid", 0, rb_h, yb_h)
    second_wave("hid", sb_h, rb_h)
    pl.loop(4, 7)(take_apart)
    pass_group("hid", 1, rb_h, yb_h)
    pl.loop(7, 12)(take_apart)
    pass_group("hid", 3, rb_h, yb_h)
    await_bytes(semaphore(rs, "ids"), r.rb_i.at[pl.ds(0, PEERS - 1)])
    origin_row = lax.broadcasted_iota(I32, (ROWS, PEERS), 0) // PER
    fetch_ids = (origin_row == lax.broadcasted_iota(I32, (ROWS, PEERS), 1)).astype(F32).astype(BF16)
    ids = jnp.where(in_place, dot(fetch_ids, r.rb_i[...].reshape(PEERS, 128).astype(BF16)), 0.0)
    ids = jnp.broadcast_to(jnp.sum(ids, axis=1, keepdims=True), (ROWS, 128))
    r.hot_t[...] = (ids[:, 0:1] == i1.astype(F32)).astype(F32).astype(BF16)
    r.hot[...] = (ids.T[0:1, :] == i0.astype(F32)).astype(F32).astype(BF16)
    pass_group("hid", 2, rb_h, yb_h)
    first_wave("grad", sb_g, rb_g)
    stream, upstream, normed = r.stream, r.upstream, r.normed
    stream[:, own_cols] = dot(r.hot[...], rb_h[...]).astype(BF16)
    await_bytes(semaphore(rs, ("hid", 9)), yb_h)
    stream[:, other_cols] = dot(r.hot[...], yb_h[...]).astype(BF16)

    @pl.loop(0, 8)
    def _(n):
        rows = block_at(n, 32)
        s = stream[rows, :].astype(F32)
        scale = lax.rsqrt(jnp.sum(s * s, axis=1, keepdims=True) * (1.0 / FULL) + norm_eps)
        r.nscale[rows, :] = jnp.broadcast_to(scale, (32, 128))
        normed[rows, :] = (s * scale * vec[PRE_GAIN, :]).astype(BF16)

    here, beside, over, cross_over = (pl.ds(n * ROWS, ROWS) for n in range(4))
    diagonal = (zpos * 4 + (1 - xpos) * 2 + (1 - core), side)

    def flip(source, flipped, keep):
        for n in range(4):
            turned = source[:, n * 384 : (n + 1) * 384].astype(F32).T.astype(BF16)
            for i in range(4):
                flipped[n, i] = turned[i * SHARE : (i + 1) * SHARE]
        keep[:, :, here] = flipped[:, xpos * 2 + core]

    others = pl.ds(ROWS, 3 * ROWS)

    def share_flipped(name, flipped, keep):
        group(name, keep.at[:, :, others])
        for dx, dc, lanes, device in ((1, 0, over, across), (1, 1, cross_over, diagonal), (0, 1, beside, sibling)):
            place = lax.rem(xpos + dx, 2) * 2 + lax.rem(core + dc, 2)
            send(flipped.at[:, place], keep.at[:, :, lanes], device, gone=name, came=name)

    masks = r.masks

    def conv_at(signal, taps, bias):
        out = bias + taps[3] * signal
        for o in range(1, 4):
            out = out + taps[3 - o] * (pltpu.roll(signal, o, 0) * masks[o - 1])
        return out

    def conv_back(signal, taps, bias, grad):
        pre = conv_at(signal, taps, bias)
        s = sigmoid(pre)
        d_pre = grad * (s * (1.0 + pre * (1.0 - s)))
        sums = [None] * 4
        sums[3] = jnp.sum(d_pre * signal, axis=0, keepdims=True)
        d_signal = taps[3] * d_pre
        for o in range(1, 4):
            masked = d_pre * masks[o - 1]
            sums[3 - o] = jnp.sum(masked * pltpu.roll(signal, o, 0), axis=0, keepdims=True)
            d_signal = d_signal + taps[3 - o] * pltpu.roll(masked, ROWS - o, 0)
        return d_signal, sums, jnp.sum(d_pre, axis=0, keepdims=True)

    def taps_at(first, cols):
        return [vec[pl.ds(first + k, 1), cols] for k in range(4)]

    gate_pre, value_pre, vconv = r.gate_pre, r.value_pre, r.vconv
    def project(n):
        cols = block_at(n, 256)
        gate_pre[:, cols] = dot(normed[...], r.wg[:, cols])
        value_pre[:, cols] = dot(normed[...], r.wv[:, cols])

    def convolve(n):
        cols = block_at(n, 128)
        pre = conv_at(value_pre[:, cols], taps_at(0, cols), vec[X_BIAS, cols])
        vconv[:, cols] = (pre * sigmoid(pre)).astype(BF16)

    pl.loop(0, 3)(project)
    second_wave("grad", sb_g, rb_g)
    pl.loop(3, 6)(project)
    pass_group("grad", 0, rb_g, yb_g)
    pass_group("grad", 1, rb_g, yb_g)
    flip(normed, r.norm_f, r.norm_t)
    share_flipped("norm", r.norm_f, r.norm_t)
    pl.loop(0, 12)(convolve)

    state_pre, sconv = r.state_pre, r.sconv
    state_pre[...] = dot(normed[...], wst[...])
    for n in range(2):
        cols = pl.ds(n * 128, 128)
        pre = conv_at(state_pre[:, cols], taps_at(12, cols), vec[BC_BIAS, cols])
        sconv[:, cols] = (pre * sigmoid(pre)).astype(BF16)

    step_in = dot_t(normed[...], wsp[...]) + vec[STEP_BIAS, 0:128]
    small_e = jnp.exp(-jnp.abs(step_in))
    series = small_e * (1.0 - small_e * (0.5 - small_e * (1.0 / 3.0 - 0.25 * small_e)))
    step = jnp.maximum(step_in, 0.0) + jnp.where(small_e < 0.01, series, jnp.log(1.0 + small_e))
    decay = -jnp.exp(vec[A_LOG, 0:128])
    r.step_in[...] = step_in
    r.step[...] = step
    lower = (i0 >= i1).astype(F32)
    cum2 = jnp.dot(lower, step * decay, precision=HIGHEST, preferred_element_type=F32) * LOG2E
    r.cum2[...] = cum2
    r.cum2_t[...] = cum2.T
    r.cum2_ls[...] = (cum2 - jnp.log(step) * LOG2E).T
    b_rows, c_rows = sconv[:, 0:128], sconv[:, 128:256]
    r.scores[...] = dot_t(c_rows, b_rows) * r.linked[...]
    r.scores_t[...] = dot_t(b_rows, c_rows) * r.linked_t[...]

    lane = lax.broadcasted_iota(I32, (ROWS, 128), 1)
    lane_half = lax.broadcasted_iota(I32, (128, 128), 1) < 64

    def column(ref, h):
        return jnp.sum(jnp.where(lane == h, ref[...], 0.0), axis=1, keepdims=True)

    pass_group("grad", 3, rb_g, yb_g)

    mixed = r.mixed

    def mix(p):
        cols = block_at(p, 128)
        x = vconv[:, cols]
        tops, lows = [], []
        for a in range(2):
            h = 2 * p + a
            cc = column(r.cum2, h)
            cr = r.cum2_ls[pl.ds(h, 1), :]
            w = jnp.exp2(jnp.minimum(cc[0:128] - cr[:, 0:128], 100.0)) * r.scores[0:128, 0:128]
            tops.append(dot(w.astype(BF16), x[0:128]))
            w = jnp.exp2(jnp.minimum(cc[128:256] - cr, 100.0)) * r.scores[128:256, :]
            lows.append(dot(w.astype(BF16), x))
        skip = jnp.where(lane_half[0:1], r.skip[2 * p], r.skip[2 * p + 1])
        xf = x.astype(F32)
        mixed[0:128, cols] = jnp.where(lane_half, tops[0], tops[1]) + skip * xf[0:128]
        mixed[128:256, cols] = jnp.where(lane_half, lows[0], lows[1]) + skip * xf[128:256]

    pl.loop(0, 6)(mix)
    pass_group("grad", 2, rb_g, yb_g)
    pl.loop(6, 12)(mix)

    upstream[:, own_cols] = dot(r.hot[...], rb_g[...]).astype(BF16)
    await_bytes(semaphore(rs, ("grad", 9)), yb_g)
    upstream[:, other_cols] = dot(r.hot[...], yb_g[...]).astype(BF16)
    wo_load.wait()
    d_scaled = r.d_scaled
    r.acc1[...] = jnp.zeros((ROWS, 128), F32)
    r.acc2[...] = jnp.zeros((ROWS, 128), F32)

    @pl.loop(0, 6)
    def _(n):
        cols = block_at(n, 256)
        ds = dot_t(upstream[...], r.wo[cols, :])
        d_scaled[:, cols] = ds
        g = gate_pre[:, cols]
        gated = mixed[:, cols] * g * sigmoid(g)
        sq = gated * gated
        cr = vec[NORM_GAIN, cols] * ds * gated
        r.acc1[...] += sq[:, 0:128] + sq[:, 128:256]
        r.acc2[...] += cr[:, 0:128] + cr[:, 128:256]

    def exchange_rows(col_a, col_b, out_buf, in_buf):
        both = jnp.where(lane == 0, col_a, jnp.where(lane == 1, col_b, 0.0))
        out_buf[...] = both.T[0:8, :]
        copy = send(out_buf, in_buf, other)

        def finish():
            copy.wait_recv()
            both = jnp.concatenate([out_buf[...] + in_buf[...], jnp.zeros((120, ROWS), F32)], axis=0)
            return both.T[:, 0:1], both.T[:, 1:2]

        return finish

    row_sums = exchange_rows(
        jnp.sum(r.acc1[...], axis=1, keepdims=True),
        jnp.sum(r.acc2[...], axis=1, keepdims=True),
        r.ex_a,
        r.ex_b,
    )
    r.cum2_ls[...] = jnp.zeros((128, ROWS), F32)
    flip(upstream, r.up_f, r.up_t)
    sum_sq, sum_cross = row_sums()
    inner = 2.0 * CH
    inverse = lax.rsqrt(sum_sq * (1.0 / inner) + norm_eps)
    cross = inverse * inverse * inverse * (1.0 / inner) * sum_cross
    r.acc1[...] = jnp.broadcast_to(inverse, (ROWS, 128))
    r.acc2[...] = jnp.broadcast_to(cross, (ROWS, 128))
    scaled4, gate4, value4, misc4 = r.scaled4, r.gate4, r.value4, r.misc4

    def gated_back(n):
        cols = block_at(n, 128)
        inv, crs = r.acc1[...], r.acc2[...]
        g, m, ds, gain = gate_pre[:, cols], mixed[:, cols], d_scaled[:, cols], vec[NORM_GAIN, cols]
        s = sigmoid(g)
        silu = g * s
        gated = m * silu
        gi = gated * inv
        scaled4[here, cols] = (gi * gain).astype(BF16)
        r.small[5:6, cols] = jnp.sum(ds * gi, axis=0, keepdims=True)
        d_gated = inv * ds * gain - gated * crs
        mixed[:, cols] = d_gated * silu
        gate4[here, cols] = (d_gated * m * (s * (1.0 + g * (1.0 - s)))).astype(BF16)

    def gated_part(n):
        pl.loop(4 * n, 4 * n + 4)(gated_back)

    half_f, half_o, half_in = d_scaled.at[:, pl.ds(0, HALF)], normed.at[:, pl.ds(0, HALF)], r.half_in
    flying = {}

    def project_other():
        @pl.loop(0, 3)
        def _(n):
            cols = pl.ds(pl.multiple_of((1 - side) * HALF + n * 256, 256), 256)
            half_o[:, block_at(n, 256)] = dot(scaled4[here, :], r.wo[:, cols]).astype(BF16)

        flying["out"] = send(half_o, half_in, other)

    def project_own():
        @pl.loop(0, 3)
        def _(n):
            cols = pl.ds(pl.multiple_of(side * HALF + n * 256, 256), 256)
            half_f[:, block_at(n, 256)] = dot(scaled4[here, :], r.wo[:, cols]) + stream[:, cols].astype(F32)

    lefts = {"out": r.up_t, "gate": r.norm_t, "value": r.norm_t, "misc": r.norm_t}
    rights = {"out": scaled4, "gate": gate4, "value": value4, "misc": misc4}
    outs = {"out": r.o_wo, "gate": r.o_gate, "value": r.o_value, "misc": r.o_misc}
    stores = []

    def store(src, dst, n):
        copy = pltpu.make_async_copy(src, dst, r.os.at[n])
        copy.start()
        return copy

    def ready(copy):
        if not copy.here:
            copy.wait_recv()

    pieces = {}
    for name, ref in rights.items():
        group(name, ref.at[pl.ds(0, 3 * ROWS)])

    def up_swap():
        share_flipped("up", r.up_f, r.up_t)

    def swap(name, first, width):
        ref, cols = rights[name], pl.ds(first, width)
        near_by = send(ref.at[here, cols], ref.at[beside, cols], sibling, gone=name)
        far_off = send(ref.at[here, cols], ref.at[over, cols], across, gone=name)
        pieces[name, first] = [width, near_by, far_off]

    def relay(name, first):
        piece = pieces[name, first]
        ref, cols = rights[name], pl.ds(first, piece[0])
        ready(piece[2])
        piece.append(send(ref.at[over, cols], ref.at[cross_over, cols], sibling, gone=name))

    class Unit:
        def __init__(self, n):
            self.name, self.first, self.width = UNITS[n]
            self.n, self.part, self.zbuf, self.kept = n, r.part[n], r.zbuf[n], r.kept[n]
            self.key = group(("unit", n), self.zbuf.at[pl.ds(0, 3)])
            self.stages = [self.compute, self.pass_outer, self.pass_inner, self.send_out, self.finish]

        def go(self, stage):
            self.stages[stage]()

        def add(self, z, slot):
            self.part[z] = self.part[z] + self.zbuf[slot]

        def hop(self, z, slot, device, by):
            return send(self.part.at[z], self.zbuf.at[slot], device, by, self.key, (self.key, slot))

        def compute(self):
            lhs_ref, rhs_ref = lefts[self.name], rights[self.name]
            first, part = self.first, self.part
            side_name = "up" if self.name == "out" else "norm"
            if side_name not in flying:
                flying[side_name] = True
                await_bytes(semaphore(rs, side_name), lhs_ref.at[:, :, others])
            for (name, start), piece in pieces.items():
                if name == self.name and start < first + self.width and first < start + piece[0]:
                    for copy in piece[1:]:
                        ready(copy)

            @pl.loop(0, self.width // 256)
            def _(n):
                lhs = lhs_ref[...].reshape(4 * SHARE, 4 * ROWS)
                rhs = rhs_ref[:, pl.ds(pl.multiple_of(first + n * 256, 256), 256)]
                part[:, :, block_at(n, 256)] = dot(lhs, rhs).astype(BF16).reshape(4, SHARE, 256)

            self.c3 = self.hop(far_outer, 0, near, is_outer)
            self.c2 = self.hop(far_inner, 1, near, is_outer)
            self.c1 = self.hop(z_inner, 2, near, is_outer)

        def pass_outer(self):
            @pl.when(is_inner)
            def _():
                self.c3.wait_recv()
                self.add(far_outer, 0)

            self.d2 = self.hop(far_outer, 3, facing, is_inner)

        def pass_inner(self):
            @pl.when(is_inner)
            def _():
                self.c2.wait_recv()
                self.add(far_inner, 1)

            self.d1 = self.hop(far_inner, 4, facing, is_inner)

        def send_out(self):
            @pl.when(is_inner)
            def _():
                self.d2.wait_recv()
                self.add(z_outer, 3)

            self.e1 = self.hop(z_outer, 0, near, is_inner)

        def finish(self):
            own = self.kept
            cols = pl.ds(self.first, self.width)

            @pl.when(is_outer)
            def _():
                self.e1.wait_recv()
                own[...] = self.part[zpos].astype(F32) + self.zbuf[0].astype(F32)

            @pl.when(is_inner)
            def _():
                self.c1.wait_recv()
                self.d1.wait_recv()
                own[...] = self.part[zpos].astype(F32) + self.zbuf[2].astype(F32) + self.zbuf[4].astype(F32)

            stores.append(store(own, outs[self.name].at[:, cols], self.n))

    units = [Unit(n) for n in range(len(UNITS))]
    head_row = lax.broadcasted_iota(I32, (32, ROWS), 0)

    def mixer_back(p):
        cols = block_at(p, 128)
        x = vconv[:, cols]
        xf = x.astype(F32)
        dy = mixed[:, cols]
        dyb = dy.astype(BF16)
        r.small[6:7, cols] = jnp.sum(dy * xf, axis=0, keepdims=True)
        d_tops, d_lows = [], []
        for a in range(2):
            h = 2 * p + a
            half = (lane < 64) if a == 0 else (lane >= 64)
            xa = jnp.where(half, xf, 0.0)
            xab = xa.astype(BF16)
            cc = column(r.cum2, h)
            st = column(r.step, h)
            cr = r.cum2_t[pl.ds(h, 1), :]
            w = jnp.exp2(jnp.minimum(cr - cc[0:128], 0.0))
            sc = r.scores_t[0:128, :]
            v_top = dot((w * sc).astype(BF16), dyb)
            q = dot_t(xab[0:128], dyb) * w * st[0:128]
            r.dst_acc[0:128, :] += q
            g_top = q * sc
            w = jnp.exp2(jnp.minimum(cr[:, 128:256] - cc[128:256], 0.0))
            sc = r.scores_t[128:256, 128:256]
            v_low = dot((w * sc).astype(BF16), dyb[128:256])
            q = dot_t(xab[128:256], dyb[128:256]) * w * st[128:256]
            r.dst_acc[128:256, 128:256] += q
            g_low = q * sc
            top_sums = jnp.sum(g_top, axis=0, keepdims=True)
            low_sums = jnp.sum(g_low, axis=0, keepdims=True)
            col_sums = jnp.concatenate([top_sums[:, 0:128], top_sums[:, 128:256] + low_sums], axis=1)
            r.cum2_ls[0:32, :] += jnp.where(head_row == h, col_sums, 0.0)
            row_sums = jnp.concatenate(
                [
                    jnp.sum(g_top[:, 0:128] + g_top[:, 128:256], axis=1, keepdims=True),
                    jnp.sum(g_low, axis=1, keepdims=True),
                ],
                axis=0,
            )
            direct = jnp.concatenate(
                [
                    jnp.sum(xa[0:128] * v_top, axis=1, keepdims=True),
                    jnp.sum(xa[128:256] * v_low, axis=1, keepdims=True),
                ],
                axis=0,
            )
            r.dcol[...] += jnp.where(lane == h, row_sums, 0.0)
            r.dsd[...] += jnp.where(lane == h, direct, 0.0)
            d_tops.append(st[0:128] * v_top)
            d_lows.append(st[128:256] * v_low)
        d_conv = jnp.concatenate(
            [jnp.where(lane_half, d_tops[0], d_tops[1]), jnp.where(lane_half, d_lows[0], d_lows[1])],
            axis=0,
        )
        d_conv = d_conv + jnp.where(lane_half[0:1], r.skip[2 * p], r.skip[2 * p + 1]) * dy
        d_value, sums, bias_sum = conv_back(value_pre[:, cols], taps_at(0, cols), vec[X_BIAS, cols], d_conv)
        value4[here, cols] = d_value.astype(BF16)
        for k in range(4):
            r.small[k : k + 1, cols] = sums[k]
        r.small[4:5, cols] = bias_sum

    def mixer_part(first, last):
        pl.loop(first, last)(mixer_back)

    def send_back(name, src, dst):
        group(name, src.at[pl.ds(0, ROWS - PER)])
        for dz in (2, 3, 1, 0):
            deal(dz, src, dst, name, name)
        dst[rows_of(me)] = src[rows_of(me)]

    def return_out():
        ready(flying["out"])
        result = (half_f[...] + half_in[...].astype(F32)).astype(BF16)
        yb_h[...] = dot(r.hot_t[...], result).astype(BF16)
        send_back("back_o", yb_h, r.back_o)

    def finish_out():
        await_bytes(semaphore(rs, "back_o"), r.back_o.at[pl.ds(0, ROWS - PER)])
        r.res_o[...] = dot(r.send_hot_t[...], r.back_o[...]).astype(BF16)
        stores.append(store(r.res_o, r.o_out, len(UNITS) + 1))

    d_state = r.d_state
    state_own = pl.ds(pl.multiple_of(side * 128, 128), 128)
    state_other = pl.ds(pl.multiple_of((1 - side) * 128, 128), 128)

    def states_back():
        d_scores_t = r.dst_acc[...] * r.linked_t[...]
        d_conv_s = r.linked
        d_conv_s[:, 0:128] = dot(d_scores_t.astype(BF16), c_rows)
        d_conv_s[:, 128:256] = dot(d_scores_t.T.astype(BF16), b_rows)
        for n in range(2):
            cols = pl.ds(n * 128, 128)
            d_pre, sums, bias_sum = conv_back(
                state_pre[:, cols], taps_at(12, cols), vec[BC_BIAS, cols], d_conv_s[:, cols]
            )
            d_state[:, cols] = d_pre
            for k in range(4):
                r.small[k : k + 1, CH + n * 128 : CH + (n + 1) * 128] = sums[k]
            r.small[4:5, CH + n * 128 : CH + (n + 1) * 128] = bias_sum
        r.st_out[...] = d_state[:, state_other].astype(BF16)
        flying["state"] = send(r.st_out, r.st_in, other)
        d_cum = r.cum2_ls[...].T - r.dcol[...]
        upper = (i0 <= i1).astype(F32)
        d_rate = jnp.dot(upper, d_cum, precision=HIGHEST, preferred_element_type=F32)
        d_step = (r.dsd[...] + d_rate * decay) * sigmoid(r.step_in[...])
        r.small[5:6, CH : CH + 128] = jnp.sum(d_step, axis=0, keepdims=True)
        r.small[6:7, CH : CH + 128] = jnp.sum(d_rate * r.step[...], axis=0, keepdims=True) * decay
        misc4[here, 128:256] = d_step.astype(BF16)
        r.acc1[...] = jnp.zeros((ROWS, 128), F32)
        r.st_low[...] = d_state[...].astype(BF16)

    def add_states():
        ready(flying["state"])
        misc4[here, 0:128] = (d_state[:, state_own] + r.st_in[...].astype(F32)).astype(BF16)

    dhalf_f, dhalf_o, dhalf_in = d_scaled.at[:, pl.ds(HALF, HALF)], normed.at[:, pl.ds(HALF, HALF)], r.dhalf_in

    def d_normed_at(first):
        rows = pl.ds(pl.multiple_of(first, 256), 256)
        out = dot_t(gate4[here, :], r.wg[rows, :]) + dot_t(value4[here, :], r.wv[rows, :])
        out = out + dot_t(r.st_low[...], r.wst[rows, :])
        out = out + dot(misc4[here, 128:256], wsp[:, rows])
        part = out * vec[PRE_GAIN, rows] * stream[:, rows].astype(F32)
        r.acc1[...] += part[:, 0:128] + part[:, 128:256]
        return out

    def normed_other():
        @pl.loop(0, 3)
        def _(n):
            dhalf_o[:, block_at(n, 256)] = d_normed_at((1 - side) * HALF + n * 256).astype(BF16)

        flying["norm"] = send(dhalf_o, dhalf_in, other)

    def normed_own():
        @pl.loop(0, 3)
        def _(n):
            dhalf_f[:, block_at(n, 256)] = d_normed_at(side * HALF + n * 256)

        flying["rows"] = exchange_rows(
            jnp.sum(r.acc1[...], axis=1, keepdims=True), jnp.zeros((ROWS, 1), F32), r.ex_c, r.ex_d
        )

    small = r.small

    def return_grad():
        row_cross, _ = flying["rows"]()
        ready(flying["norm"])
        flying["out"].wait_send()
        scale = r.nscale[:, 0:1]
        factor = scale * scale * scale * (1.0 / FULL) * row_cross
        for n in range(6):
            cols = pl.ds(n * 128, 128)
            mine = pl.ds(pl.multiple_of(side * HALF + n * 128, 128), 128)
            dn = dhalf_f[:, cols] + dhalf_in[:, cols].astype(F32)
            s = stream[:, mine].astype(F32)
            small[7:8, n * 128 : (n + 1) * 128] = jnp.sum(dn * s * scale, axis=0, keepdims=True)
            grad = upstream[:, mine].astype(F32) + scale * vec[PRE_GAIN, mine] * dn - s * factor
            half_o[:, cols] = grad.astype(BF16)
        yb_g[...] = dot(r.hot_t[...], half_o[...]).astype(BF16)
        send_back("back_g", yb_g, r.back_g)

    def finish_grad():
        await_bytes(semaphore(rs, "back_g"), r.back_g.at[pl.ds(0, ROWS - PER)])
        r.res_g[...] = dot(r.send_hot_t[...], r.back_g[...]).astype(BF16)
        stores.append(store(r.res_g, r.o_hid, len(UNITS) + 2))

    lasts = pl.ds(CH, 256)

    def small_tensor():
        flying["small"] = send(small.at[:, lasts], r.sm_y, other)

    def small_tensor_end():
        copy = flying["small"]
        copy.wait_send()
        copy.wait_recv()
        keep_rows = lax.broadcasted_iota(I32, (8, 256), 0) < 5
        small[:, lasts] = small[:, lasts] + jnp.where(keep_rows, r.sm_y[...], 0.0)

    partners = [sibling, across, near, facing]

    def small_start(n):
        flying[n] = send(small, r.sm_a[n], partners[n])

    def small_end(n):
        flying[n].wait_send()
        flying[n].wait_recv()
        small[...] = small[...] + r.sm_a[n][...]

    gated_part(0)
    gated_part(1)
    swap("gate", 256, 256)
    gated_part(2)
    project_other()
    swap("gate", 1024, 512)
    mixer_part(0, 6)
    relay("gate", 256)
    swap("value", 0, 768)
    swap("gate", 512, 512)
    units[1].go(0)
    project_own()
    return_out()
    units[1].go(1)
    relay("gate", 1024)
    mixer_part(6, 12)
    units[3].go(0)
    states_back()
    relay("value", 0)
    swap("value", 768, 768)
    normed_other()
    swap("out", 512, 512)
    units[7].go(0)
    up_swap()
    units[1].go(2)
    add_states()
    relay("gate", 512)
    swap("misc", 0, 256)
    units[2].go(0)
    units[7].go(1)
    units[2].go(1)
    swap("out", 0, 512)
    normed_own()
    swap("out", 1024, 512)
    finish_out()
    units[7].go(2)
    return_grad()
    relay("value", 768)
    units[8].go(0)
    units[3].go(1)
    units[9].go(0)
    units[3].go(2)
    units[2].go(2)
    relay("out", 512)
    relay("misc", 0)
    units[1].go(3)
    units[9].go(1)
    units[10].go(0)
    units[3].go(3)
    units[5].go(0)
    units[3].go(4)
    units[8].go(1)
    relay("out", 0)
    small_tensor()
    units[2].go(3)
    units[8].go(2)
    swap("gate", 0, 256)
    units[5].go(1)
    units[8].go(3)
    relay("out", 1024)
    units[10].go(1)
    units[4].go(0)
    small_tensor_end()
    units[7].go(3)
    units[9].go(2)
    units[5].go(2)
    units[10].go(2)
    units[6].go(0)
    units[5].go(3)
    small_start(0)
    finish_grad()
    units[4].go(1)
    small_end(0)
    relay("gate", 0)
    units[5].go(4)
    units[9].go(3)
    units[1].go(4)
    small_start(1)
    units[4].go(2)
    units[4].go(3)
    units[8].go(4)
    units[6].go(1)
    units[7].go(4)
    units[0].go(0)
    units[9].go(4)
    small_end(1)
    small_start(2)
    units[2].go(4)
    units[10].go(3)
    units[6].go(2)
    units[4].go(4)
    units[10].go(4)
    units[0].go(1)
    units[6].go(3)
    units[0].go(2)
    units[0].go(3)
    small_end(2)
    small_start(3)
    units[6].go(4)
    units[0].go(4)
    small_end(3)
    stores.append(store(small, r.o_small, len(UNITS)))
    for copy in started:
        copy.wait_send()
    for sem, ref in leaving:
        await_bytes(sem, ref)
    for copy in stores:
        copy.wait()


def scratch():
    vmem, dma = pltpu.VMEM, pltpu.SemaphoreType.DMA
    square, wide = (ROWS, ROWS), (ROWS, CH)
    def rows(dtype, width):
        return vmem((ROWS, width), dtype)

    return dict(
        wg=vmem((FULL, CH), BF16),
        wv=vmem((FULL, CH), BF16),
        wo=vmem((CH, FULL), BF16),
        pair=vmem((3, FULL, 2, 128), BF16),
        send_hot_t=vmem(square, BF16),
        hot=vmem(square, BF16),
        hot_t=vmem(square, BF16),
        sb_h=rows(BF16, HALF),
        rb_h=rows(BF16, HALF),
        sb_i=vmem((PEERS, 1, 128), F32),
        rb_i=vmem((PEERS, 1, 128), F32),
        sb_g=rows(BF16, HALF),
        rb_g=rows(BF16, HALF),
        yb_h=rows(BF16, HALF),
        yb_g=rows(BF16, HALF),
        half_in=rows(BF16, HALF),
        dhalf_in=rows(BF16, HALF),
        back_o=rows(BF16, HALF),
        back_g=rows(BF16, HALF),
        masks=vmem((3, ROWS, 128), F32),
        linked=vmem(square, F32),
        linked_t=vmem(square, F32),
        scores=vmem(square, F32),
        scores_t=vmem(square, F32),
        dst_acc=vmem(square, F32),
        small=vmem((8, CH + 256), F32),
        conv_x_v=vmem((4, CH), BF16),
        conv_bc_v=vmem((4, 256), BF16),
        w_step_v=vmem((HEADS, FULL), BF16),
        rows8_v=vmem((8, CH), F32),
        res_o=rows(BF16, HALF),
        res_g=rows(BF16, HALF),
        kept=[vmem((SHARE, width), F32) for _, _, width in UNITS],
        vec=vmem((16, CH), F32),
        wsp=vmem((128, FULL), BF16),
        wst=vmem((FULL, 256), BF16),
        cum2_t=vmem((128, ROWS), F32),
        cum2_ls=vmem((128, ROWS), F32),
        stream=vmem(wide, BF16),
        upstream=vmem(wide, BF16),
        normed=vmem(wide, BF16),
        vconv=vmem(wide, BF16),
        gate_pre=vmem(wide, F32),
        value_pre=vmem(wide, F32),
        mixed=vmem(wide, F32),
        d_scaled=vmem(wide, F32),
        state_pre=rows(F32, 256),
        d_state=rows(F32, 256),
        sconv=rows(BF16, 256),
        st_low=rows(BF16, 256),
        st_out=rows(BF16, 128),
        st_in=rows(BF16, 128),
        scaled4=vmem((4 * ROWS, CH), BF16),
        gate4=vmem((4 * ROWS, CH), BF16),
        value4=vmem((4 * ROWS, CH), BF16),
        misc4=vmem((4 * ROWS, 256), BF16),
        norm_t=vmem((4, SHARE, 4 * ROWS), BF16),
        up_t=vmem((4, SHARE, 4 * ROWS), BF16),
        norm_f=vmem((4, 4, SHARE, ROWS), BF16),
        up_f=vmem((4, 4, SHARE, ROWS), BF16),
        nscale=rows(F32, 128),
        acc1=rows(F32, 128),
        acc2=rows(F32, 128),
        dcol=rows(F32, 128),
        dsd=rows(F32, 128),
        step_in=rows(F32, 128),
        step=rows(F32, 128),
        cum2=rows(F32, 128),
        ex_a=vmem((8, ROWS), F32),
        ex_b=vmem((8, ROWS), F32),
        ex_c=vmem((8, ROWS), F32),
        ex_d=vmem((8, ROWS), F32),
        sm_y=vmem((8, 256), F32),
        sm_a=[vmem((8, CH + 256), F32) for _ in range(4)],
        part=[vmem((4, SHARE, width), BF16) for _, _, width in UNITS],
        zbuf=[vmem((5, SHARE, width), BF16) for _, _, width in UNITS],
        ss=dma((SENDS,)),
        rs=dma((ARRIVALS,)),
        ls=dma((11,)),
        os=dma((len(UNITS) + 3,)),
    )


SENDS = 25 + len(UNITS)
ARRIVALS = 55 + 5 * len(UNITS)


def finish_body(wo, gate, value, misc, small, out, hid, *outs):
    (
        o_out, o_hid, o_pre, o_in, o_state, o_step, o_cx, o_cxb, o_cb, o_cbb, o_bias, o_log, o_skip, o_gain, o_wo
    ) = outs
    o_out[...] = out[...]
    o_hid[...] = hid[...]
    o_pre[...] = small[7, 0:HALF]
    o_in[:, 0, :] = gate[...]
    o_in[:, 1, :] = value[...]
    o_state[...] = misc[:, 0:128]
    o_step[...] = misc[:, 128:256].T[0:HEADS]
    o_cx[...] = small[0:4, 0:CH]
    o_cxb[...] = small[4, 0:CH]
    o_cb[...] = small[0:4, CH:]
    o_cbb[...] = small[4, CH:]
    o_bias[...] = small[5, CH : CH + HEADS]
    o_log[...] = small[6, CH : CH + HEADS]
    head = lax.broadcasted_iota(I32, (CH, 128), 0) // (CH // HEADS)
    mine = (head == lax.broadcasted_iota(I32, (CH, 128), 1)).astype(F32)
    skips = jnp.dot(small[:, 0:CH], mine, precision=HIGHEST, preferred_element_type=F32)
    o_skip[...] = skips[6, 0:HEADS]
    o_gain[...] = small[5, 0:CH]
    o_wo[...] = wo[...]


def one_kernel(
    hidden_in,
    out_grad,
    seq_lengths,
    deal_to,
    pre_gain,
    w_in,
    w_state,
    w_step,
    conv_x,
    conv_x_bias,
    conv_bc,
    conv_bc_bias,
    step_bias,
    a_log,
    skip,
    norm_gain,
    w_out,
):
    at = lax.broadcasted_iota(I32, (8, CH), 0)
    rows8 = jnp.zeros((8, CH), F32)
    for n, v in enumerate((conv_x_bias, norm_gain, pre_gain, conv_bc_bias, step_bias, a_log)):
        v = jnp.pad(v.astype(F32), (0, CH - v.shape[0]))
        rows8 = jnp.where(at == n, v[None, :], rows8)
    inputs = dict(
        hid=hidden_in,
        ogr=out_grad,
        lens=seq_lengths,
        deal=deal_to.reshape(1, ROWS),
        rows8=rows8,
        conv_x=conv_x,
        conv_bc=conv_bc,
        skip=skip,
        w_in=w_in,
        wo_hbm=w_out,
        wst_hbm=w_state,
        w_step=w_step.T,
    )
    in_vmem = pl.BlockSpec(memory_space=pltpu.VMEM)
    places = dict(lens=pltpu.SMEM, skip=pltpu.SMEM, deal=pltpu.VMEM)
    f32_out = partial(jax.ShapeDtypeStruct, dtype=F32)
    half = jax.ShapeDtypeStruct((ROWS, HALF), BF16)
    outputs = dict(
        o_wo=f32_out((SHARE, CH)),
        o_gate=f32_out((SHARE, CH)),
        o_value=f32_out((SHARE, CH)),
        o_misc=f32_out((SHARE, 256)),
        o_small=f32_out((8, CH + 256)),
        o_out=half,
        o_hid=half,
    )
    room = scratch()
    flat = [ref for shape in room.values() for ref in (shape if isinstance(shape, list) else [shape])]
    made = pl.pallas_call(
        partial(block_body, {**inputs, **outputs, **room}),
        out_shape=list(outputs.values()),
        in_specs=[pl.BlockSpec(memory_space=places.get(n, pl.ANY)) for n in inputs],
        out_specs=[pl.BlockSpec(memory_space=pl.ANY)] * len(outputs),
        scratch_shapes=flat,
        compiler_params=pltpu.CompilerParams(
            collective_id=0, has_side_effects=True, vmem_limit_bytes=VMEM_BYTES
        ),
        name="block",
    )(*inputs.values())
    shapes = [(HALF,), (SHARE, 2, CH), (SHARE, 128), (HEADS, SHARE), (4, CH), (CH,), (4, 256), (256,)]
    shapes += [(HEADS,)] * 3 + [(CH,), (SHARE, CH)]
    results = pl.pallas_call(
        finish_body,
        out_shape=[half, half, *(f32_out(s) for s in shapes)],
        in_specs=[in_vmem] * len(made),
        out_specs=[in_vmem] * (len(shapes) + 2),
        compiler_params=pltpu.CompilerParams(vmem_limit_bytes=VMEM_BYTES),
        name="finish",
    )(*made)
    return (*results[:5], results[5].T, *results[6:14], results[14].T)


VMEM_BYTES = 65_400_000


def fits(mesh, args):
    return mesh.shape["dp"] == PEERS and mesh.shape["tensor"] == 2 and args[0].shape == (PEERS * ROWS, FULL)


def solution(mesh):
    in_specs = (
        P("dp", "tensor"),
        P("dp", "tensor"),
        P("dp", None),
        P("dp"),
        P(),
        P(None, None, "tensor"),
        P(),
        P(None, "tensor"),
        P(None, "tensor"),
        P("tensor"),
        P(),
        P(),
        P("tensor"),
        P("tensor"),
        P("tensor"),
        P("tensor"),
        P("tensor", None),
    )
    out_specs = (
        P("dp", "tensor"),
        P("dp", "tensor"),
        P("tensor"),
        P("dp", None, "tensor"),
        P("dp", "tensor"),
        P("dp", "tensor"),
        P(None, "tensor"),
        P("tensor"),
        P(),
        P(),
        P("tensor"),
        P("tensor"),
        P("tensor"),
        P("tensor"),
        P("tensor", "dp"),
    )

    def whole(*args):
        local = one_kernel if fits(mesh, args) else shards
        mapped = jax.shard_map(
            local, mesh=mesh, in_specs=in_specs, out_specs=out_specs, check_vma=False
        )
        return mapped(*args)

    return whole
```

```python
from functools import partial
from types import SimpleNamespace

import jax
import jax.numpy as jnp
from jax import lax
from jax.experimental import pallas as pl
from jax.experimental.pallas import tpu as pltpu
from jax.sharding import PartitionSpec as P

D = 1536
GROUP = 256
INNER = 3072


norm_eps = 1e-05


def segment_ids(lengths, row_count):
    index = jnp.arange(lengths.shape[0])
    ends = jnp.sum(jnp.where(index[None, :] <= index[:, None], lengths[None, :], 0), axis=1)
    position = jnp.arange(row_count, dtype=jnp.int32)
    return jnp.sum((position[:, None] >= ends[None, :]).astype(jnp.int32), axis=1, dtype=jnp.int32)


def causal_conv(signal, kernel, kernel_bias, segment):
    width = kernel.shape[0]
    total = kernel_bias[None, :] + kernel[width - 1][None, :] * signal
    for offset in range(1, width):
        moved = jnp.concatenate(
            [jnp.zeros((offset, signal.shape[1]), signal.dtype), signal[:-offset]], axis=0
        )
        earlier = jnp.concatenate([jnp.full((offset,), -1, jnp.int32), segment[:-offset]])
        inside = (earlier == segment).astype(signal.dtype)
        total = total + kernel[width - 1 - offset][None, :] * moved * inside[:, None]
    return total


def state_space(xval, b_rows, c_rows, step, decay, segment):
    highest = lax.Precision.HIGHEST
    blocks = xval.shape[0] // GROUP
    head_count = xval.shape[1]
    x_block = xval.reshape(blocks, GROUP, head_count, xval.shape[2])
    b_block = b_rows.reshape(blocks, GROUP, b_rows.shape[1])
    c_block = c_rows.reshape(blocks, GROUP, c_rows.shape[1])
    step_block = step.reshape(blocks, GROUP, head_count).transpose(0, 2, 1)
    rate_block = step_block * decay[None, :, None]
    seg_block = segment.reshape(blocks, GROUP)
    before = jnp.concatenate([jnp.full((1,), -1, jnp.int32), segment[:-1]]).reshape(blocks, GROUP)[
        :, 0
    ]
    lower_mask = jnp.tril(jnp.ones((GROUP, GROUP), dtype=bool))
    cumulative = jnp.einsum("chj,ij->chi", rate_block, lower_mask.astype(jnp.float32), precision=highest)
    linked = (seg_block[:, :, None] == seg_block[:, None, :]) & lower_mask[None]
    spread = cumulative[:, :, :, None] - cumulative[:, :, None, :]
    weight = jnp.exp(jnp.where(linked[:, None], spread, -10000.0))
    scores = jnp.einsum("cin,cjn->cij", c_block, b_block, precision=highest)
    mixing = weight * scores[:, None] * step_block[:, :, None, :]
    inside_out = jnp.einsum("chij,cjhp->cihp", mixing, x_block, precision=highest)
    final_cum = cumulative[:, :, -1]
    last_same = (seg_block == seg_block[:, -1:]).astype(jnp.float32)
    tail_weight = jnp.exp(final_cum[:, :, None] - cumulative) * last_same[:, None, :] * step_block
    fresh_state = jnp.einsum("chj,cjhp,cjn->chpn", tail_weight, x_block, b_block, precision=highest)
    carried = jnp.zeros(fresh_state.shape[1:], jnp.float32)
    entering = []
    entering.append(carried)
    entering = jnp.stack(entering)
    first_same = (seg_block == before[:, None]).astype(jnp.float32)
    head_decay = jnp.exp(cumulative) * first_same[:, None, :]
    carried_out = jnp.einsum("chi,cin,chpn->cihp", head_decay, c_block, entering, precision=highest)
    return (inside_out + carried_out).reshape(xval.shape)


def pre_norm(stream, gain):
    return stream * lax.rsqrt(jnp.mean(stream * stream, axis=1, keepdims=True) + norm_eps) * gain


def conv_piece(value_pre, state_pre, conv_x, conv_x_bias, conv_bc, conv_bc_bias, segment):
    value_conv = jax.nn.silu(causal_conv(value_pre, conv_x, conv_x_bias, segment))
    state_conv = jax.nn.silu(causal_conv(state_pre, conv_bc, conv_bc_bias, segment))
    return (value_conv, state_conv)


def mixer_piece(value_conv, state_conv, step_pre, step_bias, a_log, skip, segment):
    head_count = step_bias.shape[0]
    row_count = value_conv.shape[0]
    heads_in = value_conv.reshape(row_count, head_count, value_conv.shape[1] // head_count)
    step = jax.nn.softplus(step_pre + step_bias)
    decay = -jnp.exp(a_log)
    half_state = state_conv.shape[1] // 2
    mixed = state_space(
        heads_in, state_conv[:, :half_state], state_conv[:, half_state:], step, decay, segment
    )
    return (mixed + skip[None, :, None] * heads_in).reshape(row_count, value_conv.shape[1])


def rounded(values):
    return lax.optimization_barrier(values.astype(jnp.bfloat16)).astype(jnp.float32)


def shards(
    hidden_in,
    out_grad,
    seq_lengths,
    deal_to,
    pre_gain,
    w_in,
    w_state,
    w_step,
    conv_x,
    conv_x_bias,
    conv_bc,
    conv_bc_bias,
    step_bias,
    a_log,
    skip,
    norm_gain,
    w_out,
):
    dp_count = lax.axis_size("dp")
    row_count = hidden_in.shape[0]
    per_peer = row_count // dp_count
    feat_half = hidden_in.shape[1]
    tensor_index = lax.axis_index("tensor")
    send_order = jnp.argsort(deal_to)
    back_order = jnp.argsort(send_order)
    sent_in = hidden_in[send_order].reshape(dp_count, per_peer, feat_half)
    sent_grad = out_grad[send_order].reshape(dp_count, per_peer, feat_half)
    got_in, got_grad = (
        lax.all_to_all(sent_in, "dp", split_axis=0, concat_axis=0, tiled=True),
        lax.all_to_all(sent_grad, "dp", split_axis=0, concat_axis=0, tiled=True),
    )
    got_ids = lax.all_to_all(
        deal_to[send_order].reshape(dp_count, per_peer),
        "dp",
        split_axis=0,
        concat_axis=0,
        tiled=True,
    )
    dealt_slot = got_ids.reshape(row_count) % row_count
    settle_order = jnp.argsort(dealt_slot)
    dealt_half = got_in.reshape(row_count, feat_half)[settle_order]
    grad_half = got_grad.reshape(row_count, feat_half)[settle_order]
    full_in, grad_full = (
        lax.all_gather(dealt_half, "tensor", axis=1, tiled=True),
        lax.all_gather(grad_half, "tensor", axis=1, tiled=True),
    )
    segment = segment_ids(seq_lengths[0], row_count)
    stream = full_in.astype(jnp.float32)
    normed_f, norm_pull = jax.vjp(pre_norm, stream, pre_gain.astype(jnp.float32))
    normed = normed_f.astype(jnp.bfloat16)
    inner_half = w_in.shape[2]
    w_pair = w_in.reshape(w_in.shape[0], 2 * inner_half)
    proj_pair = jnp.dot(normed, w_pair, preferred_element_type=jnp.float32)
    gate_pre = proj_pair[:, :inner_half]
    value_pre = proj_pair[:, inner_half:]
    state_pre = jnp.dot(normed, w_state, preferred_element_type=jnp.float32)
    step_pre = jnp.dot(normed, w_step, preferred_element_type=jnp.float32)
    conv_args = (
        value_pre,
        state_pre,
        conv_x.astype(jnp.float32),
        conv_x_bias.astype(jnp.float32),
        conv_bc.astype(jnp.float32),
        conv_bc_bias.astype(jnp.float32),
    )
    (value_conv_f, state_conv_f), conv_pull = jax.vjp(
        partial(conv_piece, segment=segment), *conv_args
    )
    value_conv = rounded(value_conv_f)
    state_conv = rounded(state_conv_f)
    mixed, mixer_pull = jax.vjp(
        partial(mixer_piece, segment=segment),
        value_conv,
        state_conv,
        step_pre,
        step_bias,
        a_log,
        skip,
    )
    silu_gate = jax.nn.silu(gate_pre)
    gated = mixed * silu_gate
    total_squares = lax.psum(jnp.sum(gated * gated, axis=1), "tensor")
    inverse = lax.rsqrt(total_squares / INNER + norm_eps)
    gain_f = norm_gain.astype(jnp.float32)
    scaled = (gated * inverse[:, None] * gain_f).astype(jnp.bfloat16)
    partial_out = jnp.dot(scaled, w_out, preferred_element_type=jnp.float32)
    branch = lax.psum_scatter(partial_out, "tensor", scatter_dimension=1, tiled=True)
    result = (dealt_half.astype(jnp.float32) + branch).astype(jnp.bfloat16)
    back_out = lax.all_to_all(
        result[dealt_slot].reshape(dp_count, per_peer, feat_half),
        "dp",
        split_axis=0,
        concat_axis=0,
        tiled=True,
    )
    output = back_out.reshape(row_count, feat_half)[back_order]
    g_w_out = jnp.einsum("ti,td->id", scaled, grad_full, preferred_element_type=jnp.float32)
    d_scaled = jnp.einsum("td,id->ti", grad_full, w_out, preferred_element_type=jnp.float32)
    weighted = d_scaled * gain_f
    g_norm_gain = jnp.sum(d_scaled * gated * inverse[:, None], axis=0)
    cross_sum = lax.psum(jnp.sum(weighted * gated, axis=1), "tensor")
    d_gated = (
        inverse[:, None] * weighted
        - gated * (inverse * inverse * inverse / INNER * cross_sum)[:, None]
    )
    d_mixed = d_gated * silu_gate
    sigmoid_gate = jax.nn.sigmoid(gate_pre)
    d_gate = d_gated * mixed * (sigmoid_gate * (1.0 + gate_pre * (1.0 - sigmoid_gate)))
    d_value_conv, d_state_part, d_step_pre, g_step_bias, g_a_log, g_skip = mixer_pull(d_mixed)
    d_state_conv = lax.psum(d_state_part, "tensor")
    d_value_pre, d_state_pre, g_conv_x, g_conv_x_bias, g_conv_bc, g_conv_bc_bias = conv_pull(
        (d_value_conv, d_state_conv)
    )
    d_pair = jnp.concatenate([d_gate, d_value_pre], axis=1).astype(jnp.bfloat16)
    d_state_low = d_state_pre.astype(jnp.bfloat16)
    d_step_low = d_step_pre.astype(jnp.bfloat16)
    state_share = w_state.shape[1] // lax.axis_size("tensor")
    own_state = lax.dynamic_slice_in_dim(d_state_low, tensor_index * state_share, state_share, 1)
    own_weight = lax.dynamic_slice_in_dim(w_state, tensor_index * state_share, state_share, 1)
    g_w_in = jnp.einsum("td,tc->dc", normed, d_pair, preferred_element_type=jnp.float32).reshape(
        w_in.shape
    )
    g_w_state = jnp.einsum("td,tc->dc", normed, own_state, preferred_element_type=jnp.float32)
    g_w_step = jnp.einsum("td,th->dh", normed, d_step_low, preferred_element_type=jnp.float32)
    d_normed = jnp.einsum("tc,dc->td", d_pair, w_pair, preferred_element_type=jnp.float32)
    d_normed = d_normed + jnp.einsum(
        "th,dh->td", d_step_low, w_step, preferred_element_type=jnp.float32
    )
    d_normed = d_normed + jnp.einsum(
        "tc,dc->td", own_state, own_weight, preferred_element_type=jnp.float32
    )
    normed_share = lax.psum_scatter(d_normed, "tensor", scatter_dimension=1, tiled=True)
    row_scale = lax.rsqrt(jnp.mean(stream * stream, axis=1) + norm_eps)
    stream_share = dealt_half.astype(jnp.float32)
    gain_share = lax.dynamic_slice_in_dim(
        pre_gain.astype(jnp.float32), tensor_index * feat_half, feat_half, 0
    )
    row_cross = lax.psum(jnp.sum(gain_share * normed_share * stream_share, axis=1), "tensor")
    d_share = (
        row_scale[:, None] * gain_share * normed_share
        - stream_share * (row_scale * row_scale * row_scale / D * row_cross)[:, None]
    )
    g_pre_gain = jnp.sum(normed_share * stream_share * row_scale[:, None], axis=0)
    d_input = (d_share + grad_half.astype(jnp.float32)).astype(jnp.bfloat16)
    back_grad = lax.all_to_all(
        d_input[dealt_slot].reshape(dp_count, per_peer, feat_half),
        "dp",
        split_axis=0,
        concat_axis=0,
        tiled=True,
    )
    hidden_grad = back_grad.reshape(row_count, feat_half)[back_order]
    small = lax.psum(
        (
            g_pre_gain,
            g_conv_x,
            g_conv_x_bias,
            g_conv_bc,
            g_conv_bc_bias,
            g_step_bias,
            g_a_log,
            g_skip,
            g_norm_gain,
        ),
        "dp",
    )
    g_in_part, g_state_part, g_step_part, g_w_out_part = (
        lax.psum_scatter(g_w_in, "dp", scatter_dimension=0, tiled=True),
        lax.psum_scatter(g_w_state, "dp", scatter_dimension=0, tiled=True),
        lax.psum_scatter(g_w_step, "dp", scatter_dimension=0, tiled=True),
        lax.psum_scatter(g_w_out, "dp", scatter_dimension=1, tiled=True),
    )
    return (
        output,
        hidden_grad,
        small[0],
        g_in_part,
        g_state_part,
        g_step_part,
        small[1],
        small[2],
        small[3],
        small[4],
        small[5],
        small[6],
        small[7],
        small[8],
        g_w_out_part,
    )


F32, BF16, I32 = jnp.float32, jnp.bfloat16, jnp.int32
MESH = pl.DeviceIdType.MESH
LOG2E = 1.4426950408889634
HIGHEST = lax.Precision.HIGHEST

ROWS = 256
FULL = 1536
HALF = 768
CH = 1536
HEADS = 24
PEERS = 16
PER = ROWS // PEERS
SHARE = FULL // PEERS

X_BIAS, NORM_GAIN, PRE_GAIN, BC_BIAS, STEP_BIAS, A_LOG = (slice(n, n + 1) for n in range(4, 10))

UNITS = (
    ("gate", 0, 256),
    ("gate", 256, 256),
    ("gate", 512, 512),
    ("gate", 1024, 512),
    ("out", 0, 512),
    ("out", 512, 512),
    ("out", 1024, 512),
    ("value", 0, 512),
    ("value", 512, 512),
    ("value", 1024, 512),
    ("misc", 0, 256),
)


def dot_t(a, b):
    return lax.dot_general(a, b, (((1,), (1,)), ((), ())), preferred_element_type=F32)


def dot(a, b):
    return jnp.dot(a, b, preferred_element_type=F32)


def sigmoid(v):
    return 1.0 / (1.0 + jnp.exp(-v))


def block_at(n, width):
    return pl.ds(pl.multiple_of(n * width, width), width)


class Sent:
    def __init__(self, copy):
        self.copy, self.gone, self.here = copy, False, False

    def wait_recv(self):
        self.copy.wait_recv()
        self.here = True

    def wait_send(self):
        if not self.gone:
            self.copy.wait_send()
        self.gone = True


def await_bytes(sem, ref):
    pltpu.make_async_copy(ref, ref, sem).wait()


def block_body(room, *refs):
    left = list(refs)

    def take(shape):
        return [left.pop(0) for _ in shape] if isinstance(shape, list) else left.pop(0)

    r = SimpleNamespace(**{name: take(shape) for name, shape in room.items()})
    lens, deal_ref, vec = r.lens, r.deal, r.vec
    wst, wsp = r.wst, r.wsp
    ss, rs, ls = r.ss, r.rs, r.ls
    me, side = lax.axis_index("dp"), lax.axis_index("tensor")
    core = lax.rem(me, 2)
    xpos = lax.rem(me // 2, 2)
    zpos = me // 4
    sibling = (zpos * 4 + xpos * 2 + (1 - core), side)
    across = (zpos * 4 + (1 - xpos) * 2 + core, side)
    z_side = zpos // 2
    z_outer, z_inner = 3 * z_side, 1 + z_side
    far_outer, far_inner = 3 - z_outer, 3 - z_inner
    is_outer = zpos == z_outer
    is_inner = zpos == z_inner

    def at_z(z):
        return (z * 4 + xpos * 2 + core, side)

    near = at_z(z_outer + z_inner - zpos)
    facing = at_z(3 - zpos)
    other = (me, 1 - side)
    own_cols = pl.ds(pl.multiple_of(side * HALF, HALF), HALF)
    other_cols = pl.ds(pl.multiple_of((1 - side) * HALF, HALF), HALF)

    started, taken, leaving = [], ({}, {}), []

    def semaphore(sems, key):
        count = taken[sems is rs]
        return sems.at[count.setdefault(("own", len(count)) if key is None else key, len(count))]

    def group(key, ref):
        leaving.append((semaphore(ss, key), ref))
        return key

    def send(src, dst, device, by=None, gone=None, came=None):
        copy = pltpu.make_async_remote_copy(
            src_ref=src,
            dst_ref=dst,
            send_sem=semaphore(ss, gone),
            recv_sem=semaphore(rs, came),
            device_id=device,
            device_id_type=MESH,
        )
        if by is None:
            copy.start()
        else:
            pl.when(by)(copy.start)
        one = Sent(copy)
        if gone is None:
            started.append(one)
        return one

    def load(src, dst, n):
        copy = pltpu.make_async_copy(src, dst, ls.at[n])
        copy.start()
        return copy

    def pair_load(n, at):
        cols = pl.ds(pl.multiple_of(n * 128, 128), 128)
        return pltpu.make_async_copy(r.w_in.at[:, :, cols], r.pair.at[at], ls.at[at])

    hid_load = load(r.hid, r.half_in, 3)
    pair_load(0, 0).start()
    pair_load(1, 1).start()
    pair_load(2, 2).start()
    ogr_load = load(r.ogr, r.dhalf_in, 4)
    small_loads = [load(src, dst, 5 + n) for n, (src, dst) in enumerate(zip(r.params, r.params_v))]
    wst_load = load(r.wst_hbm, r.wst, 14)
    wo_load = load(r.wo_hbm, r.wo, 15)

    barrier = pltpu.get_barrier_semaphore()
    for k in range(1, PEERS):
        pl.semaphore_signal(
            barrier, inc=1, device_id=(lax.rem(me + k, PEERS), side), device_id_type=MESH
        )
    pl.semaphore_signal(barrier, inc=1, device_id=other, device_id_type=MESH)

    i0 = lax.broadcasted_iota(I32, (ROWS, ROWS), 0)
    i1 = lax.broadcasted_iota(I32, (ROWS, ROWS), 1)
    deal = deal_ref[...]
    dest = lax.shift_right_logical(deal, 8)
    slot = jnp.bitwise_and(deal, ROWS - 1)
    member = (dest == lax.broadcasted_iota(I32, (PEERS, ROWS), 0)).astype(F32)
    before = dot(member.astype(BF16), (i0 < i1).astype(F32).astype(BF16))
    rank = jnp.sum(member * before, axis=0, keepdims=True)
    place = dest.astype(F32) * PER + rank
    hit = i0.astype(F32) == place
    to_send = hit.astype(F32)
    send_hot = to_send.astype(BF16)
    ident = jnp.sum(to_send * slot.astype(F32), axis=1, keepdims=True)
    sb_h, sb_g, rb_h, rb_g, yb_h, yb_g = r.sb_h, r.sb_g, r.rb_h, r.rb_g, r.yb_h, r.yb_g
    hid_load.wait()
    sb_h[...] = dot(send_hot, r.half_in[...]).astype(BF16)
    row_w = lax.broadcasted_iota(I32, (ROWS, 128), 0)
    lane_w = lax.broadcasted_iota(I32, (ROWS, 128), 1)
    in_place = lax.rem(row_w, PER) == lane_w
    spread = jnp.where(in_place, ident, 0.0).astype(BF16)
    row_n = lax.broadcasted_iota(I32, (PEERS, ROWS), 0)
    lane_n = lax.broadcasted_iota(I32, (PEERS, ROWS), 1)
    gather_ids = (row_n == lane_n // PER).astype(F32).astype(BF16)
    r.sb_i[...] = dot(gather_ids, spread).reshape(PEERS, 1, 128)

    pl.semaphore_wait(barrier, PEERS)

    def rows_of(device):
        return pl.ds(pl.multiple_of(device * PER, PER), PER)

    line = (zpos, z_outer + z_inner - zpos, lax.rem(zpos + 2, 4), 3 - zpos)

    def away(dz, dx, dc):
        return line[dz] * 4 + lax.rem(xpos + dx, 2) * 2 + lax.rem(core + dc, 2)

    steps = [(dz, dx, dc) for dz in (2, 3, 1, 0) for dx in (0, 1) for dc in (0, 1)]

    def deal(dz, src, dst, gone, came, rows=rows_of):
        for step in steps:
            if step[0] == dz and step != (0, 0, 0):
                to = away(*step)
                send(src.at[rows(to)], dst.at[rows(me)], (to, side), gone=gone, came=came)

    def pass_group(name, dz, buf, dst):
        count = 4 * PER - (PER if dz == 0 else 0)
        await_bytes(semaphore(rs, (name, dz)), buf.at[pl.ds(0, count)])
        for step in steps:
            if step[0] == dz:
                origin = rows_of(away(*step))
                send(buf.at[origin], dst.at[origin], other, gone=(name, 9), came=(name, 9))

    def wave(name, dz, src, dst):
        deal(dz, src, dst, (name, "wave", dz), (name, dz))

    def wave_gone(name, dz, src):
        await_bytes(semaphore(ss, (name, "wave", dz)), src.at[pl.ds(0, 4 * PER)])

    def rest(name, src, dst):
        for dz in (1, 0):
            deal(dz, src, dst, name, (name, dz))
        group(name, src.at[pl.ds(0, 7 * PER)])

    def same(device):
        return device

    for dz in (2, 3, 1, 0):
        deal(dz, r.sb_i, r.rb_i, "ids", "ids", same)
    group("ids", r.sb_i.at[pl.ds(0, PEERS - 1)])
    wave("hid", 3, sb_h, rb_h)
    rest("hid", sb_h, rb_h)
    r.rb_i[me] = r.sb_i[me]
    rb_h[rows_of(me)] = sb_h[rows_of(me)]
    ogr_load.wait()
    sb_g[...] = dot(send_hot, r.dhalf_in[...]).astype(BF16)
    rb_g[rows_of(me)] = sb_g[rows_of(me)]
    r.send_hot_t[...] = to_send.T.astype(BF16)

    ends, total = [], 0
    for k in range(8):
        total = total + lens[0, k]
        ends.append(total)

    def seg_at(pos):
        out = jnp.zeros(pos.shape, I32)
        for e in ends:
            out = out + (pos >= e).astype(I32)
        return out

    row_col = lax.broadcasted_iota(I32, (ROWS, 128), 0)
    seg_here = seg_at(row_col)
    for o in range(1, 4):
        same = (seg_at(row_col - o) == seg_here) & (row_col >= o)
        r.masks[o - 1] = same.astype(F32)
    same = seg_at(i0) == seg_at(i1)
    r.linked[...] = (same & (i0 >= i1)).astype(F32)
    r.linked_t[...] = (same & (i0 <= i1)).astype(F32)
    r.small[...] = jnp.zeros((8, CH + 256), F32)
    for copy in small_loads:
        copy.wait()
    conv_x_v, conv_bc_v, w_step_v, *rows_v = r.params_v
    vec[...] = jnp.zeros((16, CH), F32)
    vec[0:4, :] = conv_x_v[...].astype(F32)
    for n, ref in enumerate(rows_v):
        vec[4 + n, 0 : ref.shape[0]] = ref[...].astype(F32)
    vec[12:16, 0:256] = conv_bc_v[...].astype(F32)
    wst_load.wait()
    wsp[...] = jnp.concatenate(
        [w_step_v[...].astype(F32), jnp.zeros((128 - HEADS, FULL), F32)], axis=0
    ).astype(BF16)
    r.dst_acc[...] = jnp.zeros((ROWS, ROWS), F32)
    r.dcol[...] = jnp.zeros((ROWS, 128), F32)
    r.dsd[...] = jnp.zeros((ROWS, 128), F32)

    picked = jnp.where(i0 < 128, 2 * i0, 2 * i0 - 255)
    apart = (picked == i1).astype(F32).astype(BF16)

    def take_apart(n):
        at = lax.rem(n, 3)
        pair_load(n, at).wait()
        cols = block_at(n, 128)
        flat = r.pair.at[at].reshape(2 * FULL, 128)
        for k in range(12):
            both = dot(apart, flat[k * 256 : (k + 1) * 256, :]).astype(BF16)
            r.wg[k * 128 : (k + 1) * 128, cols] = both[0:128]
            r.wv[k * 128 : (k + 1) * 128, cols] = both[128:256]

        @pl.when(n + 3 < 12)
        def _():
            pair_load(n + 3, at).start()

    group(("hid", 9), rb_h)
    group(("grad", 9), rb_g)
    pl.loop(0, 4)(take_apart)
    pass_group("hid", 0, rb_h, yb_h)
    wave_gone("hid", 3, sb_h)
    wave("hid", 2, sb_h, rb_h)
    pl.loop(4, 7)(take_apart)
    pass_group("hid", 1, rb_h, yb_h)
    pl.loop(7, 12)(take_apart)
    pass_group("hid", 3, rb_h, yb_h)
    await_bytes(semaphore(rs, "ids"), r.rb_i.at[pl.ds(0, PEERS - 1)])
    origin_row = lax.broadcasted_iota(I32, (ROWS, PEERS), 0) // PER
    fetch_ids = (origin_row == lax.broadcasted_iota(I32, (ROWS, PEERS), 1)).astype(F32).astype(BF16)
    ids = jnp.where(in_place, dot(fetch_ids, r.rb_i[...].reshape(PEERS, 128).astype(BF16)), 0.0)
    ids = jnp.broadcast_to(jnp.sum(ids, axis=1, keepdims=True), (ROWS, 128))
    r.hot_t[...] = (ids[:, 0:1] == i1.astype(F32)).astype(F32).astype(BF16)
    r.hot[...] = (ids.T[0:1, :] == i0.astype(F32)).astype(F32).astype(BF16)
    wave_gone("hid", 2, sb_h)
    wave("grad", 3, sb_g, rb_g)
    pass_group("hid", 2, rb_h, yb_h)
    rest("grad", sb_g, rb_g)
    stream, upstream, normed = r.stream, r.upstream, r.normed
    stream[:, own_cols] = dot(r.hot[...], rb_h[...]).astype(BF16)
    await_bytes(semaphore(rs, ("hid", 9)), yb_h)
    stream[:, other_cols] = dot(r.hot[...], yb_h[...]).astype(BF16)

    @pl.loop(0, 8)
    def _(n):
        rows = block_at(n, 32)
        s = stream[rows, :].astype(F32)
        scale = lax.rsqrt(jnp.sum(s * s, axis=1, keepdims=True) * (1.0 / FULL) + norm_eps)
        r.nscale[rows, :] = jnp.broadcast_to(scale, (32, 128))
        normed[rows, :] = (s * scale * vec[PRE_GAIN, :]).astype(BF16)

    here, beside, over, cross_over = (pl.ds(n * ROWS, ROWS) for n in range(4))
    diagonal = (zpos * 4 + (1 - xpos) * 2 + (1 - core), side)

    def flip(source, flipped, keep):
        for n in range(4):
            turned = source[:, n * 384 : (n + 1) * 384].astype(F32).T.astype(BF16)
            for i in range(4):
                flipped[n, i] = turned[i * SHARE : (i + 1) * SHARE]
        keep[:, :, here] = flipped[:, xpos * 2 + core]

    others = pl.ds(ROWS, 3 * ROWS)

    def share_flipped(name, flipped, keep):
        group(name, keep.at[:, :, others])
        for dx, dc, lanes, device in ((1, 0, over, across), (1, 1, cross_over, diagonal), (0, 1, beside, sibling)):
            place = lax.rem(xpos + dx, 2) * 2 + lax.rem(core + dc, 2)
            send(flipped.at[:, place], keep.at[:, :, lanes], device, gone=name, came=name)

    masks = r.masks

    def conv_at(signal, taps, bias):
        out = bias + taps[3] * signal
        for o in range(1, 4):
            out = out + taps[3 - o] * (pltpu.roll(signal, o, 0) * masks[o - 1])
        return out

    def conv_back(signal, taps, bias, grad):
        pre = conv_at(signal, taps, bias)
        s = sigmoid(pre)
        d_pre = grad * (s * (1.0 + pre * (1.0 - s)))
        sums = [None] * 4
        sums[3] = jnp.sum(d_pre * signal, axis=0, keepdims=True)
        d_signal = taps[3] * d_pre
        for o in range(1, 4):
            masked = d_pre * masks[o - 1]
            sums[3 - o] = jnp.sum(masked * pltpu.roll(signal, o, 0), axis=0, keepdims=True)
            d_signal = d_signal + taps[3 - o] * pltpu.roll(masked, ROWS - o, 0)
        return d_signal, sums, jnp.sum(d_pre, axis=0, keepdims=True)

    def taps_at(first, cols):
        return [vec[pl.ds(first + k, 1), cols] for k in range(4)]

    gate_pre, value_pre, vconv = r.gate_pre, r.value_pre, r.vconv
    def project(n):
        cols = block_at(n, 256)
        gate_pre[:, cols] = dot(normed[...], r.wg[:, cols])
        value_pre[:, cols] = dot(normed[...], r.wv[:, cols])

    def convolve(n):
        cols = block_at(n, 128)
        pre = conv_at(value_pre[:, cols], taps_at(0, cols), vec[X_BIAS, cols])
        vconv[:, cols] = (pre * sigmoid(pre)).astype(BF16)

    wave_gone("grad", 3, sb_g)
    wave("grad", 2, sb_g, rb_g)
    pl.loop(0, 6, unroll=3)(project)
    pass_group("grad", 0, rb_g, yb_g)
    pass_group("grad", 1, rb_g, yb_g)
    pl.loop(0, 12)(convolve)
    pass_group("grad", 3, rb_g, yb_g)

    state_pre, sconv = r.state_pre, r.sconv
    state_pre[...] = dot(normed[...], wst[...])
    for n in range(2):
        cols = pl.ds(n * 128, 128)
        pre = conv_at(state_pre[:, cols], taps_at(12, cols), vec[BC_BIAS, cols])
        sconv[:, cols] = (pre * sigmoid(pre)).astype(BF16)

    step_in = dot_t(normed[...], wsp[...]) + vec[STEP_BIAS, 0:128]
    small_e = jnp.exp(-jnp.abs(step_in))
    series = small_e * (1.0 - small_e * (0.5 - small_e * (1.0 / 3.0 - 0.25 * small_e)))
    step = jnp.maximum(step_in, 0.0) + jnp.where(small_e < 0.01, series, jnp.log(1.0 + small_e))
    decay = -jnp.exp(vec[A_LOG, 0:128])
    r.step_in[...] = step_in
    r.step[...] = step
    lower = (i0 >= i1).astype(F32)
    cum2 = jnp.dot(lower, step * decay, precision=HIGHEST, preferred_element_type=F32) * LOG2E
    r.cum2[...] = cum2
    r.cum2_t[...] = cum2.T
    r.cum2_ls[...] = (cum2 - jnp.log(step) * LOG2E).T
    b_rows, c_rows = sconv[:, 0:128], sconv[:, 128:256]
    r.scores[...] = dot_t(c_rows, b_rows) * r.linked[...]
    r.scores_t[...] = dot_t(b_rows, c_rows) * r.linked_t[...]

    lane = lax.broadcasted_iota(I32, (ROWS, 128), 1)
    lane_half = lax.broadcasted_iota(I32, (128, 128), 1) < 64

    def column(ref, h):
        return jnp.sum(jnp.where(lane == h, ref[...], 0.0), axis=1, keepdims=True)


    mixed = r.mixed

    def mix(p):
        cols = block_at(p, 128)
        x = vconv[:, cols]
        tops, lows = [], []
        for a in range(2):
            h = 2 * p + a
            cc = column(r.cum2, h)
            cr = r.cum2_ls[pl.ds(h, 1), :]
            w = jnp.exp2(jnp.minimum(cc[0:128] - cr[:, 0:128], 100.0)) * r.scores[0:128, 0:128]
            tops.append(dot(w.astype(BF16), x[0:128]))
            w = jnp.exp2(jnp.minimum(cc[128:256] - cr, 100.0)) * r.scores[128:256, :]
            lows.append(dot(w.astype(BF16), x))
        skip = jnp.where(lane_half[0:1], r.skip[2 * p], r.skip[2 * p + 1])
        xf = x.astype(F32)
        mixed[0:128, cols] = jnp.where(lane_half, tops[0], tops[1]) + skip * xf[0:128]
        mixed[128:256, cols] = jnp.where(lane_half, lows[0], lows[1]) + skip * xf[128:256]

    pl.loop(0, 3, unroll=3)(mix)
    pass_group("grad", 2, rb_g, yb_g)
    wave_gone("grad", 2, sb_g)
    pl.loop(3, 12, unroll=3)(mix)
    flip(normed, r.norm_f, r.norm_t)
    share_flipped("norm", r.norm_f, r.norm_t)

    upstream[:, own_cols] = dot(r.hot[...], rb_g[...]).astype(BF16)
    await_bytes(semaphore(rs, ("grad", 9)), yb_g)
    upstream[:, other_cols] = dot(r.hot[...], yb_g[...]).astype(BF16)
    wo_load.wait()
    d_scaled = r.d_scaled
    r.acc1[...] = jnp.zeros((ROWS, 128), F32)
    r.acc2[...] = jnp.zeros((ROWS, 128), F32)

    @pl.loop(0, 6, unroll=6)
    def _(n):
        cols = block_at(n, 256)
        ds = dot_t(upstream[...], r.wo[cols, :])
        d_scaled[:, cols] = ds
        g = gate_pre[:, cols]
        gated = mixed[:, cols] * g * sigmoid(g)
        sq = gated * gated
        cr = vec[NORM_GAIN, cols] * ds * gated
        r.acc1[...] += sq[:, 0:128] + sq[:, 128:256]
        r.acc2[...] += cr[:, 0:128] + cr[:, 128:256]

    def exchange_rows(col_a, col_b, out_buf, in_buf):
        both = jnp.where(lane == 0, col_a, jnp.where(lane == 1, col_b, 0.0))
        out_buf[...] = both.T[0:8, :]
        copy = send(out_buf, in_buf, other)

        def finish():
            copy.wait_recv()
            both = jnp.concatenate([out_buf[...] + in_buf[...], jnp.zeros((120, ROWS), F32)], axis=0)
            return both.T[:, 0:1], both.T[:, 1:2]

        return finish

    row_sums = exchange_rows(
        jnp.sum(r.acc1[...], axis=1, keepdims=True),
        jnp.sum(r.acc2[...], axis=1, keepdims=True),
        r.ex_a,
        r.ex_b,
    )
    r.cum2_ls[...] = jnp.zeros((128, ROWS), F32)
    flip(upstream, r.up_f, r.up_t)
    sum_sq, sum_cross = row_sums()
    inner = 2.0 * CH
    inverse = lax.rsqrt(sum_sq * (1.0 / inner) + norm_eps)
    cross = inverse * inverse * inverse * (1.0 / inner) * sum_cross
    r.acc1[...] = jnp.broadcast_to(inverse, (ROWS, 128))
    r.acc2[...] = jnp.broadcast_to(cross, (ROWS, 128))
    scaled4, gate4, value4, misc4 = r.scaled4, r.gate4, r.value4, r.misc4

    def gated_back(n):
        cols = block_at(n, 128)
        inv, crs = r.acc1[...], r.acc2[...]
        g, m, ds, gain = gate_pre[:, cols], mixed[:, cols], d_scaled[:, cols], vec[NORM_GAIN, cols]
        s = sigmoid(g)
        silu = g * s
        gated = m * silu
        gi = gated * inv
        scaled4[here, cols] = (gi * gain).astype(BF16)
        r.small[5:6, cols] = jnp.sum(ds * gi, axis=0, keepdims=True)
        d_gated = inv * ds * gain - gated * crs
        mixed[:, cols] = d_gated * silu
        gate4[here, cols] = (d_gated * m * (s * (1.0 + g * (1.0 - s)))).astype(BF16)

    def gated_part(n):
        pl.loop(4 * n, 4 * n + 4)(gated_back)

    half_f, half_o, half_in = d_scaled.at[:, pl.ds(0, HALF)], normed.at[:, pl.ds(0, HALF)], r.half_in
    flying = {}

    def project_other():
        @pl.loop(0, 3)
        def _(n):
            cols = pl.ds(pl.multiple_of((1 - side) * HALF + n * 256, 256), 256)
            half_o[:, block_at(n, 256)] = dot(scaled4[here, :], r.wo[:, cols]).astype(BF16)

        flying["out"] = send(half_o, half_in, other)

    def project_own():
        @pl.loop(0, 3)
        def _(n):
            cols = pl.ds(pl.multiple_of(side * HALF + n * 256, 256), 256)
            half_f[:, block_at(n, 256)] = dot(scaled4[here, :], r.wo[:, cols]) + stream[:, cols].astype(F32)

    lefts = {"out": r.up_t, "gate": r.norm_t, "value": r.norm_t, "misc": r.norm_t}
    rights = {"out": scaled4, "gate": gate4, "value": value4, "misc": misc4}
    outs = {"out": r.o_wo, "gate": r.o_gate, "value": r.o_value, "misc": r.o_misc}
    stores = []

    def store(src, dst, n):
        copy = pltpu.make_async_copy(src, dst, r.os.at[n])
        copy.start()
        return copy

    def ready(copy):
        if not copy.here:
            copy.wait_recv()

    pieces = {}
    for name, ref in rights.items():
        group(name, ref.at[pl.ds(0, 3 * ROWS)])

    def up_swap():
        share_flipped("up", r.up_f, r.up_t)

    def swap(name, first, width):
        ref, cols = rights[name], pl.ds(first, width)
        near_by = send(ref.at[here, cols], ref.at[beside, cols], sibling, gone=name)
        far_off = send(ref.at[here, cols], ref.at[over, cols], across, gone=name)
        pieces[name, first] = [width, near_by, far_off]

    def relay(name, first):
        piece = pieces[name, first]
        ref, cols = rights[name], pl.ds(first, piece[0])
        ready(piece[2])
        piece.append(send(ref.at[over, cols], ref.at[cross_over, cols], sibling, gone=name))

    class Unit:
        def __init__(self, n):
            self.name, self.first, self.width = UNITS[n]
            self.n, self.part, self.zbuf, self.kept = n, r.part[n], r.zbuf[n], r.kept[n]
            self.key = group(("unit", n), self.zbuf.at[pl.ds(0, 3)])
            self.stages = [self.compute, self.pass_outer, self.pass_inner, self.send_out, self.finish]

        def go(self, stage):
            self.stages[stage]()

        def add(self, z, slot):
            self.part[z] = self.part[z] + self.zbuf[slot]

        def hop(self, z, slot, device, by):
            return send(self.part.at[z], self.zbuf.at[slot], device, by, self.key, (self.key, slot))

        def compute(self):
            lhs_ref, rhs_ref = lefts[self.name], rights[self.name]
            first, part = self.first, self.part
            side_name = "up" if self.name == "out" else "norm"
            if side_name not in flying:
                flying[side_name] = True
                await_bytes(semaphore(rs, side_name), lhs_ref.at[:, :, others])
            for (name, start), piece in pieces.items():
                if name == self.name and start < first + self.width and first < start + piece[0]:
                    for copy in piece[1:]:
                        ready(copy)

            @pl.loop(0, self.width // 256)
            def _(n):
                lhs = lhs_ref[...].reshape(4 * SHARE, 4 * ROWS)
                rhs = rhs_ref[:, pl.ds(pl.multiple_of(first + n * 256, 256), 256)]
                part[:, :, block_at(n, 256)] = dot(lhs, rhs).astype(BF16).reshape(4, SHARE, 256)

            self.c3 = self.hop(far_outer, 0, near, is_outer)
            self.c2 = self.hop(far_inner, 1, near, is_outer)
            self.c1 = self.hop(z_inner, 2, near, is_outer)

        def pass_outer(self):
            @pl.when(is_inner)
            def _():
                self.c3.wait_recv()
                self.add(far_outer, 0)

            self.d2 = self.hop(far_outer, 3, facing, is_inner)

        def pass_inner(self):
            @pl.when(is_inner)
            def _():
                self.c2.wait_recv()
                self.add(far_inner, 1)

            self.d1 = self.hop(far_inner, 4, facing, is_inner)

        def send_out(self):
            @pl.when(is_inner)
            def _():
                self.d2.wait_recv()
                self.add(z_outer, 3)

            self.e1 = self.hop(z_outer, 0, near, is_inner)

        def finish(self):
            own = self.kept
            cols = pl.ds(self.first, self.width)

            @pl.when(is_outer)
            def _():
                self.e1.wait_recv()
                own[...] = self.part[zpos].astype(F32) + self.zbuf[0].astype(F32)

            @pl.when(is_inner)
            def _():
                self.c1.wait_recv()
                self.d1.wait_recv()
                own[...] = self.part[zpos].astype(F32) + self.zbuf[2].astype(F32) + self.zbuf[4].astype(F32)

            stores.append(store(own, outs[self.name].at[:, cols], self.n))

    units = [Unit(n) for n in range(len(UNITS))]
    head_row = lax.broadcasted_iota(I32, (32, ROWS), 0)

    def mixer_back(p):
        cols = block_at(p, 128)
        x = vconv[:, cols]
        xf = x.astype(F32)
        dy = mixed[:, cols]
        dyb = dy.astype(BF16)
        by_channel = jnp.sum(dy * xf, axis=0, keepdims=True)
        skips = r.small[6:7, CH + 128 : CH + 256]
        d_tops, d_lows = [], []
        for a in range(2):
            h = 2 * p + a
            half = (lane < 64) if a == 0 else (lane >= 64)
            of_head = jnp.sum(jnp.where(half[0:1], by_channel, 0.0), axis=1, keepdims=True)
            skips = skips + jnp.where(lane[0:1] == h, of_head, 0.0)
            xa = jnp.where(half, xf, 0.0)
            xab = xa.astype(BF16)
            cc = column(r.cum2, h)
            st = column(r.step, h)
            cr = r.cum2_t[pl.ds(h, 1), :]
            w = jnp.exp2(jnp.minimum(cr - cc[0:128], 0.0))
            sc = r.scores_t[0:128, :]
            v_top = dot((w * sc).astype(BF16), dyb)
            q = dot_t(xab[0:128], dyb) * w * st[0:128]
            r.dst_acc[0:128, :] += q
            g_top = q * sc
            w = jnp.exp2(jnp.minimum(cr[:, 128:256] - cc[128:256], 0.0))
            sc = r.scores_t[128:256, 128:256]
            v_low = dot((w * sc).astype(BF16), dyb[128:256])
            q = dot_t(xab[128:256], dyb[128:256]) * w * st[128:256]
            r.dst_acc[128:256, 128:256] += q
            g_low = q * sc
            top_sums = jnp.sum(g_top, axis=0, keepdims=True)
            low_sums = jnp.sum(g_low, axis=0, keepdims=True)
            col_sums = jnp.concatenate([top_sums[:, 0:128], top_sums[:, 128:256] + low_sums], axis=1)
            r.cum2_ls[0:32, :] += jnp.where(head_row == h, col_sums, 0.0)
            row_sums = jnp.concatenate(
                [
                    jnp.sum(g_top[:, 0:128] + g_top[:, 128:256], axis=1, keepdims=True),
                    jnp.sum(g_low, axis=1, keepdims=True),
                ],
                axis=0,
            )
            direct = jnp.concatenate(
                [
                    jnp.sum(xa[0:128] * v_top, axis=1, keepdims=True),
                    jnp.sum(xa[128:256] * v_low, axis=1, keepdims=True),
                ],
                axis=0,
            )
            r.dcol[...] += jnp.where(lane == h, row_sums, 0.0)
            r.dsd[...] += jnp.where(lane == h, direct, 0.0)
            d_tops.append(st[0:128] * v_top)
            d_lows.append(st[128:256] * v_low)
        r.small[6:7, CH + 128 : CH + 256] = skips
        d_conv = jnp.concatenate(
            [jnp.where(lane_half, d_tops[0], d_tops[1]), jnp.where(lane_half, d_lows[0], d_lows[1])],
            axis=0,
        )
        d_conv = d_conv + jnp.where(lane_half[0:1], r.skip[2 * p], r.skip[2 * p + 1]) * dy
        d_value, sums, bias_sum = conv_back(value_pre[:, cols], taps_at(0, cols), vec[X_BIAS, cols], d_conv)
        value4[here, cols] = d_value.astype(BF16)
        for k in range(4):
            r.small[k : k + 1, cols] = sums[k]
        r.small[4:5, cols] = bias_sum

    def mixer_part(first, last):
        pl.loop(first, last)(mixer_back)

    def send_back(name, src, dst):
        group(name, src.at[pl.ds(0, ROWS - PER)])
        for dz in (2, 3, 1, 0):
            deal(dz, src, dst, name, name)
        dst[rows_of(me)] = src[rows_of(me)]

    def return_out():
        ready(flying["out"])
        result = (half_f[...] + half_in[...].astype(F32)).astype(BF16)
        yb_h[...] = dot(r.hot_t[...], result).astype(BF16)
        send_back("back_o", yb_h, r.back_o)

    def finish_out():
        await_bytes(semaphore(rs, "back_o"), r.back_o.at[pl.ds(0, ROWS - PER)])
        r.res_o[...] = dot(r.send_hot_t[...], r.back_o[...]).astype(BF16)
        stores.append(store(r.res_o, r.o_out, len(UNITS) + 1))

    d_state = r.d_state
    state_own = pl.ds(pl.multiple_of(side * 128, 128), 128)
    state_other = pl.ds(pl.multiple_of((1 - side) * 128, 128), 128)

    def states_back():
        d_scores_t = r.dst_acc[...] * r.linked_t[...]
        d_conv_s = r.linked
        d_conv_s[:, 0:128] = dot(d_scores_t.astype(BF16), c_rows)
        d_conv_s[:, 128:256] = dot(d_scores_t.T.astype(BF16), b_rows)
        for n in range(2):
            cols = pl.ds(n * 128, 128)
            d_pre, sums, bias_sum = conv_back(
                state_pre[:, cols], taps_at(12, cols), vec[BC_BIAS, cols], d_conv_s[:, cols]
            )
            d_state[:, cols] = d_pre
            for k in range(4):
                r.small[k : k + 1, CH + n * 128 : CH + (n + 1) * 128] = sums[k]
            r.small[4:5, CH + n * 128 : CH + (n + 1) * 128] = bias_sum
        r.st_out[...] = d_state[:, state_other].astype(BF16)
        flying["state"] = send(r.st_out, r.st_in, other)
        d_cum = r.cum2_ls[...].T - r.dcol[...]
        upper = (i0 <= i1).astype(F32)
        d_rate = jnp.dot(upper, d_cum, precision=HIGHEST, preferred_element_type=F32)
        d_step = (r.dsd[...] + d_rate * decay) * sigmoid(r.step_in[...])
        r.small[5:6, CH : CH + 128] = jnp.sum(d_step, axis=0, keepdims=True)
        r.small[6:7, CH : CH + 128] = jnp.sum(d_rate * r.step[...], axis=0, keepdims=True) * decay
        misc4[here, 128:256] = d_step.astype(BF16)
        r.acc1[...] = jnp.zeros((ROWS, 128), F32)
        r.st_low[...] = d_state[...].astype(BF16)

    def add_states():
        ready(flying["state"])
        misc4[here, 0:128] = (d_state[:, state_own] + r.st_in[...].astype(F32)).astype(BF16)

    dhalf_f, dhalf_o, dhalf_in = d_scaled.at[:, pl.ds(HALF, HALF)], normed.at[:, pl.ds(HALF, HALF)], r.dhalf_in

    def d_normed_at(first):
        rows = pl.ds(pl.multiple_of(first, 256), 256)
        out = dot_t(gate4[here, :], r.wg[rows, :]) + dot_t(value4[here, :], r.wv[rows, :])
        out = out + dot_t(r.st_low[...], r.wst[rows, :])
        out = out + dot(misc4[here, 128:256], wsp[:, rows])
        part = out * vec[PRE_GAIN, rows] * stream[:, rows].astype(F32)
        r.acc1[...] += part[:, 0:128] + part[:, 128:256]
        return out

    def normed_other():
        @pl.loop(0, 3)
        def _(n):
            dhalf_o[:, block_at(n, 256)] = d_normed_at((1 - side) * HALF + n * 256).astype(BF16)

        flying["norm"] = send(dhalf_o, dhalf_in, other)

    def normed_own():
        @pl.loop(0, 3)
        def _(n):
            dhalf_f[:, block_at(n, 256)] = d_normed_at(side * HALF + n * 256)

        flying["rows"] = exchange_rows(
            jnp.sum(r.acc1[...], axis=1, keepdims=True), jnp.zeros((ROWS, 1), F32), r.ex_c, r.ex_d
        )

    small = r.small

    def return_grad():
        row_cross, _ = flying["rows"]()
        ready(flying["norm"])
        flying["out"].wait_send()
        scale = r.nscale[:, 0:1]
        factor = scale * scale * scale * (1.0 / FULL) * row_cross
        for n in range(6):
            cols = pl.ds(n * 128, 128)
            mine = pl.ds(pl.multiple_of(side * HALF + n * 128, 128), 128)
            dn = dhalf_f[:, cols] + dhalf_in[:, cols].astype(F32)
            s = stream[:, mine].astype(F32)
            small[7:8, n * 128 : (n + 1) * 128] = jnp.sum(dn * s * scale, axis=0, keepdims=True)
            grad = upstream[:, mine].astype(F32) + scale * vec[PRE_GAIN, mine] * dn - s * factor
            half_o[:, cols] = grad.astype(BF16)
        yb_g[...] = dot(r.hot_t[...], half_o[...]).astype(BF16)
        send_back("back_g", yb_g, r.back_g)

    def finish_grad():
        await_bytes(semaphore(rs, "back_g"), r.back_g.at[pl.ds(0, ROWS - PER)])
        r.res_g[...] = dot(r.send_hot_t[...], r.back_g[...]).astype(BF16)
        stores.append(store(r.res_g, r.o_hid, len(UNITS) + 2))

    lasts = pl.ds(CH, 256)

    def small_tensor():
        flying["small"] = send(small.at[:, lasts], r.sm_y, other)

    def small_tensor_end():
        copy = flying["small"]
        copy.wait_send()
        copy.wait_recv()
        keep_rows = lax.broadcasted_iota(I32, (8, 256), 0) < 5
        small[:, lasts] = small[:, lasts] + jnp.where(keep_rows, r.sm_y[...], 0.0)

    partners = [sibling, across, near, facing]

    def small_start(n):
        flying[n] = send(small, r.sm_a[n], partners[n])

    def small_end(n):
        flying[n].wait_send()
        flying[n].wait_recv()
        small[...] = small[...] + r.sm_a[n][...]

    gated_part(0)
    gated_part(1)
    swap("gate", 256, 256)
    gated_part(2)
    project_other()
    swap("gate", 1024, 512)
    mixer_part(0, 6)
    relay("gate", 256)
    swap("value", 0, 768)
    swap("gate", 512, 512)
    units[1].go(0)
    project_own()
    return_out()
    units[1].go(1)
    relay("gate", 1024)
    mixer_part(6, 12)
    units[3].go(0)
    states_back()
    relay("value", 0)
    swap("value", 768, 768)
    normed_other()
    swap("out", 512, 512)
    units[7].go(0)
    up_swap()
    units[1].go(2)
    add_states()
    relay("gate", 512)
    swap("misc", 0, 256)
    units[2].go(0)
    units[7].go(1)
    units[2].go(1)
    swap("out", 0, 512)
    normed_own()
    swap("out", 1024, 512)
    finish_out()
    units[7].go(2)
    return_grad()
    relay("value", 768)
    units[8].go(0)
    units[3].go(1)
    units[9].go(0)
    units[3].go(2)
    units[2].go(2)
    relay("out", 512)
    relay("misc", 0)
    units[1].go(3)
    units[9].go(1)
    units[10].go(0)
    units[3].go(3)
    units[5].go(0)
    units[3].go(4)
    units[8].go(1)
    relay("out", 0)
    small_tensor()
    units[2].go(3)
    units[8].go(2)
    swap("gate", 0, 256)
    units[5].go(1)
    units[8].go(3)
    relay("out", 1024)
    units[10].go(1)
    units[4].go(0)
    small_tensor_end()
    units[7].go(3)
    units[9].go(2)
    units[5].go(2)
    units[10].go(2)
    units[6].go(0)
    units[5].go(3)
    small_start(0)
    finish_grad()
    units[4].go(1)
    small_end(0)
    relay("gate", 0)
    units[5].go(4)
    units[9].go(3)
    units[1].go(4)
    small_start(1)
    units[4].go(2)
    units[4].go(3)
    units[8].go(4)
    units[6].go(1)
    units[7].go(4)
    units[0].go(0)
    units[9].go(4)
    small_end(1)
    small_start(2)
    units[2].go(4)
    units[10].go(3)
    units[6].go(2)
    units[4].go(4)
    units[10].go(4)
    units[0].go(1)
    units[6].go(3)
    units[0].go(2)
    units[0].go(3)
    small_end(2)
    small_start(3)
    units[6].go(4)
    units[0].go(4)
    small_end(3)
    stores.append(store(small, r.o_small, len(UNITS)))
    for copy in started:
        copy.wait_send()
    for sem, ref in leaving:
        await_bytes(sem, ref)
    for copy in stores:
        copy.wait()


def scratch():
    vmem, dma = pltpu.VMEM, pltpu.SemaphoreType.DMA
    square, wide = (ROWS, ROWS), (ROWS, CH)
    def rows(dtype, width):
        return vmem((ROWS, width), dtype)

    return dict(
        wg=vmem((FULL, CH), BF16),
        wv=vmem((FULL, CH), BF16),
        wo=vmem((CH, FULL), BF16),
        pair=vmem((3, FULL, 2, 128), BF16),
        send_hot_t=vmem(square, BF16),
        hot=vmem(square, BF16),
        hot_t=vmem(square, BF16),
        sb_h=rows(BF16, HALF),
        rb_h=rows(BF16, HALF),
        sb_i=vmem((PEERS, 1, 128), F32),
        rb_i=vmem((PEERS, 1, 128), F32),
        sb_g=rows(BF16, HALF),
        rb_g=rows(BF16, HALF),
        yb_h=rows(BF16, HALF),
        yb_g=rows(BF16, HALF),
        half_in=rows(BF16, HALF),
        dhalf_in=rows(BF16, HALF),
        back_o=rows(BF16, HALF),
        back_g=rows(BF16, HALF),
        masks=vmem((3, ROWS, 128), F32),
        linked=vmem(square, F32),
        linked_t=vmem(square, F32),
        scores=vmem(square, F32),
        scores_t=vmem(square, F32),
        dst_acc=vmem(square, F32),
        small=vmem((8, CH + 256), F32),
        params_v=[
            vmem((4, CH), BF16),
            vmem((4, 256), BF16),
            vmem((HEADS, FULL), BF16),
            vmem((CH,), BF16),
            vmem((CH,), BF16),
            vmem((FULL,), BF16),
            vmem((256,), BF16),
            vmem((HEADS,), F32),
            vmem((HEADS,), F32),
        ],
        res_o=rows(BF16, HALF),
        res_g=rows(BF16, HALF),
        kept=[vmem((SHARE, width), F32) for _, _, width in UNITS],
        vec=vmem((16, CH), F32),
        wsp=vmem((128, FULL), BF16),
        wst=vmem((FULL, 256), BF16),
        cum2_t=vmem((128, ROWS), F32),
        cum2_ls=vmem((128, ROWS), F32),
        stream=vmem(wide, BF16),
        upstream=vmem(wide, BF16),
        normed=vmem(wide, BF16),
        vconv=vmem(wide, BF16),
        gate_pre=vmem(wide, F32),
        value_pre=vmem(wide, F32),
        mixed=vmem(wide, F32),
        d_scaled=vmem(wide, F32),
        state_pre=rows(F32, 256),
        d_state=rows(F32, 256),
        sconv=rows(BF16, 256),
        st_low=rows(BF16, 256),
        st_out=rows(BF16, 128),
        st_in=rows(BF16, 128),
        scaled4=vmem((4 * ROWS, CH), BF16),
        gate4=vmem((4 * ROWS, CH), BF16),
        value4=vmem((4 * ROWS, CH), BF16),
        misc4=vmem((4 * ROWS, 256), BF16),
        norm_t=vmem((4, SHARE, 4 * ROWS), BF16),
        up_t=vmem((4, SHARE, 4 * ROWS), BF16),
        norm_f=vmem((4, 4, SHARE, ROWS), BF16),
        up_f=vmem((4, 4, SHARE, ROWS), BF16),
        nscale=rows(F32, 128),
        acc1=rows(F32, 128),
        acc2=rows(F32, 128),
        dcol=rows(F32, 128),
        dsd=rows(F32, 128),
        step_in=rows(F32, 128),
        step=rows(F32, 128),
        cum2=rows(F32, 128),
        ex_a=vmem((8, ROWS), F32),
        ex_b=vmem((8, ROWS), F32),
        ex_c=vmem((8, ROWS), F32),
        ex_d=vmem((8, ROWS), F32),
        sm_y=vmem((8, 256), F32),
        sm_a=[vmem((8, CH + 256), F32) for _ in range(4)],
        part=[vmem((4, SHARE, width), BF16) for _, _, width in UNITS],
        zbuf=[vmem((5, SHARE, width), BF16) for _, _, width in UNITS],
        ss=dma((SENDS,)),
        rs=dma((ARRIVALS,)),
        ls=dma((16,)),
        os=dma((len(UNITS) + 3,)),
    )


SENDS = 27 + len(UNITS)
ARRIVALS = 55 + 5 * len(UNITS)


def listed(v):
    return v if isinstance(v, list) else [v]


def finish_body(*refs):
    wo, gate, value, misc, small, out, hid = refs[:7]
    outs, scratch_refs = refs[7:22], refs[22:]
    misc_v, small_v, *held = scratch_refs[:-1]
    sems = scratch_refs[-1]
    (
        out_v, hid_v, pre, in_v, state, step, cx, cxb, cb, cbb, bias, log, skip, gain, wo_v
    ) = held

    def move(src, dst, n):
        copy = pltpu.make_async_copy(src, dst, sems.at[n])
        copy.start()
        return copy

    moves = (
        (small, small_v),
        (misc, misc_v),
        (gate, in_v.at[:, 0, :]),
        (value, in_v.at[:, 1, :]),
        (wo, wo_v),
        (out, out_v),
        (hid, hid_v),
    )
    loads = [move(src, dst, n) for n, (src, dst) in enumerate(moves)]
    stores = []

    def keep(*which):
        for n in which:
            stores.append(move(held[n], outs[n], len(moves) + n))

    loads[0].wait()
    pre[...] = small_v[7, 0:HALF]
    cx[...] = small_v[0:4, 0:CH]
    cxb[...] = small_v[4, 0:CH]
    cb[...] = small_v[0:4, CH:]
    cbb[...] = small_v[4, CH:]
    bias[...] = small_v[5, CH : CH + HEADS]
    log[...] = small_v[6, CH : CH + HEADS]
    skip[...] = small_v[6, CH + 128 : CH + 128 + HEADS]
    gain[...] = small_v[5, 0:CH]
    keep(2, 6, 7, 8, 9, 10, 11, 12, 13)
    loads[1].wait()
    state[...] = misc_v[:, 0:128]
    step[...] = misc_v[:, 128:256].T[0:HEADS]
    keep(4, 5)
    loads[2].wait()
    loads[3].wait()
    keep(3)
    for n, which in ((4, 14), (5, 0), (6, 1)):
        loads[n].wait()
        keep(which)
    for copy in stores:
        copy.wait()


def one_kernel(
    hidden_in,
    out_grad,
    seq_lengths,
    deal_to,
    pre_gain,
    w_in,
    w_state,
    w_step,
    conv_x,
    conv_x_bias,
    conv_bc,
    conv_bc_bias,
    step_bias,
    a_log,
    skip,
    norm_gain,
    w_out,
):
    inputs = dict(
        hid=hidden_in,
        ogr=out_grad,
        lens=seq_lengths,
        deal=deal_to.reshape(1, ROWS),
        skip=skip,
        w_in=w_in,
        wo_hbm=w_out,
        wst_hbm=w_state,
        params=[
            conv_x,
            conv_bc,
            w_step.T,
            conv_x_bias,
            norm_gain,
            pre_gain,
            conv_bc_bias,
            step_bias,
            a_log,
        ],
    )
    in_vmem = pl.BlockSpec(memory_space=pltpu.VMEM)
    places = dict(lens=pltpu.SMEM, skip=pltpu.SMEM, deal=pltpu.VMEM)
    f32_out = partial(jax.ShapeDtypeStruct, dtype=F32)
    half = jax.ShapeDtypeStruct((ROWS, HALF), BF16)
    outputs = dict(
        o_wo=f32_out((SHARE, CH)),
        o_gate=f32_out((SHARE, CH)),
        o_value=f32_out((SHARE, CH)),
        o_misc=f32_out((SHARE, 256)),
        o_small=f32_out((8, CH + 256)),
        o_out=half,
        o_hid=half,
    )
    room = scratch()
    flat = [ref for shape in room.values() for ref in listed(shape)]
    made = pl.pallas_call(
        partial(block_body, {**inputs, **outputs, **room}),
        out_shape=list(outputs.values()),
        in_specs=[pl.BlockSpec(memory_space=places.get(n, pl.ANY)) for n, v in inputs.items() for _ in listed(v)],
        out_specs=[pl.BlockSpec(memory_space=pl.ANY)] * len(outputs),
        scratch_shapes=flat,
        compiler_params=pltpu.CompilerParams(
            collective_id=0, has_side_effects=True, vmem_limit_bytes=VMEM_BYTES
        ),
        name="block",
    )(*(v for value in inputs.values() for v in listed(value)))
    shapes = [(HALF,), (SHARE, 2, CH), (SHARE, 128), (HEADS, SHARE), (4, CH), (CH,), (4, 256), (256,)]
    shapes += [(HEADS,)] * 3 + [(CH,), (SHARE, CH)]
    any_place = pl.BlockSpec(memory_space=pl.ANY)
    made_shapes = [half, half, *(f32_out(s) for s in shapes)]
    results = pl.pallas_call(
        finish_body,
        out_shape=made_shapes,
        in_specs=[any_place] * len(made),
        out_specs=[any_place] * len(made_shapes),
        scratch_shapes=[
            pltpu.VMEM((SHARE, 256), F32),
            pltpu.VMEM((8, CH + 256), F32),
            *(pltpu.VMEM(s.shape, s.dtype) for s in made_shapes),
            pltpu.SemaphoreType.DMA((len(made) + len(made_shapes),)),
        ],
        compiler_params=pltpu.CompilerParams(vmem_limit_bytes=VMEM_BYTES),
        name="finish",
    )(*made)
    return (*results[:5], results[5].T, *results[6:14], results[14].T)


VMEM_BYTES = 65_400_000


def fits(mesh, args):
    return mesh.shape["dp"] == PEERS and mesh.shape["tensor"] == 2 and args[0].shape == (PEERS * ROWS, FULL)


def solution(mesh):
    in_specs = (
        P("dp", "tensor"),
        P("dp", "tensor"),
        P("dp", None),
        P("dp"),
        P(),
        P(None, None, "tensor"),
        P(),
        P(None, "tensor"),
        P(None, "tensor"),
        P("tensor"),
        P(),
        P(),
        P("tensor"),
        P("tensor"),
        P("tensor"),
        P("tensor"),
        P("tensor", None),
    )
    out_specs = (
        P("dp", "tensor"),
        P("dp", "tensor"),
        P("tensor"),
        P("dp", None, "tensor"),
        P("dp", "tensor"),
        P("dp", "tensor"),
        P(None, "tensor"),
        P("tensor"),
        P(),
        P(),
        P("tensor"),
        P("tensor"),
        P("tensor"),
        P("tensor"),
        P("tensor", "dp"),
    )

    def whole(*args):
        local = one_kernel if fits(mesh, args) else shards
        mapped = jax.shard_map(
            local, mesh=mesh, in_specs=in_specs, out_specs=out_specs, check_vma=False
        )
        return mapped(*args)

    return whole
```

```python
from functools import partial
from types import SimpleNamespace

import jax
import jax.numpy as jnp
from jax import lax
from jax.experimental import pallas as pl
from jax.experimental.pallas import tpu as pltpu
from jax.sharding import PartitionSpec as P

D = 1536
GROUP = 256
INNER = 3072


norm_eps = 1e-05


def segment_ids(lengths, row_count):
    index = jnp.arange(lengths.shape[0])
    ends = jnp.sum(jnp.where(index[None, :] <= index[:, None], lengths[None, :], 0), axis=1)
    position = jnp.arange(row_count, dtype=jnp.int32)
    return jnp.sum((position[:, None] >= ends[None, :]).astype(jnp.int32), axis=1, dtype=jnp.int32)


def causal_conv(signal, kernel, kernel_bias, segment):
    width = kernel.shape[0]
    total = kernel_bias[None, :] + kernel[width - 1][None, :] * signal
    for offset in range(1, width):
        moved = jnp.concatenate(
            [jnp.zeros((offset, signal.shape[1]), signal.dtype), signal[:-offset]], axis=0
        )
        earlier = jnp.concatenate([jnp.full((offset,), -1, jnp.int32), segment[:-offset]])
        inside = (earlier == segment).astype(signal.dtype)
        total = total + kernel[width - 1 - offset][None, :] * moved * inside[:, None]
    return total


def state_space(xval, b_rows, c_rows, step, decay, segment):
    highest = lax.Precision.HIGHEST
    blocks = xval.shape[0] // GROUP
    head_count = xval.shape[1]
    x_block = xval.reshape(blocks, GROUP, head_count, xval.shape[2])
    b_block = b_rows.reshape(blocks, GROUP, b_rows.shape[1])
    c_block = c_rows.reshape(blocks, GROUP, c_rows.shape[1])
    step_block = step.reshape(blocks, GROUP, head_count).transpose(0, 2, 1)
    rate_block = step_block * decay[None, :, None]
    seg_block = segment.reshape(blocks, GROUP)
    before = jnp.concatenate([jnp.full((1,), -1, jnp.int32), segment[:-1]]).reshape(blocks, GROUP)[
        :, 0
    ]
    lower_mask = jnp.tril(jnp.ones((GROUP, GROUP), dtype=bool))
    cumulative = jnp.einsum("chj,ij->chi", rate_block, lower_mask.astype(jnp.float32), precision=highest)
    linked = (seg_block[:, :, None] == seg_block[:, None, :]) & lower_mask[None]
    spread = cumulative[:, :, :, None] - cumulative[:, :, None, :]
    weight = jnp.exp(jnp.where(linked[:, None], spread, -10000.0))
    scores = jnp.einsum("cin,cjn->cij", c_block, b_block, precision=highest)
    mixing = weight * scores[:, None] * step_block[:, :, None, :]
    inside_out = jnp.einsum("chij,cjhp->cihp", mixing, x_block, precision=highest)
    final_cum = cumulative[:, :, -1]
    last_same = (seg_block == seg_block[:, -1:]).astype(jnp.float32)
    tail_weight = jnp.exp(final_cum[:, :, None] - cumulative) * last_same[:, None, :] * step_block
    fresh_state = jnp.einsum("chj,cjhp,cjn->chpn", tail_weight, x_block, b_block, precision=highest)
    carried = jnp.zeros(fresh_state.shape[1:], jnp.float32)
    entering = []
    entering.append(carried)
    entering = jnp.stack(entering)
    first_same = (seg_block == before[:, None]).astype(jnp.float32)
    head_decay = jnp.exp(cumulative) * first_same[:, None, :]
    carried_out = jnp.einsum("chi,cin,chpn->cihp", head_decay, c_block, entering, precision=highest)
    return (inside_out + carried_out).reshape(xval.shape)


def pre_norm(stream, gain):
    return stream * lax.rsqrt(jnp.mean(stream * stream, axis=1, keepdims=True) + norm_eps) * gain


def conv_piece(value_pre, state_pre, conv_x, conv_x_bias, conv_bc, conv_bc_bias, segment):
    value_conv = jax.nn.silu(causal_conv(value_pre, conv_x, conv_x_bias, segment))
    state_conv = jax.nn.silu(causal_conv(state_pre, conv_bc, conv_bc_bias, segment))
    return (value_conv, state_conv)


def mixer_piece(value_conv, state_conv, step_pre, step_bias, a_log, skip, segment):
    head_count = step_bias.shape[0]
    row_count = value_conv.shape[0]
    heads_in = value_conv.reshape(row_count, head_count, value_conv.shape[1] // head_count)
    step = jax.nn.softplus(step_pre + step_bias)
    decay = -jnp.exp(a_log)
    half_state = state_conv.shape[1] // 2
    mixed = state_space(
        heads_in, state_conv[:, :half_state], state_conv[:, half_state:], step, decay, segment
    )
    return (mixed + skip[None, :, None] * heads_in).reshape(row_count, value_conv.shape[1])


def rounded(values):
    return lax.optimization_barrier(values.astype(jnp.bfloat16)).astype(jnp.float32)


def shards(
    hidden_in,
    out_grad,
    seq_lengths,
    deal_to,
    pre_gain,
    w_in,
    w_state,
    w_step,
    conv_x,
    conv_x_bias,
    conv_bc,
    conv_bc_bias,
    step_bias,
    a_log,
    skip,
    norm_gain,
    w_out,
):
    dp_count = lax.axis_size("dp")
    row_count = hidden_in.shape[0]
    per_peer = row_count // dp_count
    feat_half = hidden_in.shape[1]
    tensor_index = lax.axis_index("tensor")
    send_order = jnp.argsort(deal_to)
    back_order = jnp.argsort(send_order)
    sent_in = hidden_in[send_order].reshape(dp_count, per_peer, feat_half)
    sent_grad = out_grad[send_order].reshape(dp_count, per_peer, feat_half)
    got_in, got_grad = (
        lax.all_to_all(sent_in, "dp", split_axis=0, concat_axis=0, tiled=True),
        lax.all_to_all(sent_grad, "dp", split_axis=0, concat_axis=0, tiled=True),
    )
    got_ids = lax.all_to_all(
        deal_to[send_order].reshape(dp_count, per_peer),
        "dp",
        split_axis=0,
        concat_axis=0,
        tiled=True,
    )
    dealt_slot = got_ids.reshape(row_count) % row_count
    settle_order = jnp.argsort(dealt_slot)
    dealt_half = got_in.reshape(row_count, feat_half)[settle_order]
    grad_half = got_grad.reshape(row_count, feat_half)[settle_order]
    full_in, grad_full = (
        lax.all_gather(dealt_half, "tensor", axis=1, tiled=True),
        lax.all_gather(grad_half, "tensor", axis=1, tiled=True),
    )
    segment = segment_ids(seq_lengths[0], row_count)
    stream = full_in.astype(jnp.float32)
    normed_f, norm_pull = jax.vjp(pre_norm, stream, pre_gain.astype(jnp.float32))
    normed = normed_f.astype(jnp.bfloat16)
    inner_half = w_in.shape[2]
    w_pair = w_in.reshape(w_in.shape[0], 2 * inner_half)
    proj_pair = jnp.dot(normed, w_pair, preferred_element_type=jnp.float32)
    gate_pre = proj_pair[:, :inner_half]
    value_pre = proj_pair[:, inner_half:]
    state_pre = jnp.dot(normed, w_state, preferred_element_type=jnp.float32)
    step_pre = jnp.dot(normed, w_step, preferred_element_type=jnp.float32)
    conv_args = (
        value_pre,
        state_pre,
        conv_x.astype(jnp.float32),
        conv_x_bias.astype(jnp.float32),
        conv_bc.astype(jnp.float32),
        conv_bc_bias.astype(jnp.float32),
    )
    (value_conv_f, state_conv_f), conv_pull = jax.vjp(
        partial(conv_piece, segment=segment), *conv_args
    )
    value_conv = rounded(value_conv_f)
    state_conv = rounded(state_conv_f)
    mixed, mixer_pull = jax.vjp(
        partial(mixer_piece, segment=segment),
        value_conv,
        state_conv,
        step_pre,
        step_bias,
        a_log,
        skip,
    )
    silu_gate = jax.nn.silu(gate_pre)
    gated = mixed * silu_gate
    total_squares = lax.psum(jnp.sum(gated * gated, axis=1), "tensor")
    inverse = lax.rsqrt(total_squares / INNER + norm_eps)
    gain_f = norm_gain.astype(jnp.float32)
    scaled = (gated * inverse[:, None] * gain_f).astype(jnp.bfloat16)
    partial_out = jnp.dot(scaled, w_out, preferred_element_type=jnp.float32)
    branch = lax.psum_scatter(partial_out, "tensor", scatter_dimension=1, tiled=True)
    result = (dealt_half.astype(jnp.float32) + branch).astype(jnp.bfloat16)
    back_out = lax.all_to_all(
        result[dealt_slot].reshape(dp_count, per_peer, feat_half),
        "dp",
        split_axis=0,
        concat_axis=0,
        tiled=True,
    )
    output = back_out.reshape(row_count, feat_half)[back_order]
    g_w_out = jnp.einsum("ti,td->id", scaled, grad_full, preferred_element_type=jnp.float32)
    d_scaled = jnp.einsum("td,id->ti", grad_full, w_out, preferred_element_type=jnp.float32)
    weighted = d_scaled * gain_f
    g_norm_gain = jnp.sum(d_scaled * gated * inverse[:, None], axis=0)
    cross_sum = lax.psum(jnp.sum(weighted * gated, axis=1), "tensor")
    d_gated = (
        inverse[:, None] * weighted
        - gated * (inverse * inverse * inverse / INNER * cross_sum)[:, None]
    )
    d_mixed = d_gated * silu_gate
    sigmoid_gate = jax.nn.sigmoid(gate_pre)
    d_gate = d_gated * mixed * (sigmoid_gate * (1.0 + gate_pre * (1.0 - sigmoid_gate)))
    d_value_conv, d_state_part, d_step_pre, g_step_bias, g_a_log, g_skip = mixer_pull(d_mixed)
    d_state_conv = lax.psum(d_state_part, "tensor")
    d_value_pre, d_state_pre, g_conv_x, g_conv_x_bias, g_conv_bc, g_conv_bc_bias = conv_pull(
        (d_value_conv, d_state_conv)
    )
    d_pair = jnp.concatenate([d_gate, d_value_pre], axis=1).astype(jnp.bfloat16)
    d_state_low = d_state_pre.astype(jnp.bfloat16)
    d_step_low = d_step_pre.astype(jnp.bfloat16)
    state_share = w_state.shape[1] // lax.axis_size("tensor")
    own_state = lax.dynamic_slice_in_dim(d_state_low, tensor_index * state_share, state_share, 1)
    own_weight = lax.dynamic_slice_in_dim(w_state, tensor_index * state_share, state_share, 1)
    g_w_in = jnp.einsum("td,tc->dc", normed, d_pair, preferred_element_type=jnp.float32).reshape(
        w_in.shape
    )
    g_w_state = jnp.einsum("td,tc->dc", normed, own_state, preferred_element_type=jnp.float32)
    g_w_step = jnp.einsum("td,th->dh", normed, d_step_low, preferred_element_type=jnp.float32)
    d_normed = jnp.einsum("tc,dc->td", d_pair, w_pair, preferred_element_type=jnp.float32)
    d_normed = d_normed + jnp.einsum(
        "th,dh->td", d_step_low, w_step, preferred_element_type=jnp.float32
    )
    d_normed = d_normed + jnp.einsum(
        "tc,dc->td", own_state, own_weight, preferred_element_type=jnp.float32
    )
    normed_share = lax.psum_scatter(d_normed, "tensor", scatter_dimension=1, tiled=True)
    row_scale = lax.rsqrt(jnp.mean(stream * stream, axis=1) + norm_eps)
    stream_share = dealt_half.astype(jnp.float32)
    gain_share = lax.dynamic_slice_in_dim(
        pre_gain.astype(jnp.float32), tensor_index * feat_half, feat_half, 0
    )
    row_cross = lax.psum(jnp.sum(gain_share * normed_share * stream_share, axis=1), "tensor")
    d_share = (
        row_scale[:, None] * gain_share * normed_share
        - stream_share * (row_scale * row_scale * row_scale / D * row_cross)[:, None]
    )
    g_pre_gain = jnp.sum(normed_share * stream_share * row_scale[:, None], axis=0)
    d_input = (d_share + grad_half.astype(jnp.float32)).astype(jnp.bfloat16)
    back_grad = lax.all_to_all(
        d_input[dealt_slot].reshape(dp_count, per_peer, feat_half),
        "dp",
        split_axis=0,
        concat_axis=0,
        tiled=True,
    )
    hidden_grad = back_grad.reshape(row_count, feat_half)[back_order]
    small = lax.psum(
        (
            g_pre_gain,
            g_conv_x,
            g_conv_x_bias,
            g_conv_bc,
            g_conv_bc_bias,
            g_step_bias,
            g_a_log,
            g_skip,
            g_norm_gain,
        ),
        "dp",
    )
    g_in_part, g_state_part, g_step_part, g_w_out_part = (
        lax.psum_scatter(g_w_in, "dp", scatter_dimension=0, tiled=True),
        lax.psum_scatter(g_w_state, "dp", scatter_dimension=0, tiled=True),
        lax.psum_scatter(g_w_step, "dp", scatter_dimension=0, tiled=True),
        lax.psum_scatter(g_w_out, "dp", scatter_dimension=1, tiled=True),
    )
    return (
        output,
        hidden_grad,
        small[0],
        g_in_part,
        g_state_part,
        g_step_part,
        small[1],
        small[2],
        small[3],
        small[4],
        small[5],
        small[6],
        small[7],
        small[8],
        g_w_out_part,
    )


F32, BF16, I32 = jnp.float32, jnp.bfloat16, jnp.int32
MESH = pl.DeviceIdType.MESH
LOG2E = 1.4426950408889634
HIGHEST = lax.Precision.HIGHEST

ROWS = 256
FULL = 1536
HALF = 768
CH = 1536
HEADS = 24
PEERS = 16
PER = ROWS // PEERS
SHARE = FULL // PEERS

X_BIAS, NORM_GAIN, PRE_GAIN, BC_BIAS, STEP_BIAS, A_LOG = (slice(n, n + 1) for n in range(4, 10))

UNITS = (
    ("gate", 0, 256, "z"),
    ("gate", 256, 256, "g"),
    ("gate", 512, 256, "g"),
    ("gate", 768, 256, "g"),
    ("gate", 1024, 512, "g"),
    ("out", 0, 512, "g"),
    ("out", 512, 512, "g"),
    ("out", 1024, 512, "g"),
    ("value", 0, 512, "g"),
    ("value", 512, 512, "g"),
    ("value", 1024, 512, "g"),
    ("misc", 0, 256, "g"),
)


def dot_t(a, b):
    return lax.dot_general(a, b, (((1,), (1,)), ((), ())), preferred_element_type=F32)


def dot(a, b):
    return jnp.dot(a, b, preferred_element_type=F32)


def sigmoid(v):
    return 1.0 / (1.0 + jnp.exp(-v))


def block_at(n, width):
    return pl.ds(pl.multiple_of(n * width, width), width)


class Sent:
    def __init__(self, copy):
        self.copy, self.gone, self.here = copy, False, False

    def wait_recv(self):
        self.copy.wait_recv()
        self.here = True

    def wait_send(self):
        if not self.gone:
            self.copy.wait_send()
        self.gone = True


def await_bytes(sem, ref):
    pltpu.make_async_copy(ref, ref, sem).wait()


def block_body(room, *refs):
    left = list(refs)

    def take(shape):
        return [left.pop(0) for _ in shape] if isinstance(shape, list) else left.pop(0)

    r = SimpleNamespace(**{name: take(shape) for name, shape in room.items()})
    lens, deal_ref, vec = r.lens, r.deal, r.vec
    wst, wsp = r.wst, r.wsp
    ss, rs, ls = r.ss, r.rs, r.ls
    me, side = lax.axis_index("dp"), lax.axis_index("tensor")
    core = lax.rem(me, 2)
    xpos = lax.rem(me // 2, 2)
    zpos = me // 4
    sibling = (zpos * 4 + xpos * 2 + (1 - core), side)
    across = (zpos * 4 + (1 - xpos) * 2 + core, side)
    z_side = zpos // 2
    z_outer, z_inner = 3 * z_side, 1 + z_side
    far_outer, far_inner = 3 - z_outer, 3 - z_inner
    is_outer = zpos == z_outer
    is_inner = zpos == z_inner

    def at_z(z):
        return (z * 4 + xpos * 2 + core, side)

    near = at_z(z_outer + z_inner - zpos)
    facing = at_z(3 - zpos)
    other = (me, 1 - side)
    own_cols = pl.ds(pl.multiple_of(side * HALF, HALF), HALF)
    other_cols = pl.ds(pl.multiple_of((1 - side) * HALF, HALF), HALF)

    started, taken, leaving = [], ({}, {}), []

    def semaphore(sems, key):
        count = taken[sems is rs]
        return sems.at[count.setdefault(("own", len(count)) if key is None else key, len(count))]

    def group(key, ref):
        leaving.append((semaphore(ss, key), ref))
        return key

    def send(src, dst, device, by=None, gone=None, came=None):
        copy = pltpu.make_async_remote_copy(
            src_ref=src,
            dst_ref=dst,
            send_sem=semaphore(ss, gone),
            recv_sem=semaphore(rs, came),
            device_id=device,
            device_id_type=MESH,
        )
        if by is None:
            copy.start()
        else:
            pl.when(by)(copy.start)
        one = Sent(copy)
        if gone is None:
            started.append(one)
        return one

    def load(src, dst, n):
        copy = pltpu.make_async_copy(src, dst, ls.at[n])
        copy.start()
        return copy

    def pair_load(n, at):
        cols = pl.ds(pl.multiple_of(n * 128, 128), 128)
        return pltpu.make_async_copy(r.w_in.at[:, :, cols], r.pair.at[at], ls.at[at])

    hid_load = load(r.hid, r.half_in, 3)
    pair_load(0, 0).start()
    pair_load(1, 1).start()
    pair_load(2, 2).start()
    ogr_load = load(r.ogr, r.dhalf_in, 4)
    small_loads = [load(src, dst, 5 + n) for n, (src, dst) in enumerate(zip(r.params, r.params_v))]
    wst_load = load(r.wst_hbm, r.wst, 14)
    wo_load = load(r.wo_hbm, r.wo, 15)

    barrier = pltpu.get_barrier_semaphore()
    for k in range(1, PEERS):
        pl.semaphore_signal(
            barrier, inc=1, device_id=(lax.rem(me + k, PEERS), side), device_id_type=MESH
        )
    pl.semaphore_signal(barrier, inc=1, device_id=other, device_id_type=MESH)

    i0 = lax.broadcasted_iota(I32, (ROWS, ROWS), 0)
    i1 = lax.broadcasted_iota(I32, (ROWS, ROWS), 1)
    deal = deal_ref[...]
    dest = lax.shift_right_logical(deal, 8)
    slot = jnp.bitwise_and(deal, ROWS - 1)
    member = (dest == lax.broadcasted_iota(I32, (PEERS, ROWS), 0)).astype(F32)
    before = dot(member.astype(BF16), (i0 < i1).astype(F32).astype(BF16))
    rank = jnp.sum(member * before, axis=0, keepdims=True)
    place = dest.astype(F32) * PER + rank
    hit = i0.astype(F32) == place
    to_send = hit.astype(F32)
    send_hot = to_send.astype(BF16)
    ident = jnp.sum(to_send * slot.astype(F32), axis=1, keepdims=True)
    sb_h, sb_g, rb_h, rb_g, yb_h, yb_g = r.sb_h, r.sb_g, r.rb_h, r.rb_g, r.yb_h, r.yb_g
    hid_load.wait()
    sb_h[...] = dot(send_hot, r.half_in[...]).astype(BF16)
    row_w = lax.broadcasted_iota(I32, (ROWS, 128), 0)
    lane_w = lax.broadcasted_iota(I32, (ROWS, 128), 1)
    in_place = lax.rem(row_w, PER) == lane_w
    spread = jnp.where(in_place, ident, 0.0).astype(BF16)
    row_n = lax.broadcasted_iota(I32, (PEERS, ROWS), 0)
    lane_n = lax.broadcasted_iota(I32, (PEERS, ROWS), 1)
    gather_ids = (row_n == lane_n // PER).astype(F32).astype(BF16)
    r.sb_i[...] = dot(gather_ids, spread).reshape(PEERS, 1, 128)

    pl.semaphore_wait(barrier, PEERS)

    def rows_of(device):
        return pl.ds(pl.multiple_of(device * PER, PER), PER)

    line = (zpos, z_outer + z_inner - zpos, lax.rem(zpos + 2, 4), 3 - zpos)

    def away(dz, dx, dc):
        return line[dz] * 4 + lax.rem(xpos + dx, 2) * 2 + lax.rem(core + dc, 2)

    steps = [(dz, dx, dc) for dz in (2, 3, 1, 0) for dx in (0, 1) for dc in (0, 1)]

    def deal(dz, src, dst, gone, came, rows=rows_of):
        for step in steps:
            if step[0] == dz and step != (0, 0, 0):
                to = away(*step)
                send(src.at[rows(to)], dst.at[rows(me)], (to, side), gone=gone, came=came)

    def pass_group(name, dz, buf, dst):
        if dz < 2:
            count = 4 * PER - (PER if dz == 0 else 0)
            await_bytes(semaphore(rs, (name, dz)), buf.at[pl.ds(0, count)])
        for step in steps:
            if step[0] == dz:
                if dz >= 2:
                    await_bytes(semaphore(rs, (name, step)), buf.at[pl.ds(0, PER)])
                origin = rows_of(away(*step))
                send(buf.at[origin], dst.at[origin], other, gone=(name, 9), came=(name, 9))

    def wave(name, dz, src, dst):
        for step in steps:
            if step[0] == dz:
                to = away(*step)
                send(src.at[rows_of(to)], dst.at[rows_of(me)], (to, side), gone=(name, "wave", dz), came=(name, step))

    def wave_gone(name, dz, src):
        await_bytes(semaphore(ss, (name, "wave", dz)), src.at[pl.ds(0, 4 * PER)])

    def rest(name, src, dst):
        for dz in (1, 0):
            deal(dz, src, dst, name, (name, dz))
        group(name, src.at[pl.ds(0, 7 * PER)])

    def same(device):
        return device

    for dz in (2, 3, 1, 0):
        deal(dz, r.sb_i, r.rb_i, "ids", "ids", same)
    group("ids", r.sb_i.at[pl.ds(0, PEERS - 1)])
    wave("hid", 3, sb_h, rb_h)
    rest("hid", sb_h, rb_h)
    r.rb_i[me] = r.sb_i[me]
    rb_h[rows_of(me)] = sb_h[rows_of(me)]
    ogr_load.wait()
    sb_g[...] = dot(send_hot, r.dhalf_in[...]).astype(BF16)
    rb_g[rows_of(me)] = sb_g[rows_of(me)]
    r.send_hot_t[...] = to_send.T.astype(BF16)

    ends, total = [], 0
    for k in range(8):
        total = total + lens[0, k]
        ends.append(total)

    def seg_at(pos):
        out = jnp.zeros(pos.shape, I32)
        for e in ends:
            out = out + (pos >= e).astype(I32)
        return out

    row_col = lax.broadcasted_iota(I32, (ROWS, 128), 0)
    seg_here = seg_at(row_col)
    for o in range(1, 4):
        same = (seg_at(row_col - o) == seg_here) & (row_col >= o)
        r.masks[o - 1] = same.astype(F32)
    same = seg_at(i0) == seg_at(i1)
    r.linked[...] = (same & (i0 >= i1)).astype(F32)
    r.linked_t[...] = (same & (i0 <= i1)).astype(F32)
    r.small[...] = jnp.zeros((8, CH + 256), F32)
    for copy in small_loads:
        copy.wait()
    conv_x_v, conv_bc_v, w_step_v, *rows_v = r.params_v
    vec[...] = jnp.zeros((16, CH), F32)
    vec[0:4, :] = conv_x_v[...].astype(F32)
    for n, ref in enumerate(rows_v):
        vec[4 + n, 0 : ref.shape[0]] = ref[...].astype(F32)
    vec[12:16, 0:256] = conv_bc_v[...].astype(F32)
    wst_load.wait()
    wsp[...] = jnp.concatenate(
        [w_step_v[...].astype(F32), jnp.zeros((128 - HEADS, FULL), F32)], axis=0
    ).astype(BF16)
    r.dst_acc[...] = jnp.zeros((ROWS, ROWS), F32)
    r.dcol[...] = jnp.zeros((ROWS, 128), F32)
    r.dsd[...] = jnp.zeros((ROWS, 128), F32)

    picked = jnp.where(i0 < 128, 2 * i0, 2 * i0 - 255)
    apart = (picked == i1).astype(F32).astype(BF16)

    def take_apart(n):
        at = lax.rem(n, 3)
        pair_load(n, at).wait()
        cols = block_at(n, 128)
        flat = r.pair.at[at].reshape(2 * FULL, 128)
        for k in range(12):
            both = dot(apart, flat[k * 256 : (k + 1) * 256, :]).astype(BF16)
            r.wg[k * 128 : (k + 1) * 128, cols] = both[0:128]
            r.wv[k * 128 : (k + 1) * 128, cols] = both[128:256]

        @pl.when(n + 3 < 12)
        def _():
            pair_load(n + 3, at).start()

    group(("hid", 9), rb_h)
    group(("grad", 9), rb_g)
    pl.loop(0, 4)(take_apart)
    pass_group("hid", 0, rb_h, yb_h)
    wave_gone("hid", 3, sb_h)
    wave("hid", 2, sb_h, rb_h)
    pl.loop(4, 7)(take_apart)
    pass_group("hid", 1, rb_h, yb_h)
    pl.loop(7, 12)(take_apart)
    pass_group("hid", 3, rb_h, yb_h)
    await_bytes(semaphore(rs, "ids"), r.rb_i.at[pl.ds(0, PEERS - 1)])
    origin_row = lax.broadcasted_iota(I32, (ROWS, PEERS), 0) // PER
    fetch_ids = (origin_row == lax.broadcasted_iota(I32, (ROWS, PEERS), 1)).astype(F32).astype(BF16)
    ids = jnp.where(in_place, dot(fetch_ids, r.rb_i[...].reshape(PEERS, 128).astype(BF16)), 0.0)
    ids = jnp.broadcast_to(jnp.sum(ids, axis=1, keepdims=True), (ROWS, 128))
    r.hot_t[...] = (ids[:, 0:1] == i1.astype(F32)).astype(F32).astype(BF16)
    r.hot[...] = (ids.T[0:1, :] == i0.astype(F32)).astype(F32).astype(BF16)
    wave_gone("hid", 2, sb_h)
    wave("grad", 3, sb_g, rb_g)
    pass_group("hid", 2, rb_h, yb_h)
    rest("grad", sb_g, rb_g)
    stream, upstream, normed = r.stream, r.upstream, r.normed
    stream[:, own_cols] = dot(r.hot[...], rb_h[...]).astype(BF16)
    await_bytes(semaphore(rs, ("hid", 9)), yb_h)
    stream[:, other_cols] = dot(r.hot[...], yb_h[...]).astype(BF16)

    @pl.loop(0, 8)
    def _(n):
        rows = block_at(n, 32)
        s = stream[rows, :].astype(F32)
        scale = lax.rsqrt(jnp.sum(s * s, axis=1, keepdims=True) * (1.0 / FULL) + norm_eps)
        r.nscale[rows, :] = jnp.broadcast_to(scale, (32, 128))
        normed[rows, :] = (s * scale * vec[PRE_GAIN, :]).astype(BF16)

    here, beside, over, cross_over = (pl.ds(n * ROWS, ROWS) for n in range(4))
    diagonal = (zpos * 4 + (1 - xpos) * 2 + (1 - core), side)

    def flip(source, flipped, keep):
        for n in range(4):
            turned = source[:, n * 384 : (n + 1) * 384].astype(F32).T.astype(BF16)
            for i in range(4):
                flipped[n, i] = turned[i * SHARE : (i + 1) * SHARE]
        keep[:, :, here] = flipped[:, xpos * 2 + core]

    def share_early(flipped, keep):
        keep[:, :, here] = flipped[:, (1 - xpos) * 2 + core]
        send(flipped.at[:, (1 - xpos) * 2 + (1 - core)], keep.at[:, :, beside], sibling, gone="early", came="early")
        group("early", keep.at[:, :, beside])

    others, overs = pl.ds(ROWS, 3 * ROWS), pl.ds(2 * ROWS, 2 * ROWS)

    def share_flipped(name, flipped, keep, near_by):
        group(name, keep.at[:, :, others])
        for dx, dc, lanes, device in ((0, 1, beside, sibling), (1, 0, over, across), (1, 1, cross_over, diagonal)):
            place = lax.rem(xpos + dx, 2) * 2 + lax.rem(core + dc, 2)
            came = near_by if lanes is beside else name
            send(flipped.at[:, place], keep.at[:, :, lanes], device, gone=name, came=came)

    masks = r.masks

    def conv_at(signal, taps, bias):
        out = bias + taps[3] * signal
        for o in range(1, 4):
            out = out + taps[3 - o] * (pltpu.roll(signal, o, 0) * masks[o - 1])
        return out

    def conv_back(signal, taps, bias, grad):
        pre = conv_at(signal, taps, bias)
        s = sigmoid(pre)
        d_pre = grad * (s * (1.0 + pre * (1.0 - s)))
        sums = [None] * 4
        sums[3] = jnp.sum(d_pre * signal, axis=0, keepdims=True)
        d_signal = taps[3] * d_pre
        for o in range(1, 4):
            masked = d_pre * masks[o - 1]
            sums[3 - o] = jnp.sum(masked * pltpu.roll(signal, o, 0), axis=0, keepdims=True)
            d_signal = d_signal + taps[3 - o] * pltpu.roll(masked, ROWS - o, 0)
        return d_signal, sums, jnp.sum(d_pre, axis=0, keepdims=True)

    def taps_at(first, cols):
        return [vec[pl.ds(first + k, 1), cols] for k in range(4)]

    gate_pre, value_pre, vconv = r.gate_pre, r.value_pre, r.vconv
    def project(n):
        cols = block_at(n, 256)
        gate_pre[:, cols] = dot(normed[...], r.wg[:, cols])
        value_pre[:, cols] = dot(normed[...], r.wv[:, cols])

    def convolve(n):
        cols = block_at(n, 128)
        pre = conv_at(value_pre[:, cols], taps_at(0, cols), vec[X_BIAS, cols])
        vconv[:, cols] = (pre * sigmoid(pre)).astype(BF16)

    wave_gone("grad", 3, sb_g)
    wave("grad", 2, sb_g, rb_g)
    pl.loop(0, 6, unroll=3)(project)
    pass_group("grad", 0, rb_g, yb_g)
    pass_group("grad", 1, rb_g, yb_g)
    pl.loop(0, 12)(convolve)
    pass_group("grad", 3, rb_g, yb_g)

    state_pre, sconv = r.state_pre, r.sconv
    state_pre[...] = dot(normed[...], wst[...])
    for n in range(2):
        cols = pl.ds(n * 128, 128)
        pre = conv_at(state_pre[:, cols], taps_at(12, cols), vec[BC_BIAS, cols])
        sconv[:, cols] = (pre * sigmoid(pre)).astype(BF16)

    step_in = dot_t(normed[...], wsp[...]) + vec[STEP_BIAS, 0:128]
    small_e = jnp.exp(-jnp.abs(step_in))
    series = small_e * (1.0 - small_e * (0.5 - small_e * (1.0 / 3.0 - 0.25 * small_e)))
    step = jnp.maximum(step_in, 0.0) + jnp.where(small_e < 0.01, series, jnp.log(1.0 + small_e))
    decay = -jnp.exp(vec[A_LOG, 0:128])
    r.step_in[...] = step_in
    r.step[...] = step
    lower = (i0 >= i1).astype(F32)
    cum2 = jnp.dot(lower, step * decay, precision=HIGHEST, preferred_element_type=F32) * LOG2E
    r.cum2[...] = cum2
    r.cum2_t[...] = cum2.T
    r.cum2_ls[...] = (cum2 - jnp.log(step) * LOG2E).T
    b_rows, c_rows = sconv[:, 0:128], sconv[:, 128:256]
    r.scores[...] = dot_t(c_rows, b_rows) * r.linked[...]
    r.scores_t[...] = dot_t(b_rows, c_rows) * r.linked_t[...]

    lane = lax.broadcasted_iota(I32, (ROWS, 128), 1)
    lane_half = lax.broadcasted_iota(I32, (128, 128), 1) < 64

    def column(ref, h):
        return jnp.sum(jnp.where(lane == h, ref[...], 0.0), axis=1, keepdims=True)


    mixed = r.mixed

    def mix(p):
        cols = block_at(p, 128)
        x = vconv[:, cols]
        tops, lows = [], []
        for a in range(2):
            h = 2 * p + a
            cc = column(r.cum2, h)
            cr = r.cum2_ls[pl.ds(h, 1), :]
            w = jnp.exp2(jnp.minimum(cc[0:128] - cr[:, 0:128], 100.0)) * r.scores[0:128, 0:128]
            tops.append(dot(w.astype(BF16), x[0:128]))
            w = jnp.exp2(jnp.minimum(cc[128:256] - cr, 100.0)) * r.scores[128:256, :]
            lows.append(dot(w.astype(BF16), x))
        skip = jnp.where(lane_half[0:1], r.skip[2 * p], r.skip[2 * p + 1])
        xf = x.astype(F32)
        mixed[0:128, cols] = jnp.where(lane_half, tops[0], tops[1]) + skip * xf[0:128]
        mixed[128:256, cols] = jnp.where(lane_half, lows[0], lows[1]) + skip * xf[128:256]

    pl.loop(0, 3, unroll=3)(mix)
    pass_group("grad", 2, rb_g, yb_g)
    wave_gone("grad", 2, sb_g)
    pl.loop(3, 12, unroll=3)(mix)
    flip(normed, r.norm_f, r.norm_t)
    share_early(r.norm_f, r.norm_o)
    share_flipped("norm", r.norm_f, r.norm_t, "beside")

    upstream[:, own_cols] = dot(r.hot[...], rb_g[...]).astype(BF16)
    await_bytes(semaphore(rs, ("grad", 9)), yb_g)
    upstream[:, other_cols] = dot(r.hot[...], yb_g[...]).astype(BF16)
    wo_load.wait()
    d_scaled = r.d_scaled
    r.acc1[...] = jnp.zeros((ROWS, 128), F32)
    r.acc2[...] = jnp.zeros((ROWS, 128), F32)

    @pl.loop(0, 6, unroll=6)
    def _(n):
        cols = block_at(n, 256)
        ds = dot_t(upstream[...], r.wo[cols, :])
        d_scaled[:, cols] = ds
        g = gate_pre[:, cols]
        gated = mixed[:, cols] * g * sigmoid(g)
        sq = gated * gated
        cr = vec[NORM_GAIN, cols] * ds * gated
        r.acc1[...] += sq[:, 0:128] + sq[:, 128:256]
        r.acc2[...] += cr[:, 0:128] + cr[:, 128:256]

    def exchange_rows(col_a, col_b, out_buf, in_buf):
        both = jnp.where(lane == 0, col_a, jnp.where(lane == 1, col_b, 0.0))
        out_buf[...] = both.T[0:8, :]
        copy = send(out_buf, in_buf, other)

        def finish():
            copy.wait_recv()
            both = jnp.concatenate([out_buf[...] + in_buf[...], jnp.zeros((120, ROWS), F32)], axis=0)
            return both.T[:, 0:1], both.T[:, 1:2]

        return finish

    row_sums = exchange_rows(
        jnp.sum(r.acc1[...], axis=1, keepdims=True),
        jnp.sum(r.acc2[...], axis=1, keepdims=True),
        r.ex_a,
        r.ex_b,
    )
    r.cum2_ls[...] = jnp.zeros((128, ROWS), F32)
    flip(upstream, r.up_f, r.up_t)
    sum_sq, sum_cross = row_sums()
    inner = 2.0 * CH
    inverse = lax.rsqrt(sum_sq * (1.0 / inner) + norm_eps)
    cross = inverse * inverse * inverse * (1.0 / inner) * sum_cross
    r.acc1[...] = jnp.broadcast_to(inverse, (ROWS, 128))
    r.acc2[...] = jnp.broadcast_to(cross, (ROWS, 128))
    scaled4, gate4, value4, misc4 = r.scaled4, r.gate4, r.value4, r.misc4

    def gated_back(n):
        cols = block_at(n, 128)
        inv, crs = r.acc1[...], r.acc2[...]
        g, m, ds, gain = gate_pre[:, cols], mixed[:, cols], d_scaled[:, cols], vec[NORM_GAIN, cols]
        s = sigmoid(g)
        silu = g * s
        gated = m * silu
        gi = gated * inv
        scaled4[here, cols] = (gi * gain).astype(BF16)
        r.small[5:6, cols] = jnp.sum(ds * gi, axis=0, keepdims=True)
        d_gated = inv * ds * gain - gated * crs
        mixed[:, cols] = d_gated * silu
        gate4[here, cols] = (d_gated * m * (s * (1.0 + g * (1.0 - s)))).astype(BF16)

    def gated_part(first, last):
        pl.loop(first, last)(gated_back)

    half_f, half_o, half_in = d_scaled.at[:, pl.ds(0, HALF)], normed.at[:, pl.ds(0, HALF)], r.half_in
    flying = {}

    def project_other():
        @pl.loop(0, 3)
        def _(n):
            cols = pl.ds(pl.multiple_of((1 - side) * HALF + n * 256, 256), 256)
            half_o[:, block_at(n, 256)] = dot(scaled4[here, :], r.wo[:, cols]).astype(BF16)

        flying["out"] = send(half_o, half_in, other)

    def project_own():
        @pl.loop(0, 3)
        def _(n):
            cols = pl.ds(pl.multiple_of(side * HALF + n * 256, 256), 256)
            half_f[:, block_at(n, 256)] = dot(scaled4[here, :], r.wo[:, cols]) + stream[:, cols].astype(F32)

    lefts = {"out": r.up_t, "gate": r.norm_t, "value": r.norm_t, "misc": r.norm_t}
    rights = {"out": scaled4, "gate": gate4, "value": value4, "misc": misc4}
    outs = {"out": r.o_wo, "gate": r.o_gate, "value": r.o_value, "misc": r.o_misc}
    stores = []

    def store(src, dst, n):
        copy = pltpu.make_async_copy(src, dst, r.os.at[n])
        copy.start()
        return copy

    def ready(copy):
        if not copy.here:
            copy.wait_recv()

    pieces = {}
    for name, ref in rights.items():
        alone = sum(unit[2] for unit in UNITS if unit[0] == name and unit[3] == "z")
        group(name, ref.at[pl.ds(0, 3 * ROWS), pl.ds(0, ref.shape[1] - alone)])

    def up_swap():
        share_flipped("up", r.up_f, r.up_t, "up")

    def swap(name, first, width):
        ref, cols = rights[name], pl.ds(first, width)
        near_by = send(ref.at[here, cols], ref.at[beside, cols], sibling, gone=name)
        far_off = send(ref.at[here, cols], ref.at[over, cols], across, gone=name)
        pieces[name, first] = [width, near_by, far_off]

    def beside_here():
        if "beside" not in flying:
            flying["beside"] = True
            await_bytes(semaphore(rs, "beside"), r.norm_t.at[:, :, beside])

    def swap_near(name, first, width):
        ref, cols = rights[name], pl.ds(first, width)
        pieces[name, first] = [width, send(ref.at[here, cols], ref.at[beside, cols], sibling)]

    def relay(name, first):
        piece = pieces[name, first]
        ref, cols = rights[name], pl.ds(first, piece[0])
        ready(piece[2])
        piece.append(send(ref.at[over, cols], ref.at[cross_over, cols], sibling, gone=name))

    class Unit:
        def __init__(self, n):
            self.name, self.first, self.width, self.kind = UNITS[n]
            self.n, self.part, self.zbuf, self.kept = n, r.part[n], r.zbuf[n], r.kept[n]
            self.key = group(("unit", n), self.zbuf.at[pl.ds(0, 3)])
            self.stages = [self.compute if self.kind == "g" else self.compute_early, self.pass_outer, self.pass_inner, self.send_out, self.finish, self.keep_across]

        def go(self, stage):
            self.stages[stage]()

        def add(self, z, slot):
            self.part[z] = self.part[z] + self.zbuf[slot]

        def hop(self, z, slot, device, by):
            return send(self.part.at[z], self.zbuf.at[slot], device, by, self.key, (self.key, slot))

        def compute(self):
            lhs_ref, rhs_ref = lefts[self.name], rights[self.name]
            first, part = self.first, self.part
            side_name = "up" if self.name == "out" else "norm"
            if side_name == "norm":
                beside_here()
            if side_name not in flying:
                flying[side_name] = True
                await_bytes(semaphore(rs, side_name), lhs_ref.at[:, :, others if side_name == "up" else overs])
            for (name, start), piece in pieces.items():
                if name == self.name and start < first + self.width and first < start + piece[0]:
                    for copy in piece[1:]:
                        ready(copy)

            @pl.loop(0, self.width // 256)
            def _(n):
                lhs = lhs_ref[...].reshape(4 * SHARE, 4 * ROWS)
                rhs = rhs_ref[:, pl.ds(pl.multiple_of(first + n * 256, 256), 256)]
                part[:, 0, :, block_at(n, 256)] = dot(lhs, rhs).astype(BF16).reshape(4, SHARE, 256)

            self.leave()

        def compute_early(self):
            for copy in pieces[self.name, self.first][1:]:
                ready(copy)
            await_bytes(semaphore(rs, "early"), r.norm_o.at[:, :, beside])
            beside_here()
            rhs = rights[self.name][0 : 2 * ROWS, self.first : self.first + self.width]
            for n, lhs_ref in enumerate((r.norm_t, r.norm_o)):
                lhs = lhs_ref[:, :, 0 : 2 * ROWS].reshape(4 * SHARE, 2 * ROWS)
                self.part[:, n] = dot(lhs, rhs).astype(BF16).reshape(4, SHARE, self.width)
            self.leave()

        def leave(self):
            self.c3 = self.hop(far_outer, 0, near, is_outer)
            self.c2 = self.hop(far_inner, 1, near, is_outer)
            self.c1 = self.hop(z_inner, 2, near, is_outer)

        def pass_outer(self):
            @pl.when(is_inner)
            def _():
                self.c3.wait_recv()
                self.add(far_outer, 0)

            self.d2 = self.hop(far_outer, 3, facing, is_inner)

        def pass_inner(self):
            @pl.when(is_inner)
            def _():
                self.c2.wait_recv()
                self.add(far_inner, 1)

            self.d1 = self.hop(far_inner, 4, facing, is_inner)

        def send_out(self):
            @pl.when(is_inner)
            def _():
                self.d2.wait_recv()
                self.add(z_outer, 3)

            self.e1 = self.hop(z_outer, 0, near, is_inner)

        def finish(self):
            def end(*slots):
                sums = [self.part[zpos, n].astype(F32) for n in range(self.part.shape[1])]
                for slot in slots:
                    sums = [s + self.zbuf[slot, n].astype(F32) for n, s in enumerate(sums)]
                self.kept[...] = sums[0]
                if self.kind == "z":
                    r.over_out[...] = sums[1].astype(BF16)

            @pl.when(is_outer)
            def _():
                self.e1.wait_recv()
                end(0)

            @pl.when(is_inner)
            def _():
                self.c1.wait_recv()
                self.d1.wait_recv()
                end(2, 4)

            if self.kind == "z":
                self.cx = send(r.over_out, r.over_in, across)
            else:
                self.store()

        def keep_across(self):
            self.cx.wait_recv()
            self.kept[...] = self.kept[...] + r.over_in[...].astype(F32)
            self.store()

        def store(self):
            cols = pl.ds(self.first, self.width)
            stores.append(store(self.kept, outs[self.name].at[:, cols], self.n))

    units = [Unit(n) for n in range(len(UNITS))]
    head_row = lax.broadcasted_iota(I32, (32, ROWS), 0)

    def mixer_back(p):
        cols = block_at(p, 128)
        x = vconv[:, cols]
        xf = x.astype(F32)
        dy = mixed[:, cols]
        dyb = dy.astype(BF16)
        by_channel = jnp.sum(dy * xf, axis=0, keepdims=True)
        skips = r.small[6:7, CH + 128 : CH + 256]
        d_tops, d_lows = [], []
        for a in range(2):
            h = 2 * p + a
            half = (lane < 64) if a == 0 else (lane >= 64)
            of_head = jnp.sum(jnp.where(half[0:1], by_channel, 0.0), axis=1, keepdims=True)
            skips = skips + jnp.where(lane[0:1] == h, of_head, 0.0)
            xa = jnp.where(half, xf, 0.0)
            xab = xa.astype(BF16)
            cc = column(r.cum2, h)
            st = column(r.step, h)
            cr = r.cum2_t[pl.ds(h, 1), :]
            w = jnp.exp2(jnp.minimum(cr - cc[0:128], 0.0))
            sc = r.scores_t[0:128, :]
            v_top = dot((w * sc).astype(BF16), dyb)
            q = dot_t(xab[0:128], dyb) * w * st[0:128]
            r.dst_acc[0:128, :] += q
            g_top = q * sc
            w = jnp.exp2(jnp.minimum(cr[:, 128:256] - cc[128:256], 0.0))
            sc = r.scores_t[128:256, 128:256]
            v_low = dot((w * sc).astype(BF16), dyb[128:256])
            q = dot_t(xab[128:256], dyb[128:256]) * w * st[128:256]
            r.dst_acc[128:256, 128:256] += q
            g_low = q * sc
            top_sums = jnp.sum(g_top, axis=0, keepdims=True)
            low_sums = jnp.sum(g_low, axis=0, keepdims=True)
            col_sums = jnp.concatenate([top_sums[:, 0:128], top_sums[:, 128:256] + low_sums], axis=1)
            r.cum2_ls[0:32, :] += jnp.where(head_row == h, col_sums, 0.0)
            row_sums = jnp.concatenate(
                [
                    jnp.sum(g_top[:, 0:128] + g_top[:, 128:256], axis=1, keepdims=True),
                    jnp.sum(g_low, axis=1, keepdims=True),
                ],
                axis=0,
            )
            direct = jnp.concatenate(
                [
                    jnp.sum(xa[0:128] * v_top, axis=1, keepdims=True),
                    jnp.sum(xa[128:256] * v_low, axis=1, keepdims=True),
                ],
                axis=0,
            )
            r.dcol[...] += jnp.where(lane == h, row_sums, 0.0)
            r.dsd[...] += jnp.where(lane == h, direct, 0.0)
            d_tops.append(st[0:128] * v_top)
            d_lows.append(st[128:256] * v_low)
        r.small[6:7, CH + 128 : CH + 256] = skips
        d_conv = jnp.concatenate(
            [jnp.where(lane_half, d_tops[0], d_tops[1]), jnp.where(lane_half, d_lows[0], d_lows[1])],
            axis=0,
        )
        d_conv = d_conv + jnp.where(lane_half[0:1], r.skip[2 * p], r.skip[2 * p + 1]) * dy
        d_value, sums, bias_sum = conv_back(value_pre[:, cols], taps_at(0, cols), vec[X_BIAS, cols], d_conv)
        value4[here, cols] = d_value.astype(BF16)
        for k in range(4):
            r.small[k : k + 1, cols] = sums[k]
        r.small[4:5, cols] = bias_sum

    def mixer_part(first, last):
        pl.loop(first, last)(mixer_back)

    def send_back(name, src, dst):
        group(name, src.at[pl.ds(0, ROWS - PER)])
        for dz in (2, 3, 1, 0):
            deal(dz, src, dst, name, name)
        dst[rows_of(me)] = src[rows_of(me)]

    def return_out():
        ready(flying["out"])
        result = (half_f[...] + half_in[...].astype(F32)).astype(BF16)
        yb_h[...] = dot(r.hot_t[...], result).astype(BF16)
        send_back("back_o", yb_h, r.back_o)

    def finish_out():
        await_bytes(semaphore(rs, "back_o"), r.back_o.at[pl.ds(0, ROWS - PER)])
        r.res_o[...] = dot(r.send_hot_t[...], r.back_o[...]).astype(BF16)
        stores.append(store(r.res_o, r.o_out, len(UNITS) + 1))

    d_state = r.d_state
    state_own = pl.ds(pl.multiple_of(side * 128, 128), 128)
    state_other = pl.ds(pl.multiple_of((1 - side) * 128, 128), 128)

    def states_back():
        d_scores_t = r.dst_acc[...] * r.linked_t[...]
        d_conv_s = r.linked
        d_conv_s[:, 0:128] = dot(d_scores_t.astype(BF16), c_rows)
        d_conv_s[:, 128:256] = dot(d_scores_t.T.astype(BF16), b_rows)
        for n in range(2):
            cols = pl.ds(n * 128, 128)
            d_pre, sums, bias_sum = conv_back(
                state_pre[:, cols], taps_at(12, cols), vec[BC_BIAS, cols], d_conv_s[:, cols]
            )
            d_state[:, cols] = d_pre
            for k in range(4):
                r.small[k : k + 1, CH + n * 128 : CH + (n + 1) * 128] = sums[k]
            r.small[4:5, CH + n * 128 : CH + (n + 1) * 128] = bias_sum
        r.st_out[...] = d_state[:, state_other].astype(BF16)
        flying["state"] = send(r.st_out, r.st_in, other)
        d_cum = r.cum2_ls[...].T - r.dcol[...]
        upper = (i0 <= i1).astype(F32)
        d_rate = jnp.dot(upper, d_cum, precision=HIGHEST, preferred_element_type=F32)
        d_step = (r.dsd[...] + d_rate * decay) * sigmoid(r.step_in[...])
        r.small[5:6, CH : CH + 128] = jnp.sum(d_step, axis=0, keepdims=True)
        r.small[6:7, CH : CH + 128] = jnp.sum(d_rate * r.step[...], axis=0, keepdims=True) * decay
        misc4[here, 128:256] = d_step.astype(BF16)
        r.acc1[...] = jnp.zeros((ROWS, 128), F32)
        r.st_low[...] = d_state[...].astype(BF16)

    def add_states():
        ready(flying["state"])
        misc4[here, 0:128] = (d_state[:, state_own] + r.st_in[...].astype(F32)).astype(BF16)

    dhalf_f, dhalf_o, dhalf_in = d_scaled.at[:, pl.ds(HALF, HALF)], normed.at[:, pl.ds(HALF, HALF)], r.dhalf_in

    def d_normed_at(first):
        rows = pl.ds(pl.multiple_of(first, 256), 256)
        out = dot_t(gate4[here, :], r.wg[rows, :]) + dot_t(value4[here, :], r.wv[rows, :])
        out = out + dot_t(r.st_low[...], r.wst[rows, :])
        out = out + dot(misc4[here, 128:256], wsp[:, rows])
        part = out * vec[PRE_GAIN, rows] * stream[:, rows].astype(F32)
        r.acc1[...] += part[:, 0:128] + part[:, 128:256]
        return out

    def normed_other():
        @pl.loop(0, 3)
        def _(n):
            dhalf_o[:, block_at(n, 256)] = d_normed_at((1 - side) * HALF + n * 256).astype(BF16)

        flying["norm"] = send(dhalf_o, dhalf_in, other)

    def normed_own():
        @pl.loop(0, 3)
        def _(n):
            dhalf_f[:, block_at(n, 256)] = d_normed_at(side * HALF + n * 256)

        flying["rows"] = exchange_rows(
            jnp.sum(r.acc1[...], axis=1, keepdims=True), jnp.zeros((ROWS, 1), F32), r.ex_c, r.ex_d
        )

    small = r.small

    def return_grad():
        row_cross, _ = flying["rows"]()
        ready(flying["norm"])
        flying["out"].wait_send()
        scale = r.nscale[:, 0:1]
        factor = scale * scale * scale * (1.0 / FULL) * row_cross
        for n in range(6):
            cols = pl.ds(n * 128, 128)
            mine = pl.ds(pl.multiple_of(side * HALF + n * 128, 128), 128)
            dn = dhalf_f[:, cols] + dhalf_in[:, cols].astype(F32)
            s = stream[:, mine].astype(F32)
            small[7:8, n * 128 : (n + 1) * 128] = jnp.sum(dn * s * scale, axis=0, keepdims=True)
            grad = upstream[:, mine].astype(F32) + scale * vec[PRE_GAIN, mine] * dn - s * factor
            half_o[:, cols] = grad.astype(BF16)
        yb_g[...] = dot(r.hot_t[...], half_o[...]).astype(BF16)
        send_back("back_g", yb_g, r.back_g)

    def finish_grad():
        await_bytes(semaphore(rs, "back_g"), r.back_g.at[pl.ds(0, ROWS - PER)])
        r.res_g[...] = dot(r.send_hot_t[...], r.back_g[...]).astype(BF16)
        stores.append(store(r.res_g, r.o_hid, len(UNITS) + 2))

    lasts = pl.ds(CH, 256)

    def small_tensor():
        flying["small"] = send(small.at[:, lasts], r.sm_y, other)

    def small_tensor_end():
        copy = flying["small"]
        copy.wait_send()
        copy.wait_recv()
        keep_rows = lax.broadcasted_iota(I32, (8, 256), 0) < 5
        small[:, lasts] = small[:, lasts] + jnp.where(keep_rows, r.sm_y[...], 0.0)

    partners = [sibling, across, near, facing]

    def small_start(n):
        flying[n] = send(small, r.sm_a[n], partners[n])

    def small_end(n):
        flying[n].wait_send()
        flying[n].wait_recv()
        small[...] = small[...] + r.sm_a[n][...]

    gated_part(0, 2)
    swap_near("gate", 0, 256)
    gated_part(2, 4)
    swap("gate", 256, 256)
    gated_part(4, 8)
    swap("gate", 768, 256)
    swap("gate", 512, 256)
    gated_part(8, 12)
    units[0].go(0)
    mixer_part(0, 6)
    relay("gate", 768)
    relay("gate", 256)
    project_other()
    swap("value", 0, 768)
    units[3].go(0)
    units[1].go(0)
    relay("gate", 512)
    mixer_part(6, 12)
    units[2].go(0)
    swap("value", 768, 768)
    swap("out", 512, 512)
    units[2].go(1)
    units[3].go(1)
    project_own()
    units[0].go(1)
    return_out()
    relay("value", 0)
    units[3].go(2)
    units[3].go(3)
    states_back()
    units[8].go(0)
    add_states()
    up_swap()
    relay("value", 768)
    units[2].go(2)
    normed_other()
    units[10].go(0)
    units[0].go(2)
    swap("out", 1024, 512)
    units[9].go(0)
    swap("gate", 1024, 512)
    normed_own()
    swap("misc", 0, 256)
    units[8].go(1)
    units[8].go(2)
    units[1].go(1)
    units[10].go(1)
    return_grad()
    units[10].go(2)
    finish_out()
    relay("out", 512)
    small_tensor()
    units[6].go(0)
    small_tensor_end()
    relay("out", 1024)
    units[10].go(3)
    small_start(0)
    units[2].go(3)
    units[6].go(1)
    units[6].go(2)
    units[9].go(1)
    units[9].go(2)
    units[1].go(2)
    units[6].go(3)
    swap("out", 0, 512)
    units[0].go(3)
    units[7].go(0)
    relay("misc", 0)
    units[11].go(0)
    small_end(0)
    units[8].go(3)
    units[2].go(4)
    units[9].go(3)
    units[7].go(1)
    relay("gate", 1024)
    units[7].go(2)
    units[11].go(1)
    units[0].go(4)
    finish_grad()
    units[4].go(0)
    units[1].go(3)
    units[10].go(4)
    units[9].go(4)
    relay("out", 0)
    units[8].go(4)
    units[11].go(2)
    units[0].go(5)
    small_start(1)
    units[6].go(4)
    units[4].go(1)
    units[5].go(0)
    units[4].go(2)
    units[11].go(3)
    small_end(1)
    units[11].go(4)
    small_start(2)
    units[4].go(3)
    units[3].go(4)
    units[5].go(1)
    units[7].go(3)
    units[5].go(2)
    units[4].go(4)
    units[5].go(3)
    small_end(2)
    small_start(3)
    units[7].go(4)
    units[1].go(4)
    units[5].go(4)
    small_end(3)
    stores.append(store(small, r.o_small, len(UNITS)))
    for copy in started:
        copy.wait_send()
    for sem, ref in leaving:
        await_bytes(sem, ref)
    for copy in stores:
        copy.wait()


def scratch():
    vmem, dma = pltpu.VMEM, pltpu.SemaphoreType.DMA
    square, wide = (ROWS, ROWS), (ROWS, CH)
    def rows(dtype, width):
        return vmem((ROWS, width), dtype)

    return dict(
        wg=vmem((FULL, CH), BF16),
        wv=vmem((FULL, CH), BF16),
        wo=vmem((CH, FULL), BF16),
        pair=vmem((3, FULL, 2, 128), BF16),
        send_hot_t=vmem(square, BF16),
        hot=vmem(square, BF16),
        hot_t=vmem(square, BF16),
        sb_h=rows(BF16, HALF),
        rb_h=rows(BF16, HALF),
        sb_i=vmem((PEERS, 1, 128), F32),
        rb_i=vmem((PEERS, 1, 128), F32),
        sb_g=rows(BF16, HALF),
        rb_g=rows(BF16, HALF),
        yb_h=rows(BF16, HALF),
        yb_g=rows(BF16, HALF),
        half_in=rows(BF16, HALF),
        dhalf_in=rows(BF16, HALF),
        back_o=rows(BF16, HALF),
        back_g=rows(BF16, HALF),
        masks=vmem((3, ROWS, 128), F32),
        linked=vmem(square, F32),
        linked_t=vmem(square, F32),
        scores=vmem(square, F32),
        scores_t=vmem(square, F32),
        dst_acc=vmem(square, F32),
        small=vmem((8, CH + 256), F32),
        params_v=[
            vmem((4, CH), BF16),
            vmem((4, 256), BF16),
            vmem((HEADS, FULL), BF16),
            vmem((CH,), BF16),
            vmem((CH,), BF16),
            vmem((FULL,), BF16),
            vmem((256,), BF16),
            vmem((HEADS,), F32),
            vmem((HEADS,), F32),
        ],
        res_o=rows(BF16, HALF),
        res_g=rows(BF16, HALF),
        kept=[vmem((SHARE, width), F32) for _, _, width, _ in UNITS],
        vec=vmem((16, CH), F32),
        wsp=vmem((128, FULL), BF16),
        wst=vmem((FULL, 256), BF16),
        cum2_t=vmem((128, ROWS), F32),
        cum2_ls=vmem((128, ROWS), F32),
        stream=vmem(wide, BF16),
        upstream=vmem(wide, BF16),
        normed=vmem(wide, BF16),
        vconv=vmem(wide, BF16),
        gate_pre=vmem(wide, F32),
        value_pre=vmem(wide, F32),
        mixed=vmem(wide, F32),
        d_scaled=vmem(wide, F32),
        state_pre=rows(F32, 256),
        d_state=rows(F32, 256),
        sconv=rows(BF16, 256),
        st_low=rows(BF16, 256),
        st_out=rows(BF16, 128),
        st_in=rows(BF16, 128),
        scaled4=vmem((4 * ROWS, CH), BF16),
        gate4=vmem((4 * ROWS, CH), BF16),
        value4=vmem((4 * ROWS, CH), BF16),
        misc4=vmem((4 * ROWS, 256), BF16),
        norm_t=vmem((4, SHARE, 4 * ROWS), BF16),
        up_t=vmem((4, SHARE, 4 * ROWS), BF16),
        norm_f=vmem((4, 4, SHARE, ROWS), BF16),
        up_f=vmem((4, 4, SHARE, ROWS), BF16),
        nscale=rows(F32, 128),
        acc1=rows(F32, 128),
        acc2=rows(F32, 128),
        dcol=rows(F32, 128),
        dsd=rows(F32, 128),
        step_in=rows(F32, 128),
        step=rows(F32, 128),
        cum2=rows(F32, 128),
        ex_a=vmem((8, ROWS), F32),
        ex_b=vmem((8, ROWS), F32),
        ex_c=vmem((8, ROWS), F32),
        ex_d=vmem((8, ROWS), F32),
        sm_y=vmem((8, 256), F32),
        sm_a=[vmem((8, CH + 256), F32) for _ in range(4)],
        part=[vmem((4, 2 if kind == "z" else 1, SHARE, width), BF16) for _, _, width, kind in UNITS],
        zbuf=[vmem((5, 2 if kind == "z" else 1, SHARE, width), BF16) for _, _, width, kind in UNITS],
        over_out=vmem((SHARE, 256), BF16),
        over_in=vmem((SHARE, 256), BF16),
        norm_o=vmem((4, SHARE, 2 * ROWS), BF16),
        ss=dma((SENDS,)),
        rs=dma((ARRIVALS,)),
        ls=dma((16,)),
        os=dma((len(UNITS) + 3,)),
    )


SENDS = 30 + len(UNITS)
ARRIVALS = 71 + 5 * len(UNITS)


def listed(v):
    return v if isinstance(v, list) else [v]


def finish_body(*refs):
    wo, gate, value, misc, small, out, hid = refs[:7]
    outs, scratch_refs = refs[7:22], refs[22:]
    misc_v, small_v, *held = scratch_refs[:-1]
    sems = scratch_refs[-1]
    (
        out_v, hid_v, pre, in_v, state, step, cx, cxb, cb, cbb, bias, log, skip, gain, wo_v
    ) = held

    def move(src, dst, n):
        copy = pltpu.make_async_copy(src, dst, sems.at[n])
        copy.start()
        return copy

    moves = (
        (small, small_v),
        (misc, misc_v),
        (gate, in_v.at[:, 0, :]),
        (value, in_v.at[:, 1, :]),
        (wo, wo_v),
        (out, out_v),
        (hid, hid_v),
    )
    loads = [move(src, dst, n) for n, (src, dst) in enumerate(moves)]
    stores = []

    def keep(*which):
        for n in which:
            stores.append(move(held[n], outs[n], len(moves) + n))

    loads[0].wait()
    pre[...] = small_v[7, 0:HALF]
    cx[...] = small_v[0:4, 0:CH]
    cxb[...] = small_v[4, 0:CH]
    cb[...] = small_v[0:4, CH:]
    cbb[...] = small_v[4, CH:]
    bias[...] = small_v[5, CH : CH + HEADS]
    log[...] = small_v[6, CH : CH + HEADS]
    skip[...] = small_v[6, CH + 128 : CH + 128 + HEADS]
    gain[...] = small_v[5, 0:CH]
    keep(2, 6, 7, 8, 9, 10, 11, 12, 13)
    loads[1].wait()
    state[...] = misc_v[:, 0:128]
    step[...] = misc_v[:, 128:256].T[0:HEADS]
    keep(4, 5)
    loads[2].wait()
    loads[3].wait()
    keep(3)
    for n, which in ((4, 14), (5, 0), (6, 1)):
        loads[n].wait()
        keep(which)
    for copy in stores:
        copy.wait()


def one_kernel(
    hidden_in,
    out_grad,
    seq_lengths,
    deal_to,
    pre_gain,
    w_in,
    w_state,
    w_step,
    conv_x,
    conv_x_bias,
    conv_bc,
    conv_bc_bias,
    step_bias,
    a_log,
    skip,
    norm_gain,
    w_out,
):
    inputs = dict(
        hid=hidden_in,
        ogr=out_grad,
        lens=seq_lengths,
        deal=deal_to.reshape(1, ROWS),
        skip=skip,
        w_in=w_in,
        wo_hbm=w_out,
        wst_hbm=w_state,
        params=[
            conv_x,
            conv_bc,
            w_step.T,
            conv_x_bias,
            norm_gain,
            pre_gain,
            conv_bc_bias,
            step_bias,
            a_log,
        ],
    )
    in_vmem = pl.BlockSpec(memory_space=pltpu.VMEM)
    places = dict(lens=pltpu.SMEM, skip=pltpu.SMEM, deal=pltpu.VMEM)
    f32_out = partial(jax.ShapeDtypeStruct, dtype=F32)
    half = jax.ShapeDtypeStruct((ROWS, HALF), BF16)
    outputs = dict(
        o_wo=f32_out((SHARE, CH)),
        o_gate=f32_out((SHARE, CH)),
        o_value=f32_out((SHARE, CH)),
        o_misc=f32_out((SHARE, 256)),
        o_small=f32_out((8, CH + 256)),
        o_out=half,
        o_hid=half,
    )
    room = scratch()
    flat = [ref for shape in room.values() for ref in listed(shape)]
    made = pl.pallas_call(
        partial(block_body, {**inputs, **outputs, **room}),
        out_shape=list(outputs.values()),
        in_specs=[pl.BlockSpec(memory_space=places.get(n, pl.ANY)) for n, v in inputs.items() for _ in listed(v)],
        out_specs=[pl.BlockSpec(memory_space=pl.ANY)] * len(outputs),
        scratch_shapes=flat,
        compiler_params=pltpu.CompilerParams(
            collective_id=0, has_side_effects=True, vmem_limit_bytes=VMEM_BYTES
        ),
        name="block",
    )(*(v for value in inputs.values() for v in listed(value)))
    shapes = [(HALF,), (SHARE, 2, CH), (SHARE, 128), (HEADS, SHARE), (4, CH), (CH,), (4, 256), (256,)]
    shapes += [(HEADS,)] * 3 + [(CH,), (SHARE, CH)]
    any_place = pl.BlockSpec(memory_space=pl.ANY)
    made_shapes = [half, half, *(f32_out(s) for s in shapes)]
    results = pl.pallas_call(
        finish_body,
        out_shape=made_shapes,
        in_specs=[any_place] * len(made),
        out_specs=[any_place] * len(made_shapes),
        scratch_shapes=[
            pltpu.VMEM((SHARE, 256), F32),
            pltpu.VMEM((8, CH + 256), F32),
            *(pltpu.VMEM(s.shape, s.dtype) for s in made_shapes),
            pltpu.SemaphoreType.DMA((len(made) + len(made_shapes),)),
        ],
        compiler_params=pltpu.CompilerParams(vmem_limit_bytes=VMEM_BYTES),
        name="finish",
    )(*made)
    return (*results[:5], results[5].T, *results[6:14], results[14].T)


VMEM_BYTES = 65_400_000


def fits(mesh, args):
    return mesh.shape["dp"] == PEERS and mesh.shape["tensor"] == 2 and args[0].shape == (PEERS * ROWS, FULL)


def solution(mesh):
    in_specs = (
        P("dp", "tensor"),
        P("dp", "tensor"),
        P("dp", None),
        P("dp"),
        P(),
        P(None, None, "tensor"),
        P(),
        P(None, "tensor"),
        P(None, "tensor"),
        P("tensor"),
        P(),
        P(),
        P("tensor"),
        P("tensor"),
        P("tensor"),
        P("tensor"),
        P("tensor", None),
    )
    out_specs = (
        P("dp", "tensor"),
        P("dp", "tensor"),
        P("tensor"),
        P("dp", None, "tensor"),
        P("dp", "tensor"),
        P("dp", "tensor"),
        P(None, "tensor"),
        P("tensor"),
        P(),
        P(),
        P("tensor"),
        P("tensor"),
        P("tensor"),
        P("tensor"),
        P("tensor", "dp"),
    )

    def whole(*args):
        local = one_kernel if fits(mesh, args) else shards
        mapped = jax.shard_map(
            local, mesh=mesh, in_specs=in_specs, out_specs=out_specs, check_vma=False
        )
        return mapped(*args)

    return whole
```

```python
from functools import partial
from types import SimpleNamespace

import jax
import jax.numpy as jnp
from jax import lax
from jax.experimental import pallas as pl
from jax.experimental.pallas import tpu as pltpu
from jax.sharding import PartitionSpec as P

D = 1536
GROUP = 256
INNER = 3072


norm_eps = 1e-05


def segment_ids(lengths, row_count):
    index = jnp.arange(lengths.shape[0])
    ends = jnp.sum(jnp.where(index[None, :] <= index[:, None], lengths[None, :], 0), axis=1)
    position = jnp.arange(row_count, dtype=jnp.int32)
    return jnp.sum((position[:, None] >= ends[None, :]).astype(jnp.int32), axis=1, dtype=jnp.int32)


def causal_conv(signal, kernel, kernel_bias, segment):
    width = kernel.shape[0]
    total = kernel_bias[None, :] + kernel[width - 1][None, :] * signal
    for offset in range(1, width):
        moved = jnp.concatenate(
            [jnp.zeros((offset, signal.shape[1]), signal.dtype), signal[:-offset]], axis=0
        )
        earlier = jnp.concatenate([jnp.full((offset,), -1, jnp.int32), segment[:-offset]])
        inside = (earlier == segment).astype(signal.dtype)
        total = total + kernel[width - 1 - offset][None, :] * moved * inside[:, None]
    return total


def state_space(xval, b_rows, c_rows, step, decay, segment):
    highest = lax.Precision.HIGHEST
    blocks = xval.shape[0] // GROUP
    head_count = xval.shape[1]
    x_block = xval.reshape(blocks, GROUP, head_count, xval.shape[2])
    b_block = b_rows.reshape(blocks, GROUP, b_rows.shape[1])
    c_block = c_rows.reshape(blocks, GROUP, c_rows.shape[1])
    step_block = step.reshape(blocks, GROUP, head_count).transpose(0, 2, 1)
    rate_block = step_block * decay[None, :, None]
    seg_block = segment.reshape(blocks, GROUP)
    before = jnp.concatenate([jnp.full((1,), -1, jnp.int32), segment[:-1]]).reshape(blocks, GROUP)[
        :, 0
    ]
    lower_mask = jnp.tril(jnp.ones((GROUP, GROUP), dtype=bool))
    cumulative = jnp.einsum("chj,ij->chi", rate_block, lower_mask.astype(jnp.float32), precision=highest)
    linked = (seg_block[:, :, None] == seg_block[:, None, :]) & lower_mask[None]
    spread = cumulative[:, :, :, None] - cumulative[:, :, None, :]
    weight = jnp.exp(jnp.where(linked[:, None], spread, -10000.0))
    scores = jnp.einsum("cin,cjn->cij", c_block, b_block, precision=highest)
    mixing = weight * scores[:, None] * step_block[:, :, None, :]
    inside_out = jnp.einsum("chij,cjhp->cihp", mixing, x_block, precision=highest)
    final_cum = cumulative[:, :, -1]
    last_same = (seg_block == seg_block[:, -1:]).astype(jnp.float32)
    tail_weight = jnp.exp(final_cum[:, :, None] - cumulative) * last_same[:, None, :] * step_block
    fresh_state = jnp.einsum("chj,cjhp,cjn->chpn", tail_weight, x_block, b_block, precision=highest)
    carried = jnp.zeros(fresh_state.shape[1:], jnp.float32)
    entering = []
    entering.append(carried)
    entering = jnp.stack(entering)
    first_same = (seg_block == before[:, None]).astype(jnp.float32)
    head_decay = jnp.exp(cumulative) * first_same[:, None, :]
    carried_out = jnp.einsum("chi,cin,chpn->cihp", head_decay, c_block, entering, precision=highest)
    return (inside_out + carried_out).reshape(xval.shape)


def pre_norm(stream, gain):
    return stream * lax.rsqrt(jnp.mean(stream * stream, axis=1, keepdims=True) + norm_eps) * gain


def conv_piece(value_pre, state_pre, conv_x, conv_x_bias, conv_bc, conv_bc_bias, segment):
    value_conv = jax.nn.silu(causal_conv(value_pre, conv_x, conv_x_bias, segment))
    state_conv = jax.nn.silu(causal_conv(state_pre, conv_bc, conv_bc_bias, segment))
    return (value_conv, state_conv)


def mixer_piece(value_conv, state_conv, step_pre, step_bias, a_log, skip, segment):
    head_count = step_bias.shape[0]
    row_count = value_conv.shape[0]
    heads_in = value_conv.reshape(row_count, head_count, value_conv.shape[1] // head_count)
    step = jax.nn.softplus(step_pre + step_bias)
    decay = -jnp.exp(a_log)
    half_state = state_conv.shape[1] // 2
    mixed = state_space(
        heads_in, state_conv[:, :half_state], state_conv[:, half_state:], step, decay, segment
    )
    return (mixed + skip[None, :, None] * heads_in).reshape(row_count, value_conv.shape[1])


def rounded(values):
    return lax.optimization_barrier(values.astype(jnp.bfloat16)).astype(jnp.float32)


def shards(
    hidden_in,
    out_grad,
    seq_lengths,
    deal_to,
    pre_gain,
    w_in,
    w_state,
    w_step,
    conv_x,
    conv_x_bias,
    conv_bc,
    conv_bc_bias,
    step_bias,
    a_log,
    skip,
    norm_gain,
    w_out,
):
    dp_count = lax.axis_size("dp")
    row_count = hidden_in.shape[0]
    per_peer = row_count // dp_count
    feat_half = hidden_in.shape[1]
    tensor_index = lax.axis_index("tensor")
    send_order = jnp.argsort(deal_to)
    back_order = jnp.argsort(send_order)
    sent_in = hidden_in[send_order].reshape(dp_count, per_peer, feat_half)
    sent_grad = out_grad[send_order].reshape(dp_count, per_peer, feat_half)
    got_in, got_grad = (
        lax.all_to_all(sent_in, "dp", split_axis=0, concat_axis=0, tiled=True),
        lax.all_to_all(sent_grad, "dp", split_axis=0, concat_axis=0, tiled=True),
    )
    got_ids = lax.all_to_all(
        deal_to[send_order].reshape(dp_count, per_peer),
        "dp",
        split_axis=0,
        concat_axis=0,
        tiled=True,
    )
    dealt_slot = got_ids.reshape(row_count) % row_count
    settle_order = jnp.argsort(dealt_slot)
    dealt_half = got_in.reshape(row_count, feat_half)[settle_order]
    grad_half = got_grad.reshape(row_count, feat_half)[settle_order]
    full_in, grad_full = (
        lax.all_gather(dealt_half, "tensor", axis=1, tiled=True),
        lax.all_gather(grad_half, "tensor", axis=1, tiled=True),
    )
    segment = segment_ids(seq_lengths[0], row_count)
    stream = full_in.astype(jnp.float32)
    normed_f, norm_pull = jax.vjp(pre_norm, stream, pre_gain.astype(jnp.float32))
    normed = normed_f.astype(jnp.bfloat16)
    inner_half = w_in.shape[2]
    w_pair = w_in.reshape(w_in.shape[0], 2 * inner_half)
    proj_pair = jnp.dot(normed, w_pair, preferred_element_type=jnp.float32)
    gate_pre = proj_pair[:, :inner_half]
    value_pre = proj_pair[:, inner_half:]
    state_pre = jnp.dot(normed, w_state, preferred_element_type=jnp.float32)
    step_pre = jnp.dot(normed, w_step, preferred_element_type=jnp.float32)
    conv_args = (
        value_pre,
        state_pre,
        conv_x.astype(jnp.float32),
        conv_x_bias.astype(jnp.float32),
        conv_bc.astype(jnp.float32),
        conv_bc_bias.astype(jnp.float32),
    )
    (value_conv_f, state_conv_f), conv_pull = jax.vjp(
        partial(conv_piece, segment=segment), *conv_args
    )
    value_conv = rounded(value_conv_f)
    state_conv = rounded(state_conv_f)
    mixed, mixer_pull = jax.vjp(
        partial(mixer_piece, segment=segment),
        value_conv,
        state_conv,
        step_pre,
        step_bias,
        a_log,
        skip,
    )
    silu_gate = jax.nn.silu(gate_pre)
    gated = mixed * silu_gate
    total_squares = lax.psum(jnp.sum(gated * gated, axis=1), "tensor")
    inverse = lax.rsqrt(total_squares / INNER + norm_eps)
    gain_f = norm_gain.astype(jnp.float32)
    scaled = (gated * inverse[:, None] * gain_f).astype(jnp.bfloat16)
    partial_out = jnp.dot(scaled, w_out, preferred_element_type=jnp.float32)
    branch = lax.psum_scatter(partial_out, "tensor", scatter_dimension=1, tiled=True)
    result = (dealt_half.astype(jnp.float32) + branch).astype(jnp.bfloat16)
    back_out = lax.all_to_all(
        result[dealt_slot].reshape(dp_count, per_peer, feat_half),
        "dp",
        split_axis=0,
        concat_axis=0,
        tiled=True,
    )
    output = back_out.reshape(row_count, feat_half)[back_order]
    g_w_out = jnp.einsum("ti,td->id", scaled, grad_full, preferred_element_type=jnp.float32)
    d_scaled = jnp.einsum("td,id->ti", grad_full, w_out, preferred_element_type=jnp.float32)
    weighted = d_scaled * gain_f
    g_norm_gain = jnp.sum(d_scaled * gated * inverse[:, None], axis=0)
    cross_sum = lax.psum(jnp.sum(weighted * gated, axis=1), "tensor")
    d_gated = (
        inverse[:, None] * weighted
        - gated * (inverse * inverse * inverse / INNER * cross_sum)[:, None]
    )
    d_mixed = d_gated * silu_gate
    sigmoid_gate = jax.nn.sigmoid(gate_pre)
    d_gate = d_gated * mixed * (sigmoid_gate * (1.0 + gate_pre * (1.0 - sigmoid_gate)))
    d_value_conv, d_state_part, d_step_pre, g_step_bias, g_a_log, g_skip = mixer_pull(d_mixed)
    d_state_conv = lax.psum(d_state_part, "tensor")
    d_value_pre, d_state_pre, g_conv_x, g_conv_x_bias, g_conv_bc, g_conv_bc_bias = conv_pull(
        (d_value_conv, d_state_conv)
    )
    d_pair = jnp.concatenate([d_gate, d_value_pre], axis=1).astype(jnp.bfloat16)
    d_state_low = d_state_pre.astype(jnp.bfloat16)
    d_step_low = d_step_pre.astype(jnp.bfloat16)
    state_share = w_state.shape[1] // lax.axis_size("tensor")
    own_state = lax.dynamic_slice_in_dim(d_state_low, tensor_index * state_share, state_share, 1)
    own_weight = lax.dynamic_slice_in_dim(w_state, tensor_index * state_share, state_share, 1)
    g_w_in = jnp.einsum("td,tc->dc", normed, d_pair, preferred_element_type=jnp.float32).reshape(
        w_in.shape
    )
    g_w_state = jnp.einsum("td,tc->dc", normed, own_state, preferred_element_type=jnp.float32)
    g_w_step = jnp.einsum("td,th->dh", normed, d_step_low, preferred_element_type=jnp.float32)
    d_normed = jnp.einsum("tc,dc->td", d_pair, w_pair, preferred_element_type=jnp.float32)
    d_normed = d_normed + jnp.einsum(
        "th,dh->td", d_step_low, w_step, preferred_element_type=jnp.float32
    )
    d_normed = d_normed + jnp.einsum(
        "tc,dc->td", own_state, own_weight, preferred_element_type=jnp.float32
    )
    normed_share = lax.psum_scatter(d_normed, "tensor", scatter_dimension=1, tiled=True)
    row_scale = lax.rsqrt(jnp.mean(stream * stream, axis=1) + norm_eps)
    stream_share = dealt_half.astype(jnp.float32)
    gain_share = lax.dynamic_slice_in_dim(
        pre_gain.astype(jnp.float32), tensor_index * feat_half, feat_half, 0
    )
    row_cross = lax.psum(jnp.sum(gain_share * normed_share * stream_share, axis=1), "tensor")
    d_share = (
        row_scale[:, None] * gain_share * normed_share
        - stream_share * (row_scale * row_scale * row_scale / D * row_cross)[:, None]
    )
    g_pre_gain = jnp.sum(normed_share * stream_share * row_scale[:, None], axis=0)
    d_input = (d_share + grad_half.astype(jnp.float32)).astype(jnp.bfloat16)
    back_grad = lax.all_to_all(
        d_input[dealt_slot].reshape(dp_count, per_peer, feat_half),
        "dp",
        split_axis=0,
        concat_axis=0,
        tiled=True,
    )
    hidden_grad = back_grad.reshape(row_count, feat_half)[back_order]
    small = lax.psum(
        (
            g_pre_gain,
            g_conv_x,
            g_conv_x_bias,
            g_conv_bc,
            g_conv_bc_bias,
            g_step_bias,
            g_a_log,
            g_skip,
            g_norm_gain,
        ),
        "dp",
    )
    g_in_part, g_state_part, g_step_part, g_w_out_part = (
        lax.psum_scatter(g_w_in, "dp", scatter_dimension=0, tiled=True),
        lax.psum_scatter(g_w_state, "dp", scatter_dimension=0, tiled=True),
        lax.psum_scatter(g_w_step, "dp", scatter_dimension=0, tiled=True),
        lax.psum_scatter(g_w_out, "dp", scatter_dimension=1, tiled=True),
    )
    return (
        output,
        hidden_grad,
        small[0],
        g_in_part,
        g_state_part,
        g_step_part,
        small[1],
        small[2],
        small[3],
        small[4],
        small[5],
        small[6],
        small[7],
        small[8],
        g_w_out_part,
    )


F32, BF16, I32 = jnp.float32, jnp.bfloat16, jnp.int32
MESH = pl.DeviceIdType.MESH
LOG2E = 1.4426950408889634
HIGHEST = lax.Precision.HIGHEST

ROWS = 256
FULL = 1536
HALF = 768
CH = 1536
HEADS = 24
PEERS = 16
PER = ROWS // PEERS
SHARE = FULL // PEERS

X_BIAS, NORM_GAIN, PRE_GAIN, BC_BIAS, STEP_BIAS, A_LOG = (slice(n, n + 1) for n in range(4, 10))

UNITS = (
    ("gate", 0, 256, "z"),
    ("gate", 256, 256, "g"),
    ("gate", 512, 256, "g"),
    ("gate", 768, 256, "g"),
    ("gate", 1024, 512, "g"),
    ("out", 0, 512, "g"),
    ("out", 512, 512, "g"),
    ("out", 1024, 512, "g"),
    ("value", 0, 512, "g"),
    ("value", 512, 512, "g"),
    ("value", 1024, 512, "g"),
    ("misc", 0, 256, "g"),
)


def dot_t(a, b):
    return lax.dot_general(a, b, (((1,), (1,)), ((), ())), preferred_element_type=F32)


def dot(a, b):
    return jnp.dot(a, b, preferred_element_type=F32)


def sigmoid(v):
    return 1.0 / (1.0 + jnp.exp(-v))


def block_at(n, width):
    return pl.ds(pl.multiple_of(n * width, width), width)


class Sent:
    def __init__(self, copy):
        self.copy, self.gone, self.here = copy, False, False

    def wait_recv(self):
        self.copy.wait_recv()
        self.here = True

    def wait_send(self):
        if not self.gone:
            self.copy.wait_send()
        self.gone = True


def await_bytes(sem, ref):
    pltpu.make_async_copy(ref, ref, sem).wait()


def block_body(room, *refs):
    left = list(refs)

    def take(shape):
        return [left.pop(0) for _ in shape] if isinstance(shape, list) else left.pop(0)

    r = SimpleNamespace(**{name: take(shape) for name, shape in room.items()})
    lens, deal_ref, vec = r.lens, r.deal, r.vec
    wst, wsp = r.wst, r.wsp
    ss, rs, ls = r.ss, r.rs, r.ls
    me, side = lax.axis_index("dp"), lax.axis_index("tensor")
    core = lax.rem(me, 2)
    xpos = lax.rem(me // 2, 2)
    zpos = me // 4
    sibling = (zpos * 4 + xpos * 2 + (1 - core), side)
    across = (zpos * 4 + (1 - xpos) * 2 + core, side)
    z_side = zpos // 2
    z_outer, z_inner = 3 * z_side, 1 + z_side
    far_outer, far_inner = 3 - z_outer, 3 - z_inner
    is_outer = zpos == z_outer
    is_inner = zpos == z_inner

    def at_z(z):
        return (z * 4 + xpos * 2 + core, side)

    near = at_z(z_outer + z_inner - zpos)
    facing = at_z(3 - zpos)
    other = (me, 1 - side)
    own_cols = pl.ds(pl.multiple_of(side * HALF, HALF), HALF)
    other_cols = pl.ds(pl.multiple_of((1 - side) * HALF, HALF), HALF)

    started, taken, leaving = [], ({}, {}), []

    def semaphore(sems, key):
        count = taken[sems is rs]
        return sems.at[count.setdefault(("own", len(count)) if key is None else key, len(count))]

    def group(key, ref):
        leaving.append((semaphore(ss, key), ref))
        return key

    def send(src, dst, device, by=None, gone=None, came=None):
        copy = pltpu.make_async_remote_copy(
            src_ref=src,
            dst_ref=dst,
            send_sem=semaphore(ss, gone),
            recv_sem=semaphore(rs, came),
            device_id=device,
            device_id_type=MESH,
        )
        if by is None:
            copy.start()
        else:
            pl.when(by)(copy.start)
        one = Sent(copy)
        if gone is None:
            started.append(one)
        return one

    def load(src, dst, n):
        copy = pltpu.make_async_copy(src, dst, ls.at[n])
        copy.start()
        return copy

    def pair_load(n, at):
        cols = pl.ds(pl.multiple_of(n * 128, 128), 128)
        return pltpu.make_async_copy(r.w_in.at[:, :, cols], r.pair.at[at], ls.at[at])

    hid_load = load(r.hid, r.half_in, 3)
    pair_load(0, 0).start()
    pair_load(1, 1).start()
    pair_load(2, 2).start()
    ogr_load = load(r.ogr, r.dhalf_in, 4)
    small_loads = [load(src, dst, 5 + n) for n, (src, dst) in enumerate(zip(r.params, r.params_v))]
    wst_load = load(r.wst_hbm, r.wst, 14)
    wo_load = load(r.wo_hbm, r.wo, 15)

    barrier = pltpu.get_barrier_semaphore()
    for k in range(1, PEERS):
        pl.semaphore_signal(
            barrier, inc=1, device_id=(lax.rem(me + k, PEERS), side), device_id_type=MESH
        )
    pl.semaphore_signal(barrier, inc=1, device_id=other, device_id_type=MESH)

    i0 = lax.broadcasted_iota(I32, (ROWS, ROWS), 0)
    i1 = lax.broadcasted_iota(I32, (ROWS, ROWS), 1)
    deal = deal_ref[...]
    dest = lax.shift_right_logical(deal, 8)
    slot = jnp.bitwise_and(deal, ROWS - 1)
    member = (dest == lax.broadcasted_iota(I32, (PEERS, ROWS), 0)).astype(F32)
    before = dot(member.astype(BF16), (i0 < i1).astype(F32).astype(BF16))
    rank = jnp.sum(member * before, axis=0, keepdims=True)
    place = dest.astype(F32) * PER + rank
    hit = i0.astype(F32) == place
    to_send = hit.astype(F32)
    send_hot = to_send.astype(BF16)
    ident = jnp.sum(to_send * slot.astype(F32), axis=1, keepdims=True)
    sb_h, sb_g, rb_h, rb_g, yb_h, yb_g = r.sb_h, r.sb_g, r.rb_h, r.rb_g, r.yb_h, r.yb_g
    hid_load.wait()
    sb_h[...] = dot(send_hot, r.half_in[...]).astype(BF16)
    row_w = lax.broadcasted_iota(I32, (ROWS, 128), 0)
    lane_w = lax.broadcasted_iota(I32, (ROWS, 128), 1)
    in_place = lax.rem(row_w, PER) == lane_w
    spread = jnp.where(in_place, ident, 0.0).astype(BF16)
    row_n = lax.broadcasted_iota(I32, (PEERS, ROWS), 0)
    lane_n = lax.broadcasted_iota(I32, (PEERS, ROWS), 1)
    gather_ids = (row_n == lane_n // PER).astype(F32).astype(BF16)
    r.sb_i[...] = dot(gather_ids, spread).reshape(PEERS, 1, 128)

    pl.semaphore_wait(barrier, PEERS)

    def rows_of(device):
        return pl.ds(pl.multiple_of(device * PER, PER), PER)

    line = (zpos, z_outer + z_inner - zpos, lax.rem(zpos + 2, 4), 3 - zpos)

    def away(dz, dx, dc):
        return line[dz] * 4 + lax.rem(xpos + dx, 2) * 2 + lax.rem(core + dc, 2)

    steps = [(dz, dx, dc) for dz in (2, 3, 1, 0) for dx in (0, 1) for dc in (0, 1)]

    def deal(dz, src, dst, gone, came, rows=rows_of):
        for step in steps:
            if step[0] == dz and step != (0, 0, 0):
                to = away(*step)
                send(src.at[rows(to)], dst.at[rows(me)], (to, side), gone=gone, came=came)

    def pass_rows(name, first, count, buf, dst):
        rows = pl.ds(pl.multiple_of(first, count), count)
        send(buf.at[rows], dst.at[rows], other, gone=(name, 9), came=(name, 9))

    def pass_group(name, dz, buf, dst):
        if dz < 2:
            await_bytes(semaphore(rs, (name, dz)), buf.at[pl.ds(0, 4 * PER - (PER if dz == 0 else 0))])
            pass_rows(name, line[dz] * 4 * PER, 4 * PER, buf, dst)
        else:
            for dx in range(2):
                for dc in range(2):
                    await_bytes(semaphore(rs, (name, (dz, dx, dc))), buf.at[pl.ds(0, PER)])
                pass_rows(name, line[dz] * 4 * PER + lax.rem(xpos + dx, 2) * 2 * PER, 2 * PER, buf, dst)

    def wave(name, dz, src, dst):
        for step in steps:
            if step[0] == dz:
                to = away(*step)
                send(src.at[rows_of(to)], dst.at[rows_of(me)], (to, side), gone=(name, "wave", dz), came=(name, step))

    def wave_gone(name, dz, src):
        await_bytes(semaphore(ss, (name, "wave", dz)), src.at[pl.ds(0, 4 * PER)])

    def rest(name, src, dst):
        for dz in (1, 0):
            deal(dz, src, dst, name, (name, dz))
        group(name, src.at[pl.ds(0, 7 * PER)])

    def same(device):
        return device

    wave("hid", 3, sb_h, rb_h)
    rest("hid", sb_h, rb_h)
    for dz in (2, 3, 1, 0):
        deal(dz, r.sb_i, r.rb_i, "ids", "ids", same)
    group("ids", r.sb_i.at[pl.ds(0, PEERS - 1)])
    r.rb_i[me] = r.sb_i[me]
    rb_h[rows_of(me)] = sb_h[rows_of(me)]
    ogr_load.wait()
    sb_g[...] = dot(send_hot, r.dhalf_in[...]).astype(BF16)
    rb_g[rows_of(me)] = sb_g[rows_of(me)]
    r.send_hot_t[...] = to_send.T.astype(BF16)

    ends, total = [], 0
    for k in range(8):
        total = total + lens[0, k]
        ends.append(total)

    def seg_at(pos):
        out = jnp.zeros(pos.shape, I32)
        for e in ends:
            out = out + (pos >= e).astype(I32)
        return out

    row_col = lax.broadcasted_iota(I32, (ROWS, 128), 0)
    seg_here = seg_at(row_col)
    for o in range(1, 4):
        same = (seg_at(row_col - o) == seg_here) & (row_col >= o)
        r.masks[o - 1] = same.astype(F32)
    same = seg_at(i0) == seg_at(i1)
    r.linked[...] = (same & (i0 >= i1)).astype(F32)
    r.linked_t[...] = (same & (i0 <= i1)).astype(F32)
    r.small[...] = jnp.zeros((8, CH + 256), F32)
    for copy in small_loads:
        copy.wait()
    conv_x_v, conv_bc_v, w_step_v, *rows_v = r.params_v
    vec[...] = jnp.zeros((16, CH), F32)
    vec[0:4, :] = conv_x_v[...].astype(F32)
    for n, ref in enumerate(rows_v):
        vec[4 + n, 0 : ref.shape[0]] = ref[...].astype(F32)
    vec[12:16, 0:256] = conv_bc_v[...].astype(F32)
    wst_load.wait()
    wsp[...] = jnp.concatenate(
        [w_step_v[...].astype(F32), jnp.zeros((128 - HEADS, FULL), F32)], axis=0
    ).astype(BF16)
    r.dst_acc[...] = jnp.zeros((ROWS, ROWS), F32)
    r.dcol[...] = jnp.zeros((ROWS, 128), F32)
    r.dsd[...] = jnp.zeros((ROWS, 128), F32)

    picked = jnp.where(i0 < 128, 2 * i0, 2 * i0 - 255)
    apart = (picked == i1).astype(F32).astype(BF16)

    def take_apart(n):
        at = lax.rem(n, 3)
        pair_load(n, at).wait()
        cols = block_at(n, 128)
        flat = r.pair.at[at].reshape(2 * FULL, 128)
        for k in range(12):
            both = dot(apart, flat[k * 256 : (k + 1) * 256, :]).astype(BF16)
            r.wg[k * 128 : (k + 1) * 128, cols] = both[0:128]
            r.wv[k * 128 : (k + 1) * 128, cols] = both[128:256]

        @pl.when(n + 3 < 12)
        def _():
            pair_load(n + 3, at).start()

    group(("hid", 9), rb_h)
    group(("grad", 9), rb_g)
    pl.loop(0, 4)(take_apart)
    pass_group("hid", 0, rb_h, yb_h)
    wave_gone("hid", 3, sb_h)
    wave("hid", 2, sb_h, rb_h)
    pl.loop(4, 7)(take_apart)
    pass_group("hid", 1, rb_h, yb_h)
    pl.loop(7, 12)(take_apart)
    pass_group("hid", 3, rb_h, yb_h)
    await_bytes(semaphore(rs, "ids"), r.rb_i.at[pl.ds(0, PEERS - 1)])
    origin_row = lax.broadcasted_iota(I32, (ROWS, PEERS), 0) // PER
    fetch_ids = (origin_row == lax.broadcasted_iota(I32, (ROWS, PEERS), 1)).astype(F32).astype(BF16)
    ids = jnp.where(in_place, dot(fetch_ids, r.rb_i[...].reshape(PEERS, 128).astype(BF16)), 0.0)
    ids = jnp.broadcast_to(jnp.sum(ids, axis=1, keepdims=True), (ROWS, 128))
    r.hot_t[...] = (ids[:, 0:1] == i1.astype(F32)).astype(F32).astype(BF16)
    r.hot[...] = (ids.T[0:1, :] == i0.astype(F32)).astype(F32).astype(BF16)
    wave_gone("hid", 2, sb_h)
    wave("grad", 3, sb_g, rb_g)
    pass_group("hid", 2, rb_h, yb_h)
    rest("grad", sb_g, rb_g)
    stream, upstream, normed = r.stream, r.upstream, r.normed
    stream[:, own_cols] = dot(r.hot[...], rb_h[...]).astype(BF16)
    await_bytes(semaphore(rs, ("hid", 9)), yb_h)
    stream[:, other_cols] = dot(r.hot[...], yb_h[...]).astype(BF16)

    wave_gone("grad", 3, sb_g)
    wave("grad", 2, sb_g, rb_g)

    @pl.loop(0, 8)
    def _(n):
        rows = block_at(n, 32)
        s = stream[rows, :].astype(F32)
        scale = lax.rsqrt(jnp.sum(s * s, axis=1, keepdims=True) * (1.0 / FULL) + norm_eps)
        r.nscale[rows, :] = jnp.broadcast_to(scale, (32, 128))
        normed[rows, :] = (s * scale * vec[PRE_GAIN, :]).astype(BF16)

    here, beside, over, cross_over = (pl.ds(n * ROWS, ROWS) for n in range(4))
    diagonal = (zpos * 4 + (1 - xpos) * 2 + (1 - core), side)

    def flip(source, flipped, keep):
        for n in range(4):
            turned = source[:, n * 384 : (n + 1) * 384].astype(F32).T.astype(BF16)
            for i in range(4):
                flipped[n, i] = turned[i * SHARE : (i + 1) * SHARE]
        keep[:, :, here] = flipped[:, xpos * 2 + core]

    def share_early(flipped, keep):
        keep[:, :, here] = flipped[:, (1 - xpos) * 2 + core]
        send(flipped.at[:, (1 - xpos) * 2 + (1 - core)], keep.at[:, :, beside], sibling, gone="early", came="early")
        group("early", keep.at[:, :, beside])

    others, overs = pl.ds(ROWS, 3 * ROWS), pl.ds(2 * ROWS, 2 * ROWS)

    def share_flipped(name, flipped, keep, near_by):
        group(name, keep.at[:, :, others])
        for dx, dc, lanes, device in ((0, 1, beside, sibling), (1, 0, over, across), (1, 1, cross_over, diagonal)):
            place = lax.rem(xpos + dx, 2) * 2 + lax.rem(core + dc, 2)
            came = near_by if lanes is beside else name
            send(flipped.at[:, place], keep.at[:, :, lanes], device, gone=name, came=came)

    masks = r.masks

    def conv_at(signal, taps, bias):
        out = bias + taps[3] * signal
        for o in range(1, 4):
            out = out + taps[3 - o] * (pltpu.roll(signal, o, 0) * masks[o - 1])
        return out

    def conv_back(signal, taps, bias, grad):
        pre = conv_at(signal, taps, bias)
        s = sigmoid(pre)
        d_pre = grad * (s * (1.0 + pre * (1.0 - s)))
        sums = [None] * 4
        sums[3] = jnp.sum(d_pre * signal, axis=0, keepdims=True)
        d_signal = taps[3] * d_pre
        for o in range(1, 4):
            masked = d_pre * masks[o - 1]
            sums[3 - o] = jnp.sum(masked * pltpu.roll(signal, o, 0), axis=0, keepdims=True)
            d_signal = d_signal + taps[3 - o] * pltpu.roll(masked, ROWS - o, 0)
        return d_signal, sums, jnp.sum(d_pre, axis=0, keepdims=True)

    def taps_at(first, cols):
        return [vec[pl.ds(first + k, 1), cols] for k in range(4)]

    gate_pre, value_pre, vconv = r.gate_pre, r.value_pre, r.vconv
    def project(n):
        cols = block_at(n, 256)
        gate_pre[:, cols] = dot(normed[...], r.wg[:, cols])
        value_pre[:, cols] = dot(normed[...], r.wv[:, cols])

    def convolve(n):
        cols = block_at(n, 128)
        pre = conv_at(value_pre[:, cols], taps_at(0, cols), vec[X_BIAS, cols])
        vconv[:, cols] = (pre * sigmoid(pre)).astype(BF16)

    pl.loop(0, 6, unroll=3)(project)
    pass_group("grad", 0, rb_g, yb_g)
    pass_group("grad", 1, rb_g, yb_g)
    pl.loop(0, 12)(convolve)
    pass_group("grad", 3, rb_g, yb_g)

    state_pre, sconv = r.state_pre, r.sconv
    state_pre[...] = dot(normed[...], wst[...])
    for n in range(2):
        cols = pl.ds(n * 128, 128)
        pre = conv_at(state_pre[:, cols], taps_at(12, cols), vec[BC_BIAS, cols])
        sconv[:, cols] = (pre * sigmoid(pre)).astype(BF16)

    step_in = dot_t(normed[...], wsp[...]) + vec[STEP_BIAS, 0:128]
    small_e = jnp.exp(-jnp.abs(step_in))
    series = small_e * (1.0 - small_e * (0.5 - small_e * (1.0 / 3.0 - 0.25 * small_e)))
    step = jnp.maximum(step_in, 0.0) + jnp.where(small_e < 0.01, series, jnp.log(1.0 + small_e))
    decay = -jnp.exp(vec[A_LOG, 0:128])
    r.step_in[...] = step_in
    r.step[...] = step
    lower = (i0 >= i1).astype(F32)
    cum2 = jnp.dot(lower, step * decay, precision=HIGHEST, preferred_element_type=F32) * LOG2E
    r.cum2[...] = cum2
    r.cum2_t[...] = cum2.T
    r.cum2_ls[...] = (cum2 - jnp.log(step) * LOG2E).T
    b_rows, c_rows = sconv[:, 0:128], sconv[:, 128:256]
    r.scores[...] = dot_t(c_rows, b_rows) * r.linked[...]
    r.scores_t[...] = dot_t(b_rows, c_rows) * r.linked_t[...]

    lane = lax.broadcasted_iota(I32, (ROWS, 128), 1)
    lane_half = lax.broadcasted_iota(I32, (128, 128), 1) < 64

    def column(ref, h):
        return jnp.sum(jnp.where(lane == h, ref[...], 0.0), axis=1, keepdims=True)


    mixed = r.mixed

    def mix(p):
        cols = block_at(p, 128)
        x = vconv[:, cols]
        tops, lows = [], []
        for a in range(2):
            h = 2 * p + a
            cc = column(r.cum2, h)
            cr = r.cum2_ls[pl.ds(h, 1), :]
            w = jnp.exp2(jnp.minimum(cc[0:128] - cr[:, 0:128], 100.0)) * r.scores[0:128, 0:128]
            tops.append(dot(w.astype(BF16), x[0:128]))
            w = jnp.exp2(jnp.minimum(cc[128:256] - cr, 100.0)) * r.scores[128:256, :]
            lows.append(dot(w.astype(BF16), x))
        skip = jnp.where(lane_half[0:1], r.skip[2 * p], r.skip[2 * p + 1])
        xf = x.astype(F32)
        mixed[0:128, cols] = jnp.where(lane_half, tops[0], tops[1]) + skip * xf[0:128]
        mixed[128:256, cols] = jnp.where(lane_half, lows[0], lows[1]) + skip * xf[128:256]

    pl.loop(0, 3, unroll=3)(mix)
    pass_group("grad", 2, rb_g, yb_g)
    wave_gone("grad", 2, sb_g)
    pl.loop(3, 12, unroll=3)(mix)
    flip(normed, r.norm_f, r.norm_t)
    share_early(r.norm_f, r.norm_o)
    share_flipped("norm", r.norm_f, r.norm_t, "beside")

    upstream[:, own_cols] = dot(r.hot[...], rb_g[...]).astype(BF16)
    await_bytes(semaphore(rs, ("grad", 9)), yb_g)
    upstream[:, other_cols] = dot(r.hot[...], yb_g[...]).astype(BF16)
    wo_load.wait()
    d_scaled = r.d_scaled
    r.acc1[...] = jnp.zeros((ROWS, 128), F32)
    r.acc2[...] = jnp.zeros((ROWS, 128), F32)

    @pl.loop(0, 6, unroll=6)
    def _(n):
        cols = block_at(n, 256)
        ds = dot_t(upstream[...], r.wo[cols, :])
        d_scaled[:, cols] = ds
        g = gate_pre[:, cols]
        gated = mixed[:, cols] * g * sigmoid(g)
        sq = gated * gated
        cr = vec[NORM_GAIN, cols] * ds * gated
        r.acc1[...] += sq[:, 0:128] + sq[:, 128:256]
        r.acc2[...] += cr[:, 0:128] + cr[:, 128:256]

    def exchange_rows(col_a, col_b, out_buf, in_buf):
        both = jnp.where(lane == 0, col_a, jnp.where(lane == 1, col_b, 0.0))
        out_buf[...] = both.T[0:8, :]
        copy = send(out_buf, in_buf, other)

        def finish():
            copy.wait_recv()
            both = jnp.concatenate([out_buf[...] + in_buf[...], jnp.zeros((120, ROWS), F32)], axis=0)
            return both.T[:, 0:1], both.T[:, 1:2]

        return finish

    row_sums = exchange_rows(
        jnp.sum(r.acc1[...], axis=1, keepdims=True),
        jnp.sum(r.acc2[...], axis=1, keepdims=True),
        r.ex_a,
        r.ex_b,
    )
    r.cum2_ls[...] = jnp.zeros((128, ROWS), F32)
    flip(upstream, r.up_f, r.up_t)
    sum_sq, sum_cross = row_sums()
    inner = 2.0 * CH
    inverse = lax.rsqrt(sum_sq * (1.0 / inner) + norm_eps)
    cross = inverse * inverse * inverse * (1.0 / inner) * sum_cross
    r.acc1[...] = jnp.broadcast_to(inverse, (ROWS, 128))
    r.acc2[...] = jnp.broadcast_to(cross, (ROWS, 128))
    scaled4, gate4, value4, misc4 = r.scaled4, r.gate4, r.value4, r.misc4

    def gated_back(n):
        cols = block_at(n, 128)
        inv, crs = r.acc1[...], r.acc2[...]
        g, m, ds, gain = gate_pre[:, cols], mixed[:, cols], d_scaled[:, cols], vec[NORM_GAIN, cols]
        s = sigmoid(g)
        silu = g * s
        gated = m * silu
        gi = gated * inv
        scaled4[here, cols] = (gi * gain).astype(BF16)
        r.small[5:6, cols] = jnp.sum(ds * gi, axis=0, keepdims=True)
        d_gated = inv * ds * gain - gated * crs
        mixed[:, cols] = d_gated * silu
        gate4[here, cols] = (d_gated * m * (s * (1.0 + g * (1.0 - s)))).astype(BF16)

    def gated_part(first, last):
        pl.loop(first, last)(gated_back)

    half_f, half_o, half_in = d_scaled.at[:, pl.ds(0, HALF)], normed.at[:, pl.ds(0, HALF)], r.half_in
    flying = {}

    def project_other():
        @pl.loop(0, 3)
        def _(n):
            cols = pl.ds(pl.multiple_of((1 - side) * HALF + n * 256, 256), 256)
            half_o[:, block_at(n, 256)] = dot(scaled4[here, :], r.wo[:, cols]).astype(BF16)

        flying["out"] = send(half_o, half_in, other)

    def project_own():
        @pl.loop(0, 3)
        def _(n):
            cols = pl.ds(pl.multiple_of(side * HALF + n * 256, 256), 256)
            half_f[:, block_at(n, 256)] = dot(scaled4[here, :], r.wo[:, cols]) + stream[:, cols].astype(F32)

    lefts = {"out": r.up_t, "gate": r.norm_t, "value": r.norm_t, "misc": r.norm_t}
    rights = {"out": scaled4, "gate": gate4, "value": value4, "misc": misc4}
    outs = {"out": r.o_wo, "gate": r.o_gate, "value": r.o_value, "misc": r.o_misc}
    stores = []

    def store(src, dst, n):
        copy = pltpu.make_async_copy(src, dst, r.os.at[n])
        copy.start()
        return copy

    def ready(copy):
        if not copy.here:
            copy.wait_recv()

    pieces = {}
    for name, ref in rights.items():
        alone = sum(unit[2] for unit in UNITS if unit[0] == name and unit[3] == "z")
        group(name, ref.at[pl.ds(0, 3 * ROWS), pl.ds(0, ref.shape[1] - alone)])

    def up_swap():
        share_flipped("up", r.up_f, r.up_t, "up")

    def swap(name, first, width):
        ref, cols = rights[name], pl.ds(first, width)
        near_by = send(ref.at[here, cols], ref.at[beside, cols], sibling, gone=name)
        far_off = send(ref.at[here, cols], ref.at[over, cols], across, gone=name)
        pieces[name, first] = [width, near_by, far_off]

    def beside_here():
        if "beside" not in flying:
            flying["beside"] = True
            await_bytes(semaphore(rs, "beside"), r.norm_t.at[:, :, beside])

    def swap_near(name, first, width):
        ref, cols = rights[name], pl.ds(first, width)
        pieces[name, first] = [width, send(ref.at[here, cols], ref.at[beside, cols], sibling)]

    def relay(name, first):
        piece = pieces[name, first]
        ref, cols = rights[name], pl.ds(first, piece[0])
        ready(piece[2])
        piece.append(send(ref.at[over, cols], ref.at[cross_over, cols], sibling, gone=name))

    class Unit:
        def __init__(self, n):
            self.name, self.first, self.width, self.kind = UNITS[n]
            self.n, self.part, self.zbuf, self.kept = n, r.part[n], r.zbuf[n], r.kept[n]
            self.key = group(("unit", n), self.zbuf.at[pl.ds(0, 3)])
            self.stages = [self.compute if self.kind == "g" else self.compute_early, self.pass_outer, self.pass_inner, self.send_out, self.finish, self.keep_across]

        def go(self, stage):
            self.stages[stage]()

        def add(self, z, slot):
            self.part[z] = self.part[z] + self.zbuf[slot]

        def hop(self, z, slot, device, by):
            return send(self.part.at[z], self.zbuf.at[slot], device, by, self.key, (self.key, slot))

        def compute(self):
            lhs_ref, rhs_ref = lefts[self.name], rights[self.name]
            first, part = self.first, self.part
            side_name = "up" if self.name == "out" else "norm"
            if side_name == "norm":
                beside_here()
            if side_name not in flying:
                flying[side_name] = True
                await_bytes(semaphore(rs, side_name), lhs_ref.at[:, :, others if side_name == "up" else overs])
            for (name, start), piece in pieces.items():
                if name == self.name and start < first + self.width and first < start + piece[0]:
                    for copy in piece[1:]:
                        ready(copy)

            @pl.loop(0, self.width // 256)
            def _(n):
                lhs = lhs_ref[...].reshape(4 * SHARE, 4 * ROWS)
                rhs = rhs_ref[:, pl.ds(pl.multiple_of(first + n * 256, 256), 256)]
                part[:, 0, :, block_at(n, 256)] = dot(lhs, rhs).astype(BF16).reshape(4, SHARE, 256)

            self.leave()

        def compute_early(self):
            for copy in pieces[self.name, self.first][1:]:
                ready(copy)
            await_bytes(semaphore(rs, "early"), r.norm_o.at[:, :, beside])
            beside_here()
            rhs = rights[self.name][0 : 2 * ROWS, self.first : self.first + self.width]
            for n, lhs_ref in enumerate((r.norm_t, r.norm_o)):
                lhs = lhs_ref[:, :, 0 : 2 * ROWS].reshape(4 * SHARE, 2 * ROWS)
                self.part[:, n] = dot(lhs, rhs).astype(BF16).reshape(4, SHARE, self.width)
            self.leave()

        def leave(self):
            self.c3 = self.hop(far_outer, 0, near, is_outer)
            self.c2 = self.hop(far_inner, 1, near, is_outer)
            self.c1 = self.hop(z_inner, 2, near, is_outer)

        def pass_outer(self):
            @pl.when(is_inner)
            def _():
                self.c3.wait_recv()
                self.add(far_outer, 0)

            self.d2 = self.hop(far_outer, 3, facing, is_inner)

        def pass_inner(self):
            @pl.when(is_inner)
            def _():
                self.c2.wait_recv()
                self.add(far_inner, 1)

            self.d1 = self.hop(far_inner, 4, facing, is_inner)

        def send_out(self):
            @pl.when(is_inner)
            def _():
                self.d2.wait_recv()
                self.add(z_outer, 3)

            self.e1 = self.hop(z_outer, 0, near, is_inner)

        def finish(self):
            def end(*slots):
                sums = [self.part[zpos, n].astype(F32) for n in range(self.part.shape[1])]
                for slot in slots:
                    sums = [s + self.zbuf[slot, n].astype(F32) for n, s in enumerate(sums)]
                self.kept[...] = sums[0]
                if self.kind == "z":
                    r.over_out[...] = sums[1].astype(BF16)

            @pl.when(is_outer)
            def _():
                self.e1.wait_recv()
                end(0)

            @pl.when(is_inner)
            def _():
                self.c1.wait_recv()
                self.d1.wait_recv()
                end(2, 4)

            if self.kind == "z":
                self.cx = send(r.over_out, r.over_in, across)
            else:
                self.store()

        def keep_across(self):
            self.cx.wait_recv()
            self.kept[...] = self.kept[...] + r.over_in[...].astype(F32)
            self.store()

        def store(self):
            cols = pl.ds(self.first, self.width)
            stores.append(store(self.kept, outs[self.name].at[:, cols], self.n))

    units = [Unit(n) for n in range(len(UNITS))]
    head_row = lax.broadcasted_iota(I32, (32, ROWS), 0)

    def mixer_back(p):
        cols = block_at(p, 128)
        x = vconv[:, cols]
        xf = x.astype(F32)
        dy = mixed[:, cols]
        dyb = dy.astype(BF16)
        by_channel = jnp.sum(dy * xf, axis=0, keepdims=True)
        skips = r.small[6:7, CH + 128 : CH + 256]
        d_tops, d_lows = [], []
        for a in range(2):
            h = 2 * p + a
            half = (lane < 64) if a == 0 else (lane >= 64)
            of_head = jnp.sum(jnp.where(half[0:1], by_channel, 0.0), axis=1, keepdims=True)
            skips = skips + jnp.where(lane[0:1] == h, of_head, 0.0)
            xa = jnp.where(half, xf, 0.0)
            xab = xa.astype(BF16)
            cc = column(r.cum2, h)
            st = column(r.step, h)
            cr = r.cum2_t[pl.ds(h, 1), :]
            w = jnp.exp2(jnp.minimum(cr - cc[0:128], 0.0))
            sc = r.scores_t[0:128, :]
            v_top = dot((w * sc).astype(BF16), dyb)
            q = dot_t(xab[0:128], dyb) * w * st[0:128]
            r.dst_acc[0:128, :] += q
            g_top = q * sc
            w = jnp.exp2(jnp.minimum(cr[:, 128:256] - cc[128:256], 0.0))
            sc = r.scores_t[128:256, 128:256]
            v_low = dot((w * sc).astype(BF16), dyb[128:256])
            q = dot_t(xab[128:256], dyb[128:256]) * w * st[128:256]
            r.dst_acc[128:256, 128:256] += q
            g_low = q * sc
            top_sums = jnp.sum(g_top, axis=0, keepdims=True)
            low_sums = jnp.sum(g_low, axis=0, keepdims=True)
            col_sums = jnp.concatenate([top_sums[:, 0:128], top_sums[:, 128:256] + low_sums], axis=1)
            r.cum2_ls[0:32, :] += jnp.where(head_row == h, col_sums, 0.0)
            row_sums = jnp.concatenate(
                [
                    jnp.sum(g_top[:, 0:128] + g_top[:, 128:256], axis=1, keepdims=True),
                    jnp.sum(g_low, axis=1, keepdims=True),
                ],
                axis=0,
            )
            direct = jnp.concatenate(
                [
                    jnp.sum(xa[0:128] * v_top, axis=1, keepdims=True),
                    jnp.sum(xa[128:256] * v_low, axis=1, keepdims=True),
                ],
                axis=0,
            )
            r.dcol[...] += jnp.where(lane == h, row_sums, 0.0)
            r.dsd[...] += jnp.where(lane == h, direct, 0.0)
            d_tops.append(st[0:128] * v_top)
            d_lows.append(st[128:256] * v_low)
        r.small[6:7, CH + 128 : CH + 256] = skips
        d_conv = jnp.concatenate(
            [jnp.where(lane_half, d_tops[0], d_tops[1]), jnp.where(lane_half, d_lows[0], d_lows[1])],
            axis=0,
        )
        d_conv = d_conv + jnp.where(lane_half[0:1], r.skip[2 * p], r.skip[2 * p + 1]) * dy
        d_value, sums, bias_sum = conv_back(value_pre[:, cols], taps_at(0, cols), vec[X_BIAS, cols], d_conv)
        value4[here, cols] = d_value.astype(BF16)
        for k in range(4):
            r.small[k : k + 1, cols] = sums[k]
        r.small[4:5, cols] = bias_sum

    def mixer_part(first, last):
        pl.loop(first, last)(mixer_back)

    def send_back(name, src, dst):
        group(name, src.at[pl.ds(0, ROWS - PER)])
        for dz in (2, 3, 1, 0):
            deal(dz, src, dst, name, name)
        dst[rows_of(me)] = src[rows_of(me)]

    def return_out():
        ready(flying["out"])
        result = (half_f[...] + half_in[...].astype(F32)).astype(BF16)
        yb_h[...] = dot(r.hot_t[...], result).astype(BF16)
        send_back("back_o", yb_h, r.back_o)

    def finish_out():
        await_bytes(semaphore(rs, "back_o"), r.back_o.at[pl.ds(0, ROWS - PER)])
        r.res_o[...] = dot(r.send_hot_t[...], r.back_o[...]).astype(BF16)
        stores.append(store(r.res_o, r.o_out, len(UNITS) + 1))

    d_state = r.d_state
    state_own = pl.ds(pl.multiple_of(side * 128, 128), 128)
    state_other = pl.ds(pl.multiple_of((1 - side) * 128, 128), 128)

    def states_back():
        d_scores_t = r.dst_acc[...] * r.linked_t[...]
        d_conv_s = r.linked
        d_conv_s[:, 0:128] = dot(d_scores_t.astype(BF16), c_rows)
        d_conv_s[:, 128:256] = dot(d_scores_t.T.astype(BF16), b_rows)
        for n in range(2):
            cols = pl.ds(n * 128, 128)
            d_pre, sums, bias_sum = conv_back(
                state_pre[:, cols], taps_at(12, cols), vec[BC_BIAS, cols], d_conv_s[:, cols]
            )
            d_state[:, cols] = d_pre
            for k in range(4):
                r.small[k : k + 1, CH + n * 128 : CH + (n + 1) * 128] = sums[k]
            r.small[4:5, CH + n * 128 : CH + (n + 1) * 128] = bias_sum
        r.st_out[...] = d_state[:, state_other].astype(BF16)
        flying["state"] = send(r.st_out, r.st_in, other)
        d_cum = r.cum2_ls[...].T - r.dcol[...]
        upper = (i0 <= i1).astype(F32)
        d_rate = jnp.dot(upper, d_cum, precision=HIGHEST, preferred_element_type=F32)
        d_step = (r.dsd[...] + d_rate * decay) * sigmoid(r.step_in[...])
        r.small[5:6, CH : CH + 128] = jnp.sum(d_step, axis=0, keepdims=True)
        r.small[6:7, CH : CH + 128] = jnp.sum(d_rate * r.step[...], axis=0, keepdims=True) * decay
        misc4[here, 128:256] = d_step.astype(BF16)
        r.acc1[...] = jnp.zeros((ROWS, 128), F32)
        r.st_low[...] = d_state[...].astype(BF16)

    def add_states():
        ready(flying["state"])
        misc4[here, 0:128] = (d_state[:, state_own] + r.st_in[...].astype(F32)).astype(BF16)

    dhalf_f, dhalf_o, dhalf_in = d_scaled.at[:, pl.ds(HALF, HALF)], normed.at[:, pl.ds(HALF, HALF)], r.dhalf_in

    def d_normed_at(first):
        rows = pl.ds(pl.multiple_of(first, 256), 256)
        out = dot_t(gate4[here, :], r.wg[rows, :]) + dot_t(value4[here, :], r.wv[rows, :])
        out = out + dot_t(r.st_low[...], r.wst[rows, :])
        out = out + dot(misc4[here, 128:256], wsp[:, rows])
        part = out * vec[PRE_GAIN, rows] * stream[:, rows].astype(F32)
        r.acc1[...] += part[:, 0:128] + part[:, 128:256]
        return out

    def normed_other():
        @pl.loop(0, 3)
        def _(n):
            dhalf_o[:, block_at(n, 256)] = d_normed_at((1 - side) * HALF + n * 256).astype(BF16)

        flying["norm"] = send(dhalf_o, dhalf_in, other)

    def normed_own():
        @pl.loop(0, 3)
        def _(n):
            dhalf_f[:, block_at(n, 256)] = d_normed_at(side * HALF + n * 256)

        flying["rows"] = exchange_rows(
            jnp.sum(r.acc1[...], axis=1, keepdims=True), jnp.zeros((ROWS, 1), F32), r.ex_c, r.ex_d
        )

    small = r.small

    def return_grad():
        row_cross, _ = flying["rows"]()
        ready(flying["norm"])
        flying["out"].wait_send()
        scale = r.nscale[:, 0:1]
        factor = scale * scale * scale * (1.0 / FULL) * row_cross
        for n in range(6):
            cols = pl.ds(n * 128, 128)
            mine = pl.ds(pl.multiple_of(side * HALF + n * 128, 128), 128)
            dn = dhalf_f[:, cols] + dhalf_in[:, cols].astype(F32)
            s = stream[:, mine].astype(F32)
            small[7:8, n * 128 : (n + 1) * 128] = jnp.sum(dn * s * scale, axis=0, keepdims=True)
            grad = upstream[:, mine].astype(F32) + scale * vec[PRE_GAIN, mine] * dn - s * factor
            half_o[:, cols] = grad.astype(BF16)
        yb_g[...] = dot(r.hot_t[...], half_o[...]).astype(BF16)
        send_back("back_g", yb_g, r.back_g)

    def finish_grad():
        await_bytes(semaphore(rs, "back_g"), r.back_g.at[pl.ds(0, ROWS - PER)])
        r.res_g[...] = dot(r.send_hot_t[...], r.back_g[...]).astype(BF16)
        stores.append(store(r.res_g, r.o_hid, len(UNITS) + 2))

    lasts = pl.ds(CH, 256)

    def small_tensor():
        flying["small"] = send(small.at[:, lasts], r.sm_y, other)

    def small_tensor_end():
        copy = flying["small"]
        copy.wait_send()
        copy.wait_recv()
        keep_rows = lax.broadcasted_iota(I32, (8, 256), 0) < 5
        small[:, lasts] = small[:, lasts] + jnp.where(keep_rows, r.sm_y[...], 0.0)

    partners = [sibling, across, near, facing]

    def small_start(n):
        flying[n] = send(small, r.sm_a[n], partners[n])

    def small_end(n):
        flying[n].wait_send()
        flying[n].wait_recv()
        small[...] = small[...] + r.sm_a[n][...]

    gated_part(0, 2)
    swap_near("gate", 0, 256)
    gated_part(2, 4)
    swap("gate", 256, 256)
    gated_part(4, 8)
    gated_part(8, 12)
    swap("gate", 512, 256)
    units[0].go(0)
    project_other()
    swap("gate", 1024, 512)
    relay("gate", 256)
    mixer_part(0, 4)
    units[1].go(0)
    relay("gate", 512)
    project_own()
    units[0].go(1)
    swap("value", 0, 512)
    swap("out", 1024, 512)
    units[2].go(0)
    relay("gate", 1024)
    swap("gate", 768, 256)
    up_swap()
    return_out()
    mixer_part(4, 8)
    units[2].go(1)
    relay("value", 0)
    units[4].go(0)
    mixer_part(8, 12)
    units[8].go(0)
    states_back()
    relay("gate", 768)
    units[4].go(1)
    normed_other()
    units[1].go(1)
    units[2].go(2)
    swap("value", 1024, 512)
    units[0].go(2)
    units[8].go(1)
    units[2].go(3)
    relay("out", 1024)
    swap("value", 512, 512)
    swap("out", 512, 512)
    units[3].go(0)
    units[8].go(2)
    add_states()
    units[1].go(2)
    normed_own()
    swap("misc", 0, 256)
    units[7].go(0)
    swap("out", 0, 512)
    units[4].go(2)
    units[4].go(3)
    return_grad()
    units[0].go(3)
    units[8].go(3)
    relay("value", 1024)
    units[7].go(1)
    units[7].go(2)
    units[3].go(1)
    units[10].go(0)
    relay("value", 512)
    units[3].go(2)
    small_tensor()
    units[9].go(0)
    relay("out", 512)
    units[10].go(1)
    units[9].go(1)
    units[7].go(3)
    units[2].go(4)
    finish_out()
    units[6].go(0)
    small_tensor_end()
    relay("misc", 0)
    units[4].go(4)
    units[0].go(4)
    small_start(0)
    units[9].go(2)
    units[11].go(0)
    units[3].go(3)
    units[8].go(4)
    units[6].go(1)
    small_end(0)
    relay("out", 0)
    small_start(1)
    units[10].go(2)
    units[6].go(2)
    units[10].go(3)
    units[9].go(3)
    units[7].go(4)
    units[3].go(4)
    units[5].go(0)
    units[6].go(3)
    units[1].go(3)
    units[11].go(1)
    units[0].go(5)
    units[11].go(2)
    units[9].go(4)
    units[10].go(4)
    small_end(1)
    units[5].go(1)
    small_start(2)
    units[5].go(2)
    units[1].go(4)
    units[11].go(3)
    units[5].go(3)
    small_end(2)
    small_start(3)
    finish_grad()
    units[11].go(4)
    units[6].go(4)
    units[5].go(4)
    small_end(3)
    stores.append(store(small, r.o_small, len(UNITS)))
    for copy in started:
        copy.wait_send()
    assert len(taken[0]) == SENDS and len(taken[1]) == ARRIVALS
    for sem, ref in leaving:
        await_bytes(sem, ref)
    for copy in stores:
        copy.wait()


def scratch():
    vmem, dma = pltpu.VMEM, pltpu.SemaphoreType.DMA
    square, wide = (ROWS, ROWS), (ROWS, CH)
    def rows(dtype, width):
        return vmem((ROWS, width), dtype)

    return dict(
        wg=vmem((FULL, CH), BF16),
        wv=vmem((FULL, CH), BF16),
        wo=vmem((CH, FULL), BF16),
        pair=vmem((3, FULL, 2, 128), BF16),
        send_hot_t=vmem(square, BF16),
        hot=vmem(square, BF16),
        hot_t=vmem(square, BF16),
        sb_h=rows(BF16, HALF),
        rb_h=rows(BF16, HALF),
        sb_i=vmem((PEERS, 1, 128), F32),
        rb_i=vmem((PEERS, 1, 128), F32),
        sb_g=rows(BF16, HALF),
        rb_g=rows(BF16, HALF),
        yb_h=rows(BF16, HALF),
        yb_g=rows(BF16, HALF),
        half_in=rows(BF16, HALF),
        dhalf_in=rows(BF16, HALF),
        back_o=rows(BF16, HALF),
        back_g=rows(BF16, HALF),
        masks=vmem((3, ROWS, 128), F32),
        linked=vmem(square, F32),
        linked_t=vmem(square, F32),
        scores=vmem(square, F32),
        scores_t=vmem(square, F32),
        dst_acc=vmem(square, F32),
        small=vmem((8, CH + 256), F32),
        params_v=[
            vmem((4, CH), BF16),
            vmem((4, 256), BF16),
            vmem((HEADS, FULL), BF16),
            vmem((CH,), BF16),
            vmem((CH,), BF16),
            vmem((FULL,), BF16),
            vmem((256,), BF16),
            vmem((HEADS,), F32),
            vmem((HEADS,), F32),
        ],
        res_o=rows(BF16, HALF),
        res_g=rows(BF16, HALF),
        kept=[vmem((SHARE, width), F32) for _, _, width, _ in UNITS],
        vec=vmem((16, CH), F32),
        wsp=vmem((128, FULL), BF16),
        wst=vmem((FULL, 256), BF16),
        cum2_t=vmem((128, ROWS), F32),
        cum2_ls=vmem((128, ROWS), F32),
        stream=vmem(wide, BF16),
        upstream=vmem(wide, BF16),
        normed=vmem(wide, BF16),
        vconv=vmem(wide, BF16),
        gate_pre=vmem(wide, F32),
        value_pre=vmem(wide, F32),
        mixed=vmem(wide, F32),
        d_scaled=vmem(wide, F32),
        state_pre=rows(F32, 256),
        d_state=rows(F32, 256),
        sconv=rows(BF16, 256),
        st_low=rows(BF16, 256),
        st_out=rows(BF16, 128),
        st_in=rows(BF16, 128),
        scaled4=vmem((4 * ROWS, CH), BF16),
        gate4=vmem((4 * ROWS, CH), BF16),
        value4=vmem((4 * ROWS, CH), BF16),
        misc4=vmem((4 * ROWS, 256), BF16),
        norm_t=vmem((4, SHARE, 4 * ROWS), BF16),
        up_t=vmem((4, SHARE, 4 * ROWS), BF16),
        norm_f=vmem((4, 4, SHARE, ROWS), BF16),
        up_f=vmem((4, 4, SHARE, ROWS), BF16),
        nscale=rows(F32, 128),
        acc1=rows(F32, 128),
        acc2=rows(F32, 128),
        dcol=rows(F32, 128),
        dsd=rows(F32, 128),
        step_in=rows(F32, 128),
        step=rows(F32, 128),
        cum2=rows(F32, 128),
        ex_a=vmem((8, ROWS), F32),
        ex_b=vmem((8, ROWS), F32),
        ex_c=vmem((8, ROWS), F32),
        ex_d=vmem((8, ROWS), F32),
        sm_y=vmem((8, 256), F32),
        sm_a=[vmem((8, CH + 256), F32) for _ in range(4)],
        part=[vmem((4, 2 if kind == "z" else 1, SHARE, width), BF16) for _, _, width, kind in UNITS],
        zbuf=[vmem((5, 2 if kind == "z" else 1, SHARE, width), BF16) for _, _, width, kind in UNITS],
        over_out=vmem((SHARE, 256), BF16),
        over_in=vmem((SHARE, 256), BF16),
        norm_o=vmem((4, SHARE, 2 * ROWS), BF16),
        ss=dma((SENDS,)),
        rs=dma((ARRIVALS,)),
        ls=dma((16,)),
        os=dma((len(UNITS) + 3,)),
    )


SENDS = 30 + len(UNITS)
ARRIVALS = 74 + 5 * len(UNITS)


def listed(v):
    return v if isinstance(v, list) else [v]


def finish_body(*refs):
    wo, gate, value, misc, small, out, hid = refs[:7]
    outs, scratch_refs = refs[7:22], refs[22:]
    misc_v, small_v, *held = scratch_refs[:-1]
    sems = scratch_refs[-1]
    (
        out_v, hid_v, pre, in_v, state, step, cx, cxb, cb, cbb, bias, log, skip, gain, wo_v
    ) = held

    def move(src, dst, n):
        copy = pltpu.make_async_copy(src, dst, sems.at[n])
        copy.start()
        return copy

    moves = (
        (small, small_v),
        (misc, misc_v),
        (gate, in_v.at[:, 0, :]),
        (value, in_v.at[:, 1, :]),
        (wo, wo_v),
        (out, out_v),
        (hid, hid_v),
    )
    loads = [move(src, dst, n) for n, (src, dst) in enumerate(moves)]
    stores = []

    def keep(*which):
        for n in which:
            stores.append(move(held[n], outs[n], len(moves) + n))

    loads[0].wait()
    pre[...] = small_v[7, 0:HALF]
    cx[...] = small_v[0:4, 0:CH]
    cxb[...] = small_v[4, 0:CH]
    cb[...] = small_v[0:4, CH:]
    cbb[...] = small_v[4, CH:]
    bias[...] = small_v[5, CH : CH + HEADS]
    log[...] = small_v[6, CH : CH + HEADS]
    skip[...] = small_v[6, CH + 128 : CH + 128 + HEADS]
    gain[...] = small_v[5, 0:CH]
    keep(2, 6, 7, 8, 9, 10, 11, 12, 13)
    loads[1].wait()
    state[...] = misc_v[:, 0:128]
    step[...] = misc_v[:, 128:256].T[0:HEADS]
    keep(4, 5)
    loads[2].wait()
    loads[3].wait()
    keep(3)
    for n, which in ((4, 14), (5, 0), (6, 1)):
        loads[n].wait()
        keep(which)
    for copy in stores:
        copy.wait()


def one_kernel(
    hidden_in,
    out_grad,
    seq_lengths,
    deal_to,
    pre_gain,
    w_in,
    w_state,
    w_step,
    conv_x,
    conv_x_bias,
    conv_bc,
    conv_bc_bias,
    step_bias,
    a_log,
    skip,
    norm_gain,
    w_out,
):
    inputs = dict(
        hid=hidden_in,
        ogr=out_grad,
        lens=seq_lengths,
        deal=deal_to.reshape(1, ROWS),
        skip=skip,
        w_in=w_in,
        wo_hbm=w_out,
        wst_hbm=w_state,
        params=[
            conv_x,
            conv_bc,
            w_step.T,
            conv_x_bias,
            norm_gain,
            pre_gain,
            conv_bc_bias,
            step_bias,
            a_log,
        ],
    )
    in_vmem = pl.BlockSpec(memory_space=pltpu.VMEM)
    places = dict(lens=pltpu.SMEM, skip=pltpu.SMEM, deal=pltpu.VMEM)
    f32_out = partial(jax.ShapeDtypeStruct, dtype=F32)
    half = jax.ShapeDtypeStruct((ROWS, HALF), BF16)
    outputs = dict(
        o_wo=f32_out((SHARE, CH)),
        o_gate=f32_out((SHARE, CH)),
        o_value=f32_out((SHARE, CH)),
        o_misc=f32_out((SHARE, 256)),
        o_small=f32_out((8, CH + 256)),
        o_out=half,
        o_hid=half,
    )
    room = scratch()
    flat = [ref for shape in room.values() for ref in listed(shape)]
    made = pl.pallas_call(
        partial(block_body, {**inputs, **outputs, **room}),
        out_shape=list(outputs.values()),
        in_specs=[pl.BlockSpec(memory_space=places.get(n, pl.ANY)) for n, v in inputs.items() for _ in listed(v)],
        out_specs=[pl.BlockSpec(memory_space=pl.ANY)] * len(outputs),
        scratch_shapes=flat,
        compiler_params=pltpu.CompilerParams(
            collective_id=0, has_side_effects=True, vmem_limit_bytes=VMEM_BYTES
        ),
        name="block",
    )(*(v for value in inputs.values() for v in listed(value)))
    shapes = [(HALF,), (SHARE, 2, CH), (SHARE, 128), (HEADS, SHARE), (4, CH), (CH,), (4, 256), (256,)]
    shapes += [(HEADS,)] * 3 + [(CH,), (SHARE, CH)]
    any_place = pl.BlockSpec(memory_space=pl.ANY)
    made_shapes = [half, half, *(f32_out(s) for s in shapes)]
    results = pl.pallas_call(
        finish_body,
        out_shape=made_shapes,
        in_specs=[any_place] * len(made),
        out_specs=[any_place] * len(made_shapes),
        scratch_shapes=[
            pltpu.VMEM((SHARE, 256), F32),
            pltpu.VMEM((8, CH + 256), F32),
            *(pltpu.VMEM(s.shape, s.dtype) for s in made_shapes),
            pltpu.SemaphoreType.DMA((len(made) + len(made_shapes),)),
        ],
        compiler_params=pltpu.CompilerParams(vmem_limit_bytes=VMEM_BYTES),
        name="finish",
    )(*made)
    return (*results[:5], results[5].T, *results[6:14], results[14].T)


VMEM_BYTES = 65_400_000


def fits(mesh, args):
    return mesh.shape["dp"] == PEERS and mesh.shape["tensor"] == 2 and args[0].shape == (PEERS * ROWS, FULL)


def solution(mesh):
    in_specs = (
        P("dp", "tensor"),
        P("dp", "tensor"),
        P("dp", None),
        P("dp"),
        P(),
        P(None, None, "tensor"),
        P(),
        P(None, "tensor"),
        P(None, "tensor"),
        P("tensor"),
        P(),
        P(),
        P("tensor"),
        P("tensor"),
        P("tensor"),
        P("tensor"),
        P("tensor", None),
    )
    out_specs = (
        P("dp", "tensor"),
        P("dp", "tensor"),
        P("tensor"),
        P("dp", None, "tensor"),
        P("dp", "tensor"),
        P("dp", "tensor"),
        P(None, "tensor"),
        P("tensor"),
        P(),
        P(),
        P("tensor"),
        P("tensor"),
        P("tensor"),
        P("tensor"),
        P("tensor", "dp"),
    )

    def whole(*args):
        local = one_kernel if fits(mesh, args) else shards
        mapped = jax.shard_map(
            local, mesh=mesh, in_specs=in_specs, out_specs=out_specs, check_vma=False
        )
        return mapped(*args)

    return whole
```

```python
from functools import partial
from types import SimpleNamespace

import jax
import jax.numpy as jnp
from jax import lax
from jax.experimental import pallas as pl
from jax.experimental.pallas import tpu as pltpu
from jax.sharding import PartitionSpec as P

D = 1536
GROUP = 256
INNER = 3072


norm_eps = 1e-05


def segment_ids(lengths, row_count):
    index = jnp.arange(lengths.shape[0])
    ends = jnp.sum(jnp.where(index[None, :] <= index[:, None], lengths[None, :], 0), axis=1)
    position = jnp.arange(row_count, dtype=jnp.int32)
    return jnp.sum((position[:, None] >= ends[None, :]).astype(jnp.int32), axis=1, dtype=jnp.int32)


def causal_conv(signal, kernel, kernel_bias, segment):
    width = kernel.shape[0]
    total = kernel_bias[None, :] + kernel[width - 1][None, :] * signal
    for offset in range(1, width):
        moved = jnp.concatenate(
            [jnp.zeros((offset, signal.shape[1]), signal.dtype), signal[:-offset]], axis=0
        )
        earlier = jnp.concatenate([jnp.full((offset,), -1, jnp.int32), segment[:-offset]])
        inside = (earlier == segment).astype(signal.dtype)
        total = total + kernel[width - 1 - offset][None, :] * moved * inside[:, None]
    return total


def state_space(xval, b_rows, c_rows, step, decay, segment):
    highest = lax.Precision.HIGHEST
    blocks = xval.shape[0] // GROUP
    head_count = xval.shape[1]
    x_block = xval.reshape(blocks, GROUP, head_count, xval.shape[2])
    b_block = b_rows.reshape(blocks, GROUP, b_rows.shape[1])
    c_block = c_rows.reshape(blocks, GROUP, c_rows.shape[1])
    step_block = step.reshape(blocks, GROUP, head_count).transpose(0, 2, 1)
    rate_block = step_block * decay[None, :, None]
    seg_block = segment.reshape(blocks, GROUP)
    before = jnp.concatenate([jnp.full((1,), -1, jnp.int32), segment[:-1]]).reshape(blocks, GROUP)[
        :, 0
    ]
    lower_mask = jnp.tril(jnp.ones((GROUP, GROUP), dtype=bool))
    cumulative = jnp.einsum("chj,ij->chi", rate_block, lower_mask.astype(jnp.float32), precision=highest)
    linked = (seg_block[:, :, None] == seg_block[:, None, :]) & lower_mask[None]
    spread = cumulative[:, :, :, None] - cumulative[:, :, None, :]
    weight = jnp.exp(jnp.where(linked[:, None], spread, -10000.0))
    scores = jnp.einsum("cin,cjn->cij", c_block, b_block, precision=highest)
    mixing = weight * scores[:, None] * step_block[:, :, None, :]
    inside_out = jnp.einsum("chij,cjhp->cihp", mixing, x_block, precision=highest)
    final_cum = cumulative[:, :, -1]
    last_same = (seg_block == seg_block[:, -1:]).astype(jnp.float32)
    tail_weight = jnp.exp(final_cum[:, :, None] - cumulative) * last_same[:, None, :] * step_block
    fresh_state = jnp.einsum("chj,cjhp,cjn->chpn", tail_weight, x_block, b_block, precision=highest)
    carried = jnp.zeros(fresh_state.shape[1:], jnp.float32)
    entering = []
    entering.append(carried)
    entering = jnp.stack(entering)
    first_same = (seg_block == before[:, None]).astype(jnp.float32)
    head_decay = jnp.exp(cumulative) * first_same[:, None, :]
    carried_out = jnp.einsum("chi,cin,chpn->cihp", head_decay, c_block, entering, precision=highest)
    return (inside_out + carried_out).reshape(xval.shape)


def pre_norm(stream, gain):
    return stream * lax.rsqrt(jnp.mean(stream * stream, axis=1, keepdims=True) + norm_eps) * gain


def conv_piece(value_pre, state_pre, conv_x, conv_x_bias, conv_bc, conv_bc_bias, segment):
    value_conv = jax.nn.silu(causal_conv(value_pre, conv_x, conv_x_bias, segment))
    state_conv = jax.nn.silu(causal_conv(state_pre, conv_bc, conv_bc_bias, segment))
    return (value_conv, state_conv)


def mixer_piece(value_conv, state_conv, step_pre, step_bias, a_log, skip, segment):
    head_count = step_bias.shape[0]
    row_count = value_conv.shape[0]
    heads_in = value_conv.reshape(row_count, head_count, value_conv.shape[1] // head_count)
    step = jax.nn.softplus(step_pre + step_bias)
    decay = -jnp.exp(a_log)
    half_state = state_conv.shape[1] // 2
    mixed = state_space(
        heads_in, state_conv[:, :half_state], state_conv[:, half_state:], step, decay, segment
    )
    return (mixed + skip[None, :, None] * heads_in).reshape(row_count, value_conv.shape[1])


def rounded(values):
    return lax.optimization_barrier(values.astype(jnp.bfloat16)).astype(jnp.float32)


def shards(
    hidden_in,
    out_grad,
    seq_lengths,
    deal_to,
    pre_gain,
    w_in,
    w_state,
    w_step,
    conv_x,
    conv_x_bias,
    conv_bc,
    conv_bc_bias,
    step_bias,
    a_log,
    skip,
    norm_gain,
    w_out,
):
    dp_count = lax.axis_size("dp")
    row_count = hidden_in.shape[0]
    per_peer = row_count // dp_count
    feat_half = hidden_in.shape[1]
    tensor_index = lax.axis_index("tensor")
    send_order = jnp.argsort(deal_to)
    back_order = jnp.argsort(send_order)
    sent_in = hidden_in[send_order].reshape(dp_count, per_peer, feat_half)
    sent_grad = out_grad[send_order].reshape(dp_count, per_peer, feat_half)
    got_in, got_grad = (
        lax.all_to_all(sent_in, "dp", split_axis=0, concat_axis=0, tiled=True),
        lax.all_to_all(sent_grad, "dp", split_axis=0, concat_axis=0, tiled=True),
    )
    got_ids = lax.all_to_all(
        deal_to[send_order].reshape(dp_count, per_peer),
        "dp",
        split_axis=0,
        concat_axis=0,
        tiled=True,
    )
    dealt_slot = got_ids.reshape(row_count) % row_count
    settle_order = jnp.argsort(dealt_slot)
    dealt_half = got_in.reshape(row_count, feat_half)[settle_order]
    grad_half = got_grad.reshape(row_count, feat_half)[settle_order]
    full_in, grad_full = (
        lax.all_gather(dealt_half, "tensor", axis=1, tiled=True),
        lax.all_gather(grad_half, "tensor", axis=1, tiled=True),
    )
    segment = segment_ids(seq_lengths[0], row_count)
    stream = full_in.astype(jnp.float32)
    normed_f, norm_pull = jax.vjp(pre_norm, stream, pre_gain.astype(jnp.float32))
    normed = normed_f.astype(jnp.bfloat16)
    inner_half = w_in.shape[2]
    w_pair = w_in.reshape(w_in.shape[0], 2 * inner_half)
    proj_pair = jnp.dot(normed, w_pair, preferred_element_type=jnp.float32)
    gate_pre = proj_pair[:, :inner_half]
    value_pre = proj_pair[:, inner_half:]
    state_pre = jnp.dot(normed, w_state, preferred_element_type=jnp.float32)
    step_pre = jnp.dot(normed, w_step, preferred_element_type=jnp.float32)
    conv_args = (
        value_pre,
        state_pre,
        conv_x.astype(jnp.float32),
        conv_x_bias.astype(jnp.float32),
        conv_bc.astype(jnp.float32),
        conv_bc_bias.astype(jnp.float32),
    )
    (value_conv_f, state_conv_f), conv_pull = jax.vjp(
        partial(conv_piece, segment=segment), *conv_args
    )
    value_conv = rounded(value_conv_f)
    state_conv = rounded(state_conv_f)
    mixed, mixer_pull = jax.vjp(
        partial(mixer_piece, segment=segment),
        value_conv,
        state_conv,
        step_pre,
        step_bias,
        a_log,
        skip,
    )
    silu_gate = jax.nn.silu(gate_pre)
    gated = mixed * silu_gate
    total_squares = lax.psum(jnp.sum(gated * gated, axis=1), "tensor")
    inverse = lax.rsqrt(total_squares / INNER + norm_eps)
    gain_f = norm_gain.astype(jnp.float32)
    scaled = (gated * inverse[:, None] * gain_f).astype(jnp.bfloat16)
    partial_out = jnp.dot(scaled, w_out, preferred_element_type=jnp.float32)
    branch = lax.psum_scatter(partial_out, "tensor", scatter_dimension=1, tiled=True)
    result = (dealt_half.astype(jnp.float32) + branch).astype(jnp.bfloat16)
    back_out = lax.all_to_all(
        result[dealt_slot].reshape(dp_count, per_peer, feat_half),
        "dp",
        split_axis=0,
        concat_axis=0,
        tiled=True,
    )
    output = back_out.reshape(row_count, feat_half)[back_order]
    g_w_out = jnp.einsum("ti,td->id", scaled, grad_full, preferred_element_type=jnp.float32)
    d_scaled = jnp.einsum("td,id->ti", grad_full, w_out, preferred_element_type=jnp.float32)
    weighted = d_scaled * gain_f
    g_norm_gain = jnp.sum(d_scaled * gated * inverse[:, None], axis=0)
    cross_sum = lax.psum(jnp.sum(weighted * gated, axis=1), "tensor")
    d_gated = (
        inverse[:, None] * weighted
        - gated * (inverse * inverse * inverse / INNER * cross_sum)[:, None]
    )
    d_mixed = d_gated * silu_gate
    sigmoid_gate = jax.nn.sigmoid(gate_pre)
    d_gate = d_gated * mixed * (sigmoid_gate * (1.0 + gate_pre * (1.0 - sigmoid_gate)))
    d_value_conv, d_state_part, d_step_pre, g_step_bias, g_a_log, g_skip = mixer_pull(d_mixed)
    d_state_conv = lax.psum(d_state_part, "tensor")
    d_value_pre, d_state_pre, g_conv_x, g_conv_x_bias, g_conv_bc, g_conv_bc_bias = conv_pull(
        (d_value_conv, d_state_conv)
    )
    d_pair = jnp.concatenate([d_gate, d_value_pre], axis=1).astype(jnp.bfloat16)
    d_state_low = d_state_pre.astype(jnp.bfloat16)
    d_step_low = d_step_pre.astype(jnp.bfloat16)
    state_share = w_state.shape[1] // lax.axis_size("tensor")
    own_state = lax.dynamic_slice_in_dim(d_state_low, tensor_index * state_share, state_share, 1)
    own_weight = lax.dynamic_slice_in_dim(w_state, tensor_index * state_share, state_share, 1)
    g_w_in = jnp.einsum("td,tc->dc", normed, d_pair, preferred_element_type=jnp.float32).reshape(
        w_in.shape
    )
    g_w_state = jnp.einsum("td,tc->dc", normed, own_state, preferred_element_type=jnp.float32)
    g_w_step = jnp.einsum("td,th->dh", normed, d_step_low, preferred_element_type=jnp.float32)
    d_normed = jnp.einsum("tc,dc->td", d_pair, w_pair, preferred_element_type=jnp.float32)
    d_normed = d_normed + jnp.einsum(
        "th,dh->td", d_step_low, w_step, preferred_element_type=jnp.float32
    )
    d_normed = d_normed + jnp.einsum(
        "tc,dc->td", own_state, own_weight, preferred_element_type=jnp.float32
    )
    normed_share = lax.psum_scatter(d_normed, "tensor", scatter_dimension=1, tiled=True)
    row_scale = lax.rsqrt(jnp.mean(stream * stream, axis=1) + norm_eps)
    stream_share = dealt_half.astype(jnp.float32)
    gain_share = lax.dynamic_slice_in_dim(
        pre_gain.astype(jnp.float32), tensor_index * feat_half, feat_half, 0
    )
    row_cross = lax.psum(jnp.sum(gain_share * normed_share * stream_share, axis=1), "tensor")
    d_share = (
        row_scale[:, None] * gain_share * normed_share
        - stream_share * (row_scale * row_scale * row_scale / D * row_cross)[:, None]
    )
    g_pre_gain = jnp.sum(normed_share * stream_share * row_scale[:, None], axis=0)
    d_input = (d_share + grad_half.astype(jnp.float32)).astype(jnp.bfloat16)
    back_grad = lax.all_to_all(
        d_input[dealt_slot].reshape(dp_count, per_peer, feat_half),
        "dp",
        split_axis=0,
        concat_axis=0,
        tiled=True,
    )
    hidden_grad = back_grad.reshape(row_count, feat_half)[back_order]
    small = lax.psum(
        (
            g_pre_gain,
            g_conv_x,
            g_conv_x_bias,
            g_conv_bc,
            g_conv_bc_bias,
            g_step_bias,
            g_a_log,
            g_skip,
            g_norm_gain,
        ),
        "dp",
    )
    g_in_part, g_state_part, g_step_part, g_w_out_part = (
        lax.psum_scatter(g_w_in, "dp", scatter_dimension=0, tiled=True),
        lax.psum_scatter(g_w_state, "dp", scatter_dimension=0, tiled=True),
        lax.psum_scatter(g_w_step, "dp", scatter_dimension=0, tiled=True),
        lax.psum_scatter(g_w_out, "dp", scatter_dimension=1, tiled=True),
    )
    return (
        output,
        hidden_grad,
        small[0],
        g_in_part,
        g_state_part,
        g_step_part,
        small[1],
        small[2],
        small[3],
        small[4],
        small[5],
        small[6],
        small[7],
        small[8],
        g_w_out_part,
    )


F32, BF16, I32 = jnp.float32, jnp.bfloat16, jnp.int32
MESH = pl.DeviceIdType.MESH
LOG2E = 1.4426950408889634
HIGHEST = lax.Precision.HIGHEST

ROWS = 256
FULL = 1536
HALF = 768
CH = 1536
HEADS = 24
PEERS = 16
PER = ROWS // PEERS
SHARE = FULL // PEERS

X_BIAS, NORM_GAIN, PRE_GAIN, BC_BIAS, STEP_BIAS, A_LOG = (slice(n, n + 1) for n in range(4, 10))

UNITS = (
    ("gate", 0, 256, "z"),
    ("gate", 256, 256, "g"),
    ("gate", 512, 256, "g"),
    ("gate", 768, 256, "g"),
    ("gate", 1024, 512, "g"),
    ("out", 0, 512, "g"),
    ("out", 512, 512, "g"),
    ("out", 1024, 512, "g"),
    ("value", 0, 512, "g"),
    ("value", 512, 512, "g"),
    ("value", 1024, 512, "g"),
    ("misc", 0, 256, "g"),
)


def dot_t(a, b):
    return lax.dot_general(a, b, (((1,), (1,)), ((), ())), preferred_element_type=F32)


def dot(a, b):
    return jnp.dot(a, b, preferred_element_type=F32)


def sigmoid(v):
    return 1.0 / (1.0 + jnp.exp(-v))


def block_at(n, width):
    return pl.ds(pl.multiple_of(n * width, width), width)


class Sent:
    def __init__(self, copy):
        self.copy, self.gone, self.here = copy, False, False

    def wait_recv(self):
        self.copy.wait_recv()
        self.here = True

    def wait_send(self):
        if not self.gone:
            self.copy.wait_send()
        self.gone = True


def await_bytes(sem, ref):
    pltpu.make_async_copy(ref, ref, sem).wait()


def block_body(room, *refs):
    left = list(refs)

    def take(shape):
        return [left.pop(0) for _ in shape] if isinstance(shape, list) else left.pop(0)

    r = SimpleNamespace(**{name: take(shape) for name, shape in room.items()})
    lens, deal_ref, vec = r.lens, r.deal, r.vec
    wst, wsp = r.wst, r.wsp
    ss, rs, ls = r.ss, r.rs, r.ls
    me, side = lax.axis_index("dp"), lax.axis_index("tensor")
    core = lax.rem(me, 2)
    xpos = lax.rem(me // 2, 2)
    zpos = me // 4
    sibling = (zpos * 4 + xpos * 2 + (1 - core), side)
    across = (zpos * 4 + (1 - xpos) * 2 + core, side)
    z_side = zpos // 2
    z_outer, z_inner = 3 * z_side, 1 + z_side
    far_outer, far_inner = 3 - z_outer, 3 - z_inner
    is_outer = zpos == z_outer
    is_inner = zpos == z_inner

    def at_z(z):
        return (z * 4 + xpos * 2 + core, side)

    near = at_z(z_outer + z_inner - zpos)
    facing = at_z(3 - zpos)
    other = (me, 1 - side)
    own_cols = pl.ds(pl.multiple_of(side * HALF, HALF), HALF)
    other_cols = pl.ds(pl.multiple_of((1 - side) * HALF, HALF), HALF)

    started, taken, leaving = [], ({}, {}), []

    def semaphore(sems, key):
        count = taken[sems is rs]
        return sems.at[count.setdefault(("own", len(count)) if key is None else key, len(count))]

    def group(key, ref):
        leaving.append((semaphore(ss, key), ref))
        return key

    def send(src, dst, device, by=None, gone=None, came=None):
        copy = pltpu.make_async_remote_copy(
            src_ref=src,
            dst_ref=dst,
            send_sem=semaphore(ss, gone),
            recv_sem=semaphore(rs, came),
            device_id=device,
            device_id_type=MESH,
        )
        if by is None:
            copy.start()
        else:
            pl.when(by)(copy.start)
        one = Sent(copy)
        if gone is None:
            started.append(one)
        return one

    def load(src, dst, n):
        copy = pltpu.make_async_copy(src, dst, ls.at[n])
        copy.start()
        return copy

    def pair_load(n, at):
        cols = pl.ds(pl.multiple_of(n * 128, 128), 128)
        return pltpu.make_async_copy(r.w_in.at[:, :, cols], r.pair.at[at], ls.at[at])

    hid_load = load(r.hid, r.half_in, 3)
    pair_load(0, 0).start()
    pair_load(1, 1).start()
    pair_load(2, 2).start()
    ogr_load = load(r.ogr, r.dhalf_in, 4)
    small_loads = [load(src, dst, 5 + n) for n, (src, dst) in enumerate(zip(r.params, r.params_v))]
    wst_load = load(r.wst_hbm, r.wst, 14)
    wo_load = load(r.wo_hbm, r.wo, 15)

    barrier = pltpu.get_barrier_semaphore()
    for k in range(1, PEERS):
        pl.semaphore_signal(
            barrier, inc=1, device_id=(lax.rem(me + k, PEERS), side), device_id_type=MESH
        )
    pl.semaphore_signal(barrier, inc=1, device_id=other, device_id_type=MESH)

    i0 = lax.broadcasted_iota(I32, (ROWS, ROWS), 0)
    i1 = lax.broadcasted_iota(I32, (ROWS, ROWS), 1)
    deal = deal_ref[...]
    dest = lax.shift_right_logical(deal, 8)
    slot = jnp.bitwise_and(deal, ROWS - 1)
    member = (dest == lax.broadcasted_iota(I32, (PEERS, ROWS), 0)).astype(F32)
    before = dot(member.astype(BF16), (i0 < i1).astype(F32).astype(BF16))
    rank = jnp.sum(member * before, axis=0, keepdims=True)
    place = dest.astype(F32) * PER + rank
    hit = i0.astype(F32) == place
    to_send = hit.astype(F32)
    send_hot = to_send.astype(BF16)
    ident = jnp.sum(to_send * slot.astype(F32), axis=1, keepdims=True)
    sb_h, sb_g, rb_h, rb_g, yb_h, yb_g = r.sb_h, r.sb_g, r.rb_h, r.rb_g, r.yb_h, r.yb_g
    hid_load.wait()
    sb_h[...] = dot(send_hot, r.half_in[...]).astype(BF16)
    row_w = lax.broadcasted_iota(I32, (ROWS, 128), 0)
    lane_w = lax.broadcasted_iota(I32, (ROWS, 128), 1)
    in_place = lax.rem(row_w, PER) == lane_w
    spread = jnp.where(in_place, ident, 0.0).astype(BF16)
    row_n = lax.broadcasted_iota(I32, (PEERS, ROWS), 0)
    lane_n = lax.broadcasted_iota(I32, (PEERS, ROWS), 1)
    gather_ids = (row_n == lane_n // PER).astype(F32).astype(BF16)
    r.sb_i[...] = dot(gather_ids, spread).reshape(PEERS, 1, 128)

    pl.semaphore_wait(barrier, PEERS)

    def rows_of(device):
        return pl.ds(pl.multiple_of(device * PER, PER), PER)

    line = (zpos, z_outer + z_inner - zpos, lax.rem(zpos + 2, 4), 3 - zpos)

    def away(dz, dx, dc):
        return line[dz] * 4 + lax.rem(xpos + dx, 2) * 2 + lax.rem(core + dc, 2)

    steps = [(dz, dx, dc) for dz in (2, 3, 1, 0) for dx in (0, 1) for dc in (0, 1)]

    def deal(dz, src, dst, gone, came, rows=rows_of):
        for step in steps:
            if step[0] == dz and step != (0, 0, 0):
                to = away(*step)
                send(src.at[rows(to)], dst.at[rows(me)], (to, side), gone=gone, came=came)

    def pass_rows(name, first, count, buf, dst):
        rows = pl.ds(pl.multiple_of(first, count), count)
        send(buf.at[rows], dst.at[rows], other, gone=(name, 9), came=(name, 9))

    def pass_group(name, dz, buf, dst):
        if dz < 2:
            await_bytes(semaphore(rs, (name, dz)), buf.at[pl.ds(0, 4 * PER - (PER if dz == 0 else 0))])
            pass_rows(name, line[dz] * 4 * PER, 4 * PER, buf, dst)
        else:
            for dx in range(2):
                for dc in range(2):
                    await_bytes(semaphore(rs, (name, (dz, dx, dc))), buf.at[pl.ds(0, PER)])
                pass_rows(name, line[dz] * 4 * PER + lax.rem(xpos + dx, 2) * 2 * PER, 2 * PER, buf, dst)

    def wave(name, dz, src, dst):
        for step in steps:
            if step[0] == dz:
                to = away(*step)
                send(src.at[rows_of(to)], dst.at[rows_of(me)], (to, side), gone=(name, "wave", dz), came=(name, step))

    def wave_gone(name, dz, src):
        await_bytes(semaphore(ss, (name, "wave", dz)), src.at[pl.ds(0, 4 * PER)])

    def rest(name, src, dst):
        for dz in (1, 0):
            deal(dz, src, dst, name, (name, dz))
        group(name, src.at[pl.ds(0, 7 * PER)])

    def same(device):
        return device

    wave("hid", 3, sb_h, rb_h)
    rest("hid", sb_h, rb_h)
    for dz in (2, 3, 1, 0):
        deal(dz, r.sb_i, r.rb_i, "ids", "ids", same)
    group("ids", r.sb_i.at[pl.ds(0, PEERS - 1)])
    r.rb_i[me] = r.sb_i[me]
    rb_h[rows_of(me)] = sb_h[rows_of(me)]
    ogr_load.wait()
    sb_g[...] = dot(send_hot, r.dhalf_in[...]).astype(BF16)
    rb_g[rows_of(me)] = sb_g[rows_of(me)]
    r.send_hot_t[...] = to_send.T.astype(BF16)

    ends, total = [], 0
    for k in range(8):
        total = total + lens[0, k]
        ends.append(total)

    def seg_at(pos):
        out = jnp.zeros(pos.shape, I32)
        for e in ends:
            out = out + (pos >= e).astype(I32)
        return out

    row_col = lax.broadcasted_iota(I32, (ROWS, 128), 0)
    seg_here = seg_at(row_col)
    for o in range(1, 4):
        same = (seg_at(row_col - o) == seg_here) & (row_col >= o)
        r.masks[o - 1] = same.astype(F32)
    same = seg_at(i0) == seg_at(i1)
    r.linked[...] = (same & (i0 >= i1)).astype(F32)
    r.linked_t[...] = (same & (i0 <= i1)).astype(F32)
    r.small[...] = jnp.zeros((8, CH + 256), F32)
    for copy in small_loads:
        copy.wait()
    conv_x_v, conv_bc_v, w_step_v, *rows_v = r.params_v
    vec[...] = jnp.zeros((16, CH), F32)
    vec[0:4, :] = conv_x_v[...].astype(F32)
    for n, ref in enumerate(rows_v):
        vec[4 + n, 0 : ref.shape[0]] = ref[...].astype(F32)
    vec[12:16, 0:256] = conv_bc_v[...].astype(F32)
    wst_load.wait()
    wsp[...] = jnp.concatenate(
        [w_step_v[...].astype(F32), jnp.zeros((128 - HEADS, FULL), F32)], axis=0
    ).astype(BF16)
    r.dst_acc[...] = jnp.zeros((ROWS, ROWS), F32)
    r.dcol[...] = jnp.zeros((ROWS, 128), F32)
    r.dsd[...] = jnp.zeros((ROWS, 128), F32)

    picked = jnp.where(i0 < 128, 2 * i0, 2 * i0 - 255)
    apart = (picked == i1).astype(F32).astype(BF16)

    def take_apart(n):
        at = lax.rem(n, 3)
        pair_load(n, at).wait()
        cols = block_at(n, 128)
        flat = r.pair.at[at].reshape(2 * FULL, 128)
        for k in range(12):
            both = dot(apart, flat[k * 256 : (k + 1) * 256, :]).astype(BF16)
            r.wg[k * 128 : (k + 1) * 128, cols] = both[0:128]
            r.wv[k * 128 : (k + 1) * 128, cols] = both[128:256]

        @pl.when(n + 3 < 12)
        def _():
            pair_load(n + 3, at).start()

    group(("hid", 9), rb_h)
    group(("grad", 9), rb_g)
    pl.loop(0, 4)(take_apart)
    pass_group("hid", 0, rb_h, yb_h)
    wave_gone("hid", 3, sb_h)
    wave("hid", 2, sb_h, rb_h)
    pl.loop(4, 7)(take_apart)
    pass_group("hid", 1, rb_h, yb_h)
    pl.loop(7, 12)(take_apart)
    pass_group("hid", 3, rb_h, yb_h)
    await_bytes(semaphore(rs, "ids"), r.rb_i.at[pl.ds(0, PEERS - 1)])
    origin_row = lax.broadcasted_iota(I32, (ROWS, PEERS), 0) // PER
    fetch_ids = (origin_row == lax.broadcasted_iota(I32, (ROWS, PEERS), 1)).astype(F32).astype(BF16)
    ids = jnp.where(in_place, dot(fetch_ids, r.rb_i[...].reshape(PEERS, 128).astype(BF16)), 0.0)
    ids = jnp.broadcast_to(jnp.sum(ids, axis=1, keepdims=True), (ROWS, 128))
    r.hot_t[...] = (ids[:, 0:1] == i1.astype(F32)).astype(F32).astype(BF16)
    r.hot[...] = (ids.T[0:1, :] == i0.astype(F32)).astype(F32).astype(BF16)
    wave_gone("hid", 2, sb_h)
    wave("grad", 3, sb_g, rb_g)
    pass_group("hid", 2, rb_h, yb_h)
    rest("grad", sb_g, rb_g)
    stream, upstream, normed = r.stream, r.upstream, r.normed
    stream[:, own_cols] = dot(r.hot[...], rb_h[...]).astype(BF16)
    await_bytes(semaphore(rs, ("hid", 9)), yb_h)
    stream[:, other_cols] = dot(r.hot[...], yb_h[...]).astype(BF16)

    wave_gone("grad", 3, sb_g)
    wave("grad", 2, sb_g, rb_g)

    @pl.loop(0, 8)
    def _(n):
        rows = block_at(n, 32)
        s = stream[rows, :].astype(F32)
        scale = lax.rsqrt(jnp.sum(s * s, axis=1, keepdims=True) * (1.0 / FULL) + norm_eps)
        r.nscale[rows, :] = jnp.broadcast_to(scale, (32, 128))
        normed[rows, :] = (s * scale * vec[PRE_GAIN, :]).astype(BF16)

    here, beside, over, cross_over = (pl.ds(n * ROWS, ROWS) for n in range(4))
    diagonal = (zpos * 4 + (1 - xpos) * 2 + (1 - core), side)

    def flip(source, flipped, keep):
        for n in range(4):
            turned = source[:, n * 384 : (n + 1) * 384].astype(F32).T.astype(BF16)
            for i in range(4):
                flipped[n, i] = turned[i * SHARE : (i + 1) * SHARE]
        keep[:, :, here] = flipped[:, xpos * 2 + core]

    def share_early(flipped, keep):
        keep[:, :, here] = flipped[:, (1 - xpos) * 2 + core]
        send(flipped.at[:, (1 - xpos) * 2 + (1 - core)], keep.at[:, :, beside], sibling, gone="early", came="early")
        group("early", keep.at[:, :, beside])

    others, overs = pl.ds(ROWS, 3 * ROWS), pl.ds(2 * ROWS, 2 * ROWS)

    def share_flipped(name, flipped, keep, near_by):
        group(name, keep.at[:, :, others])
        for dx, dc, lanes, device in ((0, 1, beside, sibling), (1, 0, over, across), (1, 1, cross_over, diagonal)):
            place = lax.rem(xpos + dx, 2) * 2 + lax.rem(core + dc, 2)
            came = near_by if lanes is beside else name
            send(flipped.at[:, place], keep.at[:, :, lanes], device, gone=name, came=came)

    masks = r.masks

    def conv_at(signal, taps, bias):
        out = bias + taps[3] * signal
        for o in range(1, 4):
            out = out + taps[3 - o] * (pltpu.roll(signal, o, 0) * masks[o - 1])
        return out

    def conv_back(signal, taps, bias, grad):
        pre = conv_at(signal, taps, bias)
        s = sigmoid(pre)
        d_pre = grad * (s * (1.0 + pre * (1.0 - s)))
        sums = [None] * 4
        sums[3] = jnp.sum(d_pre * signal, axis=0, keepdims=True)
        d_signal = taps[3] * d_pre
        for o in range(1, 4):
            masked = d_pre * masks[o - 1]
            sums[3 - o] = jnp.sum(masked * pltpu.roll(signal, o, 0), axis=0, keepdims=True)
            d_signal = d_signal + taps[3 - o] * pltpu.roll(masked, ROWS - o, 0)
        return d_signal, sums, jnp.sum(d_pre, axis=0, keepdims=True)

    def taps_at(first, cols):
        return [vec[pl.ds(first + k, 1), cols] for k in range(4)]

    gate_pre, value_pre, vconv = r.gate_pre, r.value_pre, r.vconv
    def project(n):
        cols = block_at(n, 256)
        gate_pre[:, cols] = dot(normed[...], r.wg[:, cols])
        value_pre[:, cols] = dot(normed[...], r.wv[:, cols])

    def convolve(n):
        cols = block_at(n, 128)
        pre = conv_at(value_pre[:, cols], taps_at(0, cols), vec[X_BIAS, cols])
        vconv[:, cols] = (pre * sigmoid(pre)).astype(BF16)

    pl.loop(0, 6, unroll=3)(project)
    pass_group("grad", 0, rb_g, yb_g)
    pass_group("grad", 1, rb_g, yb_g)
    pl.loop(0, 12)(convolve)
    pass_group("grad", 3, rb_g, yb_g)

    state_pre, sconv = r.state_pre, r.sconv
    state_pre[...] = dot(normed[...], wst[...])
    for n in range(2):
        cols = pl.ds(n * 128, 128)
        pre = conv_at(state_pre[:, cols], taps_at(12, cols), vec[BC_BIAS, cols])
        sconv[:, cols] = (pre * sigmoid(pre)).astype(BF16)

    step_in = dot_t(normed[...], wsp[...]) + vec[STEP_BIAS, 0:128]
    small_e = jnp.exp(-jnp.abs(step_in))
    series = small_e * (1.0 - small_e * (0.5 - small_e * (1.0 / 3.0 - 0.25 * small_e)))
    step = jnp.maximum(step_in, 0.0) + jnp.where(small_e < 0.01, series, jnp.log(1.0 + small_e))
    decay = -jnp.exp(vec[A_LOG, 0:128])
    r.step_in[...] = step_in
    r.step[...] = step
    lower = (i0 >= i1).astype(F32)
    cum2 = jnp.dot(lower, step * decay, precision=HIGHEST, preferred_element_type=F32) * LOG2E
    r.cum2[...] = cum2
    r.cum2_t[...] = cum2.T
    r.cum2_ls[...] = (cum2 - jnp.log(step) * LOG2E).T
    b_rows, c_rows = sconv[:, 0:128], sconv[:, 128:256]
    r.scores[...] = dot_t(c_rows, b_rows) * r.linked[...]
    r.scores_t[...] = dot_t(b_rows, c_rows) * r.linked_t[...]

    lane = lax.broadcasted_iota(I32, (ROWS, 128), 1)
    lane_half = lax.broadcasted_iota(I32, (128, 128), 1) < 64

    def column(ref, h):
        return jnp.sum(jnp.where(lane == h, ref[...], 0.0), axis=1, keepdims=True)


    mixed = r.mixed

    def mix(p):
        cols = block_at(p, 128)
        x = vconv[:, cols]
        tops, lows = [], []
        for a in range(2):
            h = 2 * p + a
            cc = column(r.cum2, h)
            cr = r.cum2_ls[pl.ds(h, 1), :]
            w = jnp.exp2(jnp.minimum(cc[0:128] - cr[:, 0:128], 100.0)) * r.scores[0:128, 0:128]
            tops.append(dot(w.astype(BF16), x[0:128]))
            w = jnp.exp2(jnp.minimum(cc[128:256] - cr, 100.0)) * r.scores[128:256, :]
            lows.append(dot(w.astype(BF16), x))
        skip = jnp.where(lane_half[0:1], r.skip[2 * p], r.skip[2 * p + 1])
        xf = x.astype(F32)
        mixed[0:128, cols] = jnp.where(lane_half, tops[0], tops[1]) + skip * xf[0:128]
        mixed[128:256, cols] = jnp.where(lane_half, lows[0], lows[1]) + skip * xf[128:256]

    pl.loop(0, 3, unroll=3)(mix)
    pass_group("grad", 2, rb_g, yb_g)
    wave_gone("grad", 2, sb_g)
    pl.loop(3, 12, unroll=3)(mix)
    flip(normed, r.norm_f, r.norm_t)
    share_early(r.norm_f, r.norm_o)
    share_flipped("norm", r.norm_f, r.norm_t, "beside")

    upstream[:, own_cols] = dot(r.hot[...], rb_g[...]).astype(BF16)
    await_bytes(semaphore(rs, ("grad", 9)), yb_g)
    upstream[:, other_cols] = dot(r.hot[...], yb_g[...]).astype(BF16)
    wo_load.wait()
    d_scaled = r.d_scaled
    r.acc1[...] = jnp.zeros((ROWS, 128), F32)
    r.acc2[...] = jnp.zeros((ROWS, 128), F32)

    @pl.loop(0, 6, unroll=6)
    def _(n):
        cols = block_at(n, 256)
        ds = dot_t(upstream[...], r.wo[cols, :])
        d_scaled[:, cols] = ds
        g = gate_pre[:, cols]
        gated = mixed[:, cols] * g * sigmoid(g)
        sq = gated * gated
        cr = vec[NORM_GAIN, cols] * ds * gated
        r.acc1[...] += sq[:, 0:128] + sq[:, 128:256]
        r.acc2[...] += cr[:, 0:128] + cr[:, 128:256]

    def exchange_rows(col_a, col_b, out_buf, in_buf):
        both = jnp.where(lane == 0, col_a, jnp.where(lane == 1, col_b, 0.0))
        out_buf[...] = both.T[0:8, :]
        copy = send(out_buf, in_buf, other)

        def finish():
            copy.wait_recv()
            both = jnp.concatenate([out_buf[...] + in_buf[...], jnp.zeros((120, ROWS), F32)], axis=0)
            return both.T[:, 0:1], both.T[:, 1:2]

        return finish

    row_sums = exchange_rows(
        jnp.sum(r.acc1[...], axis=1, keepdims=True),
        jnp.sum(r.acc2[...], axis=1, keepdims=True),
        r.ex_a,
        r.ex_b,
    )
    r.cum2_ls[...] = jnp.zeros((128, ROWS), F32)
    flip(upstream, r.up_f, r.up_t)
    sum_sq, sum_cross = row_sums()
    inner = 2.0 * CH
    inverse = lax.rsqrt(sum_sq * (1.0 / inner) + norm_eps)
    cross = inverse * inverse * inverse * (1.0 / inner) * sum_cross
    r.acc1[...] = jnp.broadcast_to(inverse, (ROWS, 128))
    r.acc2[...] = jnp.broadcast_to(cross, (ROWS, 128))
    scaled4, gate4, value4, misc4 = r.scaled4, r.gate4, r.value4, r.misc4

    def gated_back(n):
        cols = block_at(n, 128)
        inv, crs = r.acc1[...], r.acc2[...]
        g, m, ds, gain = gate_pre[:, cols], mixed[:, cols], d_scaled[:, cols], vec[NORM_GAIN, cols]
        s = sigmoid(g)
        silu = g * s
        gated = m * silu
        gi = gated * inv
        scaled4[here, cols] = (gi * gain).astype(BF16)
        r.small[5:6, cols] = jnp.sum(ds * gi, axis=0, keepdims=True)
        d_gated = inv * ds * gain - gated * crs
        mixed[:, cols] = d_gated * silu
        gate4[here, cols] = (d_gated * m * (s * (1.0 + g * (1.0 - s)))).astype(BF16)

    def gated_part(first, last):
        pl.loop(first, last, unroll=2)(gated_back)

    half_f, half_o, half_in = d_scaled.at[:, pl.ds(0, HALF)], normed.at[:, pl.ds(0, HALF)], r.half_in
    flying = {}

    def project_other():
        @pl.loop(0, 3)
        def _(n):
            cols = pl.ds(pl.multiple_of((1 - side) * HALF + n * 256, 256), 256)
            half_o[:, block_at(n, 256)] = dot(scaled4[here, :], r.wo[:, cols]).astype(BF16)

        flying["out"] = send(half_o, half_in, other)

    def project_own():
        @pl.loop(0, 3)
        def _(n):
            cols = pl.ds(pl.multiple_of(side * HALF + n * 256, 256), 256)
            half_f[:, block_at(n, 256)] = dot(scaled4[here, :], r.wo[:, cols]) + stream[:, cols].astype(F32)

    lefts = {"out": r.up_t, "gate": r.norm_t, "value": r.norm_t, "misc": r.norm_t}
    rights = {"out": scaled4, "gate": gate4, "value": value4, "misc": misc4}
    outs = {"out": r.o_wo, "gate": r.o_gate, "value": r.o_value, "misc": r.o_misc}
    stores = []

    def store(src, dst, n):
        copy = pltpu.make_async_copy(src, dst, r.os.at[n])
        copy.start()
        return copy

    def ready(copy):
        if not copy.here:
            copy.wait_recv()

    pieces = {}
    for name, ref in rights.items():
        alone = sum(unit[2] for unit in UNITS if unit[0] == name and unit[3] == "z")
        group(name, ref.at[pl.ds(0, 3 * ROWS), pl.ds(0, ref.shape[1] - alone)])

    def up_swap():
        share_flipped("up", r.up_f, r.up_t, "up")

    def swap(name, first, width):
        ref, cols = rights[name], pl.ds(first, width)
        near_by = send(ref.at[here, cols], ref.at[beside, cols], sibling, gone=name)
        far_off = send(ref.at[here, cols], ref.at[over, cols], across, gone=name)
        pieces[name, first] = [width, near_by, far_off]

    def beside_here():
        if "beside" not in flying:
            flying["beside"] = True
            await_bytes(semaphore(rs, "beside"), r.norm_t.at[:, :, beside])

    def swap_near(name, first, width):
        ref, cols = rights[name], pl.ds(first, width)
        pieces[name, first] = [width, send(ref.at[here, cols], ref.at[beside, cols], sibling)]

    def relay(name, first):
        piece = pieces[name, first]
        ref, cols = rights[name], pl.ds(first, piece[0])
        ready(piece[2])
        piece.append(send(ref.at[over, cols], ref.at[cross_over, cols], sibling, gone=name))

    class Unit:
        def __init__(self, n):
            self.name, self.first, self.width, self.kind = UNITS[n]
            self.n, self.part, self.zbuf, self.kept = n, r.part[n], r.zbuf[n], r.kept[n]
            self.key = group(("unit", n), self.zbuf.at[pl.ds(0, 3)])
            self.stages = [self.compute if self.kind == "g" else self.compute_early, self.pass_outer, self.pass_inner, self.send_out, self.finish, self.keep_across]

        def go(self, stage):
            self.stages[stage]()

        def add(self, z, slot):
            self.part[z] = self.part[z] + self.zbuf[slot]

        def hop(self, z, slot, device, by):
            return send(self.part.at[z], self.zbuf.at[slot], device, by, self.key, (self.key, slot))

        def compute(self):
            lhs_ref, rhs_ref = lefts[self.name], rights[self.name]
            first, part = self.first, self.part
            side_name = "up" if self.name == "out" else "norm"
            if side_name == "norm":
                beside_here()
            if side_name not in flying:
                flying[side_name] = True
                await_bytes(semaphore(rs, side_name), lhs_ref.at[:, :, others if side_name == "up" else overs])
            for (name, start), piece in pieces.items():
                if name == self.name and start < first + self.width and first < start + piece[0]:
                    for copy in piece[1:]:
                        ready(copy)

            @pl.loop(0, self.width // 256)
            def _(n):
                lhs = lhs_ref[...].reshape(4 * SHARE, 4 * ROWS)
                rhs = rhs_ref[:, pl.ds(pl.multiple_of(first + n * 256, 256), 256)]
                part[:, 0, :, block_at(n, 256)] = dot(lhs, rhs).astype(BF16).reshape(4, SHARE, 256)

            self.leave()

        def compute_early(self):
            for copy in pieces[self.name, self.first][1:]:
                ready(copy)
            await_bytes(semaphore(rs, "early"), r.norm_o.at[:, :, beside])
            beside_here()
            rhs = rights[self.name][0 : 2 * ROWS, self.first : self.first + self.width]
            for n, lhs_ref in enumerate((r.norm_t, r.norm_o)):
                lhs = lhs_ref[:, :, 0 : 2 * ROWS].reshape(4 * SHARE, 2 * ROWS)
                self.part[:, n] = dot(lhs, rhs).astype(BF16).reshape(4, SHARE, self.width)
            self.leave()

        def leave(self):
            self.c3 = self.hop(far_outer, 0, near, is_outer)
            self.c2 = self.hop(far_inner, 1, near, is_outer)
            self.c1 = self.hop(z_inner, 2, near, is_outer)

        def pass_outer(self):
            @pl.when(is_inner)
            def _():
                self.c3.wait_recv()
                self.add(far_outer, 0)

            self.d2 = self.hop(far_outer, 3, facing, is_inner)

        def pass_inner(self):
            @pl.when(is_inner)
            def _():
                self.c2.wait_recv()
                self.add(far_inner, 1)

            self.d1 = self.hop(far_inner, 4, facing, is_inner)

        def send_out(self):
            @pl.when(is_inner)
            def _():
                self.d2.wait_recv()
                self.add(z_outer, 3)

            self.e1 = self.hop(z_outer, 0, near, is_inner)

        def finish(self):
            def end(*slots):
                sums = [self.part[zpos, n].astype(F32) for n in range(self.part.shape[1])]
                for slot in slots:
                    sums = [s + self.zbuf[slot, n].astype(F32) for n, s in enumerate(sums)]
                self.kept[...] = sums[0]
                if self.kind == "z":
                    r.over_out[...] = sums[1].astype(BF16)

            @pl.when(is_outer)
            def _():
                self.e1.wait_recv()
                end(0)

            @pl.when(is_inner)
            def _():
                self.c1.wait_recv()
                self.d1.wait_recv()
                end(2, 4)

            if self.kind == "z":
                self.cx = send(r.over_out, r.over_in, across)
            else:
                self.store()

        def keep_across(self):
            self.cx.wait_recv()
            self.kept[...] = self.kept[...] + r.over_in[...].astype(F32)
            self.store()

        def store(self):
            cols = pl.ds(self.first, self.width)
            stores.append(store(self.kept, outs[self.name].at[:, cols], self.n))

    units = [Unit(n) for n in range(len(UNITS))]
    head_row = lax.broadcasted_iota(I32, (32, ROWS), 0)

    def mixer_back(p):
        cols = block_at(p, 128)
        x = vconv[:, cols]
        xf = x.astype(F32)
        dy = mixed[:, cols]
        dyb = dy.astype(BF16)
        by_channel = jnp.sum(dy * xf, axis=0, keepdims=True)
        skips = r.small[6:7, CH + 128 : CH + 256]
        d_tops, d_lows = [], []
        for a in range(2):
            h = 2 * p + a
            half = (lane < 64) if a == 0 else (lane >= 64)
            of_head = jnp.sum(jnp.where(half[0:1], by_channel, 0.0), axis=1, keepdims=True)
            skips = skips + jnp.where(lane[0:1] == h, of_head, 0.0)
            xa = jnp.where(half, xf, 0.0)
            xab = xa.astype(BF16)
            cc = column(r.cum2, h)
            st = column(r.step, h)
            cr = r.cum2_t[pl.ds(h, 1), :]
            w = jnp.exp2(jnp.minimum(cr - cc[0:128], 0.0))
            sc = r.scores_t[0:128, :]
            v_top = dot((w * sc).astype(BF16), dyb)
            q = dot_t(xab[0:128], dyb) * w * st[0:128]
            r.dst_acc[0:128, :] += q
            g_top = q * sc
            w = jnp.exp2(jnp.minimum(cr[:, 128:256] - cc[128:256], 0.0))
            sc = r.scores_t[128:256, 128:256]
            v_low = dot((w * sc).astype(BF16), dyb[128:256])
            q = dot_t(xab[128:256], dyb[128:256]) * w * st[128:256]
            r.dst_acc[128:256, 128:256] += q
            g_low = q * sc
            top_sums = jnp.sum(g_top, axis=0, keepdims=True)
            low_sums = jnp.sum(g_low, axis=0, keepdims=True)
            col_sums = jnp.concatenate([top_sums[:, 0:128], top_sums[:, 128:256] + low_sums], axis=1)
            r.cum2_ls[0:32, :] += jnp.where(head_row == h, col_sums, 0.0)
            row_sums = jnp.concatenate(
                [
                    jnp.sum(g_top[:, 0:128] + g_top[:, 128:256], axis=1, keepdims=True),
                    jnp.sum(g_low, axis=1, keepdims=True),
                ],
                axis=0,
            )
            direct = jnp.concatenate(
                [
                    jnp.sum(xa[0:128] * v_top, axis=1, keepdims=True),
                    jnp.sum(xa[128:256] * v_low, axis=1, keepdims=True),
                ],
                axis=0,
            )
            r.dcol[...] += jnp.where(lane == h, row_sums, 0.0)
            r.dsd[...] += jnp.where(lane == h, direct, 0.0)
            d_tops.append(st[0:128] * v_top)
            d_lows.append(st[128:256] * v_low)
        r.small[6:7, CH + 128 : CH + 256] = skips
        d_conv = jnp.concatenate(
            [jnp.where(lane_half, d_tops[0], d_tops[1]), jnp.where(lane_half, d_lows[0], d_lows[1])],
            axis=0,
        )
        d_conv = d_conv + jnp.where(lane_half[0:1], r.skip[2 * p], r.skip[2 * p + 1]) * dy
        d_value, sums, bias_sum = conv_back(value_pre[:, cols], taps_at(0, cols), vec[X_BIAS, cols], d_conv)
        value4[here, cols] = d_value.astype(BF16)
        for k in range(4):
            r.small[k : k + 1, cols] = sums[k]
        r.small[4:5, cols] = bias_sum

    def mixer_part(first, last):
        pl.loop(first, last, unroll=2)(mixer_back)

    def send_back(name, src, dst):
        group(name, src.at[pl.ds(0, ROWS - PER)])
        for dz in (2, 3, 1, 0):
            deal(dz, src, dst, name, name)
        dst[rows_of(me)] = src[rows_of(me)]

    def return_out():
        ready(flying["out"])
        result = (half_f[...] + half_in[...].astype(F32)).astype(BF16)
        yb_h[...] = dot(r.hot_t[...], result).astype(BF16)
        send_back("back_o", yb_h, r.back_o)

    def finish_out():
        await_bytes(semaphore(rs, "back_o"), r.back_o.at[pl.ds(0, ROWS - PER)])
        r.res_o[...] = dot(r.send_hot_t[...], r.back_o[...]).astype(BF16)
        stores.append(store(r.res_o, r.o_out, len(UNITS) + 1))

    d_state = r.d_state
    state_own = pl.ds(pl.multiple_of(side * 128, 128), 128)
    state_other = pl.ds(pl.multiple_of((1 - side) * 128, 128), 128)

    def states_back():
        d_scores_t = r.dst_acc[...] * r.linked_t[...]
        d_conv_s = r.linked
        d_conv_s[:, 0:128] = dot(d_scores_t.astype(BF16), c_rows)
        d_conv_s[:, 128:256] = dot(d_scores_t.T.astype(BF16), b_rows)
        for n in range(2):
            cols = pl.ds(n * 128, 128)
            d_pre, sums, bias_sum = conv_back(
                state_pre[:, cols], taps_at(12, cols), vec[BC_BIAS, cols], d_conv_s[:, cols]
            )
            d_state[:, cols] = d_pre
            for k in range(4):
                r.small[k : k + 1, CH + n * 128 : CH + (n + 1) * 128] = sums[k]
            r.small[4:5, CH + n * 128 : CH + (n + 1) * 128] = bias_sum
        r.st_out[...] = d_state[:, state_other].astype(BF16)
        flying["state"] = send(r.st_out, r.st_in, other)
        d_cum = r.cum2_ls[...].T - r.dcol[...]
        upper = (i0 <= i1).astype(F32)
        d_rate = jnp.dot(upper, d_cum, precision=HIGHEST, preferred_element_type=F32)
        d_step = (r.dsd[...] + d_rate * decay) * sigmoid(r.step_in[...])
        r.small[5:6, CH : CH + 128] = jnp.sum(d_step, axis=0, keepdims=True)
        r.small[6:7, CH : CH + 128] = jnp.sum(d_rate * r.step[...], axis=0, keepdims=True) * decay
        misc4[here, 128:256] = d_step.astype(BF16)
        r.acc1[...] = jnp.zeros((ROWS, 128), F32)
        r.st_low[...] = d_state[...].astype(BF16)

    def add_states():
        ready(flying["state"])
        misc4[here, 0:128] = (d_state[:, state_own] + r.st_in[...].astype(F32)).astype(BF16)

    dhalf_f, dhalf_o, dhalf_in = d_scaled.at[:, pl.ds(HALF, HALF)], normed.at[:, pl.ds(HALF, HALF)], r.dhalf_in

    def d_normed_at(first):
        rows = pl.ds(pl.multiple_of(first, 256), 256)
        out = dot_t(gate4[here, :], r.wg[rows, :]) + dot_t(value4[here, :], r.wv[rows, :])
        out = out + dot_t(r.st_low[...], r.wst[rows, :])
        out = out + dot(misc4[here, 128:256], wsp[:, rows])
        part = out * vec[PRE_GAIN, rows] * stream[:, rows].astype(F32)
        r.acc1[...] += part[:, 0:128] + part[:, 128:256]
        return out

    def normed_other():
        @pl.loop(0, 3)
        def _(n):
            dhalf_o[:, block_at(n, 256)] = d_normed_at((1 - side) * HALF + n * 256).astype(BF16)

        flying["norm"] = send(dhalf_o, dhalf_in, other)

    def normed_own():
        @pl.loop(0, 3)
        def _(n):
            dhalf_f[:, block_at(n, 256)] = d_normed_at(side * HALF + n * 256)

        flying["rows"] = exchange_rows(
            jnp.sum(r.acc1[...], axis=1, keepdims=True), jnp.zeros((ROWS, 1), F32), r.ex_c, r.ex_d
        )

    small = r.small

    def return_grad():
        row_cross, _ = flying["rows"]()
        ready(flying["norm"])
        flying["out"].wait_send()
        scale = r.nscale[:, 0:1]
        factor = scale * scale * scale * (1.0 / FULL) * row_cross
        for n in range(6):
            cols = pl.ds(n * 128, 128)
            mine = pl.ds(pl.multiple_of(side * HALF + n * 128, 128), 128)
            dn = dhalf_f[:, cols] + dhalf_in[:, cols].astype(F32)
            s = stream[:, mine].astype(F32)
            small[7:8, n * 128 : (n + 1) * 128] = jnp.sum(dn * s * scale, axis=0, keepdims=True)
            grad = upstream[:, mine].astype(F32) + scale * vec[PRE_GAIN, mine] * dn - s * factor
            half_o[:, cols] = grad.astype(BF16)
        yb_g[...] = dot(r.hot_t[...], half_o[...]).astype(BF16)
        send_back("back_g", yb_g, r.back_g)

    def finish_grad():
        await_bytes(semaphore(rs, "back_g"), r.back_g.at[pl.ds(0, ROWS - PER)])
        r.res_g[...] = dot(r.send_hot_t[...], r.back_g[...]).astype(BF16)
        stores.append(store(r.res_g, r.o_hid, len(UNITS) + 2))

    lasts = pl.ds(CH, 256)

    def small_tensor():
        flying["small"] = send(small.at[:, lasts], r.sm_y, other)

    def small_tensor_end():
        copy = flying["small"]
        copy.wait_send()
        copy.wait_recv()
        keep_rows = lax.broadcasted_iota(I32, (8, 256), 0) < 5
        small[:, lasts] = small[:, lasts] + jnp.where(keep_rows, r.sm_y[...], 0.0)

    partners = [sibling, across, near, facing]

    def small_start(n):
        flying[n] = send(small, r.sm_a[n], partners[n])

    def small_end(n):
        flying[n].wait_send()
        flying[n].wait_recv()
        small[...] = small[...] + r.sm_a[n][...]

    gated_part(0, 2)
    swap_near("gate", 0, 256)
    gated_part(2, 4)
    swap("gate", 256, 256)
    gated_part(4, 8)
    gated_part(8, 12)
    swap("gate", 512, 256)
    units[0].go(0)
    project_other()
    swap("gate", 1024, 512)
    relay("gate", 256)
    mixer_part(0, 4)
    units[1].go(0)
    relay("gate", 512)
    project_own()
    units[0].go(1)
    swap("value", 0, 512)
    swap("out", 1024, 512)
    units[2].go(0)
    relay("gate", 1024)
    swap("gate", 768, 256)
    up_swap()
    return_out()
    mixer_part(4, 8)
    units[2].go(1)
    relay("value", 0)
    units[4].go(0)
    mixer_part(8, 12)
    units[8].go(0)
    states_back()
    relay("gate", 768)
    units[4].go(1)
    normed_other()
    units[1].go(1)
    units[2].go(2)
    swap("value", 1024, 512)
    units[0].go(2)
    units[8].go(1)
    units[2].go(3)
    relay("out", 1024)
    swap("value", 512, 512)
    swap("out", 512, 512)
    units[3].go(0)
    units[8].go(2)
    add_states()
    units[1].go(2)
    normed_own()
    swap("misc", 0, 256)
    units[7].go(0)
    swap("out", 0, 512)
    units[4].go(2)
    units[4].go(3)
    return_grad()
    units[0].go(3)
    units[8].go(3)
    relay("value", 1024)
    units[7].go(1)
    units[7].go(2)
    units[3].go(1)
    units[10].go(0)
    relay("value", 512)
    units[3].go(2)
    small_tensor()
    units[9].go(0)
    relay("out", 512)
    units[10].go(1)
    units[9].go(1)
    units[7].go(3)
    units[2].go(4)
    finish_out()
    units[6].go(0)
    small_tensor_end()
    relay("misc", 0)
    units[4].go(4)
    units[0].go(4)
    small_start(0)
    units[9].go(2)
    units[11].go(0)
    units[3].go(3)
    units[8].go(4)
    units[6].go(1)
    small_end(0)
    relay("out", 0)
    small_start(1)
    units[10].go(2)
    units[6].go(2)
    units[10].go(3)
    units[9].go(3)
    units[7].go(4)
    units[3].go(4)
    units[5].go(0)
    units[6].go(3)
    units[1].go(3)
    units[11].go(1)
    units[0].go(5)
    units[11].go(2)
    units[9].go(4)
    units[10].go(4)
    small_end(1)
    units[5].go(1)
    small_start(2)
    units[5].go(2)
    units[1].go(4)
    units[11].go(3)
    units[5].go(3)
    small_end(2)
    small_start(3)
    finish_grad()
    units[11].go(4)
    units[6].go(4)
    units[5].go(4)
    small_end(3)
    stores.append(store(small, r.o_small, len(UNITS)))
    for copy in started:
        copy.wait_send()
    assert len(taken[0]) == SENDS and len(taken[1]) == ARRIVALS
    for sem, ref in leaving:
        await_bytes(sem, ref)
    for copy in stores:
        copy.wait()


def scratch():
    vmem, dma = pltpu.VMEM, pltpu.SemaphoreType.DMA
    square, wide = (ROWS, ROWS), (ROWS, CH)
    def rows(dtype, width):
        return vmem((ROWS, width), dtype)

    return dict(
        wg=vmem((FULL, CH), BF16),
        wv=vmem((FULL, CH), BF16),
        wo=vmem((CH, FULL), BF16),
        pair=vmem((3, FULL, 2, 128), BF16),
        send_hot_t=vmem(square, BF16),
        hot=vmem(square, BF16),
        hot_t=vmem(square, BF16),
        sb_h=rows(BF16, HALF),
        rb_h=rows(BF16, HALF),
        sb_i=vmem((PEERS, 1, 128), F32),
        rb_i=vmem((PEERS, 1, 128), F32),
        sb_g=rows(BF16, HALF),
        rb_g=rows(BF16, HALF),
        yb_h=rows(BF16, HALF),
        yb_g=rows(BF16, HALF),
        half_in=rows(BF16, HALF),
        dhalf_in=rows(BF16, HALF),
        back_o=rows(BF16, HALF),
        back_g=rows(BF16, HALF),
        masks=vmem((3, ROWS, 128), F32),
        linked=vmem(square, F32),
        linked_t=vmem(square, F32),
        scores=vmem(square, F32),
        scores_t=vmem(square, F32),
        dst_acc=vmem(square, F32),
        small=vmem((8, CH + 256), F32),
        params_v=[
            vmem((4, CH), BF16),
            vmem((4, 256), BF16),
            vmem((HEADS, FULL), BF16),
            vmem((CH,), BF16),
            vmem((CH,), BF16),
            vmem((FULL,), BF16),
            vmem((256,), BF16),
            vmem((HEADS,), F32),
            vmem((HEADS,), F32),
        ],
        res_o=rows(BF16, HALF),
        res_g=rows(BF16, HALF),
        kept=[vmem((SHARE, width), F32) for _, _, width, _ in UNITS],
        vec=vmem((16, CH), F32),
        wsp=vmem((128, FULL), BF16),
        wst=vmem((FULL, 256), BF16),
        cum2_t=vmem((128, ROWS), F32),
        cum2_ls=vmem((128, ROWS), F32),
        stream=vmem(wide, BF16),
        upstream=vmem(wide, BF16),
        normed=vmem(wide, BF16),
        vconv=vmem(wide, BF16),
        gate_pre=vmem(wide, F32),
        value_pre=vmem(wide, F32),
        mixed=vmem(wide, F32),
        d_scaled=vmem(wide, F32),
        state_pre=rows(F32, 256),
        d_state=rows(F32, 256),
        sconv=rows(BF16, 256),
        st_low=rows(BF16, 256),
        st_out=rows(BF16, 128),
        st_in=rows(BF16, 128),
        scaled4=vmem((4 * ROWS, CH), BF16),
        gate4=vmem((4 * ROWS, CH), BF16),
        value4=vmem((4 * ROWS, CH), BF16),
        misc4=vmem((4 * ROWS, 256), BF16),
        norm_t=vmem((4, SHARE, 4 * ROWS), BF16),
        up_t=vmem((4, SHARE, 4 * ROWS), BF16),
        norm_f=vmem((4, 4, SHARE, ROWS), BF16),
        up_f=vmem((4, 4, SHARE, ROWS), BF16),
        nscale=rows(F32, 128),
        acc1=rows(F32, 128),
        acc2=rows(F32, 128),
        dcol=rows(F32, 128),
        dsd=rows(F32, 128),
        step_in=rows(F32, 128),
        step=rows(F32, 128),
        cum2=rows(F32, 128),
        ex_a=vmem((8, ROWS), F32),
        ex_b=vmem((8, ROWS), F32),
        ex_c=vmem((8, ROWS), F32),
        ex_d=vmem((8, ROWS), F32),
        sm_y=vmem((8, 256), F32),
        sm_a=[vmem((8, CH + 256), F32) for _ in range(4)],
        part=[vmem((4, 2 if kind == "z" else 1, SHARE, width), BF16) for _, _, width, kind in UNITS],
        zbuf=[vmem((5, 2 if kind == "z" else 1, SHARE, width), BF16) for _, _, width, kind in UNITS],
        over_out=vmem((SHARE, 256), BF16),
        over_in=vmem((SHARE, 256), BF16),
        norm_o=vmem((4, SHARE, 2 * ROWS), BF16),
        ss=dma((SENDS,)),
        rs=dma((ARRIVALS,)),
        ls=dma((16,)),
        os=dma((len(UNITS) + 3,)),
    )


SENDS = 30 + len(UNITS)
ARRIVALS = 74 + 5 * len(UNITS)


def listed(v):
    return v if isinstance(v, list) else [v]


def finish_body(*refs):
    wo, gate, value, misc, small, out, hid = refs[:7]
    outs, scratch_refs = refs[7:22], refs[22:]
    misc_v, small_v, *held = scratch_refs[:-1]
    sems = scratch_refs[-1]
    (
        out_v, hid_v, pre, in_v, state, step, cx, cxb, cb, cbb, bias, log, skip, gain, wo_v
    ) = held

    def move(src, dst, n):
        copy = pltpu.make_async_copy(src, dst, sems.at[n])
        copy.start()
        return copy

    moves = (
        (small, small_v),
        (misc, misc_v),
        (gate, in_v.at[:, 0, :]),
        (value, in_v.at[:, 1, :]),
        (wo, wo_v),
        (out, out_v),
        (hid, hid_v),
    )
    loads = [move(src, dst, n) for n, (src, dst) in enumerate(moves)]
    stores = []

    def keep(*which):
        for n in which:
            stores.append(move(held[n], outs[n], len(moves) + n))

    loads[0].wait()
    pre[...] = small_v[7, 0:HALF]
    cx[...] = small_v[0:4, 0:CH]
    cxb[...] = small_v[4, 0:CH]
    cb[...] = small_v[0:4, CH:]
    cbb[...] = small_v[4, CH:]
    bias[...] = small_v[5, CH : CH + HEADS]
    log[...] = small_v[6, CH : CH + HEADS]
    skip[...] = small_v[6, CH + 128 : CH + 128 + HEADS]
    gain[...] = small_v[5, 0:CH]
    keep(2, 6, 7, 8, 9, 10, 11, 12, 13)
    loads[1].wait()
    state[...] = misc_v[:, 0:128]
    step[...] = misc_v[:, 128:256].T[0:HEADS]
    keep(4, 5)
    loads[2].wait()
    loads[3].wait()
    keep(3)
    for n, which in ((4, 14), (5, 0), (6, 1)):
        loads[n].wait()
        keep(which)
    for copy in stores:
        copy.wait()


def one_kernel(
    hidden_in,
    out_grad,
    seq_lengths,
    deal_to,
    pre_gain,
    w_in,
    w_state,
    w_step,
    conv_x,
    conv_x_bias,
    conv_bc,
    conv_bc_bias,
    step_bias,
    a_log,
    skip,
    norm_gain,
    w_out,
):
    inputs = dict(
        hid=hidden_in,
        ogr=out_grad,
        lens=seq_lengths,
        deal=deal_to.reshape(1, ROWS),
        skip=skip,
        w_in=w_in,
        wo_hbm=w_out,
        wst_hbm=w_state,
        params=[
            conv_x,
            conv_bc,
            w_step.T,
            conv_x_bias,
            norm_gain,
            pre_gain,
            conv_bc_bias,
            step_bias,
            a_log,
        ],
    )
    in_vmem = pl.BlockSpec(memory_space=pltpu.VMEM)
    places = dict(lens=pltpu.SMEM, skip=pltpu.SMEM, deal=pltpu.VMEM)
    f32_out = partial(jax.ShapeDtypeStruct, dtype=F32)
    half = jax.ShapeDtypeStruct((ROWS, HALF), BF16)
    outputs = dict(
        o_wo=f32_out((SHARE, CH)),
        o_gate=f32_out((SHARE, CH)),
        o_value=f32_out((SHARE, CH)),
        o_misc=f32_out((SHARE, 256)),
        o_small=f32_out((8, CH + 256)),
        o_out=half,
        o_hid=half,
    )
    room = scratch()
    flat = [ref for shape in room.values() for ref in listed(shape)]
    made = pl.pallas_call(
        partial(block_body, {**inputs, **outputs, **room}),
        out_shape=list(outputs.values()),
        in_specs=[pl.BlockSpec(memory_space=places.get(n, pl.ANY)) for n, v in inputs.items() for _ in listed(v)],
        out_specs=[pl.BlockSpec(memory_space=pl.ANY)] * len(outputs),
        scratch_shapes=flat,
        compiler_params=pltpu.CompilerParams(
            collective_id=0, has_side_effects=True, vmem_limit_bytes=VMEM_BYTES
        ),
        name="block",
    )(*(v for value in inputs.values() for v in listed(value)))
    shapes = [(HALF,), (SHARE, 2, CH), (SHARE, 128), (HEADS, SHARE), (4, CH), (CH,), (4, 256), (256,)]
    shapes += [(HEADS,)] * 3 + [(CH,), (SHARE, CH)]
    any_place = pl.BlockSpec(memory_space=pl.ANY)
    made_shapes = [half, half, *(f32_out(s) for s in shapes)]
    results = pl.pallas_call(
        finish_body,
        out_shape=made_shapes,
        in_specs=[any_place] * len(made),
        out_specs=[any_place] * len(made_shapes),
        scratch_shapes=[
            pltpu.VMEM((SHARE, 256), F32),
            pltpu.VMEM((8, CH + 256), F32),
            *(pltpu.VMEM(s.shape, s.dtype) for s in made_shapes),
            pltpu.SemaphoreType.DMA((len(made) + len(made_shapes),)),
        ],
        compiler_params=pltpu.CompilerParams(vmem_limit_bytes=VMEM_BYTES),
        name="finish",
    )(*made)
    return (*results[:5], results[5].T, *results[6:14], results[14].T)


VMEM_BYTES = 65_400_000


def fits(mesh, args):
    return mesh.shape["dp"] == PEERS and mesh.shape["tensor"] == 2 and args[0].shape == (PEERS * ROWS, FULL)


def solution(mesh):
    in_specs = (
        P("dp", "tensor"),
        P("dp", "tensor"),
        P("dp", None),
        P("dp"),
        P(),
        P(None, None, "tensor"),
        P(),
        P(None, "tensor"),
        P(None, "tensor"),
        P("tensor"),
        P(),
        P(),
        P("tensor"),
        P("tensor"),
        P("tensor"),
        P("tensor"),
        P("tensor", None),
    )
    out_specs = (
        P("dp", "tensor"),
        P("dp", "tensor"),
        P("tensor"),
        P("dp", None, "tensor"),
        P("dp", "tensor"),
        P("dp", "tensor"),
        P(None, "tensor"),
        P("tensor"),
        P(),
        P(),
        P("tensor"),
        P("tensor"),
        P("tensor"),
        P("tensor"),
        P("tensor", "dp"),
    )

    def whole(*args):
        local = one_kernel if fits(mesh, args) else shards
        mapped = jax.shard_map(
            local, mesh=mesh, in_specs=in_specs, out_specs=out_specs, check_vma=False
        )
        return mapped(*args)

    return whole
```
